32 devices in a mesh: group: 4 (over z), expert: 8 (over y, x, core).
Axes of the slice: x: 2, y: 2, z: 4, core: 2. Of those that a mesh axis runs over, the one named last changes fastest.
Arguments:
- tokens: bfloat16 [2, 4096, 1536], P(None, ('group', 'expert')), may hold values from -6 to 6
- cotangent: bfloat16 [2, 4096, 1536], P(None, ('group', 'expert')), may hold values from -6 to 6
- routes: int32 [2, 4096, 8], P(None, ('group', 'expert')), may hold values from 0 to 31, all different within a row; in each aligned block of 128 rows (0 to 127, 128 to 255, ..., all dimensions but the last counted through in order) at most 48 rows name the same one
- norm_one: bfloat16 [1536], P('group'), may hold values from 0.5 to 1.5
- query_key_value_weight: bfloat16 [1536, 2560], P('group'), may hold values from -0.15625 to 0.15625
- out_weight: bfloat16 [1536, 1536], P('group'), may hold values from -3.5 to 3.5
- norm_two: bfloat16 [1536], P('group'), may hold values from 0.5 to 1.5
- router_weight: bfloat16 [1536, 32], P('group'), may hold values from -0.078125 to 0.078125
- gate_weight: bfloat16 [32, 1536, 512], P('expert', 'group'), may hold values from -0.15625 to 0.15625
- up_weight: bfloat16 [32, 1536, 512], P('expert', 'group'), may hold values from -0.15625 to 0.15625
- down_weight: bfloat16 [32, 512, 1536], P('expert', None, 'group'), may hold values from -1 to 1
Outputs:
- block_out: bfloat16 [2, 4096, 1536], P(None, ('group', 'expert'))
- input_grad: float32 [2, 4096, 1536], P(None, ('group', 'expert'))
- norm_one_grad: float32 [1536], P('group')
- qkv_grad: float32 [1536, 2560], P('group')
- out_grad: float32 [1536, 1536], P('group')
- norm_two_grad: float32 [1536], P('group')
- router_grad: float32 [1536, 32], P('group')
- gate_grad: float32 [32, 1536, 512], P('expert', 'group')
- up_grad: float32 [32, 1536, 512], P('expert', 'group')
- down_grad: float32 [32, 512, 1536], P('expert', None, 'group')
The draws below stay inside these ranges and needn't reach their ends.
Inputs may be any that keep to these rules, and one draw needn't show every extreme that they name: `routes`: in the rows of one device in one micro-batch (aligned blocks of 128 rows) no expert is named more than 48 times, and in some blocks one is named exactly 48 times; a row names 8 different experts.
All inputs are finite; a program needn't handle non-finite values.
Results may differ from the reference program's by a relative error of at most 0.022.
Values may be sent and summed in bfloat16 or wider, within the bound.
A program may use at most 256 MiB of HBM per device.

```python
import math
import jax
import jax.numpy as jnp
import numpy as np
from jax import lax

MODEL_WIDTH = 1536
QUERY_HEADS = 24
KEY_VALUE_HEADS = 8
HEAD_SIZE = 64
FF = 512
TOPK = 8
EXPERTS = 32
MB = 2
CONT = 256
PR_DEV = 64
PROMPT = 512
MOST = 48
TOKENS = 4096
N_GROUP = 4
N_EXPERT = 8


def shard_levels(stream_key, extent, pieces, smallest, top_value):
    level = 1.0
    for axis_at, shards_of in pieces:
        steps = jax.random.uniform(jax.random.fold_in(jax.random.fold_in(stream_key, 6), axis_at), (shards_of,), jnp.float32, smallest / len(pieces), top_value / len(pieces))
        level = level * jnp.repeat(jnp.exp(steps), extent[axis_at] // shards_of).reshape((-1,) + (1,) * (len(extent) - 1 - axis_at))
    return level


def assign_block(stream_key, own, number, rows, number_of, top, most, slope):
    order = jax.random.permutation(stream_key, number_of)
    crowded, ordinary = shares(number_of, rows * top, most, slope, True), shares(number_of, rows * top, most, slope, False)
    places = jnp.arange(number_of)

    def named(sizes, turn):
        used = int((sizes > 0).sum())
        fixed = max(1, used // 4)
        moved = fixed + (places - fixed + turn * (used - fixed)) % max(1, number_of - fixed)
        return jnp.zeros((number_of,), jnp.int32).at[order[jnp.where(places < fixed, places, moved)]].set(jnp.asarray(sizes, jnp.int32))

    sizes = jnp.where(number % 4 == 0, named(crowded, number // 4), named(ordinary, number - number // 4 - 1))
    mixed = jax.random.permutation(jax.random.fold_in(own, 3), number_of)
    donor, sink = mixed[0:number_of // 2 * 2:2], mixed[1:number_of // 2 * 2:2]
    room = jnp.minimum(sizes[donor] - 1, most - sizes[sink]) // 2
    room = jnp.where((donor == order[0]) | (sink == order[0]) | (sizes[sink] == 0), 0, jnp.maximum(room, 0))
    moved = jax.random.randint(jax.random.fold_in(own, 4), (number_of // 2,), 0, 1 << 20) % (room + 1)
    sizes = sizes.at[donor].add(-moved).at[sink].add(moved)
    items = jnp.searchsorted(jnp.cumsum(sizes), jnp.arange(rows * top), side="right").astype(jnp.int32)
    grid = items.reshape(top, rows).T
    grid = grid[jax.random.permutation(jax.random.fold_in(own, 1), rows)]
    turn = jax.random.randint(jax.random.fold_in(own, 2), (rows, 1), 0, top)
    return jnp.take_along_axis(grid, (jnp.arange(top)[None, :] + turn) % top, axis=1)


def shares(amount, total, bound, lean, full):
    portions = [(1 << 20) // math.isqrt(grade ** lean) + 1 for grade in range(1, amount + 1)]
    largest = bound if full else min(bound, max(-(-total // amount), total * portions[0] // sum(portions)))
    least = 1 if total - largest >= amount - 1 else 0
    holding, rest = [largest] + [least] * (amount - 1), total - largest - least * (amount - 1)
    while rest > 0:
        movable = [i for i in range(1, amount) if holding[i] < largest] or [i for i in range(1, amount) if holding[i] < bound]
        pool, left = sum([portions[i] for i in movable]), rest
        for i in movable:
            addition = min(bound - holding[i], max(1, left * portions[i] // pool), rest)
            holding[i] = holding[i] + addition
            rest = rest - addition
    return np.array(holding)


def bell_draw(rng, shape, width, reach, cuts=(), kind=jnp.bfloat16):
    loudness = shard_levels(rng, shape, cuts, -0.22, 0.18) if cuts else 1.0
    values = jax.random.normal(rng, shape, jnp.float32) * width * loudness
    return jnp.minimum(jnp.maximum(values, -reach), reach).astype(kind)


def setup_inputs(seed: int = 0) -> dict:
    splits = jax.random.split(jax.random.key(seed), 12)
    tokens = bell_draw(splits[0], (MB, TOKENS, MODEL_WIDTH), 1.0, 6.0, ((1, 32),))
    cotangent = bell_draw(splits[1], (MB, TOKENS, MODEL_WIDTH), 1.0, 6.0, ((1, 32),))
    routes_keys = jax.random.split(jax.random.fold_in(splits[2], 1), MB * TOKENS // (2 * PR_DEV))
    routes_turns = jax.random.permutation(jax.random.fold_in(splits[2], 3), MB * TOKENS // (2 * PR_DEV))
    routes = jax.vmap(lambda own, number: assign_block(jax.random.fold_in(splits[2], 2), own, number, 2 * PR_DEV, EXPERTS, TOPK, MOST, 1))(routes_keys, routes_turns).reshape((MB, TOKENS, TOPK))
    norm_one = jnp.clip(1.0 + 0.1 * jax.random.normal(splits[3], (MODEL_WIDTH,), jnp.float32), 0.5, 1.5).astype(jnp.bfloat16)
    query_key_value_weight = bell_draw(splits[4], (MODEL_WIDTH, (QUERY_HEADS + 2 * KEY_VALUE_HEADS) * HEAD_SIZE), MODEL_WIDTH ** -0.5, 0.15625, ((0, 4),))
    out_weight = bell_draw(splits[5], (QUERY_HEADS * HEAD_SIZE, MODEL_WIDTH), (max(1, QUERY_HEADS * HEAD_SIZE // 512)) ** -0.5, 3.5, ((0, 4),))
    norm_two = jnp.clip(1.0 + 0.1 * jax.random.normal(splits[6], (MODEL_WIDTH,), jnp.float32), 0.5, 1.5).astype(jnp.bfloat16)
    router_weight = bell_draw(splits[7], (MODEL_WIDTH, EXPERTS), (4 * MODEL_WIDTH) ** -0.5, 0.078125, ((0, 4),))
    gate_weight = bell_draw(splits[8], (EXPERTS, MODEL_WIDTH, FF), MODEL_WIDTH ** -0.5, 0.15625, ((0, 8), (1, 4)))
    up_weight = bell_draw(splits[9], (EXPERTS, MODEL_WIDTH, FF), MODEL_WIDTH ** -0.5, 0.15625, ((0, 8), (1, 4)))
    down_weight = bell_draw(splits[10], (EXPERTS, FF, MODEL_WIDTH), (FF // 16) ** -0.5, 1.0, ((0, 8), (2, 4)))
    return dict(tokens=tokens, cotangent=cotangent, routes=routes, norm_one=norm_one, query_key_value_weight=query_key_value_weight, out_weight=out_weight, norm_two=norm_two, router_weight=router_weight, gate_weight=gate_weight, up_weight=up_weight, down_weight=down_weight)


@jax.custom_vjp
def lower_precision(v):
    return lax.optimization_barrier(v.astype(jnp.bfloat16)).astype(jnp.float32)

@jax.custom_vjp
def low_back(v):
    return v

def low_keep(v):
    return (lower_precision(v), None)

def low_pass(kept, grad):
    return (grad,)

def back_keep(v):
    return (v, None)

def back_low(kept, grad):
    return (lower_precision(grad),)
lower_precision.defvjp(low_keep, low_pass)
low_back.defvjp(back_keep, back_low)
HIGHEST = lax.Precision.HIGHEST
SCORE_SCALE = 0.125

def rms_scale(values, gain):
    return values * lax.rsqrt(lax.optimization_barrier(jnp.mean(values * values, axis=-1, keepdims=True)) + 1e-05) * gain

def rotate_halves(values, positions):
    half_dim = values.shape[-1] // 2
    frequency = 10000.0 ** (-jnp.arange(half_dim, dtype=jnp.float32) * (2.0 / values.shape[-1]))
    angle_table = positions.astype(jnp.float32)[:, None] * frequency[None, :]
    cosine_table = jnp.cos(angle_table)[:, None, :]
    sine_table = jnp.sin(angle_table)[:, None, :]
    first_half = values[..., :half_dim]
    second = values[..., half_dim:]
    return jnp.concatenate([first_half * cosine_table - second * sine_table, second * cosine_table + first_half * sine_table], axis=-1)

def token_meta(index):
    tokens_per_device = 2 * PR_DEV
    device_id = index // tokens_per_device
    local_id = index % tokens_per_device
    is_prompt = local_id < PR_DEV
    cont_index = device_id * PR_DEV + local_id - PR_DEV
    seq_id = jnp.where(is_prompt, -1, cont_index // CONT).astype(jnp.int32)
    position = jnp.where(is_prompt, device_id * PR_DEV + local_id, PROMPT + cont_index % CONT).astype(jnp.int32)
    return (is_prompt, seq_id, position)

def micro_forward(params, inputs, route_rows):
    norm_one, query_key_value_weight, out_weight, norm_two, router_weight, gate_weight, up_weight, down_weight = params
    tokens_per_device = 2 * PR_DEV
    row_length = N_EXPERT * tokens_per_device
    query_width = QUERY_HEADS * HEAD_SIZE
    key_value_width = KEY_VALUE_HEADS * HEAD_SIZE
    repeat_heads = QUERY_HEADS // KEY_VALUE_HEADS
    normed = lower_precision(rms_scale(inputs, norm_one))
    project_inputs = jnp.dot(normed, query_key_value_weight, precision=HIGHEST)
    query_pre = low_back(project_inputs[:, :query_width])
    key_before_rotation = low_back(project_inputs[:, query_width:query_width + key_value_width])
    value_before_split = low_back(project_inputs[:, query_width + key_value_width:])
    is_prompt, seq_id, position = token_meta(jnp.arange(row_length, dtype=jnp.int32))
    every_position = jnp.tile(position, N_GROUP)
    heads_of_query = lower_precision(rotate_halves(query_pre.reshape(-1, QUERY_HEADS, HEAD_SIZE), every_position))
    heads_of_key = lower_precision(rotate_halves(key_before_rotation.reshape(-1, KEY_VALUE_HEADS, HEAD_SIZE), every_position))
    heads_of_value = lower_precision(value_before_split.reshape(-1, KEY_VALUE_HEADS, HEAD_SIZE))
    allowed = (is_prompt[None, :] | (seq_id[:, None] == seq_id[None, :])) & (position[None, :] <= position[:, None])

    def attend_single_row(row_inputs):
        query_for_row, key_for_row, value_for_row = row_inputs
        grouped_rows = query_for_row.reshape(row_length, KEY_VALUE_HEADS, repeat_heads, HEAD_SIZE)
        scores = jnp.einsum('qgrd,kgd->grqk', grouped_rows, key_for_row, precision=HIGHEST) * SCORE_SCALE
        scores = low_back(jnp.where(allowed[None, None], scores, -1e+30))
        weights = lower_precision(jax.nn.softmax(scores, axis=-1))
        mixed_heads = jnp.einsum('grqk,kgd->qgrd', weights, value_for_row, precision=HIGHEST)
        return mixed_heads.reshape(row_length, query_width)
    rows_mixed_heads = lax.map(jax.checkpoint(attend_single_row), (heads_of_query.reshape(N_GROUP, row_length, QUERY_HEADS, HEAD_SIZE), heads_of_key.reshape(N_GROUP, row_length, KEY_VALUE_HEADS, HEAD_SIZE), heads_of_value.reshape(N_GROUP, row_length, KEY_VALUE_HEADS, HEAD_SIZE)))
    mixed_low = lower_precision(low_back(rows_mixed_heads.reshape(-1, query_width)))
    attended = low_back(jnp.dot(mixed_low, out_weight, precision=HIGHEST))
    hidden = inputs + attended
    normed_two = lower_precision(rms_scale(hidden, norm_two))
    logits = jnp.dot(normed_two, router_weight, precision=HIGHEST)
    picked = jnp.take_along_axis(logits, route_rows, axis=1)
    gate_probs = jax.nn.softmax(picked, axis=-1)
    devices_all = N_GROUP * N_EXPERT
    pair_expert = route_rows.reshape(devices_all, tokens_per_device * TOPK)

    def rank_of(expert_row):
        onehot_hits = (expert_row[:, None] == jnp.arange(EXPERTS, dtype=jnp.int32)[None, :]).astype(jnp.int32)
        return lax.optimization_barrier(jnp.sum((jnp.cumsum(onehot_hits, axis=0) - 1) * onehot_hits, axis=1)).astype(jnp.int32)
    slot_rank = lax.map(rank_of, pair_expert)
    device_id = jnp.arange(devices_all, dtype=jnp.int32)[:, None]
    slot_place = (((device_id // N_EXPERT * EXPERTS + pair_expert) * N_EXPERT + device_id % N_EXPERT) * MOST + slot_rank).reshape(-1).astype(jnp.int32)
    token_of = (jnp.arange(devices_all * tokens_per_device * TOPK, dtype=jnp.int32) // TOPK).astype(jnp.int32)
    buffer = jnp.zeros((N_GROUP * EXPERTS * N_EXPERT * MOST, MODEL_WIDTH), jnp.float32).at[slot_place].set(normed_two[token_of])
    buffer = low_back(buffer)
    stacked = buffer.reshape(N_GROUP, EXPERTS, N_EXPERT * MOST, MODEL_WIDTH).transpose(1, 0, 2, 3)

    def run_expert(expert_inputs):
        row_block, gate_one, up_one, down_one = expert_inputs
        gate_pre = low_back(jnp.einsum('grd,df->grf', row_block, gate_one, precision=HIGHEST))
        up_pre = low_back(jnp.einsum('grd,df->grf', row_block, up_one, precision=HIGHEST))
        active = lower_precision(jax.nn.silu(gate_pre) * up_pre)
        return low_back(lower_precision(jnp.einsum('grf,fd->grd', active, down_one, precision=HIGHEST)))
    expert_out = lax.map(jax.checkpoint(run_expert), (stacked, gate_weight, up_weight, down_weight))
    expert_out = expert_out.transpose(1, 0, 2, 3).reshape(-1, MODEL_WIDTH)
    chosen = expert_out[slot_place].reshape(-1, TOPK, MODEL_WIDTH)
    mixture = low_back(lax.optimization_barrier(jnp.sum(gate_probs[:, :, None] * chosen, axis=1)))
    return hidden + mixture

def reference(tokens, cotangent, routes, norm_one, query_key_value_weight, out_weight, norm_two, router_weight, gate_weight, up_weight, down_weight):
    params = (norm_one.astype(jnp.float32), query_key_value_weight.astype(jnp.float32), out_weight.astype(jnp.float32), norm_two.astype(jnp.float32), router_weight.astype(jnp.float32), gate_weight.astype(jnp.float32), up_weight.astype(jnp.float32), down_weight.astype(jnp.float32))
    inputs = tokens.astype(jnp.float32)

    def whole_layer(layer_params, layer_inputs):
        return jnp.stack([micro_forward(layer_params, layer_inputs[micro_index], routes[micro_index]) for micro_index in range(MB)])
    result, pullback = jax.vjp(whole_layer, params, inputs)
    weight_grads, input_grad = pullback(cotangent.astype(jnp.float32))
    return (result.astype(jnp.bfloat16), input_grad, weight_grads[0], weight_grads[1], weight_grads[2], weight_grads[3], weight_grads[4], weight_grads[5], weight_grads[6], weight_grads[7])
```

```python
import functools

import jax
import jax.numpy as jnp
from jax import lax
from jax.experimental import pallas as pl
from jax.experimental.pallas import tpu as pltpu
from jax.sharding import PartitionSpec as P

QUERY_HEADS = 24
KEY_VALUE_HEADS = 8
HEAD_SIZE = 64
TOPK = 8
CONT = 256
PR_DEV = 64
LANES = 128
SCORE_SCALE = 0.125
NEG_FILL = -1e30
HIGHEST = lax.Precision.HIGHEST
F32 = jnp.float32
BF16 = jnp.bfloat16

NN = (((1,), (0,)), ((), ()))
NT = (((1,), (1,)), ((), ()))
TN = (((0,), (0,)), ((), ()))


def mm(a, b, dims=NN):
    return lax.dot_general(a, b, dims, preferred_element_type=F32)


def swap(x, bit):
    n = lax.axis_size("expert")
    return lax.ppermute(x, "expert", [(i, i ^ bit) for i in range(n)])


def shift(x, step):
    n = lax.axis_size("group")
    return lax.ppermute(x, "group", [(i, (i + step) % n) for i in range(n)])


def turn(x, step, split):
    n = lax.axis_size("group")
    return lax.ppermute(
        x, "group", [((i // split) * split + (i + step) % split, i) for i in range(n)]
    )


def outer_bits(n):
    return [1 << i for i in range(1, n.bit_length() - 1)]


def spread(x, order):
    n = lax.axis_size("expert")
    outer = outer_bits(n)
    if len(outer) == 2:
        a, b = outer
        xa, xb = swap(x, a), swap(x, b)
        slots = {0: x, a: xa, b: xb, a ^ b: swap(xa, b) if order == 0 else swap(xb, a)}
    else:
        slots = {0: x}
        for bit in outer:
            slots.update({r ^ bit: swap(y, bit) for r, y in list(slots.items())})
    if n > 1:
        slots.update({r ^ 1: swap(y, 1) for r, y in list(slots.items())})
    return [slots[r] for r in range(n)]


def plus(a, b):
    return (a.astype(F32) + b.astype(F32)).astype(BF16)


def collect(parts, order):
    n = lax.axis_size("expert")
    outer = outer_bits(n)
    keep = {r: parts[r] for r in range(n)}
    if n > 1:
        keep = {r: plus(keep[r], swap(keep[r ^ 1], 1)) for r in range(0, n, 2)}
    if len(outer) == 2:
        a, b = outer
        if order == 0:
            keep[a] = plus(keep[a], swap(keep[a ^ b], b))
        else:
            keep[b] = plus(keep[b], swap(keep[a ^ b], a))
        return (
            keep[0].astype(F32) + swap(keep[a], a).astype(F32) + swap(keep[b], b).astype(F32)
        )
    for bit in reversed(outer):
        keep = {r: plus(keep[r], swap(keep[r ^ bit], bit)) for r in keep if not r & bit}
    return keep[0].astype(F32)


def full_spec(shape):
    return pl.BlockSpec(shape, lambda *_: (0,) * len(shape))


SMEM_SPEC = pl.BlockSpec(memory_space=pltpu.SMEM)
ANY_SPEC = pl.BlockSpec(memory_space=pl.ANY)


def cost(flops, moved):
    return pl.CostEstimate(flops=int(flops), bytes_accessed=int(moved), transcendentals=0)


def assemble(pieces, place, shape, where):
    count = len(pieces)

    def kernel(at_ref, *refs):
        ins, out, sems = refs[:count], refs[count], refs[count + 1]
        copies = []
        for i in range(count):
            row, column = place(i, at_ref[0], at_ref[1])
            r, c = pieces[i].shape
            copies.append(
                pltpu.make_async_copy(
                    ins[i],
                    out.at[pl.ds(pl.multiple_of(row, 16), r), pl.ds(pl.multiple_of(column, 128), c)],
                    sems.at[i],
                )
            )
        for one in copies:
            one.start()
        for one in copies:
            one.wait()

    return pl.pallas_call(
        kernel,
        grid=(1,),
        in_specs=[SMEM_SPEC] + [ANY_SPEC] * count,
        out_specs=full_spec(shape),
        out_shape=jax.ShapeDtypeStruct(shape, pieces[0].dtype),
        scratch_shapes=[pltpu.SemaphoreType.DMA((count,))],
        cost_estimate=cost(0, 4 * shape[0] * shape[1]),
        name="assemble",
    )(where, *pieces)


def gather_dense(piece, cuts, where):
    groups, n = lax.axis_size("group"), lax.axis_size("expert")
    rows, columns = piece.shape
    own = [piece[:, lo:hi] for lo, hi in cuts]
    far = [[shift(x, s) for x in own] for s in range(1, groups)]
    names, pieces = [], []
    for h, (lo, hi) in enumerate(cuts):
        joined = jnp.concatenate([far[s - 1][h] for s in range(1, groups)], axis=0)
        for r, x in enumerate(spread(own[h], h % 2)):
            names.append((0, r, lo))
            pieces.append(x)
        for r, x in enumerate(spread(joined, h % 2)):
            for s in range(1, groups):
                names.append((s, r, lo))
                pieces.append((x, (s - 1) * rows, rows))
    total = groups * n * rows
    arrays, index = [], []
    for entry in pieces:
        if isinstance(entry, tuple):
            if not arrays or arrays[-1] is not entry[0]:
                arrays.append(entry[0])
            index.append((len(arrays) - 1, entry[1], entry[2]))
        else:
            arrays.append(entry)
            index.append((len(arrays) - 1, 0, rows))
    count, held = len(index), len(arrays)

    def kernel(at_ref, *refs):
        ins, out, sems = refs[:held], refs[held], refs[held + 1]
        copies = []
        for i, (which, start, size) in enumerate(index):
            s, r, lo = names[i]
            z = lax.rem(at_ref[0] - s + groups, groups)
            e = jnp.bitwise_xor(at_ref[1], r)
            row = pl.multiple_of((z * n + e) * rows, 16)
            width = arrays[which].shape[1]
            copies.append(
                pltpu.make_async_copy(
                    ins[which].at[pl.ds(start, size)],
                    out.at[pl.ds(row, rows), pl.ds(lo, width)],
                    sems.at[i],
                )
            )
        for one in copies:
            one.start()
        for one in copies:
            one.wait()

    whole = pl.pallas_call(
        kernel,
        grid=(1,),
        in_specs=[SMEM_SPEC] + [ANY_SPEC] * held,
        out_specs=full_spec((total, columns)),
        out_shape=jax.ShapeDtypeStruct((total, columns), piece.dtype),
        scratch_shapes=[pltpu.SemaphoreType.DMA((count,))],
        cost_estimate=cost(0, 4 * total * columns),
        name="join_rows",
    )(where, *arrays)
    return whole, far


def sliced_outer(a, b, extra, groups, n, where):
    depth = a.shape[1]
    columns = b.shape[1]
    more = 0 if extra is None else extra.shape[1]
    rows = depth // (groups * n)

    def kernel(at_ref, a_ref, b_ref, *refs):
        if more:
            x_ref, refs = refs[0], refs[1:]
        outs, acc = refs[:n], refs[n]
        acc[:, :columns] = mm(a_ref[...], b_ref[...], TN)
        if more:
            acc[:, columns:] = x_ref[...]
        for r in range(n):
            e = jnp.bitwise_xor(at_ref[1], r)
            for s in range(groups):
                z = lax.rem(at_ref[0] + s, groups)
                row = pl.multiple_of((z * n + e) * rows, 16)
                outs[r][s] = acc[pl.ds(row, rows), :].astype(BF16)

    width = columns + more
    return pl.pallas_call(
        kernel,
        grid=(1,),
        in_specs=[SMEM_SPEC, full_spec(a.shape), full_spec(b.shape)]
        + ([full_spec(extra.shape)] if more else []),
        out_specs=[full_spec((groups, rows, width))] * n,
        out_shape=[jax.ShapeDtypeStruct((groups, rows, width), BF16)] * n,
        scratch_shapes=[pltpu.VMEM((depth, width), F32)],
        cost_estimate=cost(2 * a.shape[0] * depth * columns, 2 * depth * width),
        name="sliced_outer",
    )(where, a, b, *([extra] if more else []))


def reduce_dense(parts, order, where):
    groups, n = lax.axis_size("group"), lax.axis_size("expert")
    mine = collect(parts, order)
    total = mine[0]
    low = mine.astype(BF16)
    for s in range(1, groups):
        total = total + shift(low[s], s).astype(F32)
    rows, width = total.shape
    slots = spread(total.astype(BF16), order)

    def kernel(at_ref, *refs):
        out = refs[n]
        for r in range(n):
            e = jnp.bitwise_xor(at_ref[1], r)
            out[pl.ds(pl.multiple_of(e * rows, 16), rows), :] = refs[r][...].astype(F32)

    return pl.pallas_call(
        kernel,
        grid=(1,),
        in_specs=[SMEM_SPEC] + [full_spec((rows, width))] * n,
        out_specs=full_spec((n * rows, width)),
        out_shape=jax.ShapeDtypeStruct((n * rows, width), F32),
        cost_estimate=cost(0, 6 * n * rows * width),
        name="join_sums",
    )(where, *slots)


def attention_masks(n, me):
    shape = (3 * PR_DEV, n * PR_DEV)
    token = lax.rem(lax.broadcasted_iota(jnp.int32, shape, 0), PR_DEV)
    column = lax.broadcasted_iota(jnp.int32, shape, 1)
    key_pos = jnp.bitwise_xor(column // PR_DEV, me) * PR_DEV + lax.rem(column, PR_DEV)
    prompt_ok = key_pos <= me * PR_DEV + token
    slots = CONT // PR_DEV
    shape = (3 * PR_DEV, CONT)
    token = lax.rem(lax.broadcasted_iota(jnp.int32, shape, 0), PR_DEV)
    column = lax.broadcasted_iota(jnp.int32, shape, 1)
    owner = jnp.bitwise_xor(column // PR_DEV, lax.rem(me, slots))
    cont_ok = owner * PR_DEV + lax.rem(column, PR_DEV) <= lax.rem(me, slots) * PR_DEV + token
    return prompt_ok, cont_ok


def head_rows(x, base):
    return jnp.concatenate(
        [x[:, base + i * HEAD_SIZE : base + (i + 1) * HEAD_SIZE] for i in range(3)], axis=0
    )


def row_heads(x):
    return jnp.concatenate([x[i * PR_DEV : (i + 1) * PR_DEV] for i in range(3)], axis=1)


def softmax(scores):
    top = jnp.max(scores, axis=1, keepdims=True)
    weight = jnp.exp(scores - top)
    return weight * (1.0 / jnp.sum(weight, axis=1, keepdims=True))


def load_keys(n, kv_refs, keys):
    for r in range(n):
        keys[r * PR_DEV : (r + 1) * PR_DEV, :] = kv_refs[r][:PR_DEV, :]
    for r in range(CONT // PR_DEV):
        lo = (n + r) * PR_DEV
        keys[lo : lo + PR_DEV, :] = kv_refs[r][PR_DEV:, :]


def group_probs(q_top, q_low, key, prompt_ok, cont_ok, n):
    pr = n * PR_DEV
    top = mm(q_top, key[:pr], NT) * SCORE_SCALE
    top = softmax(jnp.where(prompt_ok, top, NEG_FILL))
    low = mm(q_low, key, NT) * SCORE_SCALE
    low = jnp.concatenate([low[:, :pr], jnp.where(cont_ok, low[:, pr:], NEG_FILL)], axis=1)
    return top, softmax(low)


def attention_forward(query, slots, where):
    n = len(slots)
    width = KEY_VALUE_HEADS * HEAD_SIZE
    tokens = 2 * PR_DEV
    total = n * PR_DEV + CONT

    def kernel(at_ref, q_ref, *refs):
        kv_refs, out_ref, keys = refs[:n], refs[n], refs[n + 1]
        load_keys(n, kv_refs, keys)
        prompt_ok, cont_ok = attention_masks(n, at_ref[1])

        def pair(j, carry):
            q_at = pl.ds(pl.multiple_of(j * 384, 128), 384)
            k_at = pl.ds(pl.multiple_of(j * 128, 128), 128)
            v_at = pl.ds(pl.multiple_of(width + j * 128, 128), 128)
            q_top, q_low = q_ref[:PR_DEV, q_at], q_ref[PR_DEV:, q_at]
            k_two, v_two = keys[:, k_at], keys[:, v_at]
            tops, lows = [], []
            for g in range(2):
                key = k_two[:, g * HEAD_SIZE : (g + 1) * HEAD_SIZE]
                value = v_two[:, g * HEAD_SIZE : (g + 1) * HEAD_SIZE]
                top, low = group_probs(
                    head_rows(q_top, g * 192), head_rows(q_low, g * 192), key, prompt_ok, cont_ok, n
                )
                tops.append(row_heads(mm(top.astype(BF16), value[: n * PR_DEV])))
                lows.append(row_heads(mm(low.astype(BF16), value)))
            out_ref[:PR_DEV, q_at] = jnp.concatenate(tops, axis=1).astype(BF16)
            out_ref[PR_DEV:, q_at] = jnp.concatenate(lows, axis=1).astype(BF16)
            return carry

        lax.fori_loop(0, KEY_VALUE_HEADS // 2, pair, 0)

    return pl.pallas_call(
        kernel,
        grid=(1,),
        in_specs=[SMEM_SPEC, full_spec(query.shape)] + [full_spec((tokens, 2 * width))] * n,
        out_specs=full_spec(query.shape),
        out_shape=jax.ShapeDtypeStruct(query.shape, BF16),
        scratch_shapes=[pltpu.VMEM((total, 2 * width), BF16)],
        cost_estimate=cost(8e9, 4e6),
        name="attention_forward",
    )(where, query, *slots)


def attention_backward(query, slots, d_mixed, where):
    n = len(slots)
    width = KEY_VALUE_HEADS * HEAD_SIZE
    tokens = 2 * PR_DEV
    pr = n * PR_DEV
    total = pr + CONT

    def kernel(at_ref, q_ref, d_ref, *refs):
        kv_refs, refs = refs[:n], refs[n:]
        dq_ref, outs, keys, grads = refs[0], refs[1 : 1 + n], refs[1 + n], refs[2 + n]
        load_keys(n, kv_refs, keys)
        prompt_ok, cont_ok = attention_masks(n, at_ref[1])

        def one_side(prob, d_rows, key, value, q_rows):
            d_prob = mm(d_rows, value, NT)
            delta = jnp.sum(prob * d_prob, axis=1, keepdims=True)
            d_score = (prob * (d_prob - delta)).astype(BF16)
            return (
                mm(d_score, key) * SCORE_SCALE,
                mm(d_score, q_rows, TN) * SCORE_SCALE,
                mm(prob.astype(BF16), d_rows, TN),
            )

        def pair(j, carry):
            q_at = pl.ds(pl.multiple_of(j * 384, 128), 384)
            k_at = pl.ds(pl.multiple_of(j * 128, 128), 128)
            v_at = pl.ds(pl.multiple_of(width + j * 128, 128), 128)
            q_top, q_low = q_ref[:PR_DEV, q_at], q_ref[PR_DEV:, q_at]
            d_top, d_low = d_ref[:PR_DEV, q_at], d_ref[PR_DEV:, q_at]
            k_two, v_two = keys[:, k_at], keys[:, v_at]
            dq_tops, dq_lows, dks, dvs = [], [], [], []
            for g in range(2):
                key = k_two[:, g * HEAD_SIZE : (g + 1) * HEAD_SIZE]
                value = v_two[:, g * HEAD_SIZE : (g + 1) * HEAD_SIZE]
                rows_top, rows_low = head_rows(q_top, g * 192), head_rows(q_low, g * 192)
                top, low = group_probs(rows_top, rows_low, key, prompt_ok, cont_ok, n)
                dq_top, dk_top, dv_top = one_side(
                    top, head_rows(d_top, g * 192), key[:pr], value[:pr], rows_top
                )
                dq_low, dk_low, dv_low = one_side(
                    low, head_rows(d_low, g * 192), key, value, rows_low
                )
                dq_tops.append(row_heads(dq_top))
                dq_lows.append(row_heads(dq_low))
                dks.append(jnp.concatenate([dk_low[:pr] + dk_top, dk_low[pr:]], axis=0))
                dvs.append(jnp.concatenate([dv_low[:pr] + dv_top, dv_low[pr:]], axis=0))
            dq_ref[:PR_DEV, q_at] = jnp.concatenate(dq_tops, axis=1)
            dq_ref[PR_DEV:, q_at] = jnp.concatenate(dq_lows, axis=1)
            grads[:, k_at] = jnp.concatenate(dks, axis=1).astype(BF16)
            grads[:, v_at] = jnp.concatenate(dvs, axis=1).astype(BF16)
            return carry

        lax.fori_loop(0, KEY_VALUE_HEADS // 2, pair, 0)
        for r in range(n):
            outs[r][:PR_DEV, :] = grads[r * PR_DEV : (r + 1) * PR_DEV, :]
            if r < CONT // PR_DEV:
                lo = (n + r) * PR_DEV
                outs[r][PR_DEV:, :] = grads[lo : lo + PR_DEV, :]
            else:
                outs[r][PR_DEV:, :] = jnp.zeros((PR_DEV, 2 * width), BF16)

    out = pl.pallas_call(
        kernel,
        grid=(1,),
        in_specs=[SMEM_SPEC, full_spec(query.shape), full_spec(query.shape)]
        + [full_spec((tokens, 2 * width))] * n,
        out_specs=[full_spec(query.shape)] + [full_spec((tokens, 2 * width))] * n,
        out_shape=[jax.ShapeDtypeStruct(query.shape, F32)]
        + [jax.ShapeDtypeStruct((tokens, 2 * width), BF16)] * n,
        scratch_shapes=[pltpu.VMEM((total, 2 * width), BF16), pltpu.VMEM((total, 2 * width), BF16)],
        cost_estimate=cost(2e10, 8e6),
        name="attention_backward",
    )(where, query, d_mixed, *slots)
    return out[0], out[1:]


def pick(slot_row, cap):
    rows = lax.broadcasted_iota(jnp.int32, (cap, slot_row.shape[1]), 0).astype(F32)
    return jnp.where(slot_row == rows, 1.0, 0.0).astype(BF16)


def dispatch_grads(arrays, at, per, cap, model, buffers, place, blocks_total):
    count = len(arrays)
    split, tokens, width = arrays[0].shape
    blocks = count * split
    first = buffers is None

    def kernel(at_ref, *refs):
        ins = refs[:count]
        out, ranks = refs[-3], refs[-2]
        flags = refs[-1]
        row = lax.broadcasted_iota(jnp.int32, (tokens, tokens), 0)
        col = lax.broadcasted_iota(jnp.int32, (tokens, tokens), 1)
        before = jnp.where(row < col, 1.0, 0.0).astype(BF16)
        for i in range(count):
            for j in range(split):
                b = i * split + j
                payload = ins[i][j]
                flags[...] = payload[:, model:].astype(F32).T
                picked = jnp.concatenate(
                    [flags[pl.ds(at_ref[2] + k, 1), :] for k in range(per)], axis=0
                )
                rank = mm(picked.astype(BF16), before)
                slot = jnp.where(picked > 0.0, rank, -1.0)
                ranks[b] = slot
                for k in range(per):
                    out[k, b * cap : (b + 1) * cap, :] = mm(
                        pick(slot[k : k + 1], cap), payload[:, :model]
                    ).astype(BF16)

    shapes = [
        jax.ShapeDtypeStruct((per, blocks_total * cap, model), BF16),
        jax.ShapeDtypeStruct((blocks_total, per, tokens), F32),
    ]
    return pl.pallas_call(
        kernel,
        grid=(1,),
        in_specs=[SMEM_SPEC]
        + [full_spec(arrays[0].shape)] * count
        + ([] if first else [ANY_SPEC] * 2),
        out_specs=[
            pl.BlockSpec((per, blocks * cap, model), lambda *_: (0, place, 0)),
            pl.BlockSpec((blocks, per, tokens), lambda *_: (place, 0, 0)),
        ],
        out_shape=shapes,
        scratch_shapes=[pltpu.VMEM((LANES, tokens), F32)],
        input_output_aliases={} if first else {1 + count: 0, 2 + count: 1},
        cost_estimate=cost(1e9, 6e6),
        name="dispatch_grads",
    )(at, *arrays, *([] if first else buffers))


def dispatch_rows(arrays, ranks, at, per, cap, model, experts, buffers, place, blocks_total):
    count = len(arrays)
    split, tokens, width = arrays[0].shape
    blocks = count * split
    first = buffers is None

    def kernel(at_ref, rank_ref, *refs):
        ins = refs[:count]
        out, weights = refs[-2], refs[-1]
        lane = lax.broadcasted_iota(jnp.int32, (cap, LANES), 1)
        for i in range(count):
            for j in range(split):
                b = i * split + j
                payload = ins[i][j]
                for k in range(per):
                    got = mm(pick(rank_ref[b, k : k + 1, :], cap), payload)
                    out[k, b * cap : (b + 1) * cap, :] = got[:, :model].astype(BF16)
                    tail = got[:, model:]
                    e = at_ref[2] + k
                    mine = (lane == e) | (lane == e + experts)
                    total = jnp.sum(jnp.where(mine, tail, 0.0), axis=1, keepdims=True)
                    weights[k, b * cap : (b + 1) * cap, :] = jnp.broadcast_to(total, (cap, LANES))

    shapes = [
        jax.ShapeDtypeStruct((per, blocks_total * cap, model), BF16),
        jax.ShapeDtypeStruct((per, blocks_total * cap, LANES), F32),
    ]
    return pl.pallas_call(
        kernel,
        grid=(1,),
        in_specs=[SMEM_SPEC, pl.BlockSpec((blocks, per, tokens), lambda *_: (place, 0, 0))]
        + [full_spec(arrays[0].shape)] * count
        + ([] if first else [ANY_SPEC] * 2),
        out_specs=[
            pl.BlockSpec((per, blocks * cap, model), lambda *_: (0, place, 0)),
            pl.BlockSpec((per, blocks * cap, LANES), lambda *_: (0, place, 0)),
        ],
        out_shape=shapes,
        input_output_aliases={} if first else {2 + count: 0, 3 + count: 1},
        cost_estimate=cost(1e9, 6e6),
        name="dispatch_rows",
    )(at, ranks, *arrays, *([] if first else buffers))


def run_expert(k, at, rows_in, grads_in, weights, gate, up, down, experts, tile, groups, cut):
    per, total, model = rows_in.shape
    ff = gate.shape[1]
    part = model // groups
    steps = total // tile

    def kernel(at_ref, x_ref, d_ref, w_ref, gate_ref, up_ref, down_ref, o_ref, r_ref, *refs):
        outs, (acc_gate, acc_up, acc_down) = refs[:-3], refs[-3:]
        step = pl.program_id(0)
        x, d = x_ref[0], d_ref[0]
        w = w_ref[0, :, 0:1]
        gate_pre = mm(x, gate_ref[...])
        up_pre = mm(x, up_ref[...])
        sig = 1.0 / (1.0 + jnp.exp(-gate_pre))
        silu = gate_pre * sig
        active_wide = silu * up_pre
        active = active_wide.astype(BF16)
        out = mm(active, down_ref[...])
        o_ref[...] = (out * w).astype(BF16)
        d_raw = mm(d, down_ref[...], NT)
        d_gates = jnp.sum(active.astype(F32) * d_raw, axis=1, keepdims=True)
        d_active = d_raw * w
        d_up = (d_active * silu).astype(BF16)
        d_gate = (d_active * up_pre * sig * (1.0 + gate_pre * (1.0 - sig))).astype(BF16)
        d_row = mm(d_gate, gate_ref[...], NT) + mm(d_up, up_ref[...], NT)
        r_ref[:, :model] = d_row.astype(BF16)
        high = d_gates.astype(BF16).astype(F32)
        lane = lax.broadcasted_iota(jnp.int32, (tile, LANES), 1)
        e = at_ref[2] + k
        r_ref[:, model:] = (
            jnp.where(lane == e, high, 0.0) + jnp.where(lane == e + experts, d_gates - high, 0.0)
        ).astype(BF16)
        new_gate = mm(x, d_gate, TN)
        new_up = mm(x, d_up, TN)
        new_down = mm((active_wide * w).astype(BF16), d, TN)

        @pl.when(step == 0)
        def _():
            acc_gate[...] = new_gate
            acc_up[...] = new_up
            acc_down[...] = new_down

        @pl.when(step > 0)
        def _():
            acc_gate[...] += new_gate
            acc_up[...] += new_up
            acc_down[...] += new_down

        @pl.when(step == steps - 1)
        def _():
            if cut:
                for s in range(groups):
                    z = lax.rem(at_ref[0] + s, groups)
                    at_z = pl.ds(pl.multiple_of(z * part, 128), part)
                    outs[s][...] = acc_gate[at_z, :].astype(BF16)
                    outs[groups + s][...] = acc_up[at_z, :].astype(BF16)
                    outs[2 * groups + s][...] = acc_down[:, at_z].astype(BF16)
            else:
                outs[0][...] = acc_gate[...].astype(BF16)
                outs[1][...] = acc_up[...].astype(BF16)
                outs[2][...] = acc_down[...].astype(BF16)

    if cut:
        grads = [(part, ff)] * (2 * groups) + [(ff, part)] * groups
    else:
        grads = [(model, ff)] * 2 + [(ff, model)]
    row_spec = pl.BlockSpec((1, tile, model), lambda t: (k, t, 0))
    held = lambda shape: pl.BlockSpec(shape, lambda t: (0, 0), pipeline_mode=pl.Buffered(1))
    out = pl.pallas_call(
        kernel,
        grid=(steps,),
        in_specs=[
            SMEM_SPEC,
            row_spec,
            row_spec,
            pl.BlockSpec((1, tile, LANES), lambda t: (k, t, 0)),
            held((model, ff)),
            held((model, ff)),
            held((ff, model)),
        ],
        out_specs=[
            pl.BlockSpec((tile, model), lambda t: (t, 0)),
            pl.BlockSpec((tile, model + LANES), lambda t: (t, 0)),
        ]
        + [held(shape) for shape in grads],
        out_shape=[
            jax.ShapeDtypeStruct((total, model), BF16),
            jax.ShapeDtypeStruct((total, model + LANES), BF16),
        ]
        + [jax.ShapeDtypeStruct(shape, BF16) for shape in grads],
        scratch_shapes=[
            pltpu.VMEM((model, ff), F32),
            pltpu.VMEM((model, ff), F32),
            pltpu.VMEM((ff, model), F32),
        ],
        compiler_params=pltpu.CompilerParams(vmem_limit_bytes=62 * 1024 * 1024),
        cost_estimate=cost(18 * total * model * ff, 10 * total * model),
        name="run_expert",
    )(at, rows_in, grads_in, weights, gate, up, down)
    return out[0], out[1], out[2:]


def combine(rows, ranks, count, split, tokens, cap, place):
    per = len(rows)
    width = rows[0].shape[1]
    blocks = count * split

    def kernel(rank_ref, *refs):
        ins, outs = refs[:per], refs[per:]
        for i in range(count):
            for j in range(split):
                b = i * split + j
                total = None
                for k in range(per):
                    one = mm(
                        pick(rank_ref[b, k : k + 1, :], cap), ins[k][b * cap : (b + 1) * cap, :], TN
                    )
                    total = one if total is None else total + one
                outs[i][j] = total.astype(BF16)

    return pl.pallas_call(
        kernel,
        grid=(1,),
        in_specs=[pl.BlockSpec((blocks, per, tokens), lambda *_: (place, 0, 0))]
        + [pl.BlockSpec((blocks * cap, width), lambda *_: (place, 0))] * per,
        out_specs=[full_spec((split, tokens, width))] * count,
        out_shape=[jax.ShapeDtypeStruct((split, tokens, width), BF16)] * count,
        cost_estimate=cost(1e9, 6e6),
        name="combine",
    )(ranks, *rows)


def rope_tables(my_index, prompt_len):
    half = HEAD_SIZE // 2
    local = jnp.arange(2 * PR_DEV, dtype=jnp.int32)
    cont = my_index * PR_DEV + local - PR_DEV
    position = jnp.where(local < PR_DEV, my_index * PR_DEV + local, prompt_len + cont % CONT)
    frequency = 10000.0 ** (-jnp.arange(half, dtype=F32) * (2.0 / HEAD_SIZE))
    angle = position.astype(F32)[:, None] * frequency[None, :]
    return jnp.cos(angle), jnp.sin(angle)


def rotate(x, cosine, sine):
    half = HEAD_SIZE // 2
    column = lax.broadcasted_iota(jnp.int32, x.shape, 1)
    other = jnp.where(column % HEAD_SIZE < half, jnp.roll(x, -half, axis=1), jnp.roll(x, half, axis=1))
    return x * cosine + other * sine


def layer_general(
    tokens,
    cotangent,
    routes,
    norm_one,
    query_key_value_weight,
    out_weight,
    norm_two,
    router_weight,
    gate_weight,
    up_weight,
    down_weight,
):
    n = lax.axis_size("expert")
    groups = lax.axis_size("group")
    me = lax.axis_index("expert")
    z = lax.axis_index("group")
    micro, count, model = tokens.shape
    exp_here, part, ff = gate_weight.shape
    experts = router_weight.shape[1]
    split = 2 if exp_here % 2 == 0 and groups % 2 == 0 else 1
    per = exp_here // split
    query_width = QUERY_HEADS * HEAD_SIZE
    kv_width = KEY_VALUE_HEADS * HEAD_SIZE
    cap = max(2, 3 * TOPK * PR_DEV // experts)
    where = jnp.stack([z, me, me * exp_here + (z % split) * per]).astype(jnp.int32)
    rows_here = part // n if part % n == 0 else 0
    aligned = rows_here > 0 and rows_here % 16 == 0 and part % LANES == 0

    misc = jnp.concatenate(
        [
            norm_one[:, None],
            norm_two[:, None],
            jnp.zeros((part, experts - 2), BF16),
            router_weight,
            jnp.zeros((part, LANES - 2 * experts), BF16),
        ],
        axis=1,
    )
    if aligned:
        first = jnp.concatenate([query_key_value_weight, misc], axis=1)
        cut = lambda x: lax.dynamic_slice_in_dim(x, me * rows_here, rows_here, axis=0)
        width = first.shape[1]
        middle = width // 2 // LANES * LANES
        first_full, far = gather_dense(cut(first), [(0, middle), (middle, width)], where)
        out_full, far_out = gather_dense(
            cut(out_weight), [(0, model // 2), (model // 2, model)], where
        )
        after = (far, far_out)
    else:
        first_full = lax.all_gather(
            jnp.concatenate([query_key_value_weight, misc], axis=1), "group", axis=0, tiled=True
        )
        out_full = lax.all_gather(out_weight, "group", axis=0, tiled=True)
        after = ()
    qkv_columns = query_key_value_weight.shape[1]
    qkv_full = first_full[:, :qkv_columns]
    misc_full = first_full[:, qkv_columns:]
    gain_one = misc_full[:, 0].astype(F32)
    gain_two = misc_full[:, 1].astype(F32)
    router_full = misc_full[:, experts : 2 * experts]

    weights_held = []
    gate_from, up_from, down_from = gate_weight, up_weight, down_weight
    if aligned:
        (gate_from, up_from, down_from), after = lax.optimization_barrier(
            ((gate_weight, up_weight, down_weight), after)
        )
    for k in range(per):
        held = []
        for array, axis in ((gate_from, 0), (up_from, 0), (down_from, 1)):
            if not aligned:
                held.append(lax.all_gather(array[k], "group", axis=axis, tiled=True))
                continue
            pieces = []
            for s in range(groups):
                index = ((z + s) % split) * per + k
                chunk = lax.dynamic_index_in_dim(array, index, 0, keepdims=False)
                pieces.append(shift(chunk, s) if s else chunk)

            def place(i, at_z, at_e, axis=axis):
                start = lax.rem(at_z - i + groups, groups) * part
                return (start, 0) if axis == 0 else (0, start)

            shape = (model, ff) if axis == 0 else (ff, model)
            held.append(assemble(pieces, place, shape, where))
        weights_held.append(held)

    expert_ids = jnp.arange(experts, dtype=jnp.int32)
    named = jnp.any(routes[..., None] == expert_ids, axis=2)
    pad = jnp.zeros((micro, count, LANES - experts), BF16)
    d_payload = jnp.concatenate([cotangent, named.astype(BF16), pad], axis=2)

    def to_experts(payload):
        held = []
        for m in range(micro):
            own = payload[m]
            both = jnp.stack([own] + [turn(own, j, split) for j in range(1, split)])
            held.append(spread(both, m % 2))
        return held

    def to_owners(parts):
        held = []
        for m in range(micro):
            total = collect(parts[m], m % 2)
            mine = total[0]
            for j in range(1, split):
                mine = mine + turn(total[j].astype(BF16), split - j, split).astype(F32)
            held.append(mine)
        return jnp.stack(held)

    slots_per = 2 if n % 2 == 0 else 1
    batches = [list(range(g * slots_per, (g + 1) * slots_per)) for g in range(n // slots_per)]
    blocks_total = n * micro * split

    d_slots = to_experts(d_payload)
    buffers = None
    for g, batch in enumerate(batches):
        buffers = dispatch_grads(
            [d_slots[m][r] for r in batch for m in range(micro)],
            where, per, cap, model, buffers, g, blocks_total,
        )
    grads_in, ranks = buffers

    rows = micro * count
    x = tokens.reshape(rows, model).astype(F32)
    inverse_one = lax.rsqrt(jnp.mean(x * x, axis=-1, keepdims=True) + 1e-05)
    normed = (x * inverse_one * gain_one).astype(BF16)
    cosine, sine = rope_tables(me, PR_DEV * n)
    heads_rope = QUERY_HEADS + KEY_VALUE_HEADS
    cosine = jnp.tile(jnp.concatenate([cosine, cosine], axis=1), (micro, heads_rope))
    sine = jnp.tile(jnp.concatenate([-sine, sine], axis=1), (micro, heads_rope))
    cosine, sine = lax.optimization_barrier((cosine, sine))
    project = mm(normed, qkv_full)
    roped = rotate(project[:, : query_width + kv_width], cosine, sine).astype(BF16)
    query = roped[:, :query_width]
    key_value = jnp.concatenate(
        [roped[:, query_width:], project[:, query_width + kv_width :].astype(BF16)], axis=1
    ).reshape(micro, count, 2 * kv_width)
    query = query.reshape(micro, count, query_width)
    kv_slots = [spread(key_value[m], m % 2) for m in range(micro)]
    mixed = jnp.concatenate(
        [attention_forward(query[m], kv_slots[m], where) for m in range(micro)], axis=0
    )
    hidden = x + mm(mixed, out_full)
    inverse_two = lax.rsqrt(jnp.mean(hidden * hidden, axis=-1, keepdims=True) + 1e-05)
    normed_two = (hidden * inverse_two * gain_two).astype(BF16)
    logits = mm(normed_two, router_full)
    chosen = named.reshape(rows, experts)
    logits = jnp.where(chosen, logits, NEG_FILL)
    top = jnp.max(logits, axis=-1, keepdims=True)
    raised = jnp.where(chosen, jnp.exp(logits - top), 0.0)
    gate_probs = raised / jnp.sum(raised, axis=-1, keepdims=True)

    high = gate_probs.astype(BF16)
    low = (gate_probs - high.astype(F32)).astype(BF16)
    payload = jnp.concatenate(
        [normed_two, high, low, jnp.zeros((rows, LANES - 2 * experts), BF16)], axis=1
    ).reshape(micro, count, model + LANES)
    x_slots = to_experts(payload)
    buffers = None
    for g, batch in enumerate(batches):
        buffers = dispatch_rows(
            [x_slots[m][r] for r in batch for m in range(micro)],
            ranks, where, per, cap, model, experts, buffers, g, blocks_total,
        )
    rows_in, row_weights = buffers
    tile = slots_per * micro * split * cap
    outs, backs, weight_terms = [], [], []
    for k in range(per):
        out_rows, back_rows, terms = run_expert(
            k, where, rows_in, grads_in, row_weights, *weights_held[k], experts, tile, groups, aligned
        )
        outs.append(out_rows)
        backs.append(back_rows)
        weight_terms.append(terms)

    def returned(row_arrays):
        parts = [[None] * n for _ in range(micro)]
        for g in reversed(range(len(batches))):
            got = combine(
                row_arrays, ranks, len(batches[g]) * micro, split, count, cap, g
            )
            for i, (r, m) in enumerate((r, m) for r in batches[g] for m in range(micro)):
                parts[m][r] = got[i]
        return to_owners(parts)

    back = returned(backs).reshape(rows, model + LANES)
    mixture = returned(outs).reshape(rows, model)
    block_out = (hidden + mixture).astype(BF16).reshape(tokens.shape)

    expert_grads = []
    for which in range(3):
        per_class = []
        for k in range(per):
            if not aligned:
                axis = 1 if which == 2 else 0
                per_class.append(
                    [lax.psum_scatter(weight_terms[k][which], "group", scatter_dimension=axis, tiled=True).astype(F32)]
                )
                continue
            sums = [None] * split
            for s in range(groups):
                term = weight_terms[k][which * groups + s]
                term = (shift(term, s) if s else term).astype(F32)
                c = s % split
                sums[c] = term if sums[c] is None else sums[c] + term
            per_class.append(
                [lax.select_n((z - p) % split, *sums) if split > 1 else sums[0] for p in range(split)]
            )
        expert_grads.append(
            jnp.stack([per_class[k][p] for p in range(split) for k in range(per)])
        )

    d_out = cotangent.reshape(rows, model).astype(F32)
    d_gates = back[:, model : model + experts] + back[:, model + experts : model + 2 * experts]
    d_logits = gate_probs * (d_gates - jnp.sum(gate_probs * d_gates, axis=-1, keepdims=True))
    router_grad = lax.dot_general(normed_two.astype(F32), d_logits, TN, precision=HIGHEST)
    d_normed_two = back[:, :model] + lax.dot_general(
        d_logits, router_full.astype(F32), NT, precision=HIGHEST
    )

    def rms_back(inputs, inverse, gain, upstream):
        scaled = gain * upstream
        return inverse * scaled - inputs * inverse * inverse * inverse * jnp.mean(
            scaled * inputs, axis=-1, keepdims=True
        )

    grad_two = jnp.sum(d_normed_two * hidden * inverse_two, axis=0)
    d_hidden = d_out + rms_back(hidden, inverse_two, gain_two, d_normed_two)
    d_attn = d_hidden.astype(BF16)
    d_mixed = mm(d_attn, out_full, NT).astype(BF16).reshape(micro, count, query_width)
    d_query, kv_terms = [], []
    for m in range(micro):
        got, terms = attention_backward(query[m], kv_slots[m], d_mixed[m], where)
        d_query.append(got)
        kv_terms.append(terms)
    d_query = jnp.concatenate(d_query, axis=0)
    q_cos, q_sin = cosine[:, :query_width], sine[:, :query_width]
    d_query_low = rotate(d_query, q_cos, -q_sin).astype(BF16)
    d_kv = jnp.concatenate([collect(kv_terms[m], m % 2) for m in range(micro)], axis=0)
    d_key_low = rotate(d_kv[:, :kv_width], q_cos[:, :kv_width], -q_sin[:, :kv_width]).astype(BF16)
    d_kv_low = jnp.concatenate([d_key_low, d_kv[:, kv_width:].astype(BF16)], axis=1)
    d_normed = mm(d_query_low, qkv_full[:, :query_width], NT) + mm(
        d_kv_low, qkv_full[:, query_width:], NT
    )
    grad_one = jnp.sum(d_normed * x * inverse_one, axis=0)
    input_grad = (d_hidden + rms_back(x, inverse_one, gain_one, d_normed)).reshape(tokens.shape)
    misc_grad = jnp.concatenate(
        [
            grad_one[:, None],
            grad_two[:, None],
            jnp.zeros((model, experts - 2), F32),
            router_grad,
            jnp.zeros((model, LANES - 2 * experts), F32),
        ],
        axis=1,
    )
    if aligned:
        grad_out = reduce_dense(sliced_outer(mixed, d_attn, None, groups, n, where), 0, where)
        grad_q = reduce_dense(sliced_outer(normed, d_query_low, None, groups, n, where), 1, where)
        grad_rest = reduce_dense(
            sliced_outer(normed, d_kv_low, misc_grad, groups, n, where), 0, where
        )
    else:

        def whole(value):
            low = lax.psum_scatter(value.astype(BF16), "group", scatter_dimension=0, tiled=True)
            return lax.psum(low, "expert").astype(F32)

        grad_out = whole(mm(mixed, d_attn, TN))
        grad_q = whole(mm(normed, d_query_low, TN))
        grad_rest = whole(jnp.concatenate([mm(normed, d_kv_low, TN), misc_grad], axis=1))
    grad_qkv = jnp.concatenate([grad_q, grad_rest[:, : 2 * kv_width]], axis=1)
    misc_sum = grad_rest[:, 2 * kv_width :]
    return (
        block_out,
        input_grad,
        misc_sum[:, 0],
        grad_qkv,
        grad_out,
        misc_sum[:, 1],
        misc_sum[:, experts : 2 * experts],
        *expert_grads,
    )


def flip(e, r):
    for bit in (1, 2, 4):
        if r & bit:
            e = e + bit - 2 * bit * lax.rem(e // bit, 2)
    return e


def partner(z):
    return z + 1 - 2 * lax.rem(z, 2)


def remote(src, dst, send, recv, device):
    return pltpu.make_async_remote_copy(
        src_ref=src,
        dst_ref=dst,
        send_sem=send,
        recv_sem=recv,
        device_id=device,
        device_id_type=pl.DeviceIdType.MESH,
    )


def greet(devices):
    barrier = pltpu.get_barrier_semaphore()
    for device in devices:
        pl.semaphore_signal(barrier, inc=1, device_id=device, device_id_type=pl.DeviceIdType.MESH)
    pl.semaphore_wait(barrier, len(devices))


def plane_devices(e):
    return [{"expert": flip(e, bit)} for bit in (1, 2, 4)]


class Gather:
    def __init__(self, e, own, loc, paths, send, recv):
        self.e, self.own, self.loc, self.paths, self.send, self.recv = e, own, loc, paths, send, recv

    def copy(self, r, bit, c):
        q = r ^ bit
        src = self.own(c) if r == 0 else self.loc(r, r, c)
        return remote(
            src, self.loc(r, q, c), self.send.at[q, c], self.recv.at[q, c],
            {"expert": flip(self.e, bit)},
        )

    def begin(self, c):
        for bit in (2, 4, 1):
            self.copy(0, bit, c).start()

    def arrived(self, q, c):
        here = self.loc(q, q, c)
        remote(
            here, here, self.send.at[q, c], self.recv.at[q, c], {"expert": flip(self.e, 1)}
        ).wait_recv()

    def pass_on(self, q, c):
        if q == 2 and self.paths[c] == 0:
            self.copy(2, 4, c).start()
        if q == 4 and self.paths[c] == 1:
            self.copy(4, 2, c).start()
        if q in (2, 4, 6):
            self.copy(q, 1, c).start()

    def finish(self, c):
        for bit in (2, 4, 1):
            self.copy(0, bit, c).wait_send()
        if self.paths[c] == 0:
            self.copy(2, 4, c).wait_send()
        else:
            self.copy(4, 2, c).wait_send()
        for q in (2, 4, 6):
            self.copy(q, 1, c).wait_send()

    def forward_all(self, chunks, use=None):
        for c in chunks:
            for q in (2, 4):
                self.arrived(q, c)
                self.pass_on(q, c)
        if use:
            for c in chunks:
                self.arrived(1, c)
                use(1, c)
                use(2, c)
                use(4, c)
        for c in chunks:
            self.arrived(6, c)
            self.pass_on(6, c)
            if use:
                use(6, c)
        for c in chunks:
            for q in (3, 5, 7) if use else (1, 3, 5, 7):
                self.arrived(q, c)
                if use:
                    use(q, c)


def add_rows(dst, sources, step=16):
    rows = sources[0].shape[0]

    def one(i, carry):
        at = pl.ds(pl.multiple_of(i * step, step), step)
        total = sources[0][at, :].astype(F32)
        for source in sources[1:]:
            total = total + source[at, :].astype(F32)
        dst[at, :] = total.astype(dst.dtype)
        return carry

    lax.fori_loop(0, rows // step, one, 0)


class Reduce:
    def __init__(self, e, part, paths, core, diag, near, acc, send, recv):
        self.e, self.part, self.paths = e, part, paths
        self.core, self.diag, self.near, self.acc = core, diag, near, acc
        self.send, self.recv = send, recv

    def core_copy(self, h, c):
        return remote(
            self.part(2 * h + 1, c), self.core.at[h, c], self.send.at[h, c], self.recv.at[h, c],
            {"expert": flip(self.e, 1)},
        )

    def diag_copy(self, c):
        return remote(
            self.acc.at[2, c], self.diag.at[c], self.send.at[4, c], self.recv.at[4, c],
            {"expert": flip(self.e, 4 if self.paths[c] == 0 else 2)},
        )

    def near_copy(self, i, c):
        return remote(
            self.acc.at[i, c], self.near.at[i, c], self.send.at[5 + i, c], self.recv.at[5 + i, c],
            {"expert": flip(self.e, 2 if i == 0 else 4)},
        )

    def begin(self, r, c):
        self.core_copy(r // 2, c).start()

    def diagonal(self, chunks):
        for c in chunks:
            self.core_copy(3, c).wait_recv()
            add_rows(self.acc.at[2, c], [self.part(6, c), self.core.at[3, c]])
            self.diag_copy(c).start()

    def sides(self, chunks):
        for c in chunks:
            for i in (0, 1) if self.paths[c] == 1 else (1, 0):
                self.core_copy(1 + i, c).wait_recv()
                terms = [self.part(2 + 2 * i, c), self.core.at[1 + i, c]]
                if self.paths[c] == i:
                    self.diag_copy(c).wait_recv()
                    terms.append(self.diag.at[c])
                add_rows(self.acc.at[i, c], terms)
                self.near_copy(i, c).start()

    def total(self, c):
        self.core_copy(0, c).wait_recv()
        self.near_copy(0, c).wait_recv()
        self.near_copy(1, c).wait_recv()
        return [self.part(0, c), self.core.at[0, c], self.near.at[0, c], self.near.at[1, c]]

    def finish(self, c):
        for h in range(4):
            self.core_copy(h, c).wait_send()
        self.diag_copy(c).wait_send()
        for i in range(2):
            self.near_copy(i, c).wait_send()


def reduce_scratch(count, rows, width):
    return [
        pltpu.VMEM((4, count, rows, width), BF16),
        pltpu.VMEM((count, rows, width), BF16),
        pltpu.VMEM((2, count, rows, width), BF16),
        pltpu.VMEM((3, count, rows, width), BF16),
        pltpu.SemaphoreType.DMA((7, count)),
        pltpu.SemaphoreType.DMA((7, count)),
    ]


def params(identity, vmem=62):
    return pltpu.CompilerParams(
        collective_id=identity, has_side_effects=True, vmem_limit_bytes=vmem * 1024 * 1024
    )


def plane_weights(sets):
    groups, n = len(sets[0]), 8
    rows = sets[0][0].shape[0]
    kinds = len(sets)
    count = groups * kinds

    def kernel(*refs):
        ins, outs = refs[:count], refs[count : count + kinds]
        send, recv, local = refs[count + kinds :]
        e, z = lax.axis_index("expert"), lax.axis_index("group")

        def loc(r, q, c):
            s, kind = c // kinds, c % kinds
            row = (lax.rem(z - s + groups, groups) * n + flip(e, r)) * rows
            return outs[kind].at[pl.ds(pl.multiple_of(row, 16), rows), :]

        gather = Gather(e, lambda c: ins[c], loc, [c // kinds % 2 for c in range(count)], send, recv)
        greet(plane_devices(e))
        for c in range(count):
            gather.begin(c)
            pltpu.make_async_copy(ins[c], loc(0, 0, c), local.at[c]).start()
        gather.forward_all(range(count))
        for c in range(count):
            gather.finish(c)
            pltpu.make_async_copy(ins[c], loc(0, 0, c), local.at[c]).wait()

    flat = [sets[kind][s] for s in range(groups) for kind in range(kinds)]
    shapes = [(groups * n * rows, one[0].shape[1]) for one in sets]
    return pl.pallas_call(
        kernel,
        in_specs=[pl.BlockSpec(memory_space=pltpu.VMEM)] * count,
        out_specs=[pl.BlockSpec(memory_space=pltpu.VMEM)] * kinds,
        out_shape=[jax.ShapeDtypeStruct(shape, BF16) for shape in shapes],
        scratch_shapes=[
            pltpu.SemaphoreType.DMA((n, count)),
            pltpu.SemaphoreType.DMA((n, count)),
            pltpu.SemaphoreType.DMA((count,)),
        ],
        compiler_params=params(1),
        cost_estimate=cost(5e10, 6e7),
        name="plane_weights",
    )(*flat)


def attention_pairs(n, at_me, q_ref, keys, out_ref):
    width = KEY_VALUE_HEADS * HEAD_SIZE
    prompt_ok, cont_ok = attention_masks_plain(n, at_me)

    def pair(j, carry):
        q_at = pl.ds(pl.multiple_of(j * 384, 128), 384)
        k_at = pl.ds(pl.multiple_of(j * 128, 128), 128)
        v_at = pl.ds(pl.multiple_of(width + j * 128, 128), 128)
        q_top, q_low = q_ref[:PR_DEV, q_at], q_ref[PR_DEV:, q_at]
        k_two, v_two = keys[:, k_at], keys[:, v_at]
        tops, lows = [], []
        for g in range(2):
            key = k_two[:, g * HEAD_SIZE : (g + 1) * HEAD_SIZE]
            value = v_two[:, g * HEAD_SIZE : (g + 1) * HEAD_SIZE]
            top, low = group_probs(
                head_rows(q_top, g * 192), head_rows(q_low, g * 192), key, prompt_ok, cont_ok, n
            )
            tops.append(row_heads(mm(top.astype(BF16), value[: n * PR_DEV])))
            lows.append(row_heads(mm(low.astype(BF16), value)))
        out_ref[:PR_DEV, q_at] = jnp.concatenate(tops, axis=1).astype(BF16)
        out_ref[PR_DEV:, q_at] = jnp.concatenate(lows, axis=1).astype(BF16)
        return carry

    lax.fori_loop(0, KEY_VALUE_HEADS // 2, pair, 0)


def flip_columns(slot, me, limit):
    bit, total = 1, jnp.zeros_like(slot)
    while bit < limit:
        total = total + bit * lax.rem(slot // bit + me // bit, 2)
        bit *= 2
    return total


def attention_masks_plain(n, me):
    shape = (3 * PR_DEV, n * PR_DEV)
    token = lax.rem(lax.broadcasted_iota(jnp.int32, shape, 0), PR_DEV)
    column = lax.broadcasted_iota(jnp.int32, shape, 1)
    owner = flip_columns(column // PR_DEV, me, n)
    prompt_ok = owner * PR_DEV + lax.rem(column, PR_DEV) <= me * PR_DEV + token
    slots = CONT // PR_DEV
    shape = (3 * PR_DEV, CONT)
    token = lax.rem(lax.broadcasted_iota(jnp.int32, shape, 0), PR_DEV)
    column = lax.broadcasted_iota(jnp.int32, shape, 1)
    local = lax.rem(me, slots)
    owner = flip_columns(column // PR_DEV, local, slots)
    cont_ok = owner * PR_DEV + lax.rem(column, PR_DEV) <= local * PR_DEV + token
    return prompt_ok, cont_ok


def plane_attention(query, key_value):
    micro, tokens, width = key_value.shape
    n = 8

    def kernel(q_ref, kv_ref, out_ref, slots, keys, send, recv, local):
        e = lax.axis_index("expert")
        gather = Gather(
            e, lambda c: kv_ref.at[c], lambda r, q, c: slots.at[q, c], [c % 2 for c in range(micro)],
            send, recv,
        )
        greet(plane_devices(e))
        for c in range(micro):
            gather.begin(c)
            pltpu.make_async_copy(kv_ref.at[c], slots.at[0, c], local.at[c]).start()
        gather.forward_all(range(micro))
        for c in range(micro):
            pltpu.make_async_copy(kv_ref.at[c], slots.at[0, c], local.at[c]).wait()
            load_keys(n, [slots.at[r, c] for r in range(n)], keys)
            attention_pairs(n, e, q_ref.at[c], keys, out_ref.at[c])
        for c in range(micro):
            gather.finish(c)

    vmem = pl.BlockSpec(memory_space=pltpu.VMEM)
    return pl.pallas_call(
        kernel,
        in_specs=[vmem, vmem],
        out_specs=[vmem, vmem],
        out_shape=[
            jax.ShapeDtypeStruct(query.shape, BF16),
            jax.ShapeDtypeStruct((n, micro, tokens, width), BF16),
        ],
        scratch_shapes=[
            pltpu.VMEM((n * PR_DEV + CONT, width), BF16),
            pltpu.SemaphoreType.DMA((n, micro)),
            pltpu.SemaphoreType.DMA((n, micro)),
            pltpu.SemaphoreType.DMA((micro,)),
        ],
        compiler_params=params(2),
        cost_estimate=cost(3e10, 2e7),
        name="plane_attention",
    )(query, key_value)


def plane_attention_backward(query, slots, d_mixed):
    n, micro, tokens, width = slots.shape
    half = width // 2
    pr = n * PR_DEV
    total = pr + CONT

    def kernel(q_ref, d_ref, kv_ref, dq_ref, dkv_ref, keys, grads, parts, *scratch):
        e = lax.axis_index("expert")
        red = Reduce(e, lambda r, c: parts.at[r, c], [c % 2 for c in range(micro)], *scratch)
        greet(plane_devices(e))
        prompt_ok, cont_ok = attention_masks_plain(n, e)

        def one_side(prob, d_rows, key, value, q_rows):
            d_prob = mm(d_rows, value, NT)
            delta = jnp.sum(prob * d_prob, axis=1, keepdims=True)
            d_score = (prob * (d_prob - delta)).astype(BF16)
            return (
                mm(d_score, key) * SCORE_SCALE,
                mm(d_score, q_rows, TN) * SCORE_SCALE,
                mm(prob.astype(BF16), d_rows, TN),
            )

        for c in range(micro):
            load_keys(n, [kv_ref.at[r, c] for r in range(n)], keys)

            def pair(j, carry):
                q_at = pl.ds(pl.multiple_of(j * 384, 128), 384)
                k_at = pl.ds(pl.multiple_of(j * 128, 128), 128)
                v_at = pl.ds(pl.multiple_of(half + j * 128, 128), 128)
                q_top, q_low = q_ref[c, :PR_DEV, q_at], q_ref[c, PR_DEV:, q_at]
                d_top, d_low = d_ref[c, :PR_DEV, q_at], d_ref[c, PR_DEV:, q_at]
                k_two, v_two = keys[:, k_at], keys[:, v_at]
                dq_tops, dq_lows, dks, dvs = [], [], [], []
                for g in range(2):
                    key = k_two[:, g * HEAD_SIZE : (g + 1) * HEAD_SIZE]
                    value = v_two[:, g * HEAD_SIZE : (g + 1) * HEAD_SIZE]
                    rows_top, rows_low = head_rows(q_top, g * 192), head_rows(q_low, g * 192)
                    top, low = group_probs(rows_top, rows_low, key, prompt_ok, cont_ok, n)
                    dq_top, dk_top, dv_top = one_side(
                        top, head_rows(d_top, g * 192), key[:pr], value[:pr], rows_top
                    )
                    dq_low, dk_low, dv_low = one_side(
                        low, head_rows(d_low, g * 192), key, value, rows_low
                    )
                    dq_tops.append(row_heads(dq_top))
                    dq_lows.append(row_heads(dq_low))
                    dks.append(jnp.concatenate([dk_low[:pr] + dk_top, dk_low[pr:]], axis=0))
                    dvs.append(jnp.concatenate([dv_low[:pr] + dv_top, dv_low[pr:]], axis=0))
                dq_ref[c, :PR_DEV, q_at] = jnp.concatenate(dq_tops, axis=1)
                dq_ref[c, PR_DEV:, q_at] = jnp.concatenate(dq_lows, axis=1)
                grads[:, k_at] = jnp.concatenate(dks, axis=1).astype(BF16)
                grads[:, v_at] = jnp.concatenate(dvs, axis=1).astype(BF16)
                return carry

            lax.fori_loop(0, KEY_VALUE_HEADS // 2, pair, 0)
            for r in (7, 5, 3, 1, 6, 2, 4, 0):
                parts[r, c, :PR_DEV, :] = grads[r * PR_DEV : (r + 1) * PR_DEV, :]
                if r < CONT // PR_DEV:
                    lo = (n + r) * PR_DEV
                    parts[r, c, PR_DEV:, :] = grads[lo : lo + PR_DEV, :]
                else:
                    parts[r, c, PR_DEV:, :] = jnp.zeros((PR_DEV, width), BF16)
                if r % 2:
                    red.begin(r, c)
        red.diagonal(range(micro))
        red.sides(range(micro))
        for c in range(micro):
            add_rows(dkv_ref.at[c], red.total(c))
        for c in range(micro):
            red.finish(c)

    vmem = pl.BlockSpec(memory_space=pltpu.VMEM)
    return pl.pallas_call(
        kernel,
        in_specs=[vmem] * 3,
        out_specs=[vmem] * 2,
        out_shape=[
            jax.ShapeDtypeStruct(query.shape, F32),
            jax.ShapeDtypeStruct((micro, tokens, width), F32),
        ],
        scratch_shapes=[
            pltpu.VMEM((total, width), BF16),
            pltpu.VMEM((total, width), BF16),
            pltpu.VMEM((n, micro, tokens, width), BF16),
        ]
        + reduce_scratch(micro, tokens, width),
        compiler_params=params(3),
        cost_estimate=cost(5e10, 2e7),
        name="plane_attention_backward",
    )(query, d_mixed, slots)


def plane_dispatch(payload, ranks, where, per, cap, model, experts):
    micro, tokens, width = payload.shape
    n, split = 8, 2
    count = split * micro

    def kernel(at_ref, own_ref, rank_ref, out, weights, slots, z_send, z_recv, send, recv):
        e, z = lax.axis_index("expert"), lax.axis_index("group")
        lane = lax.broadcasted_iota(jnp.int32, (cap, LANES), 1)

        def own(c):
            return own_ref.at[c] if c < micro else slots.at[0, c]

        gather = Gather(
            e, own, lambda r, q, c: slots.at[q, c], [c % 2 for c in range(count)], send, recv
        )

        def turned(m):
            return remote(
                own_ref.at[m], slots.at[0, micro + m], z_send.at[m], z_recv.at[m],
                {"group": partner(z)},
            )

        def use(r, c):
            rows = own(c)[...] if r == 0 else slots[r, c]
            b = r * count + c
            for k in range(per):
                got = mm(pick(rank_ref[b, k : k + 1, :], cap), rows)
                out[k, b * cap : (b + 1) * cap, :] = got[:, :model].astype(BF16)
                first = at_ref[2] + k
                mine = (lane == first) | (lane == first + experts)
                total = jnp.sum(jnp.where(mine, got[:, model:], 0.0), axis=1, keepdims=True)
                weights[k, b * cap : (b + 1) * cap, :] = jnp.broadcast_to(total, (cap, LANES))

        greet(plane_devices(e) + [{"group": partner(z)}])
        for m in range(micro):
            turned(m).start()
        for m in range(micro):
            gather.begin(m)
        for m in range(micro):
            use(0, m)
        for m in range(micro):
            turned(m).wait_recv()
            gather.begin(micro + m)
            use(0, micro + m)
        gather.forward_all(range(count), use)
        for m in range(micro):
            turned(m).wait_send()
        for c in range(count):
            gather.finish(c)

    vmem = pl.BlockSpec(memory_space=pltpu.VMEM)
    total = n * count * cap
    return pl.pallas_call(
        kernel,
        in_specs=[SMEM_SPEC, vmem, vmem],
        out_specs=[vmem, vmem],
        out_shape=[
            jax.ShapeDtypeStruct((per, total, model), BF16),
            jax.ShapeDtypeStruct((per, total, LANES), F32),
        ],
        scratch_shapes=[
            pltpu.VMEM((n, count, tokens, width), BF16),
            pltpu.SemaphoreType.DMA((micro,)),
            pltpu.SemaphoreType.DMA((micro,)),
            pltpu.SemaphoreType.DMA((n, count)),
            pltpu.SemaphoreType.DMA((n, count)),
        ],
        compiler_params=params(4),
        cost_estimate=cost(6e10, 4e7),
        name="plane_dispatch",
    )(where, payload, ranks)


def plane_return(rows, ranks, micro, tokens, cap):
    per = len(rows)
    width = rows[0].shape[1]
    n, split = 8, 2
    count = split * micro
    chunks = list(range(micro, count)) + list(range(micro))

    def kernel(rank_ref, *refs):
        ins, out, refs = refs[:per], refs[per], refs[per + 1 :]
        parts, z_out, z_in, z_send, z_recv, scratch = *refs[:5], refs[5:]
        e, z = lax.axis_index("expert"), lax.axis_index("group")
        red = Reduce(e, lambda r, c: parts.at[r, c], [c % 2 for c in range(count)], *scratch)

        def produce(r, c):
            b = r * count + c
            total = None
            for k in range(per):
                one = mm(
                    pick(rank_ref[b, k : k + 1, :], cap), ins[k][b * cap : (b + 1) * cap, :], TN
                )
                total = one if total is None else total + one
            parts[r, c] = total.astype(BF16)

        def turned(m):
            return remote(
                z_out.at[m], z_in.at[m], z_send.at[m], z_recv.at[m], {"group": partner(z)}
            )

        greet(plane_devices(e) + [{"group": partner(z)}])
        for r in (7, 3, 5):
            for c in chunks:
                produce(r, c)
                red.begin(r, c)
        for c in chunks:
            produce(6, c)
        red.diagonal(chunks)
        for r in (2, 4):
            for c in chunks:
                produce(r, c)
        red.sides(chunks)
        for c in chunks:
            produce(1, c)
            red.begin(1, c)
        for c in chunks:
            produce(0, c)
        for c in chunks:
            terms = red.total(c)
            if c >= micro:
                add_rows(z_out.at[c - micro], terms)
                turned(c - micro).start()
            else:
                turned(c).wait_recv()
                add_rows(out.at[c], terms + [z_in.at[c]])
        for m in range(micro):
            turned(m).wait_send()
        for c in chunks:
            red.finish(c)

    vmem = pl.BlockSpec(memory_space=pltpu.VMEM)
    return pl.pallas_call(
        kernel,
        in_specs=[vmem] * (1 + per),
        out_specs=vmem,
        out_shape=jax.ShapeDtypeStruct((micro, tokens, width), F32),
        scratch_shapes=[
            pltpu.VMEM((n, count, tokens, width), BF16),
            pltpu.VMEM((micro, tokens, width), BF16),
            pltpu.VMEM((micro, tokens, width), BF16),
            pltpu.SemaphoreType.DMA((micro,)),
            pltpu.SemaphoreType.DMA((micro,)),
        ]
        + reduce_scratch(count, tokens, width),
        compiler_params=params(5),
        cost_estimate=cost(6e10, 4e7),
        name="plane_return",
    )(ranks, *rows)


def plane_gradients(products, extra, groups):
    n = 8
    depth = products[0][0].shape[1]
    widths = [b.shape[1] for a, b in products]
    width = sum(widths) + extra.shape[1]
    rows = depth // (groups * n)
    tile = 512
    flat = [x for pair in products for x in pair]

    def kernel(*refs):
        ins, extra_ref, refs = refs[: len(flat)], refs[len(flat)], refs[len(flat) + 1 :]
        out, wide, parts, z_out, z_in, slots, z_send, z_recv, send, recv, local = refs[:11]
        scratch = refs[11:]
        e, z = lax.axis_index("expert"), lax.axis_index("group")
        red = Reduce(e, lambda r, c: parts.at[r, c], [c % 2 for c in range(groups)], *scratch)
        greet(
            plane_devices(e)
            + [{"group": lax.rem(z + s, groups)} for s in range(1, groups)]
        )

        def cut(lo, size):
            for r in range(n):
                for s in range(groups):
                    row = (lax.rem(z + s, groups) * n + flip(e, r)) * rows
                    at = pl.ds(pl.multiple_of(row, 16), rows)
                    parts[r, s, :, lo : lo + size] = wide[at, :size].astype(BF16)

        lo = 0
        for i, count in enumerate(widths):
            for start in range(0, count, tile):
                size = min(tile, count - start)
                wide[:, :size] = mm(ins[2 * i][...], ins[2 * i + 1][:, start : start + size], TN)
                cut(lo, size)
                lo += size
        wide[:, : extra_ref.shape[1]] = extra_ref[...]
        cut(lo, extra_ref.shape[1])

        chunks = list(range(1, groups)) + [0]
        for r in (7, 3, 5, 1):
            for c in chunks:
                red.begin(r, c)
        red.diagonal(chunks)
        red.sides(chunks)

        def far(s):
            return remote(
                z_out.at[s], z_in.at[s], z_send.at[s], z_recv.at[s],
                {"group": lax.rem(z + s, groups)},
            )

        for c in chunks:
            add_rows(z_out.at[c], red.total(c))
            if c:
                far(c).start()
        for c in range(1, groups):
            far(c).wait_recv()
        add_rows(slots.at[0], [z_out.at[0]] + [z_in.at[c] for c in range(1, groups)])

        middle = width // 2 // LANES * LANES
        spans = [(0, middle), (middle, width)]

        def loc(r, q, c):
            return slots.at[q, :, spans[c][0] : spans[c][1]]

        gather = Gather(e, lambda c: loc(0, 0, c), loc, [0, 1], send, recv)
        for c in range(2):
            gather.begin(c)
        gather.forward_all(range(2))
        for r in range(n):
            row = pl.multiple_of(flip(e, r) * rows, 16)
            out[pl.ds(row, rows), :] = slots[r].astype(F32)
        for c in range(2):
            gather.finish(c)
        for c in range(1, groups):
            far(c).wait_send()
        for c in chunks:
            red.finish(c)

    vmem = pl.BlockSpec(memory_space=pltpu.VMEM)
    return pl.pallas_call(
        kernel,
        in_specs=[vmem] * (len(flat) + 1),
        out_specs=vmem,
        out_shape=jax.ShapeDtypeStruct((n * rows, width), F32),
        scratch_shapes=[
            pltpu.VMEM((depth, tile), F32),
            pltpu.VMEM((n, groups, rows, width), BF16),
            pltpu.VMEM((groups, rows, width), BF16),
            pltpu.VMEM((groups, rows, width), BF16),
            pltpu.VMEM((n, rows, width), BF16),
            pltpu.SemaphoreType.DMA((groups,)),
            pltpu.SemaphoreType.DMA((groups,)),
            pltpu.SemaphoreType.DMA((n, 2)),
            pltpu.SemaphoreType.DMA((n, 2)),
            pltpu.SemaphoreType.DMA((2,)),
        ]
        + reduce_scratch(groups, rows, width),
        compiler_params=params(6),
        cost_estimate=cost(8e10, 4e7),
        name="plane_gradients",
    )(*flat, extra)


def gather_flags(slots, where, per, cap, model):
    n, count, tokens, width = slots.shape

    def kernel(at_ref, in_ref, out, ranks, flags):
        row = lax.broadcasted_iota(jnp.int32, (tokens, tokens), 0)
        col = lax.broadcasted_iota(jnp.int32, (tokens, tokens), 1)
        before = jnp.where(row < col, 1.0, 0.0).astype(BF16)
        for b in range(count):
            payload = in_ref[0, b]
            flags[...] = payload[:, model:].astype(F32).T
            picked = jnp.concatenate(
                [flags[pl.ds(at_ref[2] + k, 1), :] for k in range(per)], axis=0
            )
            slot = jnp.where(picked > 0.0, mm(picked.astype(BF16), before), -1.0)
            ranks[b] = slot
            for k in range(per):
                out[k, b * cap : (b + 1) * cap, :] = mm(
                    pick(slot[k : k + 1], cap), payload[:, :model]
                ).astype(BF16)

    return pl.pallas_call(
        kernel,
        grid_spec=pltpu.PrefetchScalarGridSpec(
            num_scalar_prefetch=1,
            grid=(n,),
            in_specs=[
                pl.BlockSpec(
                    (1, count, tokens, width),
                    lambda r, at: (jnp.bitwise_xor(at[1], r), 0, 0, 0),
                )
            ],
            out_specs=[
                pl.BlockSpec((per, count * cap, model), lambda r, at: (0, r, 0)),
                pl.BlockSpec((count, per, tokens), lambda r, at: (r, 0, 0)),
            ],
            scratch_shapes=[pltpu.VMEM((LANES, tokens), F32)],
        ),
        out_shape=[
            jax.ShapeDtypeStruct((per, n * count * cap, model), BF16),
            jax.ShapeDtypeStruct((n * count, per, tokens), F32),
        ],
        cost_estimate=cost(5e9, 3e7),
        name="gather_flags",
    )(where, slots)


def scatter_rows(rows, ranks, where, n, count, tokens, cap):
    per, width = len(rows), rows[0].shape[1]

    def kernel(at_ref, rank_ref, *refs):
        ins, out = refs[:per], refs[per]
        for b in range(count):
            total = None
            for k in range(per):
                one = mm(
                    pick(rank_ref[b, k : k + 1, :], cap), ins[k][b * cap : (b + 1) * cap, :], TN
                )
                total = one if total is None else total + one
            out[0, b] = total.astype(BF16)

    return pl.pallas_call(
        kernel,
        grid_spec=pltpu.PrefetchScalarGridSpec(
            num_scalar_prefetch=1,
            grid=(n,),
            in_specs=[pl.BlockSpec((count, per, tokens), lambda r, at: (r, 0, 0))]
            + [pl.BlockSpec((count * cap, width), lambda r, at: (r, 0))] * per,
            out_specs=pl.BlockSpec(
                (1, count, tokens, width), lambda r, at: (jnp.bitwise_xor(at[1], r), 0, 0, 0)
            ),
        ),
        out_shape=jax.ShapeDtypeStruct((n, count, tokens, width), BF16),
        cost_estimate=cost(5e9, 3e7),
        name="scatter_rows",
    )(where, ranks, *rows)


def expert_step(k, at, rows_in, grads_in, weights, own, far, experts, tile):
    per, total, model = rows_in.shape
    part, ff = own[0].shape[1:]
    groups = model // part
    steps = total // tile
    held_count = 3 + 2 * (groups - 1)

    def kernel(at_ref, x_ref, d_ref, w_ref, *refs):
        sources, refs = refs[:held_count], refs[held_count:]
        o_ref, r_ref, refs = refs[0], refs[1], refs[2:]
        outs, refs = refs[: 2 * groups], refs[2 * groups :]
        acc_gate, acc_up, acc_down, gate_ref, up_ref, down_ref, sems = refs
        step = pl.program_id(0)

        @pl.when(step == 0)
        def _():
            copies = []
            for s in range(groups):
                z = lax.rem(at_ref[0] - s + groups, groups)
                at_z = pl.ds(pl.multiple_of(z * part, 128), part)
                if s == 0:
                    mine = at_ref[3] + k
                    three = [sources[i].at[mine] for i in range(3)]
                else:
                    pair = sources[3 + 2 * (s - 1)]
                    three = [pair.at[0], pair.at[1], sources[4 + 2 * (s - 1)]]
                for i, dst in enumerate(
                    [gate_ref.at[at_z, :], up_ref.at[at_z, :], down_ref.at[:, at_z]]
                ):
                    copies.append(pltpu.make_async_copy(three[i], dst, sems.at[3 * s + i]))
            for one in copies:
                one.start()
            for one in copies:
                one.wait()

        x, d = x_ref[0], d_ref[0]
        w = w_ref[0, :, 0:1]
        gate_pre = mm(x, gate_ref[...])
        up_pre = mm(x, up_ref[...])
        sig = 1.0 / (1.0 + jnp.exp(-gate_pre))
        silu = gate_pre * sig
        active_wide = silu * up_pre
        active = active_wide.astype(BF16)
        o_ref[...] = (mm(active, down_ref[...]) * w).astype(BF16)
        d_raw = mm(d, down_ref[...], NT)
        d_gates = jnp.sum(active.astype(F32) * d_raw, axis=1, keepdims=True)
        d_active = d_raw * w
        d_up = (d_active * silu).astype(BF16)
        d_gate = (d_active * up_pre * sig * (1.0 + gate_pre * (1.0 - sig))).astype(BF16)
        d_row = mm(d_gate, gate_ref[...], NT) + mm(d_up, up_ref[...], NT)
        r_ref[:, :model] = d_row.astype(BF16)
        high = d_gates.astype(BF16).astype(F32)
        lane = lax.broadcasted_iota(jnp.int32, (tile, LANES), 1)
        e = at_ref[2] + k
        r_ref[:, model:] = (
            jnp.where(lane == e, high, 0.0) + jnp.where(lane == e + experts, d_gates - high, 0.0)
        ).astype(BF16)
        new_gate = mm(x, d_gate, TN)
        new_up = mm(x, d_up, TN)
        new_down = mm((active_wide * w).astype(BF16), d, TN)

        @pl.when(step == 0)
        def _():
            acc_gate[...] = new_gate
            acc_up[...] = new_up
            acc_down[...] = new_down

        @pl.when(step > 0)
        def _():
            acc_gate[...] += new_gate
            acc_up[...] += new_up
            acc_down[...] += new_down

        @pl.when(step == steps - 1)
        def _():
            for s in range(groups):
                z = lax.rem(at_ref[0] + s, groups)
                at_z = pl.ds(pl.multiple_of(z * part, 128), part)
                outs[2 * s][0] = acc_gate[at_z, :].astype(BF16)
                outs[2 * s][1] = acc_up[at_z, :].astype(BF16)
                outs[2 * s + 1][...] = acc_down[:, at_z].astype(BF16)

    def held(shape):
        return pl.BlockSpec(shape, lambda t: (0,) * len(shape), pipeline_mode=pl.Buffered(1))

    grads = [(2, part, ff), (ff, part)] * groups
    row_spec = pl.BlockSpec((1, tile, model), lambda t: (k, t, 0))
    out = pl.pallas_call(
        kernel,
        grid=(steps,),
        in_specs=[SMEM_SPEC, row_spec, row_spec, pl.BlockSpec((1, tile, LANES), lambda t: (k, t, 0))]
        + [ANY_SPEC] * held_count,
        out_specs=[
            pl.BlockSpec((tile, model), lambda t: (t, 0)),
            pl.BlockSpec((tile, model + LANES), lambda t: (t, 0)),
        ]
        + [held(shape) for shape in grads],
        out_shape=[
            jax.ShapeDtypeStruct((total, model), BF16),
            jax.ShapeDtypeStruct((total, model + LANES), BF16),
        ]
        + [jax.ShapeDtypeStruct(shape, BF16) for shape in grads],
        scratch_shapes=[
            pltpu.VMEM((model, ff), F32),
            pltpu.VMEM((model, ff), F32),
            pltpu.VMEM((ff, model), F32),
            pltpu.VMEM((model, ff), BF16),
            pltpu.VMEM((model, ff), BF16),
            pltpu.VMEM((ff, model), BF16),
            pltpu.SemaphoreType.DMA((3 * groups,)),
        ],
        compiler_params=pltpu.CompilerParams(vmem_limit_bytes=62 * 1024 * 1024),
        cost_estimate=cost(36 * total * model * ff, 10 * total * model),
        name="expert_step",
    )(at, rows_in, grads_in, weights, *own, *[x for pair in far for x in pair])
    return out[0], out[1], [(out[2 + 2 * s], out[3 + 2 * s]) for s in range(groups)]


def layer_plane(
    tokens,
    cotangent,
    routes,
    norm_one,
    query_key_value_weight,
    out_weight,
    norm_two,
    router_weight,
    gate_weight,
    up_weight,
    down_weight,
):
    n = lax.axis_size("expert")
    groups = lax.axis_size("group")
    me = lax.axis_index("expert")
    z = lax.axis_index("group")
    micro, count, model = tokens.shape
    exp_here, part, ff = gate_weight.shape
    experts = router_weight.shape[1]
    split = 2
    per = exp_here // split
    query_width = QUERY_HEADS * HEAD_SIZE
    kv_width = KEY_VALUE_HEADS * HEAD_SIZE
    cap = max(2, 3 * TOPK * PR_DEV // experts)
    where = jnp.stack([z, me, me * exp_here + (z % split) * per, (z % split) * per]).astype(jnp.int32)
    rows_here = part // n
    rows = micro * count

    misc = jnp.concatenate(
        [
            norm_one[:, None],
            norm_two[:, None],
            jnp.zeros((part, experts - 2), BF16),
            router_weight,
            jnp.zeros((part, LANES - 2 * experts), BF16),
        ],
        axis=1,
    )
    cut = lambda x: lax.dynamic_slice_in_dim(x, me * rows_here, rows_here, axis=0)
    shares = [cut(query_key_value_weight), jnp.concatenate([cut(out_weight), cut(misc)], axis=1)]
    sets = [[x] + [shift(x, s) for s in range(1, groups)] for x in shares]
    (gate_from, up_from, down_from), sets = lax.optimization_barrier(
        ((gate_weight, up_weight, down_weight), sets)
    )
    weights_far = []
    for k in range(per):
        far = []
        for s in range(1, groups):
            index = ((z + s) % split) * per + k
            take = lambda x: lax.dynamic_index_in_dim(x, index, 0, keepdims=False)
            far.append(
                (shift(jnp.stack([take(gate_from), take(up_from)]), s), shift(take(down_from), s))
            )
        weights_far.append(far)
    qkv_full, rest_full = plane_weights(sets)
    out_full, misc_full = rest_full[:, :model], rest_full[:, model:]
    gain_one = misc_full[:, 0].astype(F32)
    gain_two = misc_full[:, 1].astype(F32)
    router_full = misc_full[:, experts : 2 * experts]

    expert_ids = jnp.arange(experts, dtype=jnp.int32)
    named = jnp.any(routes[..., None] == expert_ids, axis=2)
    pad = jnp.zeros((micro, count, LANES - experts), BF16)
    d_payload = jnp.concatenate([cotangent, named.astype(BF16), pad], axis=2)
    both = jnp.concatenate([d_payload, turn(d_payload, 1, split)], axis=0)
    d_slots = lax.all_gather(both, "expert", axis=0)
    grads_in, ranks = gather_flags(d_slots, where, per, cap, model)

    x = tokens.reshape(rows, model).astype(F32)
    inverse_one = lax.rsqrt(jnp.mean(x * x, axis=-1, keepdims=True) + 1e-05)
    normed = (x * inverse_one * gain_one).astype(BF16)
    cosine, sine = rope_tables(me, PR_DEV * n)
    heads_rope = QUERY_HEADS + KEY_VALUE_HEADS
    cosine = jnp.tile(jnp.concatenate([cosine, cosine], axis=1), (micro, heads_rope))
    sine = jnp.tile(jnp.concatenate([-sine, sine], axis=1), (micro, heads_rope))
    cosine, sine = lax.optimization_barrier((cosine, sine))
    project = mm(normed, qkv_full)
    roped = rotate(project[:, : query_width + kv_width], cosine, sine).astype(BF16)
    query = roped[:, :query_width].reshape(micro, count, query_width)
    key_value = jnp.concatenate(
        [roped[:, query_width:], project[:, query_width + kv_width :].astype(BF16)], axis=1
    ).reshape(micro, count, 2 * kv_width)
    mixed, kv_slots = plane_attention(query, key_value)
    mixed = mixed.reshape(rows, query_width)
    hidden = x + mm(mixed, out_full)
    inverse_two = lax.rsqrt(jnp.mean(hidden * hidden, axis=-1, keepdims=True) + 1e-05)
    normed_two = (hidden * inverse_two * gain_two).astype(BF16)
    logits = mm(normed_two, router_full)
    chosen = named.reshape(rows, experts)
    logits = jnp.where(chosen, logits, NEG_FILL)
    top = jnp.max(logits, axis=-1, keepdims=True)
    raised = jnp.where(chosen, jnp.exp(logits - top), 0.0)
    gate_probs = raised / jnp.sum(raised, axis=-1, keepdims=True)

    high = gate_probs.astype(BF16)
    low = (gate_probs - high.astype(F32)).astype(BF16)
    payload = jnp.concatenate(
        [normed_two, high, low, jnp.zeros((rows, LANES - 2 * experts), BF16)], axis=1
    ).reshape(micro, count, model + LANES)
    rows_in, row_weights = plane_dispatch(payload, ranks, where, per, cap, model, experts)
    tile = 2 * micro * split * cap
    outs, backs, weight_terms = [], [], []
    for k in range(per):
        out_rows, back_rows, terms = expert_step(
            k, where, rows_in, grads_in, row_weights, (gate_weight, up_weight, down_weight),
            weights_far[k], experts, tile,
        )
        outs.append(out_rows)
        backs.append(back_rows)
        weight_terms.append(terms)
    back = plane_return(backs, ranks, micro, count, cap).reshape(rows, model + LANES)

    mixture_parts = scatter_rows(outs, ranks, where, n, micro * split, count, cap)
    mixture_sum = lax.psum_scatter(mixture_parts, "expert", scatter_dimension=0, tiled=False)
    mixture = mixture_sum[:micro].astype(F32) + turn(mixture_sum[micro:], 1, split).astype(F32)
    block_out = (hidden + mixture.reshape(rows, model)).astype(BF16).reshape(tokens.shape)

    sums = [[None, None] for _ in range(split)]
    merged = []
    for k in range(per):
        sums = [None] * split
        for s in range(groups):
            pair, down = weight_terms[k][s]
            got = [(shift(t, s) if s else t).astype(F32) for t in (pair, down)]
            c = s % split
            sums[c] = got if sums[c] is None else [a + b for a, b in zip(sums[c], got)]
        merged.append(
            [
                [lax.select_n((z - p) % split, sums[0][i], sums[1][i]) for i in range(2)]
                for p in range(split)
            ]
        )
    order = [(p, k) for p in range(split) for k in range(per)]
    gate_grad = jnp.stack([merged[k][p][0][0] for p, k in order])
    up_grad = jnp.stack([merged[k][p][0][1] for p, k in order])
    down_grad = jnp.stack([merged[k][p][1] for p, k in order])

    d_out = cotangent.reshape(rows, model).astype(F32)
    d_gates = back[:, model : model + experts] + back[:, model + experts : model + 2 * experts]
    d_logits = gate_probs * (d_gates - jnp.sum(gate_probs * d_gates, axis=-1, keepdims=True))
    router_grad = lax.dot_general(normed_two.astype(F32), d_logits, TN, precision=HIGHEST)
    d_normed_two = back[:, :model] + lax.dot_general(
        d_logits, router_full.astype(F32), NT, precision=HIGHEST
    )

    def rms_back(inputs, inverse, gain, upstream):
        scaled = gain * upstream
        return inverse * scaled - inputs * inverse * inverse * inverse * jnp.mean(
            scaled * inputs, axis=-1, keepdims=True
        )

    grad_two = jnp.sum(d_normed_two * hidden * inverse_two, axis=0)
    d_hidden = d_out + rms_back(hidden, inverse_two, gain_two, d_normed_two)
    d_attn = d_hidden.astype(BF16)
    d_mixed = mm(d_attn, out_full, NT).astype(BF16).reshape(micro, count, query_width)
    d_query, d_kv = plane_attention_backward(query, kv_slots, d_mixed)
    d_query = d_query.reshape(rows, query_width)
    d_kv = d_kv.reshape(rows, 2 * kv_width)
    q_cos, q_sin = cosine[:, :query_width], sine[:, :query_width]
    d_query_low = rotate(d_query, q_cos, -q_sin).astype(BF16)
    d_key_low = rotate(d_kv[:, :kv_width], q_cos[:, :kv_width], -q_sin[:, :kv_width]).astype(BF16)
    d_project = jnp.concatenate(
        [d_query_low, d_key_low, d_kv[:, kv_width:].astype(BF16)], axis=1
    )
    d_normed = mm(d_project, qkv_full, NT)
    grad_one = jnp.sum(d_normed * x * inverse_one, axis=0)
    input_grad = (d_hidden + rms_back(x, inverse_one, gain_one, d_normed)).reshape(tokens.shape)
    misc_grad = jnp.concatenate(
        [
            grad_one[:, None],
            grad_two[:, None],
            jnp.zeros((model, experts - 2), F32),
            router_grad,
            jnp.zeros((model, LANES - 2 * experts), F32),
        ],
        axis=1,
    )
    dense = plane_gradients([(mixed, d_attn), (normed, d_project)], misc_grad, groups)
    misc_sum = dense[:, model + query_width + 2 * kv_width :]
    return (
        block_out,
        input_grad,
        misc_sum[:, 0],
        dense[:, model : model + query_width + 2 * kv_width],
        dense[:, :model],
        misc_sum[:, 1],
        misc_sum[:, experts : 2 * experts],
        gate_grad,
        up_grad,
        down_grad,
    )


def per_device(*arrays):
    n, groups = lax.axis_size("expert"), lax.axis_size("group")
    exp_here, part, ff = arrays[8].shape
    plane = (
        n == 8
        and exp_here % 2 == 0
        and groups % 2 == 0
        and part % (16 * n) == 0
        and part % LANES == 0
        and arrays[0].shape[0] == 2
    )
    return (layer_plane if plane else layer_general)(*arrays)


def solution(mesh):
    rows = P(None, ("group", "expert"), None)
    return jax.shard_map(
        per_device,
        mesh=mesh,
        in_specs=(
            rows,
            rows,
            rows,
            P("group"),
            P("group", None),
            P("group", None),
            P("group"),
            P("group", None),
            P("expert", "group", None),
            P("expert", "group", None),
            P("expert", None, "group"),
        ),
        out_specs=(
            rows,
            rows,
            P("group"),
            P("group", None),
            P("group", None),
            P("group"),
            P("group", None),
            P("expert", "group", None),
            P("expert", "group", None),
            P("expert", None, "group"),
        ),
        check_vma=False,
    )
```

```python
import functools

import jax
import jax.numpy as jnp
from jax import lax
from jax.experimental import pallas as pl
from jax.experimental.pallas import tpu as pltpu
from jax.sharding import PartitionSpec as P

QUERY_HEADS = 24
KEY_VALUE_HEADS = 8
HEAD_SIZE = 64
TOPK = 8
CONT = 256
PR_DEV = 64
LANES = 128
SCORE_SCALE = 0.125
NEG_FILL = -1e30
HIGHEST = lax.Precision.HIGHEST
F32 = jnp.float32
BF16 = jnp.bfloat16

NN = (((1,), (0,)), ((), ()))
NT = (((1,), (1,)), ((), ()))
TN = (((0,), (0,)), ((), ()))


def mm(a, b, dims=NN):
    return lax.dot_general(a, b, dims, preferred_element_type=F32)


def swap(x, bit):
    n = lax.axis_size("expert")
    return lax.ppermute(x, "expert", [(i, i ^ bit) for i in range(n)])


def shift(x, step):
    n = lax.axis_size("group")
    return lax.ppermute(x, "group", [(i, (i + step) % n) for i in range(n)])


def turn(x, step, split):
    n = lax.axis_size("group")
    return lax.ppermute(
        x, "group", [((i // split) * split + (i + step) % split, i) for i in range(n)]
    )


def outer_bits(n):
    return [1 << i for i in range(1, n.bit_length() - 1)]


def spread(x, order):
    n = lax.axis_size("expert")
    outer = outer_bits(n)
    if len(outer) == 2:
        a, b = outer
        xa, xb = swap(x, a), swap(x, b)
        slots = {0: x, a: xa, b: xb, a ^ b: swap(xa, b) if order == 0 else swap(xb, a)}
    else:
        slots = {0: x}
        for bit in outer:
            slots.update({r ^ bit: swap(y, bit) for r, y in list(slots.items())})
    if n > 1:
        slots.update({r ^ 1: swap(y, 1) for r, y in list(slots.items())})
    return [slots[r] for r in range(n)]


def plus(a, b):
    return (a.astype(F32) + b.astype(F32)).astype(BF16)


def collect(parts, order):
    n = lax.axis_size("expert")
    outer = outer_bits(n)
    keep = {r: parts[r] for r in range(n)}
    if n > 1:
        keep = {r: plus(keep[r], swap(keep[r ^ 1], 1)) for r in range(0, n, 2)}
    if len(outer) == 2:
        a, b = outer
        if order == 0:
            keep[a] = plus(keep[a], swap(keep[a ^ b], b))
        else:
            keep[b] = plus(keep[b], swap(keep[a ^ b], a))
        return (
            keep[0].astype(F32) + swap(keep[a], a).astype(F32) + swap(keep[b], b).astype(F32)
        )
    for bit in reversed(outer):
        keep = {r: plus(keep[r], swap(keep[r ^ bit], bit)) for r in keep if not r & bit}
    return keep[0].astype(F32)


def full_spec(shape):
    return pl.BlockSpec(shape, lambda *_: (0,) * len(shape))


SMEM_SPEC = pl.BlockSpec(memory_space=pltpu.SMEM)
ANY_SPEC = pl.BlockSpec(memory_space=pl.ANY)


def cost(flops, moved):
    return pl.CostEstimate(flops=int(flops), bytes_accessed=int(moved), transcendentals=0)


def assemble(pieces, place, shape, where):
    count = len(pieces)

    def kernel(at_ref, *refs):
        ins, out, sems = refs[:count], refs[count], refs[count + 1]
        copies = []
        for i in range(count):
            row, column = place(i, at_ref[0], at_ref[1])
            r, c = pieces[i].shape
            copies.append(
                pltpu.make_async_copy(
                    ins[i],
                    out.at[pl.ds(pl.multiple_of(row, 16), r), pl.ds(pl.multiple_of(column, 128), c)],
                    sems.at[i],
                )
            )
        for one in copies:
            one.start()
        for one in copies:
            one.wait()

    return pl.pallas_call(
        kernel,
        grid=(1,),
        in_specs=[SMEM_SPEC] + [ANY_SPEC] * count,
        out_specs=full_spec(shape),
        out_shape=jax.ShapeDtypeStruct(shape, pieces[0].dtype),
        scratch_shapes=[pltpu.SemaphoreType.DMA((count,))],
        cost_estimate=cost(0, 4 * shape[0] * shape[1]),
        name="assemble",
    )(where, *pieces)


def gather_dense(piece, cuts, where):
    groups, n = lax.axis_size("group"), lax.axis_size("expert")
    rows, columns = piece.shape
    own = [piece[:, lo:hi] for lo, hi in cuts]
    far = [[shift(x, s) for x in own] for s in range(1, groups)]
    names, pieces = [], []
    for h, (lo, hi) in enumerate(cuts):
        joined = jnp.concatenate([far[s - 1][h] for s in range(1, groups)], axis=0)
        for r, x in enumerate(spread(own[h], h % 2)):
            names.append((0, r, lo))
            pieces.append(x)
        for r, x in enumerate(spread(joined, h % 2)):
            for s in range(1, groups):
                names.append((s, r, lo))
                pieces.append((x, (s - 1) * rows, rows))
    total = groups * n * rows
    arrays, index = [], []
    for entry in pieces:
        if isinstance(entry, tuple):
            if not arrays or arrays[-1] is not entry[0]:
                arrays.append(entry[0])
            index.append((len(arrays) - 1, entry[1], entry[2]))
        else:
            arrays.append(entry)
            index.append((len(arrays) - 1, 0, rows))
    count, held = len(index), len(arrays)

    def kernel(at_ref, *refs):
        ins, out, sems = refs[:held], refs[held], refs[held + 1]
        copies = []
        for i, (which, start, size) in enumerate(index):
            s, r, lo = names[i]
            z = lax.rem(at_ref[0] - s + groups, groups)
            e = jnp.bitwise_xor(at_ref[1], r)
            row = pl.multiple_of((z * n + e) * rows, 16)
            width = arrays[which].shape[1]
            copies.append(
                pltpu.make_async_copy(
                    ins[which].at[pl.ds(start, size)],
                    out.at[pl.ds(row, rows), pl.ds(lo, width)],
                    sems.at[i],
                )
            )
        for one in copies:
            one.start()
        for one in copies:
            one.wait()

    whole = pl.pallas_call(
        kernel,
        grid=(1,),
        in_specs=[SMEM_SPEC] + [ANY_SPEC] * held,
        out_specs=full_spec((total, columns)),
        out_shape=jax.ShapeDtypeStruct((total, columns), piece.dtype),
        scratch_shapes=[pltpu.SemaphoreType.DMA((count,))],
        cost_estimate=cost(0, 4 * total * columns),
        name="join_rows",
    )(where, *arrays)
    return whole, far


def sliced_outer(a, b, extra, groups, n, where):
    depth = a.shape[1]
    columns = b.shape[1]
    more = 0 if extra is None else extra.shape[1]
    rows = depth // (groups * n)

    def kernel(at_ref, a_ref, b_ref, *refs):
        if more:
            x_ref, refs = refs[0], refs[1:]
        outs, acc = refs[:n], refs[n]
        acc[:, :columns] = mm(a_ref[...], b_ref[...], TN)
        if more:
            acc[:, columns:] = x_ref[...]
        for r in range(n):
            e = jnp.bitwise_xor(at_ref[1], r)
            for s in range(groups):
                z = lax.rem(at_ref[0] + s, groups)
                row = pl.multiple_of((z * n + e) * rows, 16)
                outs[r][s] = acc[pl.ds(row, rows), :].astype(BF16)

    width = columns + more
    return pl.pallas_call(
        kernel,
        grid=(1,),
        in_specs=[SMEM_SPEC, full_spec(a.shape), full_spec(b.shape)]
        + ([full_spec(extra.shape)] if more else []),
        out_specs=[full_spec((groups, rows, width))] * n,
        out_shape=[jax.ShapeDtypeStruct((groups, rows, width), BF16)] * n,
        scratch_shapes=[pltpu.VMEM((depth, width), F32)],
        cost_estimate=cost(2 * a.shape[0] * depth * columns, 2 * depth * width),
        name="sliced_outer",
    )(where, a, b, *([extra] if more else []))


def reduce_dense(parts, order, where):
    groups, n = lax.axis_size("group"), lax.axis_size("expert")
    mine = collect(parts, order)
    total = mine[0]
    low = mine.astype(BF16)
    for s in range(1, groups):
        total = total + shift(low[s], s).astype(F32)
    rows, width = total.shape
    slots = spread(total.astype(BF16), order)

    def kernel(at_ref, *refs):
        out = refs[n]
        for r in range(n):
            e = jnp.bitwise_xor(at_ref[1], r)
            out[pl.ds(pl.multiple_of(e * rows, 16), rows), :] = refs[r][...].astype(F32)

    return pl.pallas_call(
        kernel,
        grid=(1,),
        in_specs=[SMEM_SPEC] + [full_spec((rows, width))] * n,
        out_specs=full_spec((n * rows, width)),
        out_shape=jax.ShapeDtypeStruct((n * rows, width), F32),
        cost_estimate=cost(0, 6 * n * rows * width),
        name="join_sums",
    )(where, *slots)


def attention_masks(n, me):
    shape = (3 * PR_DEV, n * PR_DEV)
    token = lax.rem(lax.broadcasted_iota(jnp.int32, shape, 0), PR_DEV)
    column = lax.broadcasted_iota(jnp.int32, shape, 1)
    key_pos = jnp.bitwise_xor(column // PR_DEV, me) * PR_DEV + lax.rem(column, PR_DEV)
    prompt_ok = key_pos <= me * PR_DEV + token
    slots = CONT // PR_DEV
    shape = (3 * PR_DEV, CONT)
    token = lax.rem(lax.broadcasted_iota(jnp.int32, shape, 0), PR_DEV)
    column = lax.broadcasted_iota(jnp.int32, shape, 1)
    owner = jnp.bitwise_xor(column // PR_DEV, lax.rem(me, slots))
    cont_ok = owner * PR_DEV + lax.rem(column, PR_DEV) <= lax.rem(me, slots) * PR_DEV + token
    return prompt_ok, cont_ok


def head_rows(x, base):
    return jnp.concatenate(
        [x[:, base + i * HEAD_SIZE : base + (i + 1) * HEAD_SIZE] for i in range(3)], axis=0
    )


def row_heads(x):
    return jnp.concatenate([x[i * PR_DEV : (i + 1) * PR_DEV] for i in range(3)], axis=1)


def softmax(scores):
    top = jnp.max(scores, axis=1, keepdims=True)
    weight = jnp.exp(scores - top)
    return weight * (1.0 / jnp.sum(weight, axis=1, keepdims=True))


def load_keys(n, kv_refs, keys):
    for r in range(n):
        keys[r * PR_DEV : (r + 1) * PR_DEV, :] = kv_refs[r][:PR_DEV, :]
    for r in range(CONT // PR_DEV):
        lo = (n + r) * PR_DEV
        keys[lo : lo + PR_DEV, :] = kv_refs[r][PR_DEV:, :]


def group_probs(q_top, q_low, key, prompt_ok, cont_ok, n):
    pr = n * PR_DEV
    top = mm(q_top, key[:pr], NT) * SCORE_SCALE
    top = softmax(jnp.where(prompt_ok, top, NEG_FILL))
    low = mm(q_low, key, NT) * SCORE_SCALE
    low = jnp.concatenate([low[:, :pr], jnp.where(cont_ok, low[:, pr:], NEG_FILL)], axis=1)
    return top, softmax(low)


def attention_forward(query, slots, where):
    n = len(slots)
    width = KEY_VALUE_HEADS * HEAD_SIZE
    tokens = 2 * PR_DEV
    total = n * PR_DEV + CONT

    def kernel(at_ref, q_ref, *refs):
        kv_refs, out_ref, keys = refs[:n], refs[n], refs[n + 1]
        load_keys(n, kv_refs, keys)
        prompt_ok, cont_ok = attention_masks(n, at_ref[1])

        def pair(j, carry):
            q_at = pl.ds(pl.multiple_of(j * 384, 128), 384)
            k_at = pl.ds(pl.multiple_of(j * 128, 128), 128)
            v_at = pl.ds(pl.multiple_of(width + j * 128, 128), 128)
            q_top, q_low = q_ref[:PR_DEV, q_at], q_ref[PR_DEV:, q_at]
            k_two, v_two = keys[:, k_at], keys[:, v_at]
            tops, lows = [], []
            for g in range(2):
                key = k_two[:, g * HEAD_SIZE : (g + 1) * HEAD_SIZE]
                value = v_two[:, g * HEAD_SIZE : (g + 1) * HEAD_SIZE]
                top, low = group_probs(
                    head_rows(q_top, g * 192), head_rows(q_low, g * 192), key, prompt_ok, cont_ok, n
                )
                tops.append(row_heads(mm(top.astype(BF16), value[: n * PR_DEV])))
                lows.append(row_heads(mm(low.astype(BF16), value)))
            out_ref[:PR_DEV, q_at] = jnp.concatenate(tops, axis=1).astype(BF16)
            out_ref[PR_DEV:, q_at] = jnp.concatenate(lows, axis=1).astype(BF16)
            return carry

        lax.fori_loop(0, KEY_VALUE_HEADS // 2, pair, 0)

    return pl.pallas_call(
        kernel,
        grid=(1,),
        in_specs=[SMEM_SPEC, full_spec(query.shape)] + [full_spec((tokens, 2 * width))] * n,
        out_specs=full_spec(query.shape),
        out_shape=jax.ShapeDtypeStruct(query.shape, BF16),
        scratch_shapes=[pltpu.VMEM((total, 2 * width), BF16)],
        cost_estimate=cost(8e9, 4e6),
        name="attention_forward",
    )(where, query, *slots)


def attention_backward(query, slots, d_mixed, where):
    n = len(slots)
    width = KEY_VALUE_HEADS * HEAD_SIZE
    tokens = 2 * PR_DEV
    pr = n * PR_DEV
    total = pr + CONT

    def kernel(at_ref, q_ref, d_ref, *refs):
        kv_refs, refs = refs[:n], refs[n:]
        dq_ref, outs, keys, grads = refs[0], refs[1 : 1 + n], refs[1 + n], refs[2 + n]
        load_keys(n, kv_refs, keys)
        prompt_ok, cont_ok = attention_masks(n, at_ref[1])

        def one_side(prob, d_rows, key, value, q_rows):
            d_prob = mm(d_rows, value, NT)
            delta = jnp.sum(prob * d_prob, axis=1, keepdims=True)
            d_score = (prob * (d_prob - delta)).astype(BF16)
            return (
                mm(d_score, key) * SCORE_SCALE,
                mm(d_score, q_rows, TN) * SCORE_SCALE,
                mm(prob.astype(BF16), d_rows, TN),
            )

        def pair(j, carry):
            q_at = pl.ds(pl.multiple_of(j * 384, 128), 384)
            k_at = pl.ds(pl.multiple_of(j * 128, 128), 128)
            v_at = pl.ds(pl.multiple_of(width + j * 128, 128), 128)
            q_top, q_low = q_ref[:PR_DEV, q_at], q_ref[PR_DEV:, q_at]
            d_top, d_low = d_ref[:PR_DEV, q_at], d_ref[PR_DEV:, q_at]
            k_two, v_two = keys[:, k_at], keys[:, v_at]
            dq_tops, dq_lows, dks, dvs = [], [], [], []
            for g in range(2):
                key = k_two[:, g * HEAD_SIZE : (g + 1) * HEAD_SIZE]
                value = v_two[:, g * HEAD_SIZE : (g + 1) * HEAD_SIZE]
                rows_top, rows_low = head_rows(q_top, g * 192), head_rows(q_low, g * 192)
                top, low = group_probs(rows_top, rows_low, key, prompt_ok, cont_ok, n)
                dq_top, dk_top, dv_top = one_side(
                    top, head_rows(d_top, g * 192), key[:pr], value[:pr], rows_top
                )
                dq_low, dk_low, dv_low = one_side(
                    low, head_rows(d_low, g * 192), key, value, rows_low
                )
                dq_tops.append(row_heads(dq_top))
                dq_lows.append(row_heads(dq_low))
                dks.append(jnp.concatenate([dk_low[:pr] + dk_top, dk_low[pr:]], axis=0))
                dvs.append(jnp.concatenate([dv_low[:pr] + dv_top, dv_low[pr:]], axis=0))
            dq_ref[:PR_DEV, q_at] = jnp.concatenate(dq_tops, axis=1)
            dq_ref[PR_DEV:, q_at] = jnp.concatenate(dq_lows, axis=1)
            grads[:, k_at] = jnp.concatenate(dks, axis=1).astype(BF16)
            grads[:, v_at] = jnp.concatenate(dvs, axis=1).astype(BF16)
            return carry

        lax.fori_loop(0, KEY_VALUE_HEADS // 2, pair, 0)
        for r in range(n):
            outs[r][:PR_DEV, :] = grads[r * PR_DEV : (r + 1) * PR_DEV, :]
            if r < CONT // PR_DEV:
                lo = (n + r) * PR_DEV
                outs[r][PR_DEV:, :] = grads[lo : lo + PR_DEV, :]
            else:
                outs[r][PR_DEV:, :] = jnp.zeros((PR_DEV, 2 * width), BF16)

    out = pl.pallas_call(
        kernel,
        grid=(1,),
        in_specs=[SMEM_SPEC, full_spec(query.shape), full_spec(query.shape)]
        + [full_spec((tokens, 2 * width))] * n,
        out_specs=[full_spec(query.shape)] + [full_spec((tokens, 2 * width))] * n,
        out_shape=[jax.ShapeDtypeStruct(query.shape, F32)]
        + [jax.ShapeDtypeStruct((tokens, 2 * width), BF16)] * n,
        scratch_shapes=[pltpu.VMEM((total, 2 * width), BF16), pltpu.VMEM((total, 2 * width), BF16)],
        cost_estimate=cost(2e10, 8e6),
        name="attention_backward",
    )(where, query, d_mixed, *slots)
    return out[0], out[1:]


def pick(slot_row, cap):
    rows = lax.broadcasted_iota(jnp.int32, (cap, slot_row.shape[1]), 0).astype(F32)
    return jnp.where(slot_row == rows, 1.0, 0.0).astype(BF16)


def dispatch_grads(arrays, at, per, cap, model, buffers, place, blocks_total):
    count = len(arrays)
    split, tokens, width = arrays[0].shape
    blocks = count * split
    first = buffers is None

    def kernel(at_ref, *refs):
        ins = refs[:count]
        out, ranks = refs[-3], refs[-2]
        flags = refs[-1]
        row = lax.broadcasted_iota(jnp.int32, (tokens, tokens), 0)
        col = lax.broadcasted_iota(jnp.int32, (tokens, tokens), 1)
        before = jnp.where(row < col, 1.0, 0.0).astype(BF16)
        for i in range(count):
            for j in range(split):
                b = i * split + j
                payload = ins[i][j]
                flags[...] = payload[:, model:].astype(F32).T
                picked = jnp.concatenate(
                    [flags[pl.ds(at_ref[2] + k, 1), :] for k in range(per)], axis=0
                )
                rank = mm(picked.astype(BF16), before)
                slot = jnp.where(picked > 0.0, rank, -1.0)
                ranks[b] = slot
                for k in range(per):
                    out[k, b * cap : (b + 1) * cap, :] = mm(
                        pick(slot[k : k + 1], cap), payload[:, :model]
                    ).astype(BF16)

    shapes = [
        jax.ShapeDtypeStruct((per, blocks_total * cap, model), BF16),
        jax.ShapeDtypeStruct((blocks_total, per, tokens), F32),
    ]
    return pl.pallas_call(
        kernel,
        grid=(1,),
        in_specs=[SMEM_SPEC]
        + [full_spec(arrays[0].shape)] * count
        + ([] if first else [ANY_SPEC] * 2),
        out_specs=[
            pl.BlockSpec((per, blocks * cap, model), lambda *_: (0, place, 0)),
            pl.BlockSpec((blocks, per, tokens), lambda *_: (place, 0, 0)),
        ],
        out_shape=shapes,
        scratch_shapes=[pltpu.VMEM((LANES, tokens), F32)],
        input_output_aliases={} if first else {1 + count: 0, 2 + count: 1},
        cost_estimate=cost(1e9, 6e6),
        name="dispatch_grads",
    )(at, *arrays, *([] if first else buffers))


def dispatch_rows(arrays, ranks, at, per, cap, model, experts, buffers, place, blocks_total):
    count = len(arrays)
    split, tokens, width = arrays[0].shape
    blocks = count * split
    first = buffers is None

    def kernel(at_ref, rank_ref, *refs):
        ins = refs[:count]
        out, weights = refs[-2], refs[-1]
        lane = lax.broadcasted_iota(jnp.int32, (cap, LANES), 1)
        for i in range(count):
            for j in range(split):
                b = i * split + j
                payload = ins[i][j]
                for k in range(per):
                    got = mm(pick(rank_ref[b, k : k + 1, :], cap), payload)
                    out[k, b * cap : (b + 1) * cap, :] = got[:, :model].astype(BF16)
                    tail = got[:, model:]
                    e = at_ref[2] + k
                    mine = (lane == e) | (lane == e + experts)
                    total = jnp.sum(jnp.where(mine, tail, 0.0), axis=1, keepdims=True)
                    weights[k, b * cap : (b + 1) * cap, :] = jnp.broadcast_to(total, (cap, LANES))

    shapes = [
        jax.ShapeDtypeStruct((per, blocks_total * cap, model), BF16),
        jax.ShapeDtypeStruct((per, blocks_total * cap, LANES), F32),
    ]
    return pl.pallas_call(
        kernel,
        grid=(1,),
        in_specs=[SMEM_SPEC, pl.BlockSpec((blocks, per, tokens), lambda *_: (place, 0, 0))]
        + [full_spec(arrays[0].shape)] * count
        + ([] if first else [ANY_SPEC] * 2),
        out_specs=[
            pl.BlockSpec((per, blocks * cap, model), lambda *_: (0, place, 0)),
            pl.BlockSpec((per, blocks * cap, LANES), lambda *_: (0, place, 0)),
        ],
        out_shape=shapes,
        input_output_aliases={} if first else {2 + count: 0, 3 + count: 1},
        cost_estimate=cost(1e9, 6e6),
        name="dispatch_rows",
    )(at, ranks, *arrays, *([] if first else buffers))


def run_expert(k, at, rows_in, grads_in, weights, gate, up, down, experts, tile, groups, cut):
    per, total, model = rows_in.shape
    ff = gate.shape[1]
    part = model // groups
    steps = total // tile

    def kernel(at_ref, x_ref, d_ref, w_ref, gate_ref, up_ref, down_ref, o_ref, r_ref, *refs):
        outs, (acc_gate, acc_up, acc_down) = refs[:-3], refs[-3:]
        step = pl.program_id(0)
        x, d = x_ref[0], d_ref[0]
        w = w_ref[0, :, 0:1]
        gate_pre = mm(x, gate_ref[...])
        up_pre = mm(x, up_ref[...])
        sig = 1.0 / (1.0 + jnp.exp(-gate_pre))
        silu = gate_pre * sig
        active_wide = silu * up_pre
        active = active_wide.astype(BF16)
        out = mm(active, down_ref[...])
        o_ref[...] = (out * w).astype(BF16)
        d_raw = mm(d, down_ref[...], NT)
        d_gates = jnp.sum(active.astype(F32) * d_raw, axis=1, keepdims=True)
        d_active = d_raw * w
        d_up = (d_active * silu).astype(BF16)
        d_gate = (d_active * up_pre * sig * (1.0 + gate_pre * (1.0 - sig))).astype(BF16)
        d_row = mm(d_gate, gate_ref[...], NT) + mm(d_up, up_ref[...], NT)
        r_ref[:, :model] = d_row.astype(BF16)
        high = d_gates.astype(BF16).astype(F32)
        lane = lax.broadcasted_iota(jnp.int32, (tile, LANES), 1)
        e = at_ref[2] + k
        r_ref[:, model:] = (
            jnp.where(lane == e, high, 0.0) + jnp.where(lane == e + experts, d_gates - high, 0.0)
        ).astype(BF16)
        new_gate = mm(x, d_gate, TN)
        new_up = mm(x, d_up, TN)
        new_down = mm((active_wide * w).astype(BF16), d, TN)

        @pl.when(step == 0)
        def _():
            acc_gate[...] = new_gate
            acc_up[...] = new_up
            acc_down[...] = new_down

        @pl.when(step > 0)
        def _():
            acc_gate[...] += new_gate
            acc_up[...] += new_up
            acc_down[...] += new_down

        @pl.when(step == steps - 1)
        def _():
            if cut:
                for s in range(groups):
                    z = lax.rem(at_ref[0] + s, groups)
                    at_z = pl.ds(pl.multiple_of(z * part, 128), part)
                    outs[s][...] = acc_gate[at_z, :].astype(BF16)
                    outs[groups + s][...] = acc_up[at_z, :].astype(BF16)
                    outs[2 * groups + s][...] = acc_down[:, at_z].astype(BF16)
            else:
                outs[0][...] = acc_gate[...].astype(BF16)
                outs[1][...] = acc_up[...].astype(BF16)
                outs[2][...] = acc_down[...].astype(BF16)

    if cut:
        grads = [(part, ff)] * (2 * groups) + [(ff, part)] * groups
    else:
        grads = [(model, ff)] * 2 + [(ff, model)]
    row_spec = pl.BlockSpec((1, tile, model), lambda t: (k, t, 0))
    held = lambda shape: pl.BlockSpec(shape, lambda t: (0, 0), pipeline_mode=pl.Buffered(1))
    out = pl.pallas_call(
        kernel,
        grid=(steps,),
        in_specs=[
            SMEM_SPEC,
            row_spec,
            row_spec,
            pl.BlockSpec((1, tile, LANES), lambda t: (k, t, 0)),
            held((model, ff)),
            held((model, ff)),
            held((ff, model)),
        ],
        out_specs=[
            pl.BlockSpec((tile, model), lambda t: (t, 0)),
            pl.BlockSpec((tile, model + LANES), lambda t: (t, 0)),
        ]
        + [held(shape) for shape in grads],
        out_shape=[
            jax.ShapeDtypeStruct((total, model), BF16),
            jax.ShapeDtypeStruct((total, model + LANES), BF16),
        ]
        + [jax.ShapeDtypeStruct(shape, BF16) for shape in grads],
        scratch_shapes=[
            pltpu.VMEM((model, ff), F32),
            pltpu.VMEM((model, ff), F32),
            pltpu.VMEM((ff, model), F32),
        ],
        compiler_params=pltpu.CompilerParams(vmem_limit_bytes=62 * 1024 * 1024),
        cost_estimate=cost(18 * total * model * ff, 10 * total * model),
        name="run_expert",
    )(at, rows_in, grads_in, weights, gate, up, down)
    return out[0], out[1], out[2:]


def combine(rows, ranks, count, split, tokens, cap, place):
    per = len(rows)
    width = rows[0].shape[1]
    blocks = count * split

    def kernel(rank_ref, *refs):
        ins, outs = refs[:per], refs[per:]
        for i in range(count):
            for j in range(split):
                b = i * split + j
                total = None
                for k in range(per):
                    one = mm(
                        pick(rank_ref[b, k : k + 1, :], cap), ins[k][b * cap : (b + 1) * cap, :], TN
                    )
                    total = one if total is None else total + one
                outs[i][j] = total.astype(BF16)

    return pl.pallas_call(
        kernel,
        grid=(1,),
        in_specs=[pl.BlockSpec((blocks, per, tokens), lambda *_: (place, 0, 0))]
        + [pl.BlockSpec((blocks * cap, width), lambda *_: (place, 0))] * per,
        out_specs=[full_spec((split, tokens, width))] * count,
        out_shape=[jax.ShapeDtypeStruct((split, tokens, width), BF16)] * count,
        cost_estimate=cost(1e9, 6e6),
        name="combine",
    )(ranks, *rows)


def rope_tables(my_index, prompt_len):
    half = HEAD_SIZE // 2
    local = jnp.arange(2 * PR_DEV, dtype=jnp.int32)
    cont = my_index * PR_DEV + local - PR_DEV
    position = jnp.where(local < PR_DEV, my_index * PR_DEV + local, prompt_len + cont % CONT)
    frequency = 10000.0 ** (-jnp.arange(half, dtype=F32) * (2.0 / HEAD_SIZE))
    angle = position.astype(F32)[:, None] * frequency[None, :]
    return jnp.cos(angle), jnp.sin(angle)


def rotate(x, cosine, sine):
    half = HEAD_SIZE // 2
    column = lax.broadcasted_iota(jnp.int32, x.shape, 1)
    other = jnp.where(column % HEAD_SIZE < half, jnp.roll(x, -half, axis=1), jnp.roll(x, half, axis=1))
    return x * cosine + other * sine


def layer_general(
    tokens,
    cotangent,
    routes,
    norm_one,
    query_key_value_weight,
    out_weight,
    norm_two,
    router_weight,
    gate_weight,
    up_weight,
    down_weight,
):
    n = lax.axis_size("expert")
    groups = lax.axis_size("group")
    me = lax.axis_index("expert")
    z = lax.axis_index("group")
    micro, count, model = tokens.shape
    exp_here, part, ff = gate_weight.shape
    experts = router_weight.shape[1]
    split = 2 if exp_here % 2 == 0 and groups % 2 == 0 else 1
    per = exp_here // split
    query_width = QUERY_HEADS * HEAD_SIZE
    kv_width = KEY_VALUE_HEADS * HEAD_SIZE
    cap = max(2, 3 * TOPK * PR_DEV // experts)
    where = jnp.stack([z, me, me * exp_here + (z % split) * per]).astype(jnp.int32)
    rows_here = part // n if part % n == 0 else 0
    aligned = rows_here > 0 and rows_here % 16 == 0 and part % LANES == 0

    misc = jnp.concatenate(
        [
            norm_one[:, None],
            norm_two[:, None],
            jnp.zeros((part, experts - 2), BF16),
            router_weight,
            jnp.zeros((part, LANES - 2 * experts), BF16),
        ],
        axis=1,
    )
    if aligned:
        first = jnp.concatenate([query_key_value_weight, misc], axis=1)
        cut = lambda x: lax.dynamic_slice_in_dim(x, me * rows_here, rows_here, axis=0)
        width = first.shape[1]
        middle = width // 2 // LANES * LANES
        first_full, far = gather_dense(cut(first), [(0, middle), (middle, width)], where)
        out_full, far_out = gather_dense(
            cut(out_weight), [(0, model // 2), (model // 2, model)], where
        )
        after = (far, far_out)
    else:
        first_full = lax.all_gather(
            jnp.concatenate([query_key_value_weight, misc], axis=1), "group", axis=0, tiled=True
        )
        out_full = lax.all_gather(out_weight, "group", axis=0, tiled=True)
        after = ()
    qkv_columns = query_key_value_weight.shape[1]
    qkv_full = first_full[:, :qkv_columns]
    misc_full = first_full[:, qkv_columns:]
    gain_one = misc_full[:, 0].astype(F32)
    gain_two = misc_full[:, 1].astype(F32)
    router_full = misc_full[:, experts : 2 * experts]

    weights_held = []
    gate_from, up_from, down_from = gate_weight, up_weight, down_weight
    if aligned:
        (gate_from, up_from, down_from), after = lax.optimization_barrier(
            ((gate_weight, up_weight, down_weight), after)
        )
    for k in range(per):
        held = []
        for array, axis in ((gate_from, 0), (up_from, 0), (down_from, 1)):
            if not aligned:
                held.append(lax.all_gather(array[k], "group", axis=axis, tiled=True))
                continue
            pieces = []
            for s in range(groups):
                index = ((z + s) % split) * per + k
                chunk = lax.dynamic_index_in_dim(array, index, 0, keepdims=False)
                pieces.append(shift(chunk, s) if s else chunk)

            def place(i, at_z, at_e, axis=axis):
                start = lax.rem(at_z - i + groups, groups) * part
                return (start, 0) if axis == 0 else (0, start)

            shape = (model, ff) if axis == 0 else (ff, model)
            held.append(assemble(pieces, place, shape, where))
        weights_held.append(held)

    expert_ids = jnp.arange(experts, dtype=jnp.int32)
    named = jnp.any(routes[..., None] == expert_ids, axis=2)
    pad = jnp.zeros((micro, count, LANES - experts), BF16)
    d_payload = jnp.concatenate([cotangent, named.astype(BF16), pad], axis=2)

    def to_experts(payload):
        held = []
        for m in range(micro):
            own = payload[m]
            both = jnp.stack([own] + [turn(own, j, split) for j in range(1, split)])
            held.append(spread(both, m % 2))
        return held

    def to_owners(parts):
        held = []
        for m in range(micro):
            total = collect(parts[m], m % 2)
            mine = total[0]
            for j in range(1, split):
                mine = mine + turn(total[j].astype(BF16), split - j, split).astype(F32)
            held.append(mine)
        return jnp.stack(held)

    slots_per = 2 if n % 2 == 0 else 1
    batches = [list(range(g * slots_per, (g + 1) * slots_per)) for g in range(n // slots_per)]
    blocks_total = n * micro * split

    d_slots = to_experts(d_payload)
    buffers = None
    for g, batch in enumerate(batches):
        buffers = dispatch_grads(
            [d_slots[m][r] for r in batch for m in range(micro)],
            where, per, cap, model, buffers, g, blocks_total,
        )
    grads_in, ranks = buffers

    rows = micro * count
    x = tokens.reshape(rows, model).astype(F32)
    inverse_one = lax.rsqrt(jnp.mean(x * x, axis=-1, keepdims=True) + 1e-05)
    normed = (x * inverse_one * gain_one).astype(BF16)
    cosine, sine = rope_tables(me, PR_DEV * n)
    heads_rope = QUERY_HEADS + KEY_VALUE_HEADS
    cosine = jnp.tile(jnp.concatenate([cosine, cosine], axis=1), (micro, heads_rope))
    sine = jnp.tile(jnp.concatenate([-sine, sine], axis=1), (micro, heads_rope))
    cosine, sine = lax.optimization_barrier((cosine, sine))
    project = mm(normed, qkv_full)
    roped = rotate(project[:, : query_width + kv_width], cosine, sine).astype(BF16)
    query = roped[:, :query_width]
    key_value = jnp.concatenate(
        [roped[:, query_width:], project[:, query_width + kv_width :].astype(BF16)], axis=1
    ).reshape(micro, count, 2 * kv_width)
    query = query.reshape(micro, count, query_width)
    kv_slots = [spread(key_value[m], m % 2) for m in range(micro)]
    mixed = jnp.concatenate(
        [attention_forward(query[m], kv_slots[m], where) for m in range(micro)], axis=0
    )
    hidden = x + mm(mixed, out_full)
    inverse_two = lax.rsqrt(jnp.mean(hidden * hidden, axis=-1, keepdims=True) + 1e-05)
    normed_two = (hidden * inverse_two * gain_two).astype(BF16)
    logits = mm(normed_two, router_full)
    chosen = named.reshape(rows, experts)
    logits = jnp.where(chosen, logits, NEG_FILL)
    top = jnp.max(logits, axis=-1, keepdims=True)
    raised = jnp.where(chosen, jnp.exp(logits - top), 0.0)
    gate_probs = raised / jnp.sum(raised, axis=-1, keepdims=True)

    high = gate_probs.astype(BF16)
    low = (gate_probs - high.astype(F32)).astype(BF16)
    payload = jnp.concatenate(
        [normed_two, high, low, jnp.zeros((rows, LANES - 2 * experts), BF16)], axis=1
    ).reshape(micro, count, model + LANES)
    x_slots = to_experts(payload)
    buffers = None
    for g, batch in enumerate(batches):
        buffers = dispatch_rows(
            [x_slots[m][r] for r in batch for m in range(micro)],
            ranks, where, per, cap, model, experts, buffers, g, blocks_total,
        )
    rows_in, row_weights = buffers
    tile = slots_per * micro * split * cap
    outs, backs, weight_terms = [], [], []
    for k in range(per):
        out_rows, back_rows, terms = run_expert(
            k, where, rows_in, grads_in, row_weights, *weights_held[k], experts, tile, groups, aligned
        )
        outs.append(out_rows)
        backs.append(back_rows)
        weight_terms.append(terms)

    def returned(row_arrays):
        parts = [[None] * n for _ in range(micro)]
        for g in reversed(range(len(batches))):
            got = combine(
                row_arrays, ranks, len(batches[g]) * micro, split, count, cap, g
            )
            for i, (r, m) in enumerate((r, m) for r in batches[g] for m in range(micro)):
                parts[m][r] = got[i]
        return to_owners(parts)

    back = returned(backs).reshape(rows, model + LANES)
    mixture = returned(outs).reshape(rows, model)
    block_out = (hidden + mixture).astype(BF16).reshape(tokens.shape)

    expert_grads = []
    for which in range(3):
        per_class = []
        for k in range(per):
            if not aligned:
                axis = 1 if which == 2 else 0
                per_class.append(
                    [lax.psum_scatter(weight_terms[k][which], "group", scatter_dimension=axis, tiled=True).astype(F32)]
                )
                continue
            sums = [None] * split
            for s in range(groups):
                term = weight_terms[k][which * groups + s]
                term = (shift(term, s) if s else term).astype(F32)
                c = s % split
                sums[c] = term if sums[c] is None else sums[c] + term
            per_class.append(
                [lax.select_n((z - p) % split, *sums) if split > 1 else sums[0] for p in range(split)]
            )
        expert_grads.append(
            jnp.stack([per_class[k][p] for p in range(split) for k in range(per)])
        )

    d_out = cotangent.reshape(rows, model).astype(F32)
    d_gates = back[:, model : model + experts] + back[:, model + experts : model + 2 * experts]
    d_logits = gate_probs * (d_gates - jnp.sum(gate_probs * d_gates, axis=-1, keepdims=True))
    router_grad = lax.dot_general(normed_two.astype(F32), d_logits, TN, precision=HIGHEST)
    d_normed_two = back[:, :model] + lax.dot_general(
        d_logits, router_full.astype(F32), NT, precision=HIGHEST
    )

    def rms_back(inputs, inverse, gain, upstream):
        scaled = gain * upstream
        return inverse * scaled - inputs * inverse * inverse * inverse * jnp.mean(
            scaled * inputs, axis=-1, keepdims=True
        )

    grad_two = jnp.sum(d_normed_two * hidden * inverse_two, axis=0)
    d_hidden = d_out + rms_back(hidden, inverse_two, gain_two, d_normed_two)
    d_attn = d_hidden.astype(BF16)
    d_mixed = mm(d_attn, out_full, NT).astype(BF16).reshape(micro, count, query_width)
    d_query, kv_terms = [], []
    for m in range(micro):
        got, terms = attention_backward(query[m], kv_slots[m], d_mixed[m], where)
        d_query.append(got)
        kv_terms.append(terms)
    d_query = jnp.concatenate(d_query, axis=0)
    q_cos, q_sin = cosine[:, :query_width], sine[:, :query_width]
    d_query_low = rotate(d_query, q_cos, -q_sin).astype(BF16)
    d_kv = jnp.concatenate([collect(kv_terms[m], m % 2) for m in range(micro)], axis=0)
    d_key_low = rotate(d_kv[:, :kv_width], q_cos[:, :kv_width], -q_sin[:, :kv_width]).astype(BF16)
    d_kv_low = jnp.concatenate([d_key_low, d_kv[:, kv_width:].astype(BF16)], axis=1)
    d_normed = mm(d_query_low, qkv_full[:, :query_width], NT) + mm(
        d_kv_low, qkv_full[:, query_width:], NT
    )
    grad_one = jnp.sum(d_normed * x * inverse_one, axis=0)
    input_grad = (d_hidden + rms_back(x, inverse_one, gain_one, d_normed)).reshape(tokens.shape)
    misc_grad = jnp.concatenate(
        [
            grad_one[:, None],
            grad_two[:, None],
            jnp.zeros((model, experts - 2), F32),
            router_grad,
            jnp.zeros((model, LANES - 2 * experts), F32),
        ],
        axis=1,
    )
    if aligned:
        grad_out = reduce_dense(sliced_outer(mixed, d_attn, None, groups, n, where), 0, where)
        grad_q = reduce_dense(sliced_outer(normed, d_query_low, None, groups, n, where), 1, where)
        grad_rest = reduce_dense(
            sliced_outer(normed, d_kv_low, misc_grad, groups, n, where), 0, where
        )
    else:

        def whole(value):
            low = lax.psum_scatter(value.astype(BF16), "group", scatter_dimension=0, tiled=True)
            return lax.psum(low, "expert").astype(F32)

        grad_out = whole(mm(mixed, d_attn, TN))
        grad_q = whole(mm(normed, d_query_low, TN))
        grad_rest = whole(jnp.concatenate([mm(normed, d_kv_low, TN), misc_grad], axis=1))
    grad_qkv = jnp.concatenate([grad_q, grad_rest[:, : 2 * kv_width]], axis=1)
    misc_sum = grad_rest[:, 2 * kv_width :]
    return (
        block_out,
        input_grad,
        misc_sum[:, 0],
        grad_qkv,
        grad_out,
        misc_sum[:, 1],
        misc_sum[:, experts : 2 * experts],
        *expert_grads,
    )


def flip(e, r):
    for bit in (1, 2, 4):
        if r & bit:
            e = e + bit - 2 * bit * lax.rem(e // bit, 2)
    return e


def partner(z):
    return z + 1 - 2 * lax.rem(z, 2)


def remote(src, dst, send, recv, device):
    return pltpu.make_async_remote_copy(
        src_ref=src,
        dst_ref=dst,
        send_sem=send,
        recv_sem=recv,
        device_id=device,
        device_id_type=pl.DeviceIdType.MESH,
    )


def greet(devices):
    barrier = pltpu.get_barrier_semaphore()
    for device in devices:
        pl.semaphore_signal(barrier, inc=1, device_id=device, device_id_type=pl.DeviceIdType.MESH)
    pl.semaphore_wait(barrier, len(devices))


def plane_devices(e):
    return [{"expert": flip(e, bit)} for bit in (1, 2, 4)]


class Gather:
    def __init__(self, e, own, loc, paths, send, recv):
        self.e, self.own, self.loc, self.paths, self.send, self.recv = e, own, loc, paths, send, recv

    def copy(self, r, bit, c):
        q = r ^ bit
        src = self.own(c) if r == 0 else self.loc(r, r, c)
        return remote(
            src, self.loc(r, q, c), self.send.at[q, c], self.recv.at[q, c],
            {"expert": flip(self.e, bit)},
        )

    def begin(self, c):
        for bit in (2, 4, 1):
            self.copy(0, bit, c).start()

    def arrived(self, q, c):
        here = self.loc(q, q, c)
        remote(
            here, here, self.send.at[q, c], self.recv.at[q, c], {"expert": flip(self.e, 1)}
        ).wait_recv()

    def pass_on(self, q, c):
        if q == 2 and self.paths[c] == 0:
            self.copy(2, 4, c).start()
        if q == 4 and self.paths[c] == 1:
            self.copy(4, 2, c).start()
        if q in (2, 4, 6):
            self.copy(q, 1, c).start()

    def finish(self, c):
        for bit in (2, 4, 1):
            self.copy(0, bit, c).wait_send()
        if self.paths[c] == 0:
            self.copy(2, 4, c).wait_send()
        else:
            self.copy(4, 2, c).wait_send()
        for q in (2, 4, 6):
            self.copy(q, 1, c).wait_send()

    def stage(self, chunks, slots):
        for c in chunks:
            for q in slots:
                self.arrived(q, c)
                self.pass_on(q, c)

    def forward_all(self, chunks, use=None):
        for c in chunks:
            for q in (2, 4):
                self.arrived(q, c)
                self.pass_on(q, c)
        if use:
            for c in chunks:
                self.arrived(1, c)
                use(1, c)
                use(2, c)
                use(4, c)
        for c in chunks:
            self.arrived(6, c)
            self.pass_on(6, c)
            if use:
                use(6, c)
        for c in chunks:
            for q in (3, 5, 7) if use else (1, 3, 5, 7):
                self.arrived(q, c)
                if use:
                    use(q, c)


def add_rows(dst, sources, step=16):
    rows = sources[0].shape[0]

    def one(i, carry):
        at = pl.ds(pl.multiple_of(i * step, step), step)
        total = sources[0][at, :].astype(F32)
        for source in sources[1:]:
            total = total + source[at, :].astype(F32)
        dst[at, :] = total.astype(dst.dtype)
        return carry

    lax.fori_loop(0, rows // step, one, 0)


class Reduce:
    def __init__(self, e, part, paths, core, diag, near, acc, send, recv):
        self.e, self.part, self.paths = e, part, paths
        self.core, self.diag, self.near, self.acc = core, diag, near, acc
        self.send, self.recv = send, recv

    def core_copy(self, h, c):
        return remote(
            self.part(2 * h + 1, c), self.core.at[h, c], self.send.at[h, c], self.recv.at[h, c],
            {"expert": flip(self.e, 1)},
        )

    def diag_copy(self, c):
        return remote(
            self.acc.at[2, c], self.diag.at[c], self.send.at[4, c], self.recv.at[4, c],
            {"expert": flip(self.e, 4 if self.paths[c] == 0 else 2)},
        )

    def near_copy(self, i, c):
        return remote(
            self.acc.at[i, c], self.near.at[i, c], self.send.at[5 + i, c], self.recv.at[5 + i, c],
            {"expert": flip(self.e, 2 if i == 0 else 4)},
        )

    def begin(self, r, c):
        self.core_copy(r // 2, c).start()

    def diagonal(self, chunks):
        for c in chunks:
            self.core_copy(3, c).wait_recv()
            add_rows(self.acc.at[2, c], [self.part(6, c), self.core.at[3, c]])
            self.diag_copy(c).start()

    def sides(self, chunks):
        for c in chunks:
            for i in (0, 1) if self.paths[c] == 1 else (1, 0):
                self.core_copy(1 + i, c).wait_recv()
                terms = [self.part(2 + 2 * i, c), self.core.at[1 + i, c]]
                if self.paths[c] == i:
                    self.diag_copy(c).wait_recv()
                    terms.append(self.diag.at[c])
                add_rows(self.acc.at[i, c], terms)
                self.near_copy(i, c).start()

    def total(self, c):
        self.core_copy(0, c).wait_recv()
        self.near_copy(0, c).wait_recv()
        self.near_copy(1, c).wait_recv()
        return [self.part(0, c), self.core.at[0, c], self.near.at[0, c], self.near.at[1, c]]

    def finish(self, c):
        for h in range(4):
            self.core_copy(h, c).wait_send()
        self.diag_copy(c).wait_send()
        for i in range(2):
            self.near_copy(i, c).wait_send()


def reduce_scratch(count, rows, width):
    return [
        pltpu.VMEM((4, count, rows, width), BF16),
        pltpu.VMEM((count, rows, width), BF16),
        pltpu.VMEM((2, count, rows, width), BF16),
        pltpu.VMEM((3, count, rows, width), BF16),
        pltpu.SemaphoreType.DMA((7, count)),
        pltpu.SemaphoreType.DMA((7, count)),
    ]


def params(identity, vmem=62):
    return pltpu.CompilerParams(
        collective_id=identity, has_side_effects=True, vmem_limit_bytes=vmem * 1024 * 1024
    )


def plane_weights(shares, bank, per):
    n, split = 8, 2
    groups = lax.axis_size("group")
    rows = shares[0].shape[0]
    kinds = len(shares)
    count = groups * kinds

    def kernel(*refs):
        ins, bank_ref, refs = refs[:kinds], refs[kinds], refs[kinds + 1 :]
        outs, far_ref, refs = refs[:kinds], refs[kinds], refs[kinds + 1 :]
        z_send, z_recv, send, recv, local, b_send, b_recv = refs
        e, z = lax.axis_index("expert"), lax.axis_index("group")

        def loc(r, q, c):
            s, kind = c // kinds, c % kinds
            row = (lax.rem(z - s + groups, groups) * n + flip(e, r)) * rows
            return outs[kind].at[pl.ds(pl.multiple_of(row, 16), rows), :]

        def far(c):
            s, kind = c // kinds, c % kinds
            return remote(
                ins[kind], loc(0, 0, kind), z_send.at[c], z_recv.at[c],
                {"group": lax.rem(z + s, groups)},
            )

        def landed(c):
            remote(
                loc(0, 0, c), loc(0, 0, c), z_send.at[c], z_recv.at[c],
                {"group": lax.rem(z + c // kinds, groups)},
            ).wait_recv()

        first = lax.rem(z + 1, split) * per
        follow = remote(
            bank_ref.at[pl.ds(first, per)], far_ref, b_send, b_recv, {"group": lax.rem(z + 1, groups)}
        )
        gather = Gather(
            e, lambda c: ins[c] if c < kinds else loc(0, 0, c), loc,
            [c // kinds % 2 for c in range(count)], send, recv,
        )
        near = list(range(kinds))
        later = list(range(kinds, count))
        greet(
            plane_devices(e) + [{"group": lax.rem(z + s, groups)} for s in range(1, groups)]
        )
        for c in later:
            far(c).start()
        for c in near:
            gather.begin(c)
            pltpu.make_async_copy(ins[c], loc(0, 0, c), local.at[c]).start()
        follow.start()
        gather.stage(near, (2, 4))
        gather.stage(near, (6,))
        for c in later:
            landed(c)
            gather.begin(c)
        gather.stage(later, (2, 4))
        gather.stage(later, (6,))
        gather.stage(near + later, (1, 3, 5, 7))
        for c in later:
            far(c).wait_send()
        for c in near + later:
            gather.finish(c)
        for c in near:
            pltpu.make_async_copy(ins[c], loc(0, 0, c), local.at[c]).wait()
        follow.wait()

    vmem = pl.BlockSpec(memory_space=pltpu.VMEM)
    shapes = [(groups * n * rows, one.shape[1]) for one in shares]
    return pl.pallas_call(
        kernel,
        in_specs=[vmem] * kinds + [ANY_SPEC],
        out_specs=[vmem] * kinds + [ANY_SPEC],
        out_shape=[jax.ShapeDtypeStruct(shape, BF16) for shape in shapes]
        + [jax.ShapeDtypeStruct((per,) + bank.shape[1:], BF16)],
        scratch_shapes=[
            pltpu.SemaphoreType.DMA((count,)),
            pltpu.SemaphoreType.DMA((count,)),
            pltpu.SemaphoreType.DMA((n, count)),
            pltpu.SemaphoreType.DMA((n, count)),
            pltpu.SemaphoreType.DMA((kinds,)),
            pltpu.SemaphoreType.DMA,
            pltpu.SemaphoreType.DMA,
        ],
        compiler_params=params(1),
        cost_estimate=cost(1e9, 1e6),
        name="plane_weights",
    )(*shares, bank)


def attention_pairs(n, at_me, q_ref, keys, out_ref):
    width = KEY_VALUE_HEADS * HEAD_SIZE
    prompt_ok, cont_ok = attention_masks_plain(n, at_me)

    def pair(j, carry):
        q_at = pl.ds(pl.multiple_of(j * 384, 128), 384)
        k_at = pl.ds(pl.multiple_of(j * 128, 128), 128)
        v_at = pl.ds(pl.multiple_of(width + j * 128, 128), 128)
        q_top, q_low = q_ref[:PR_DEV, q_at], q_ref[PR_DEV:, q_at]
        k_two, v_two = keys[:, k_at], keys[:, v_at]
        tops, lows = [], []
        for g in range(2):
            key = k_two[:, g * HEAD_SIZE : (g + 1) * HEAD_SIZE]
            value = v_two[:, g * HEAD_SIZE : (g + 1) * HEAD_SIZE]
            top, low = group_probs(
                head_rows(q_top, g * 192), head_rows(q_low, g * 192), key, prompt_ok, cont_ok, n
            )
            tops.append(row_heads(mm(top.astype(BF16), value[: n * PR_DEV])))
            lows.append(row_heads(mm(low.astype(BF16), value)))
        out_ref[:PR_DEV, q_at] = jnp.concatenate(tops, axis=1).astype(BF16)
        out_ref[PR_DEV:, q_at] = jnp.concatenate(lows, axis=1).astype(BF16)
        return carry

    lax.fori_loop(0, KEY_VALUE_HEADS // 2, pair, 0)


def flip_columns(slot, me, limit):
    bit, total = 1, jnp.zeros_like(slot)
    while bit < limit:
        total = total + bit * lax.rem(slot // bit + me // bit, 2)
        bit *= 2
    return total


def attention_masks_plain(n, me):
    shape = (3 * PR_DEV, n * PR_DEV)
    token = lax.rem(lax.broadcasted_iota(jnp.int32, shape, 0), PR_DEV)
    column = lax.broadcasted_iota(jnp.int32, shape, 1)
    owner = flip_columns(column // PR_DEV, me, n)
    prompt_ok = owner * PR_DEV + lax.rem(column, PR_DEV) <= me * PR_DEV + token
    slots = CONT // PR_DEV
    shape = (3 * PR_DEV, CONT)
    token = lax.rem(lax.broadcasted_iota(jnp.int32, shape, 0), PR_DEV)
    column = lax.broadcasted_iota(jnp.int32, shape, 1)
    local = lax.rem(me, slots)
    owner = flip_columns(column // PR_DEV, local, slots)
    cont_ok = owner * PR_DEV + lax.rem(column, PR_DEV) <= local * PR_DEV + token
    return prompt_ok, cont_ok


def plane_attention(query, key_value):
    micro, tokens, width = key_value.shape
    n = 8

    def kernel(q_ref, kv_ref, out_ref, slots, keys, send, recv, local):
        e = lax.axis_index("expert")
        gather = Gather(
            e, lambda c: kv_ref.at[c], lambda r, q, c: slots.at[q, c], [c % 2 for c in range(micro)],
            send, recv,
        )
        greet(plane_devices(e))
        for c in range(micro):
            gather.begin(c)
            pltpu.make_async_copy(kv_ref.at[c], slots.at[0, c], local.at[c]).start()
        gather.forward_all(range(micro))
        for c in range(micro):
            pltpu.make_async_copy(kv_ref.at[c], slots.at[0, c], local.at[c]).wait()
            load_keys(n, [slots.at[r, c] for r in range(n)], keys)
            attention_pairs(n, e, q_ref.at[c], keys, out_ref.at[c])
        for c in range(micro):
            gather.finish(c)

    vmem = pl.BlockSpec(memory_space=pltpu.VMEM)
    return pl.pallas_call(
        kernel,
        in_specs=[vmem, vmem],
        out_specs=[vmem, vmem],
        out_shape=[
            jax.ShapeDtypeStruct(query.shape, BF16),
            jax.ShapeDtypeStruct((n, micro, tokens, width), BF16),
        ],
        scratch_shapes=[
            pltpu.VMEM((n * PR_DEV + CONT, width), BF16),
            pltpu.SemaphoreType.DMA((n, micro)),
            pltpu.SemaphoreType.DMA((n, micro)),
            pltpu.SemaphoreType.DMA((micro,)),
        ],
        compiler_params=params(2),
        cost_estimate=cost(1e9, 1e6),
        name="plane_attention",
    )(query, key_value)


def plane_attention_backward(query, slots, d_mixed):
    n, micro, tokens, width = slots.shape
    half = width // 2
    pr = n * PR_DEV
    total = pr + CONT

    def kernel(q_ref, d_ref, kv_ref, dq_ref, dkv_ref, keys, grads, parts, *scratch):
        e = lax.axis_index("expert")
        red = Reduce(e, lambda r, c: parts.at[r, c], [c % 2 for c in range(micro)], *scratch)
        greet(plane_devices(e))
        prompt_ok, cont_ok = attention_masks_plain(n, e)

        def one_side(prob, d_rows, key, value, q_rows):
            d_prob = mm(d_rows, value, NT)
            delta = jnp.sum(prob * d_prob, axis=1, keepdims=True)
            d_score = (prob * (d_prob - delta)).astype(BF16)
            return (
                mm(d_score, key) * SCORE_SCALE,
                mm(d_score, q_rows, TN) * SCORE_SCALE,
                mm(prob.astype(BF16), d_rows, TN),
            )

        for c in range(micro):
            load_keys(n, [kv_ref.at[r, c] for r in range(n)], keys)

            def pair(j, carry):
                q_at = pl.ds(pl.multiple_of(j * 384, 128), 384)
                k_at = pl.ds(pl.multiple_of(j * 128, 128), 128)
                v_at = pl.ds(pl.multiple_of(half + j * 128, 128), 128)
                q_top, q_low = q_ref[c, :PR_DEV, q_at], q_ref[c, PR_DEV:, q_at]
                d_top, d_low = d_ref[c, :PR_DEV, q_at], d_ref[c, PR_DEV:, q_at]
                k_two, v_two = keys[:, k_at], keys[:, v_at]
                dq_tops, dq_lows, dks, dvs = [], [], [], []
                for g in range(2):
                    key = k_two[:, g * HEAD_SIZE : (g + 1) * HEAD_SIZE]
                    value = v_two[:, g * HEAD_SIZE : (g + 1) * HEAD_SIZE]
                    rows_top, rows_low = head_rows(q_top, g * 192), head_rows(q_low, g * 192)
                    top, low = group_probs(rows_top, rows_low, key, prompt_ok, cont_ok, n)
                    dq_top, dk_top, dv_top = one_side(
                        top, head_rows(d_top, g * 192), key[:pr], value[:pr], rows_top
                    )
                    dq_low, dk_low, dv_low = one_side(
                        low, head_rows(d_low, g * 192), key, value, rows_low
                    )
                    dq_tops.append(row_heads(dq_top))
                    dq_lows.append(row_heads(dq_low))
                    dks.append(jnp.concatenate([dk_low[:pr] + dk_top, dk_low[pr:]], axis=0))
                    dvs.append(jnp.concatenate([dv_low[:pr] + dv_top, dv_low[pr:]], axis=0))
                dq_ref[c, :PR_DEV, q_at] = jnp.concatenate(dq_tops, axis=1)
                dq_ref[c, PR_DEV:, q_at] = jnp.concatenate(dq_lows, axis=1)
                grads[:, k_at] = jnp.concatenate(dks, axis=1).astype(BF16)
                grads[:, v_at] = jnp.concatenate(dvs, axis=1).astype(BF16)
                return carry

            lax.fori_loop(0, KEY_VALUE_HEADS // 2, pair, 0)
            for r in (7, 5, 3, 1, 6, 2, 4, 0):
                parts[r, c, :PR_DEV, :] = grads[r * PR_DEV : (r + 1) * PR_DEV, :]
                if r < CONT // PR_DEV:
                    lo = (n + r) * PR_DEV
                    parts[r, c, PR_DEV:, :] = grads[lo : lo + PR_DEV, :]
                else:
                    parts[r, c, PR_DEV:, :] = jnp.zeros((PR_DEV, width), BF16)
                if r % 2:
                    red.begin(r, c)
        red.diagonal(range(micro))
        red.sides(range(micro))
        for c in range(micro):
            add_rows(dkv_ref.at[c], red.total(c))
        for c in range(micro):
            red.finish(c)

    vmem = pl.BlockSpec(memory_space=pltpu.VMEM)
    return pl.pallas_call(
        kernel,
        in_specs=[vmem] * 3,
        out_specs=[vmem] * 2,
        out_shape=[
            jax.ShapeDtypeStruct(query.shape, F32),
            jax.ShapeDtypeStruct((micro, tokens, width), F32),
        ],
        scratch_shapes=[
            pltpu.VMEM((total, width), BF16),
            pltpu.VMEM((total, width), BF16),
            pltpu.VMEM((n, micro, tokens, width), BF16),
        ]
        + reduce_scratch(micro, tokens, width),
        compiler_params=params(3),
        cost_estimate=cost(1e9, 1e6),
        name="plane_attention_backward",
    )(query, d_mixed, slots)


def plane_dispatch(payload, ranks, where, per, cap, model, experts):
    micro, tokens, width = payload.shape
    n, split = 8, 2
    count = split * micro

    def kernel(at_ref, own_ref, rank_ref, out, weights, slots, z_send, z_recv, send, recv):
        e, z = lax.axis_index("expert"), lax.axis_index("group")
        lane = lax.broadcasted_iota(jnp.int32, (cap, LANES), 1)

        def own(c):
            return own_ref.at[c] if c < micro else slots.at[0, c]

        gather = Gather(
            e, own, lambda r, q, c: slots.at[q, c], [c % 2 for c in range(count)], send, recv
        )

        def turned(m):
            return remote(
                own_ref.at[m], slots.at[0, micro + m], z_send.at[m], z_recv.at[m],
                {"group": partner(z)},
            )

        def use(r, c):
            rows = own(c)[...] if r == 0 else slots[r, c]
            b = r * count + c
            for k in range(per):
                got = mm(pick(rank_ref[b, k : k + 1, :], cap), rows)
                out[k, b * cap : (b + 1) * cap, :] = got[:, :model].astype(BF16)
                first = at_ref[2] + k
                mine = (lane == first) | (lane == first + experts)
                total = jnp.sum(jnp.where(mine, got[:, model:], 0.0), axis=1, keepdims=True)
                weights[k, b * cap : (b + 1) * cap, :] = jnp.broadcast_to(total, (cap, LANES))

        greet(plane_devices(e) + [{"group": partner(z)}])
        for m in range(micro):
            turned(m).start()
        for m in range(micro):
            gather.begin(m)
        for m in range(micro):
            use(0, m)
        for m in range(micro):
            turned(m).wait_recv()
            gather.begin(micro + m)
            use(0, micro + m)
        gather.forward_all(range(count), use)
        for m in range(micro):
            turned(m).wait_send()
        for c in range(count):
            gather.finish(c)

    vmem = pl.BlockSpec(memory_space=pltpu.VMEM)
    total = n * count * cap
    return pl.pallas_call(
        kernel,
        in_specs=[SMEM_SPEC, vmem, vmem],
        out_specs=[vmem, vmem],
        out_shape=[
            jax.ShapeDtypeStruct((per, total, model), BF16),
            jax.ShapeDtypeStruct((per, total, LANES), F32),
        ],
        scratch_shapes=[
            pltpu.VMEM((n, count, tokens, width), BF16),
            pltpu.SemaphoreType.DMA((micro,)),
            pltpu.SemaphoreType.DMA((micro,)),
            pltpu.SemaphoreType.DMA((n, count)),
            pltpu.SemaphoreType.DMA((n, count)),
        ],
        compiler_params=params(4),
        cost_estimate=cost(1e9, 1e6),
        name="plane_dispatch",
    )(where, payload, ranks)


def plane_return(rows, ranks, micro, tokens, cap):
    per, _, width = rows.shape
    n, split = 8, 2
    count = split * micro
    chunks = list(range(micro, count)) + list(range(micro))

    def kernel(rank_ref, in_ref, out, *refs):
        parts, z_out, z_in, z_send, z_recv, scratch = *refs[:5], refs[5:]
        e, z = lax.axis_index("expert"), lax.axis_index("group")
        red = Reduce(e, lambda r, c: parts.at[r, c], [c % 2 for c in range(count)], *scratch)

        def produce(r, c):
            b = r * count + c
            total = None
            for k in range(per):
                one = mm(
                    pick(rank_ref[b, k : k + 1, :], cap), in_ref[k, b * cap : (b + 1) * cap, :], TN
                )
                total = one if total is None else total + one
            parts[r, c] = total.astype(BF16)

        def turned(m):
            return remote(
                z_out.at[m], z_in.at[m], z_send.at[m], z_recv.at[m], {"group": partner(z)}
            )

        greet(plane_devices(e) + [{"group": partner(z)}])
        for r in (7, 3, 5):
            for c in chunks:
                produce(r, c)
                red.begin(r, c)
        for c in chunks:
            produce(6, c)
        red.diagonal(chunks)
        for r in (2, 4):
            for c in chunks:
                produce(r, c)
        red.sides(chunks)
        for c in chunks:
            produce(1, c)
            red.begin(1, c)
        for c in chunks:
            produce(0, c)
        for c in chunks:
            terms = red.total(c)
            if c >= micro:
                add_rows(z_out.at[c - micro], terms)
                turned(c - micro).start()
            else:
                turned(c).wait_recv()
                add_rows(out.at[c], terms + [z_in.at[c]])
        for m in range(micro):
            turned(m).wait_send()
        for c in chunks:
            red.finish(c)

    vmem = pl.BlockSpec(memory_space=pltpu.VMEM)
    return pl.pallas_call(
        kernel,
        in_specs=[vmem] * 2,
        out_specs=vmem,
        out_shape=jax.ShapeDtypeStruct((micro, tokens, width), F32),
        scratch_shapes=[
            pltpu.VMEM((n, count, tokens, width), BF16),
            pltpu.VMEM((micro, tokens, width), BF16),
            pltpu.VMEM((micro, tokens, width), BF16),
            pltpu.SemaphoreType.DMA((micro,)),
            pltpu.SemaphoreType.DMA((micro,)),
        ]
        + reduce_scratch(count, tokens, width),
        compiler_params=params(5),
        cost_estimate=cost(1e9, 1e6),
        name="plane_return",
    )(ranks, rows)


def plane_gradients(products, extra, groups):
    n = 8
    depth = products[0][0].shape[1]
    widths = [b.shape[1] for a, b in products]
    width = sum(widths) + extra.shape[1]
    rows = depth // (groups * n)
    tile = 512
    flat = [x for pair in products for x in pair]

    def kernel(*refs):
        ins, extra_ref, refs = refs[: len(flat)], refs[len(flat)], refs[len(flat) + 1 :]
        out, wide, parts, z_out, z_in, slots, z_send, z_recv, send, recv, local = refs[:11]
        scratch = refs[11:]
        e, z = lax.axis_index("expert"), lax.axis_index("group")
        red = Reduce(e, lambda r, c: parts.at[r, c], [c % 2 for c in range(groups)], *scratch)
        greet(
            plane_devices(e)
            + [{"group": lax.rem(z + s, groups)} for s in range(1, groups)]
        )

        def cut(lo, size):
            for r in range(n):
                for s in range(groups):
                    row = (lax.rem(z + s, groups) * n + flip(e, r)) * rows
                    at = pl.ds(pl.multiple_of(row, 16), rows)
                    parts[r, s, :, lo : lo + size] = wide[at, :size].astype(BF16)

        lo = 0
        for i, count in enumerate(widths):
            for start in range(0, count, tile):
                size = min(tile, count - start)
                wide[:, :size] = mm(ins[2 * i][...], ins[2 * i + 1][:, start : start + size], TN)
                cut(lo, size)
                lo += size
        wide[:, : extra_ref.shape[1]] = extra_ref[...]
        cut(lo, extra_ref.shape[1])

        chunks = list(range(1, groups)) + [0]
        for r in (7, 3, 5, 1):
            for c in chunks:
                red.begin(r, c)
        red.diagonal(chunks)
        red.sides(chunks)

        def far(s):
            return remote(
                z_out.at[s], z_in.at[s], z_send.at[s], z_recv.at[s],
                {"group": lax.rem(z + s, groups)},
            )

        for c in chunks:
            add_rows(z_out.at[c], red.total(c))
            if c:
                far(c).start()
        for c in range(1, groups):
            far(c).wait_recv()
        add_rows(slots.at[0], [z_out.at[0]] + [z_in.at[c] for c in range(1, groups)])

        middle = width // 2 // LANES * LANES
        spans = [(0, middle), (middle, width)]

        def loc(r, q, c):
            return slots.at[q, :, spans[c][0] : spans[c][1]]

        gather = Gather(e, lambda c: loc(0, 0, c), loc, [0, 1], send, recv)
        for c in range(2):
            gather.begin(c)
        gather.forward_all(range(2))
        for r in range(n):
            row = pl.multiple_of(flip(e, r) * rows, 16)
            out[pl.ds(row, rows), :] = slots[r].astype(F32)
        for c in range(2):
            gather.finish(c)
        for c in range(1, groups):
            far(c).wait_send()
        for c in chunks:
            red.finish(c)

    vmem = pl.BlockSpec(memory_space=pltpu.VMEM)
    return pl.pallas_call(
        kernel,
        in_specs=[vmem] * (len(flat) + 1),
        out_specs=vmem,
        out_shape=jax.ShapeDtypeStruct((n * rows, width), F32),
        scratch_shapes=[
            pltpu.VMEM((depth, tile), F32),
            pltpu.VMEM((n, groups, rows, width), BF16),
            pltpu.VMEM((groups, rows, width), BF16),
            pltpu.VMEM((groups, rows, width), BF16),
            pltpu.VMEM((n, rows, width), BF16),
            pltpu.SemaphoreType.DMA((groups,)),
            pltpu.SemaphoreType.DMA((groups,)),
            pltpu.SemaphoreType.DMA((n, 2)),
            pltpu.SemaphoreType.DMA((n, 2)),
            pltpu.SemaphoreType.DMA((2,)),
        ]
        + reduce_scratch(groups, rows, width),
        compiler_params=params(6),
        cost_estimate=cost(1e9, 1e6),
        name="plane_gradients",
    )(*flat, extra)


def gather_flags(slots, where, per, cap, model):
    n, count, tokens, width = slots.shape

    def kernel(at_ref, in_ref, out, ranks, flags):
        row = lax.broadcasted_iota(jnp.int32, (tokens, tokens), 0)
        col = lax.broadcasted_iota(jnp.int32, (tokens, tokens), 1)
        before = jnp.where(row < col, 1.0, 0.0).astype(BF16)
        for b in range(count):
            payload = in_ref[0, b]
            flags[...] = payload[:, model:].astype(F32).T
            picked = jnp.concatenate(
                [flags[pl.ds(at_ref[2] + k, 1), :] for k in range(per)], axis=0
            )
            slot = jnp.where(picked > 0.0, mm(picked.astype(BF16), before), -1.0)
            ranks[b] = slot
            for k in range(per):
                out[k, b * cap : (b + 1) * cap, :] = mm(
                    pick(slot[k : k + 1], cap), payload[:, :model]
                ).astype(BF16)

    return pl.pallas_call(
        kernel,
        grid_spec=pltpu.PrefetchScalarGridSpec(
            num_scalar_prefetch=1,
            grid=(n,),
            in_specs=[
                pl.BlockSpec(
                    (1, count, tokens, width),
                    lambda r, at: (jnp.bitwise_xor(at[1], r), 0, 0, 0),
                )
            ],
            out_specs=[
                pl.BlockSpec((per, count * cap, model), lambda r, at: (0, r, 0)),
                pl.BlockSpec((count, per, tokens), lambda r, at: (r, 0, 0)),
            ],
            scratch_shapes=[pltpu.VMEM((LANES, tokens), F32)],
        ),
        out_shape=[
            jax.ShapeDtypeStruct((per, n * count * cap, model), BF16),
            jax.ShapeDtypeStruct((n * count, per, tokens), F32),
        ],
        cost_estimate=cost(5e9, 3e7),
        name="gather_flags",
    )(where, slots)


def scatter_rows(rows, ranks, where, n, count, tokens, cap):
    per, _, width = rows.shape

    def kernel(at_ref, rank_ref, in_ref, out):
        for b in range(count):
            total = None
            for k in range(per):
                one = mm(
                    pick(rank_ref[b, k : k + 1, :], cap), in_ref[k, b * cap : (b + 1) * cap, :], TN
                )
                total = one if total is None else total + one
            out[0, b] = total.astype(BF16)

    return pl.pallas_call(
        kernel,
        grid_spec=pltpu.PrefetchScalarGridSpec(
            num_scalar_prefetch=1,
            grid=(n,),
            in_specs=[
                pl.BlockSpec((count, per, tokens), lambda r, at: (r, 0, 0)),
                pl.BlockSpec((per, count * cap, width), lambda r, at: (0, r, 0)),
            ],
            out_specs=pl.BlockSpec(
                (1, count, tokens, width), lambda r, at: (jnp.bitwise_xor(at[1], r), 0, 0, 0)
            ),
        ),
        out_shape=jax.ShapeDtypeStruct((n, count, tokens, width), BF16),
        cost_estimate=cost(5e9, 3e7),
        name="scatter_rows",
    )(where, ranks, rows)


def expert_steps(at, rows_in, grads_in, weights, bank, far, experts, tile):
    per, total, model = rows_in.shape
    part, ff = bank.shape[2:]
    groups = model // part
    steps = total // tile

    def kernel(at_ref, x_ref, d_ref, w_ref, *refs):
        sources, o_ref, r_ref, refs = refs[:groups], refs[groups], refs[groups + 1], refs[groups + 2 :]
        outs, (acc_wide, acc_down, wide_all, down_all, sems) = refs[:groups], refs[groups:]
        k, step = pl.program_id(0), pl.program_id(1)

        def loads(index):
            copies = []
            for s in range(groups):
                z = lax.rem(at_ref[0] - s + groups, groups)
                at_z = pl.ds(pl.multiple_of(z * part, 128), part)
                source = sources[s].at[at_ref[3] + index if s == 0 else index]
                wide, down = wide_all.at[index], down_all.at[index]
                for i, dst in enumerate([wide.at[at_z, :ff], wide.at[at_z, ff:], down.at[at_z, :]]):
                    copies.append(
                        pltpu.make_async_copy(source.at[i], dst, sems.at[index, 3 * s + i])
                    )
            return copies

        for index in range(per):

            @pl.when((k == 0) & (step == 0))
            def _():
                for one in loads(index):
                    one.start()

        for index in range(per):

            @pl.when((k == index) & (step == 0))
            def _():
                for one in loads(index):
                    one.wait()

        wide_ref, down_ref = wide_all.at[k], down_all.at[k]
        x, d = x_ref[0], d_ref[0]
        w = w_ref[0, :, 0:1]
        pre = mm(x, wide_ref[...])
        gate_pre, up_pre = pre[:, :ff], pre[:, ff:]
        sig = 1.0 / (1.0 + jnp.exp(-gate_pre))
        silu = gate_pre * sig
        active_wide = silu * up_pre
        active = active_wide.astype(BF16)
        o_ref[0] = (mm(active, down_ref[...], NT) * w).astype(BF16)
        d_raw = mm(d, down_ref[...])
        d_gates = jnp.sum(active.astype(F32) * d_raw, axis=1, keepdims=True)
        d_active = d_raw * w
        d_up = (d_active * silu).astype(BF16)
        d_gate = (d_active * up_pre * sig * (1.0 + gate_pre * (1.0 - sig))).astype(BF16)
        d_both = jnp.concatenate([d_gate, d_up], axis=1)
        r_ref[0, :, :model] = mm(d_both, wide_ref[...], NT).astype(BF16)
        high = d_gates.astype(BF16).astype(F32)
        lane = lax.broadcasted_iota(jnp.int32, (tile, LANES), 1)
        e = at_ref[2] + k
        r_ref[0, :, model:] = (
            jnp.where(lane == e, high, 0.0) + jnp.where(lane == e + experts, d_gates - high, 0.0)
        ).astype(BF16)
        new_wide = mm(x, d_both, TN)
        new_down = mm((active_wide * w).astype(BF16), d, TN)

        @pl.when(step == 0)
        def _():
            acc_wide[...] = new_wide
            acc_down[...] = new_down

        @pl.when(step > 0)
        def _():
            acc_wide[...] += new_wide
            acc_down[...] += new_down

        @pl.when(step == steps - 1)
        def _():
            for s in range(groups):
                z = lax.rem(at_ref[0] + s, groups)
                at_z = pl.ds(pl.multiple_of(z * part, 128), part)
                outs[s][0, 0] = acc_wide[at_z, :ff].astype(BF16)
                outs[s][0, 1] = acc_wide[at_z, ff:].astype(BF16)
                outs[s][0, 2] = acc_down[:, at_z].T.astype(BF16)

    grad = pl.BlockSpec((1, 3, part, ff), lambda k, t: (k, 0, 0, 0), pipeline_mode=pl.Buffered(1))
    rows = lambda width: pl.BlockSpec((1, tile, width), lambda k, t: (k, t, 0))
    out = pl.pallas_call(
        kernel,
        grid=(per, steps),
        in_specs=[SMEM_SPEC, rows(model), rows(model), rows(LANES)] + [ANY_SPEC] * groups,
        out_specs=[rows(model), rows(model + LANES)] + [grad] * groups,
        out_shape=[
            jax.ShapeDtypeStruct((per, total, model), BF16),
            jax.ShapeDtypeStruct((per, total, model + LANES), BF16),
        ]
        + [jax.ShapeDtypeStruct((per, 3, part, ff), BF16)] * groups,
        scratch_shapes=[
            pltpu.VMEM((model, 2 * ff), F32),
            pltpu.VMEM((ff, model), F32),
            pltpu.VMEM((per, model, 2 * ff), BF16),
            pltpu.VMEM((per, model, ff), BF16),
            pltpu.SemaphoreType.DMA((per, 3 * groups)),
        ],
        compiler_params=pltpu.CompilerParams(vmem_limit_bytes=62 * 1024 * 1024),
        cost_estimate=cost(18 * per * total * model * ff, 10 * per * total * model),
        name="expert_steps",
    )(at, rows_in, grads_in, weights, bank, *far)
    return out[0], out[1], list(out[2:])


def merge_grads(which, at, terms):
    per, _, part, ff = terms[0].shape
    split = 2
    tile = LANES

    def kernel(at_ref, *refs):
        ins, out = refs[: len(terms)], refs[len(terms)]
        for k in range(per):
            for parity in range(split):
                value = None
                for one in ins[parity::split]:
                    more = one[k, 0].astype(F32)
                    value = more if value is None else value + more
                index = lax.rem(at_ref[0] + parity, split) * per + k
                out[index] = value.T if which == 2 else value

    if which == 2:
        spec = pl.BlockSpec((split * per, ff, tile), lambda t: (0, 0, t))
        shape = (split * per, ff, part)
    else:
        spec = pl.BlockSpec((split * per, tile, ff), lambda t: (0, t, 0))
        shape = (split * per, part, ff)
    return pl.pallas_call(
        kernel,
        grid=(part // tile,),
        in_specs=[SMEM_SPEC]
        + [pl.BlockSpec((per, 1, tile, ff), lambda t: (0, which, t, 0))] * len(terms),
        out_specs=spec,
        out_shape=jax.ShapeDtypeStruct(shape, F32),
        cost_estimate=cost(1e8, 6e6),
        name="merge_grads",
    )(at, *terms)


def layer_plane(
    tokens,
    cotangent,
    routes,
    norm_one,
    query_key_value_weight,
    out_weight,
    norm_two,
    router_weight,
    gate_weight,
    up_weight,
    down_weight,
):
    n = lax.axis_size("expert")
    groups = lax.axis_size("group")
    me = lax.axis_index("expert")
    z = lax.axis_index("group")
    micro, count, model = tokens.shape
    exp_here, part, ff = gate_weight.shape
    experts = router_weight.shape[1]
    split = 2
    per = exp_here // split
    query_width = QUERY_HEADS * HEAD_SIZE
    kv_width = KEY_VALUE_HEADS * HEAD_SIZE
    cap = max(2, 3 * TOPK * PR_DEV // experts)
    where = jnp.stack([z, me, me * exp_here + (z % split) * per, (z % split) * per]).astype(jnp.int32)
    rows_here = part // n
    rows = micro * count

    misc = jnp.concatenate(
        [
            norm_one[:, None],
            norm_two[:, None],
            jnp.zeros((part, experts - 2), BF16),
            router_weight,
            jnp.zeros((part, LANES - 2 * experts), BF16),
        ],
        axis=1,
    )
    cut = lambda x: lax.dynamic_slice_in_dim(x, me * rows_here, rows_here, axis=0)
    shares = [cut(query_key_value_weight), jnp.concatenate([cut(out_weight), cut(misc)], axis=1)]
    bank = jnp.stack([gate_weight, up_weight, jnp.swapaxes(down_weight, 1, 2)], axis=1)

    expert_ids = jnp.arange(experts, dtype=jnp.int32)
    named = jnp.any(routes[..., None] == expert_ids, axis=2)
    pad = jnp.zeros((micro, count, LANES - experts), BF16)
    d_payload = jnp.concatenate([cotangent, named.astype(BF16), pad], axis=2)
    d_turned = turn(d_payload, 1, split)

    qkv_full, rest_full, far_one = plane_weights(shares, bank, per)
    (bank_late, d_payload, d_turned), qkv_full = lax.optimization_barrier(
        ((bank, d_payload, d_turned), qkv_full)
    )
    weights_far = [far_one]
    for s in range(2, groups):
        first = ((z + s) % split) * per
        weights_far.append(shift(lax.dynamic_slice_in_dim(bank_late, first, per, axis=0), s))
    both = jnp.concatenate([d_payload, d_turned], axis=0)
    d_slots = lax.all_gather(both, "expert", axis=0)
    out_full, misc_full = rest_full[:, :model], rest_full[:, model:]
    gain_one = misc_full[:, 0].astype(F32)
    gain_two = misc_full[:, 1].astype(F32)
    router_full = misc_full[:, experts : 2 * experts]

    grads_in, ranks = gather_flags(d_slots, where, per, cap, model)

    x = tokens.reshape(rows, model).astype(F32)
    inverse_one = lax.rsqrt(jnp.mean(x * x, axis=-1, keepdims=True) + 1e-05)
    normed = (x * inverse_one * gain_one).astype(BF16)
    cosine, sine = rope_tables(me, PR_DEV * n)
    heads_rope = QUERY_HEADS + KEY_VALUE_HEADS
    cosine = jnp.tile(jnp.concatenate([cosine, cosine], axis=1), (micro, heads_rope))
    sine = jnp.tile(jnp.concatenate([-sine, sine], axis=1), (micro, heads_rope))
    cosine, sine = lax.optimization_barrier((cosine, sine))
    project = mm(normed, qkv_full)
    roped = rotate(project[:, : query_width + kv_width], cosine, sine).astype(BF16)
    query = roped[:, :query_width].reshape(micro, count, query_width)
    key_value = jnp.concatenate(
        [roped[:, query_width:], project[:, query_width + kv_width :].astype(BF16)], axis=1
    ).reshape(micro, count, 2 * kv_width)
    mixed, kv_slots = plane_attention(query, key_value)
    mixed = mixed.reshape(rows, query_width)
    hidden = x + mm(mixed, out_full)
    inverse_two = lax.rsqrt(jnp.mean(hidden * hidden, axis=-1, keepdims=True) + 1e-05)
    normed_two = (hidden * inverse_two * gain_two).astype(BF16)
    logits = mm(normed_two, router_full)
    chosen = named.reshape(rows, experts)
    logits = jnp.where(chosen, logits, NEG_FILL)
    top = jnp.max(logits, axis=-1, keepdims=True)
    raised = jnp.where(chosen, jnp.exp(logits - top), 0.0)
    gate_probs = raised / jnp.sum(raised, axis=-1, keepdims=True)

    high = gate_probs.astype(BF16)
    low = (gate_probs - high.astype(F32)).astype(BF16)
    payload = jnp.concatenate(
        [normed_two, high, low, jnp.zeros((rows, LANES - 2 * experts), BF16)], axis=1
    ).reshape(micro, count, model + LANES)
    rows_in, row_weights = plane_dispatch(payload, ranks, where, per, cap, model, experts)
    tile = 2 * micro * split * cap
    outs, backs, weight_terms = expert_steps(
        where, rows_in, grads_in, row_weights, bank, weights_far, experts, tile
    )
    back = plane_return(backs, ranks, micro, count, cap).reshape(rows, model + LANES)

    mixture_parts = scatter_rows(outs, ranks, where, n, micro * split, count, cap)
    mixture_sum = lax.psum_scatter(mixture_parts, "expert", scatter_dimension=0, tiled=False)
    mixture = mixture_sum[:micro].astype(F32) + turn(mixture_sum[micro:], 1, split).astype(F32)
    block_out = (hidden + mixture.reshape(rows, model)).astype(BF16).reshape(tokens.shape)

    terms = weight_terms[:1] + [shift(weight_terms[s], s) for s in range(1, groups)]
    gate_grad, up_grad, down_grad = [merge_grads(which, where, terms) for which in range(3)]

    d_out = cotangent.reshape(rows, model).astype(F32)
    d_gates = back[:, model : model + experts] + back[:, model + experts : model + 2 * experts]
    d_logits = gate_probs * (d_gates - jnp.sum(gate_probs * d_gates, axis=-1, keepdims=True))
    router_grad = lax.dot_general(normed_two.astype(F32), d_logits, TN, precision=HIGHEST)
    d_normed_two = back[:, :model] + lax.dot_general(
        d_logits, router_full.astype(F32), NT, precision=HIGHEST
    )

    def rms_back(inputs, inverse, gain, upstream):
        scaled = gain * upstream
        return inverse * scaled - inputs * inverse * inverse * inverse * jnp.mean(
            scaled * inputs, axis=-1, keepdims=True
        )

    grad_two = jnp.sum(d_normed_two * hidden * inverse_two, axis=0)
    d_hidden = d_out + rms_back(hidden, inverse_two, gain_two, d_normed_two)
    d_attn = d_hidden.astype(BF16)
    d_mixed = mm(d_attn, out_full, NT).astype(BF16).reshape(micro, count, query_width)
    d_query, d_kv = plane_attention_backward(query, kv_slots, d_mixed)
    d_query = d_query.reshape(rows, query_width)
    d_kv = d_kv.reshape(rows, 2 * kv_width)
    q_cos, q_sin = cosine[:, :query_width], sine[:, :query_width]
    d_query_low = rotate(d_query, q_cos, -q_sin).astype(BF16)
    d_key_low = rotate(d_kv[:, :kv_width], q_cos[:, :kv_width], -q_sin[:, :kv_width]).astype(BF16)
    d_project = jnp.concatenate(
        [d_query_low, d_key_low, d_kv[:, kv_width:].astype(BF16)], axis=1
    )
    d_normed = mm(d_project, qkv_full, NT)
    grad_one = jnp.sum(d_normed * x * inverse_one, axis=0)
    input_grad = (d_hidden + rms_back(x, inverse_one, gain_one, d_normed)).reshape(tokens.shape)
    misc_grad = jnp.concatenate(
        [
            grad_one[:, None],
            grad_two[:, None],
            jnp.zeros((model, experts - 2), F32),
            router_grad,
            jnp.zeros((model, LANES - 2 * experts), F32),
        ],
        axis=1,
    )
    dense = plane_gradients([(mixed, d_attn), (normed, d_project)], misc_grad, groups)
    misc_sum = dense[:, model + query_width + 2 * kv_width :]
    return (
        block_out,
        input_grad,
        misc_sum[:, 0],
        dense[:, model : model + query_width + 2 * kv_width],
        dense[:, :model],
        misc_sum[:, 1],
        misc_sum[:, experts : 2 * experts],
        gate_grad,
        up_grad,
        down_grad,
    )


def per_device(*arrays):
    n, groups = lax.axis_size("expert"), lax.axis_size("group")
    exp_here, part, ff = arrays[8].shape
    plane = (
        n == 8
        and exp_here % 2 == 0
        and groups == 4
        and part % (16 * n) == 0
        and part % LANES == 0
        and arrays[0].shape[0] == 2
    )
    return (layer_plane if plane else layer_general)(*arrays)


def solution(mesh):
    rows = P(None, ("group", "expert"), None)
    return jax.shard_map(
        per_device,
        mesh=mesh,
        in_specs=(
            rows,
            rows,
            rows,
            P("group"),
            P("group", None),
            P("group", None),
            P("group"),
            P("group", None),
            P("expert", "group", None),
            P("expert", "group", None),
            P("expert", None, "group"),
        ),
        out_specs=(
            rows,
            rows,
            P("group"),
            P("group", None),
            P("group", None),
            P("group"),
            P("group", None),
            P("expert", "group", None),
            P("expert", "group", None),
            P("expert", None, "group"),
        ),
        check_vma=False,
    )
```

```python
import functools

import jax
import jax.numpy as jnp
from jax import lax
from jax.experimental import pallas as pl
from jax.experimental.pallas import tpu as pltpu
from jax.sharding import PartitionSpec as P

QUERY_HEADS = 24
KEY_VALUE_HEADS = 8
HEAD_SIZE = 64
TOPK = 8
CONT = 256
PR_DEV = 64
LANES = 128
SCORE_SCALE = 0.125
NEG_FILL = -1e30
HIGHEST = lax.Precision.HIGHEST
F32 = jnp.float32
BF16 = jnp.bfloat16

NN = (((1,), (0,)), ((), ()))
NT = (((1,), (1,)), ((), ()))
TN = (((0,), (0,)), ((), ()))


def mm(a, b, dims=NN):
    return lax.dot_general(a, b, dims, preferred_element_type=F32)


def swap(x, bit):
    n = lax.axis_size("expert")
    return lax.ppermute(x, "expert", [(i, i ^ bit) for i in range(n)])


def shift(x, step):
    n = lax.axis_size("group")
    return lax.ppermute(x, "group", [(i, (i + step) % n) for i in range(n)])


def turn(x, step, split):
    n = lax.axis_size("group")
    return lax.ppermute(
        x, "group", [((i // split) * split + (i + step) % split, i) for i in range(n)]
    )


def outer_bits(n):
    return [1 << i for i in range(1, n.bit_length() - 1)]


def spread(x, order):
    n = lax.axis_size("expert")
    outer = outer_bits(n)
    if len(outer) == 2:
        a, b = outer
        xa, xb = swap(x, a), swap(x, b)
        slots = {0: x, a: xa, b: xb, a ^ b: swap(xa, b) if order == 0 else swap(xb, a)}
    else:
        slots = {0: x}
        for bit in outer:
            slots.update({r ^ bit: swap(y, bit) for r, y in list(slots.items())})
    if n > 1:
        slots.update({r ^ 1: swap(y, 1) for r, y in list(slots.items())})
    return [slots[r] for r in range(n)]


def plus(a, b):
    return (a.astype(F32) + b.astype(F32)).astype(BF16)


def collect(parts, order):
    n = lax.axis_size("expert")
    outer = outer_bits(n)
    keep = {r: parts[r] for r in range(n)}
    if n > 1:
        keep = {r: plus(keep[r], swap(keep[r ^ 1], 1)) for r in range(0, n, 2)}
    if len(outer) == 2:
        a, b = outer
        if order == 0:
            keep[a] = plus(keep[a], swap(keep[a ^ b], b))
        else:
            keep[b] = plus(keep[b], swap(keep[a ^ b], a))
        return (
            keep[0].astype(F32) + swap(keep[a], a).astype(F32) + swap(keep[b], b).astype(F32)
        )
    for bit in reversed(outer):
        keep = {r: plus(keep[r], swap(keep[r ^ bit], bit)) for r in keep if not r & bit}
    return keep[0].astype(F32)


def full_spec(shape):
    return pl.BlockSpec(shape, lambda *_: (0,) * len(shape))


SMEM_SPEC = pl.BlockSpec(memory_space=pltpu.SMEM)
ANY_SPEC = pl.BlockSpec(memory_space=pl.ANY)


def cost(flops, moved):
    return pl.CostEstimate(flops=int(flops), bytes_accessed=int(moved), transcendentals=0)


def assemble(pieces, place, shape, where):
    count = len(pieces)

    def kernel(at_ref, *refs):
        ins, out, sems = refs[:count], refs[count], refs[count + 1]
        copies = []
        for i in range(count):
            row, column = place(i, at_ref[0], at_ref[1])
            r, c = pieces[i].shape
            copies.append(
                pltpu.make_async_copy(
                    ins[i],
                    out.at[pl.ds(pl.multiple_of(row, 16), r), pl.ds(pl.multiple_of(column, 128), c)],
                    sems.at[i],
                )
            )
        for one in copies:
            one.start()
        for one in copies:
            one.wait()

    return pl.pallas_call(
        kernel,
        grid=(1,),
        in_specs=[SMEM_SPEC] + [ANY_SPEC] * count,
        out_specs=full_spec(shape),
        out_shape=jax.ShapeDtypeStruct(shape, pieces[0].dtype),
        scratch_shapes=[pltpu.SemaphoreType.DMA((count,))],
        cost_estimate=cost(0, 4 * shape[0] * shape[1]),
        name="assemble",
    )(where, *pieces)


def gather_dense(piece, cuts, where):
    groups, n = lax.axis_size("group"), lax.axis_size("expert")
    rows, columns = piece.shape
    own = [piece[:, lo:hi] for lo, hi in cuts]
    far = [[shift(x, s) for x in own] for s in range(1, groups)]
    names, pieces = [], []
    for h, (lo, hi) in enumerate(cuts):
        joined = jnp.concatenate([far[s - 1][h] for s in range(1, groups)], axis=0)
        for r, x in enumerate(spread(own[h], h % 2)):
            names.append((0, r, lo))
            pieces.append(x)
        for r, x in enumerate(spread(joined, h % 2)):
            for s in range(1, groups):
                names.append((s, r, lo))
                pieces.append((x, (s - 1) * rows, rows))
    total = groups * n * rows
    arrays, index = [], []
    for entry in pieces:
        if isinstance(entry, tuple):
            if not arrays or arrays[-1] is not entry[0]:
                arrays.append(entry[0])
            index.append((len(arrays) - 1, entry[1], entry[2]))
        else:
            arrays.append(entry)
            index.append((len(arrays) - 1, 0, rows))
    count, held = len(index), len(arrays)

    def kernel(at_ref, *refs):
        ins, out, sems = refs[:held], refs[held], refs[held + 1]
        copies = []
        for i, (which, start, size) in enumerate(index):
            s, r, lo = names[i]
            z = lax.rem(at_ref[0] - s + groups, groups)
            e = jnp.bitwise_xor(at_ref[1], r)
            row = pl.multiple_of((z * n + e) * rows, 16)
            width = arrays[which].shape[1]
            copies.append(
                pltpu.make_async_copy(
                    ins[which].at[pl.ds(start, size)],
                    out.at[pl.ds(row, rows), pl.ds(lo, width)],
                    sems.at[i],
                )
            )
        for one in copies:
            one.start()
        for one in copies:
            one.wait()

    whole = pl.pallas_call(
        kernel,
        grid=(1,),
        in_specs=[SMEM_SPEC] + [ANY_SPEC] * held,
        out_specs=full_spec((total, columns)),
        out_shape=jax.ShapeDtypeStruct((total, columns), piece.dtype),
        scratch_shapes=[pltpu.SemaphoreType.DMA((count,))],
        cost_estimate=cost(0, 4 * total * columns),
        name="join_rows",
    )(where, *arrays)
    return whole, far


def sliced_outer(a, b, extra, groups, n, where):
    depth = a.shape[1]
    columns = b.shape[1]
    more = 0 if extra is None else extra.shape[1]
    rows = depth // (groups * n)

    def kernel(at_ref, a_ref, b_ref, *refs):
        if more:
            x_ref, refs = refs[0], refs[1:]
        outs, acc = refs[:n], refs[n]
        acc[:, :columns] = mm(a_ref[...], b_ref[...], TN)
        if more:
            acc[:, columns:] = x_ref[...]
        for r in range(n):
            e = jnp.bitwise_xor(at_ref[1], r)
            for s in range(groups):
                z = lax.rem(at_ref[0] + s, groups)
                row = pl.multiple_of((z * n + e) * rows, 16)
                outs[r][s] = acc[pl.ds(row, rows), :].astype(BF16)

    width = columns + more
    return pl.pallas_call(
        kernel,
        grid=(1,),
        in_specs=[SMEM_SPEC, full_spec(a.shape), full_spec(b.shape)]
        + ([full_spec(extra.shape)] if more else []),
        out_specs=[full_spec((groups, rows, width))] * n,
        out_shape=[jax.ShapeDtypeStruct((groups, rows, width), BF16)] * n,
        scratch_shapes=[pltpu.VMEM((depth, width), F32)],
        cost_estimate=cost(2 * a.shape[0] * depth * columns, 2 * depth * width),
        name="sliced_outer",
    )(where, a, b, *([extra] if more else []))


def reduce_dense(parts, order, where):
    groups, n = lax.axis_size("group"), lax.axis_size("expert")
    mine = collect(parts, order)
    total = mine[0]
    low = mine.astype(BF16)
    for s in range(1, groups):
        total = total + shift(low[s], s).astype(F32)
    rows, width = total.shape
    slots = spread(total.astype(BF16), order)

    def kernel(at_ref, *refs):
        out = refs[n]
        for r in range(n):
            e = jnp.bitwise_xor(at_ref[1], r)
            out[pl.ds(pl.multiple_of(e * rows, 16), rows), :] = refs[r][...].astype(F32)

    return pl.pallas_call(
        kernel,
        grid=(1,),
        in_specs=[SMEM_SPEC] + [full_spec((rows, width))] * n,
        out_specs=full_spec((n * rows, width)),
        out_shape=jax.ShapeDtypeStruct((n * rows, width), F32),
        cost_estimate=cost(0, 6 * n * rows * width),
        name="join_sums",
    )(where, *slots)


def attention_masks(n, me):
    shape = (3 * PR_DEV, n * PR_DEV)
    token = lax.rem(lax.broadcasted_iota(jnp.int32, shape, 0), PR_DEV)
    column = lax.broadcasted_iota(jnp.int32, shape, 1)
    key_pos = jnp.bitwise_xor(column // PR_DEV, me) * PR_DEV + lax.rem(column, PR_DEV)
    prompt_ok = key_pos <= me * PR_DEV + token
    slots = CONT // PR_DEV
    shape = (3 * PR_DEV, CONT)
    token = lax.rem(lax.broadcasted_iota(jnp.int32, shape, 0), PR_DEV)
    column = lax.broadcasted_iota(jnp.int32, shape, 1)
    owner = jnp.bitwise_xor(column // PR_DEV, lax.rem(me, slots))
    cont_ok = owner * PR_DEV + lax.rem(column, PR_DEV) <= lax.rem(me, slots) * PR_DEV + token
    return prompt_ok, cont_ok


def head_rows(x, base):
    return jnp.concatenate(
        [x[:, base + i * HEAD_SIZE : base + (i + 1) * HEAD_SIZE] for i in range(3)], axis=0
    )


def row_heads(x):
    return jnp.concatenate([x[i * PR_DEV : (i + 1) * PR_DEV] for i in range(3)], axis=1)


def softmax(scores):
    top = jnp.max(scores, axis=1, keepdims=True)
    weight = jnp.exp(scores - top)
    return weight * (1.0 / jnp.sum(weight, axis=1, keepdims=True))


def load_keys(n, kv_refs, keys):
    for r in range(n):
        keys[r * PR_DEV : (r + 1) * PR_DEV, :] = kv_refs[r][:PR_DEV, :]
    for r in range(CONT // PR_DEV):
        lo = (n + r) * PR_DEV
        keys[lo : lo + PR_DEV, :] = kv_refs[r][PR_DEV:, :]


def group_probs(q_top, q_low, key, prompt_ok, cont_ok, n):
    pr = n * PR_DEV
    top = mm(q_top, key[:pr], NT) * SCORE_SCALE
    top = softmax(jnp.where(prompt_ok, top, NEG_FILL))
    low = mm(q_low, key, NT) * SCORE_SCALE
    low = jnp.concatenate([low[:, :pr], jnp.where(cont_ok, low[:, pr:], NEG_FILL)], axis=1)
    return top, softmax(low)


def attention_forward(query, slots, where):
    n = len(slots)
    width = KEY_VALUE_HEADS * HEAD_SIZE
    tokens = 2 * PR_DEV
    total = n * PR_DEV + CONT

    def kernel(at_ref, q_ref, *refs):
        kv_refs, out_ref, keys = refs[:n], refs[n], refs[n + 1]
        load_keys(n, kv_refs, keys)
        prompt_ok, cont_ok = attention_masks(n, at_ref[1])

        def pair(j, carry):
            q_at = pl.ds(pl.multiple_of(j * 384, 128), 384)
            k_at = pl.ds(pl.multiple_of(j * 128, 128), 128)
            v_at = pl.ds(pl.multiple_of(width + j * 128, 128), 128)
            q_top, q_low = q_ref[:PR_DEV, q_at], q_ref[PR_DEV:, q_at]
            k_two, v_two = keys[:, k_at], keys[:, v_at]
            tops, lows = [], []
            for g in range(2):
                key = k_two[:, g * HEAD_SIZE : (g + 1) * HEAD_SIZE]
                value = v_two[:, g * HEAD_SIZE : (g + 1) * HEAD_SIZE]
                top, low = group_probs(
                    head_rows(q_top, g * 192), head_rows(q_low, g * 192), key, prompt_ok, cont_ok, n
                )
                tops.append(row_heads(mm(top.astype(BF16), value[: n * PR_DEV])))
                lows.append(row_heads(mm(low.astype(BF16), value)))
            out_ref[:PR_DEV, q_at] = jnp.concatenate(tops, axis=1).astype(BF16)
            out_ref[PR_DEV:, q_at] = jnp.concatenate(lows, axis=1).astype(BF16)
            return carry

        lax.fori_loop(0, KEY_VALUE_HEADS // 2, pair, 0)

    return pl.pallas_call(
        kernel,
        grid=(1,),
        in_specs=[SMEM_SPEC, full_spec(query.shape)] + [full_spec((tokens, 2 * width))] * n,
        out_specs=full_spec(query.shape),
        out_shape=jax.ShapeDtypeStruct(query.shape, BF16),
        scratch_shapes=[pltpu.VMEM((total, 2 * width), BF16)],
        cost_estimate=cost(8e9, 4e6),
        name="attention_forward",
    )(where, query, *slots)


def attention_backward(query, slots, d_mixed, where):
    n = len(slots)
    width = KEY_VALUE_HEADS * HEAD_SIZE
    tokens = 2 * PR_DEV
    pr = n * PR_DEV
    total = pr + CONT

    def kernel(at_ref, q_ref, d_ref, *refs):
        kv_refs, refs = refs[:n], refs[n:]
        dq_ref, outs, keys, grads = refs[0], refs[1 : 1 + n], refs[1 + n], refs[2 + n]
        load_keys(n, kv_refs, keys)
        prompt_ok, cont_ok = attention_masks(n, at_ref[1])

        def one_side(prob, d_rows, key, value, q_rows):
            d_prob = mm(d_rows, value, NT)
            delta = jnp.sum(prob * d_prob, axis=1, keepdims=True)
            d_score = (prob * (d_prob - delta)).astype(BF16)
            return (
                mm(d_score, key) * SCORE_SCALE,
                mm(d_score, q_rows, TN) * SCORE_SCALE,
                mm(prob.astype(BF16), d_rows, TN),
            )

        def pair(j, carry):
            q_at = pl.ds(pl.multiple_of(j * 384, 128), 384)
            k_at = pl.ds(pl.multiple_of(j * 128, 128), 128)
            v_at = pl.ds(pl.multiple_of(width + j * 128, 128), 128)
            q_top, q_low = q_ref[:PR_DEV, q_at], q_ref[PR_DEV:, q_at]
            d_top, d_low = d_ref[:PR_DEV, q_at], d_ref[PR_DEV:, q_at]
            k_two, v_two = keys[:, k_at], keys[:, v_at]
            dq_tops, dq_lows, dks, dvs = [], [], [], []
            for g in range(2):
                key = k_two[:, g * HEAD_SIZE : (g + 1) * HEAD_SIZE]
                value = v_two[:, g * HEAD_SIZE : (g + 1) * HEAD_SIZE]
                rows_top, rows_low = head_rows(q_top, g * 192), head_rows(q_low, g * 192)
                top, low = group_probs(rows_top, rows_low, key, prompt_ok, cont_ok, n)
                dq_top, dk_top, dv_top = one_side(
                    top, head_rows(d_top, g * 192), key[:pr], value[:pr], rows_top
                )
                dq_low, dk_low, dv_low = one_side(
                    low, head_rows(d_low, g * 192), key, value, rows_low
                )
                dq_tops.append(row_heads(dq_top))
                dq_lows.append(row_heads(dq_low))
                dks.append(jnp.concatenate([dk_low[:pr] + dk_top, dk_low[pr:]], axis=0))
                dvs.append(jnp.concatenate([dv_low[:pr] + dv_top, dv_low[pr:]], axis=0))
            dq_ref[:PR_DEV, q_at] = jnp.concatenate(dq_tops, axis=1)
            dq_ref[PR_DEV:, q_at] = jnp.concatenate(dq_lows, axis=1)
            grads[:, k_at] = jnp.concatenate(dks, axis=1).astype(BF16)
            grads[:, v_at] = jnp.concatenate(dvs, axis=1).astype(BF16)
            return carry

        lax.fori_loop(0, KEY_VALUE_HEADS // 2, pair, 0)
        for r in range(n):
            outs[r][:PR_DEV, :] = grads[r * PR_DEV : (r + 1) * PR_DEV, :]
            if r < CONT // PR_DEV:
                lo = (n + r) * PR_DEV
                outs[r][PR_DEV:, :] = grads[lo : lo + PR_DEV, :]
            else:
                outs[r][PR_DEV:, :] = jnp.zeros((PR_DEV, 2 * width), BF16)

    out = pl.pallas_call(
        kernel,
        grid=(1,),
        in_specs=[SMEM_SPEC, full_spec(query.shape), full_spec(query.shape)]
        + [full_spec((tokens, 2 * width))] * n,
        out_specs=[full_spec(query.shape)] + [full_spec((tokens, 2 * width))] * n,
        out_shape=[jax.ShapeDtypeStruct(query.shape, F32)]
        + [jax.ShapeDtypeStruct((tokens, 2 * width), BF16)] * n,
        scratch_shapes=[pltpu.VMEM((total, 2 * width), BF16), pltpu.VMEM((total, 2 * width), BF16)],
        cost_estimate=cost(2e10, 8e6),
        name="attention_backward",
    )(where, query, d_mixed, *slots)
    return out[0], out[1:]


def pick(slot_row, cap):
    rows = lax.broadcasted_iota(jnp.int32, (cap, slot_row.shape[1]), 0).astype(F32)
    return jnp.where(slot_row == rows, 1.0, 0.0).astype(BF16)


def dispatch_grads(arrays, at, per, cap, model, buffers, place, blocks_total):
    count = len(arrays)
    split, tokens, width = arrays[0].shape
    blocks = count * split
    first = buffers is None

    def kernel(at_ref, *refs):
        ins = refs[:count]
        out, ranks = refs[-3], refs[-2]
        flags = refs[-1]
        row = lax.broadcasted_iota(jnp.int32, (tokens, tokens), 0)
        col = lax.broadcasted_iota(jnp.int32, (tokens, tokens), 1)
        before = jnp.where(row < col, 1.0, 0.0).astype(BF16)
        for i in range(count):
            for j in range(split):
                b = i * split + j
                payload = ins[i][j]
                flags[...] = payload[:, model:].astype(F32).T
                picked = jnp.concatenate(
                    [flags[pl.ds(at_ref[2] + k, 1), :] for k in range(per)], axis=0
                )
                rank = mm(picked.astype(BF16), before)
                slot = jnp.where(picked > 0.0, rank, -1.0)
                ranks[b] = slot
                for k in range(per):
                    out[k, b * cap : (b + 1) * cap, :] = mm(
                        pick(slot[k : k + 1], cap), payload[:, :model]
                    ).astype(BF16)

    shapes = [
        jax.ShapeDtypeStruct((per, blocks_total * cap, model), BF16),
        jax.ShapeDtypeStruct((blocks_total, per, tokens), F32),
    ]
    return pl.pallas_call(
        kernel,
        grid=(1,),
        in_specs=[SMEM_SPEC]
        + [full_spec(arrays[0].shape)] * count
        + ([] if first else [ANY_SPEC] * 2),
        out_specs=[
            pl.BlockSpec((per, blocks * cap, model), lambda *_: (0, place, 0)),
            pl.BlockSpec((blocks, per, tokens), lambda *_: (place, 0, 0)),
        ],
        out_shape=shapes,
        scratch_shapes=[pltpu.VMEM((LANES, tokens), F32)],
        input_output_aliases={} if first else {1 + count: 0, 2 + count: 1},
        cost_estimate=cost(1e9, 6e6),
        name="dispatch_grads",
    )(at, *arrays, *([] if first else buffers))


def dispatch_rows(arrays, ranks, at, per, cap, model, experts, buffers, place, blocks_total):
    count = len(arrays)
    split, tokens, width = arrays[0].shape
    blocks = count * split
    first = buffers is None

    def kernel(at_ref, rank_ref, *refs):
        ins = refs[:count]
        out, weights = refs[-2], refs[-1]
        lane = lax.broadcasted_iota(jnp.int32, (cap, LANES), 1)
        for i in range(count):
            for j in range(split):
                b = i * split + j
                payload = ins[i][j]
                for k in range(per):
                    got = mm(pick(rank_ref[b, k : k + 1, :], cap), payload)
                    out[k, b * cap : (b + 1) * cap, :] = got[:, :model].astype(BF16)
                    tail = got[:, model:]
                    e = at_ref[2] + k
                    mine = (lane == e) | (lane == e + experts)
                    total = jnp.sum(jnp.where(mine, tail, 0.0), axis=1, keepdims=True)
                    weights[k, b * cap : (b + 1) * cap, :] = jnp.broadcast_to(total, (cap, LANES))

    shapes = [
        jax.ShapeDtypeStruct((per, blocks_total * cap, model), BF16),
        jax.ShapeDtypeStruct((per, blocks_total * cap, LANES), F32),
    ]
    return pl.pallas_call(
        kernel,
        grid=(1,),
        in_specs=[SMEM_SPEC, pl.BlockSpec((blocks, per, tokens), lambda *_: (place, 0, 0))]
        + [full_spec(arrays[0].shape)] * count
        + ([] if first else [ANY_SPEC] * 2),
        out_specs=[
            pl.BlockSpec((per, blocks * cap, model), lambda *_: (0, place, 0)),
            pl.BlockSpec((per, blocks * cap, LANES), lambda *_: (0, place, 0)),
        ],
        out_shape=shapes,
        input_output_aliases={} if first else {2 + count: 0, 3 + count: 1},
        cost_estimate=cost(1e9, 6e6),
        name="dispatch_rows",
    )(at, ranks, *arrays, *([] if first else buffers))


def run_expert(k, at, rows_in, grads_in, weights, gate, up, down, experts, tile, groups, cut):
    per, total, model = rows_in.shape
    ff = gate.shape[1]
    part = model // groups
    steps = total // tile

    def kernel(at_ref, x_ref, d_ref, w_ref, gate_ref, up_ref, down_ref, o_ref, r_ref, *refs):
        outs, (acc_gate, acc_up, acc_down) = refs[:-3], refs[-3:]
        step = pl.program_id(0)
        x, d = x_ref[0], d_ref[0]
        w = w_ref[0, :, 0:1]
        gate_pre = mm(x, gate_ref[...])
        up_pre = mm(x, up_ref[...])
        sig = 1.0 / (1.0 + jnp.exp(-gate_pre))
        silu = gate_pre * sig
        active_wide = silu * up_pre
        active = active_wide.astype(BF16)
        out = mm(active, down_ref[...])
        o_ref[...] = (out * w).astype(BF16)
        d_raw = mm(d, down_ref[...], NT)
        d_gates = jnp.sum(active.astype(F32) * d_raw, axis=1, keepdims=True)
        d_active = d_raw * w
        d_up = (d_active * silu).astype(BF16)
        d_gate = (d_active * up_pre * sig * (1.0 + gate_pre * (1.0 - sig))).astype(BF16)
        d_row = mm(d_gate, gate_ref[...], NT) + mm(d_up, up_ref[...], NT)
        r_ref[:, :model] = d_row.astype(BF16)
        high = d_gates.astype(BF16).astype(F32)
        lane = lax.broadcasted_iota(jnp.int32, (tile, LANES), 1)
        e = at_ref[2] + k
        r_ref[:, model:] = (
            jnp.where(lane == e, high, 0.0) + jnp.where(lane == e + experts, d_gates - high, 0.0)
        ).astype(BF16)
        new_gate = mm(x, d_gate, TN)
        new_up = mm(x, d_up, TN)
        new_down = mm((active_wide * w).astype(BF16), d, TN)

        @pl.when(step == 0)
        def _():
            acc_gate[...] = new_gate
            acc_up[...] = new_up
            acc_down[...] = new_down

        @pl.when(step > 0)
        def _():
            acc_gate[...] += new_gate
            acc_up[...] += new_up
            acc_down[...] += new_down

        @pl.when(step == steps - 1)
        def _():
            if cut:
                for s in range(groups):
                    z = lax.rem(at_ref[0] + s, groups)
                    at_z = pl.ds(pl.multiple_of(z * part, 128), part)
                    outs[s][...] = acc_gate[at_z, :].astype(BF16)
                    outs[groups + s][...] = acc_up[at_z, :].astype(BF16)
                    outs[2 * groups + s][...] = acc_down[:, at_z].astype(BF16)
            else:
                outs[0][...] = acc_gate[...].astype(BF16)
                outs[1][...] = acc_up[...].astype(BF16)
                outs[2][...] = acc_down[...].astype(BF16)

    if cut:
        grads = [(part, ff)] * (2 * groups) + [(ff, part)] * groups
    else:
        grads = [(model, ff)] * 2 + [(ff, model)]
    row_spec = pl.BlockSpec((1, tile, model), lambda t: (k, t, 0))
    held = lambda shape: pl.BlockSpec(shape, lambda t: (0, 0), pipeline_mode=pl.Buffered(1))
    out = pl.pallas_call(
        kernel,
        grid=(steps,),
        in_specs=[
            SMEM_SPEC,
            row_spec,
            row_spec,
            pl.BlockSpec((1, tile, LANES), lambda t: (k, t, 0)),
            held((model, ff)),
            held((model, ff)),
            held((ff, model)),
        ],
        out_specs=[
            pl.BlockSpec((tile, model), lambda t: (t, 0)),
            pl.BlockSpec((tile, model + LANES), lambda t: (t, 0)),
        ]
        + [held(shape) for shape in grads],
        out_shape=[
            jax.ShapeDtypeStruct((total, model), BF16),
            jax.ShapeDtypeStruct((total, model + LANES), BF16),
        ]
        + [jax.ShapeDtypeStruct(shape, BF16) for shape in grads],
        scratch_shapes=[
            pltpu.VMEM((model, ff), F32),
            pltpu.VMEM((model, ff), F32),
            pltpu.VMEM((ff, model), F32),
        ],
        compiler_params=pltpu.CompilerParams(vmem_limit_bytes=62 * 1024 * 1024),
        cost_estimate=cost(18 * total * model * ff, 10 * total * model),
        name="run_expert",
    )(at, rows_in, grads_in, weights, gate, up, down)
    return out[0], out[1], out[2:]


def combine(rows, ranks, count, split, tokens, cap, place):
    per = len(rows)
    width = rows[0].shape[1]
    blocks = count * split

    def kernel(rank_ref, *refs):
        ins, outs = refs[:per], refs[per:]
        for i in range(count):
            for j in range(split):
                b = i * split + j
                total = None
                for k in range(per):
                    one = mm(
                        pick(rank_ref[b, k : k + 1, :], cap), ins[k][b * cap : (b + 1) * cap, :], TN
                    )
                    total = one if total is None else total + one
                outs[i][j] = total.astype(BF16)

    return pl.pallas_call(
        kernel,
        grid=(1,),
        in_specs=[pl.BlockSpec((blocks, per, tokens), lambda *_: (place, 0, 0))]
        + [pl.BlockSpec((blocks * cap, width), lambda *_: (place, 0))] * per,
        out_specs=[full_spec((split, tokens, width))] * count,
        out_shape=[jax.ShapeDtypeStruct((split, tokens, width), BF16)] * count,
        cost_estimate=cost(1e9, 6e6),
        name="combine",
    )(ranks, *rows)


def rope_tables(my_index, prompt_len):
    half = HEAD_SIZE // 2
    local = jnp.arange(2 * PR_DEV, dtype=jnp.int32)
    cont = my_index * PR_DEV + local - PR_DEV
    position = jnp.where(local < PR_DEV, my_index * PR_DEV + local, prompt_len + cont % CONT)
    frequency = 10000.0 ** (-jnp.arange(half, dtype=F32) * (2.0 / HEAD_SIZE))
    angle = position.astype(F32)[:, None] * frequency[None, :]
    return jnp.cos(angle), jnp.sin(angle)


def rotate(x, cosine, sine):
    half = HEAD_SIZE // 2
    column = lax.broadcasted_iota(jnp.int32, x.shape, 1)
    other = jnp.where(column % HEAD_SIZE < half, jnp.roll(x, -half, axis=1), jnp.roll(x, half, axis=1))
    return x * cosine + other * sine


def layer_general(
    tokens,
    cotangent,
    routes,
    norm_one,
    query_key_value_weight,
    out_weight,
    norm_two,
    router_weight,
    gate_weight,
    up_weight,
    down_weight,
):
    n = lax.axis_size("expert")
    groups = lax.axis_size("group")
    me = lax.axis_index("expert")
    z = lax.axis_index("group")
    micro, count, model = tokens.shape
    exp_here, part, ff = gate_weight.shape
    experts = router_weight.shape[1]
    split = 2 if exp_here % 2 == 0 and groups % 2 == 0 else 1
    per = exp_here // split
    query_width = QUERY_HEADS * HEAD_SIZE
    kv_width = KEY_VALUE_HEADS * HEAD_SIZE
    cap = max(2, 3 * TOPK * PR_DEV // experts)
    where = jnp.stack([z, me, me * exp_here + (z % split) * per]).astype(jnp.int32)
    rows_here = part // n if part % n == 0 else 0
    aligned = rows_here > 0 and rows_here % 16 == 0 and part % LANES == 0

    misc = jnp.concatenate(
        [
            norm_one[:, None],
            norm_two[:, None],
            jnp.zeros((part, experts - 2), BF16),
            router_weight,
            jnp.zeros((part, LANES - 2 * experts), BF16),
        ],
        axis=1,
    )
    if aligned:
        first = jnp.concatenate([query_key_value_weight, misc], axis=1)
        cut = lambda x: lax.dynamic_slice_in_dim(x, me * rows_here, rows_here, axis=0)
        width = first.shape[1]
        middle = width // 2 // LANES * LANES
        first_full, far = gather_dense(cut(first), [(0, middle), (middle, width)], where)
        out_full, far_out = gather_dense(
            cut(out_weight), [(0, model // 2), (model // 2, model)], where
        )
        after = (far, far_out)
    else:
        first_full = lax.all_gather(
            jnp.concatenate([query_key_value_weight, misc], axis=1), "group", axis=0, tiled=True
        )
        out_full = lax.all_gather(out_weight, "group", axis=0, tiled=True)
        after = ()
    qkv_columns = query_key_value_weight.shape[1]
    qkv_full = first_full[:, :qkv_columns]
    misc_full = first_full[:, qkv_columns:]
    gain_one = misc_full[:, 0].astype(F32)
    gain_two = misc_full[:, 1].astype(F32)
    router_full = misc_full[:, experts : 2 * experts]

    weights_held = []
    gate_from, up_from, down_from = gate_weight, up_weight, down_weight
    if aligned:
        (gate_from, up_from, down_from), after = lax.optimization_barrier(
            ((gate_weight, up_weight, down_weight), after)
        )
    for k in range(per):
        held = []
        for array, axis in ((gate_from, 0), (up_from, 0), (down_from, 1)):
            if not aligned:
                held.append(lax.all_gather(array[k], "group", axis=axis, tiled=True))
                continue
            pieces = []
            for s in range(groups):
                index = ((z + s) % split) * per + k
                chunk = lax.dynamic_index_in_dim(array, index, 0, keepdims=False)
                pieces.append(shift(chunk, s) if s else chunk)

            def place(i, at_z, at_e, axis=axis):
                start = lax.rem(at_z - i + groups, groups) * part
                return (start, 0) if axis == 0 else (0, start)

            shape = (model, ff) if axis == 0 else (ff, model)
            held.append(assemble(pieces, place, shape, where))
        weights_held.append(held)

    expert_ids = jnp.arange(experts, dtype=jnp.int32)
    named = jnp.any(routes[..., None] == expert_ids, axis=2)
    pad = jnp.zeros((micro, count, LANES - experts), BF16)
    d_payload = jnp.concatenate([cotangent, named.astype(BF16), pad], axis=2)

    def to_experts(payload):
        held = []
        for m in range(micro):
            own = payload[m]
            both = jnp.stack([own] + [turn(own, j, split) for j in range(1, split)])
            held.append(spread(both, m % 2))
        return held

    def to_owners(parts):
        held = []
        for m in range(micro):
            total = collect(parts[m], m % 2)
            mine = total[0]
            for j in range(1, split):
                mine = mine + turn(total[j].astype(BF16), split - j, split).astype(F32)
            held.append(mine)
        return jnp.stack(held)

    slots_per = 2 if n % 2 == 0 else 1
    batches = [list(range(g * slots_per, (g + 1) * slots_per)) for g in range(n // slots_per)]
    blocks_total = n * micro * split

    d_slots = to_experts(d_payload)
    buffers = None
    for g, batch in enumerate(batches):
        buffers = dispatch_grads(
            [d_slots[m][r] for r in batch for m in range(micro)],
            where, per, cap, model, buffers, g, blocks_total,
        )
    grads_in, ranks = buffers

    rows = micro * count
    x = tokens.reshape(rows, model).astype(F32)
    inverse_one = lax.rsqrt(jnp.mean(x * x, axis=-1, keepdims=True) + 1e-05)
    normed = (x * inverse_one * gain_one).astype(BF16)
    cosine, sine = rope_tables(me, PR_DEV * n)
    heads_rope = QUERY_HEADS + KEY_VALUE_HEADS
    cosine = jnp.tile(jnp.concatenate([cosine, cosine], axis=1), (micro, heads_rope))
    sine = jnp.tile(jnp.concatenate([-sine, sine], axis=1), (micro, heads_rope))
    cosine, sine = lax.optimization_barrier((cosine, sine))
    project = mm(normed, qkv_full)
    roped = rotate(project[:, : query_width + kv_width], cosine, sine).astype(BF16)
    query = roped[:, :query_width]
    key_value = jnp.concatenate(
        [roped[:, query_width:], project[:, query_width + kv_width :].astype(BF16)], axis=1
    ).reshape(micro, count, 2 * kv_width)
    query = query.reshape(micro, count, query_width)
    kv_slots = [spread(key_value[m], m % 2) for m in range(micro)]
    mixed = jnp.concatenate(
        [attention_forward(query[m], kv_slots[m], where) for m in range(micro)], axis=0
    )
    hidden = x + mm(mixed, out_full)
    inverse_two = lax.rsqrt(jnp.mean(hidden * hidden, axis=-1, keepdims=True) + 1e-05)
    normed_two = (hidden * inverse_two * gain_two).astype(BF16)
    logits = mm(normed_two, router_full)
    chosen = named.reshape(rows, experts)
    logits = jnp.where(chosen, logits, NEG_FILL)
    top = jnp.max(logits, axis=-1, keepdims=True)
    raised = jnp.where(chosen, jnp.exp(logits - top), 0.0)
    gate_probs = raised / jnp.sum(raised, axis=-1, keepdims=True)

    high = gate_probs.astype(BF16)
    low = (gate_probs - high.astype(F32)).astype(BF16)
    payload = jnp.concatenate(
        [normed_two, high, low, jnp.zeros((rows, LANES - 2 * experts), BF16)], axis=1
    ).reshape(micro, count, model + LANES)
    x_slots = to_experts(payload)
    buffers = None
    for g, batch in enumerate(batches):
        buffers = dispatch_rows(
            [x_slots[m][r] for r in batch for m in range(micro)],
            ranks, where, per, cap, model, experts, buffers, g, blocks_total,
        )
    rows_in, row_weights = buffers
    tile = slots_per * micro * split * cap
    outs, backs, weight_terms = [], [], []
    for k in range(per):
        out_rows, back_rows, terms = run_expert(
            k, where, rows_in, grads_in, row_weights, *weights_held[k], experts, tile, groups, aligned
        )
        outs.append(out_rows)
        backs.append(back_rows)
        weight_terms.append(terms)

    def returned(row_arrays):
        parts = [[None] * n for _ in range(micro)]
        for g in reversed(range(len(batches))):
            got = combine(
                row_arrays, ranks, len(batches[g]) * micro, split, count, cap, g
            )
            for i, (r, m) in enumerate((r, m) for r in batches[g] for m in range(micro)):
                parts[m][r] = got[i]
        return to_owners(parts)

    back = returned(backs).reshape(rows, model + LANES)
    mixture = returned(outs).reshape(rows, model)
    block_out = (hidden + mixture).astype(BF16).reshape(tokens.shape)

    expert_grads = []
    for which in range(3):
        per_class = []
        for k in range(per):
            if not aligned:
                axis = 1 if which == 2 else 0
                per_class.append(
                    [lax.psum_scatter(weight_terms[k][which], "group", scatter_dimension=axis, tiled=True).astype(F32)]
                )
                continue
            sums = [None] * split
            for s in range(groups):
                term = weight_terms[k][which * groups + s]
                term = (shift(term, s) if s else term).astype(F32)
                c = s % split
                sums[c] = term if sums[c] is None else sums[c] + term
            per_class.append(
                [lax.select_n((z - p) % split, *sums) if split > 1 else sums[0] for p in range(split)]
            )
        expert_grads.append(
            jnp.stack([per_class[k][p] for p in range(split) for k in range(per)])
        )

    d_out = cotangent.reshape(rows, model).astype(F32)
    d_gates = back[:, model : model + experts] + back[:, model + experts : model + 2 * experts]
    d_logits = gate_probs * (d_gates - jnp.sum(gate_probs * d_gates, axis=-1, keepdims=True))
    router_grad = lax.dot_general(normed_two.astype(F32), d_logits, TN, precision=HIGHEST)
    d_normed_two = back[:, :model] + lax.dot_general(
        d_logits, router_full.astype(F32), NT, precision=HIGHEST
    )

    def rms_back(inputs, inverse, gain, upstream):
        scaled = gain * upstream
        return inverse * scaled - inputs * inverse * inverse * inverse * jnp.mean(
            scaled * inputs, axis=-1, keepdims=True
        )

    grad_two = jnp.sum(d_normed_two * hidden * inverse_two, axis=0)
    d_hidden = d_out + rms_back(hidden, inverse_two, gain_two, d_normed_two)
    d_attn = d_hidden.astype(BF16)
    d_mixed = mm(d_attn, out_full, NT).astype(BF16).reshape(micro, count, query_width)
    d_query, kv_terms = [], []
    for m in range(micro):
        got, terms = attention_backward(query[m], kv_slots[m], d_mixed[m], where)
        d_query.append(got)
        kv_terms.append(terms)
    d_query = jnp.concatenate(d_query, axis=0)
    q_cos, q_sin = cosine[:, :query_width], sine[:, :query_width]
    d_query_low = rotate(d_query, q_cos, -q_sin).astype(BF16)
    d_kv = jnp.concatenate([collect(kv_terms[m], m % 2) for m in range(micro)], axis=0)
    d_key_low = rotate(d_kv[:, :kv_width], q_cos[:, :kv_width], -q_sin[:, :kv_width]).astype(BF16)
    d_kv_low = jnp.concatenate([d_key_low, d_kv[:, kv_width:].astype(BF16)], axis=1)
    d_normed = mm(d_query_low, qkv_full[:, :query_width], NT) + mm(
        d_kv_low, qkv_full[:, query_width:], NT
    )
    grad_one = jnp.sum(d_normed * x * inverse_one, axis=0)
    input_grad = (d_hidden + rms_back(x, inverse_one, gain_one, d_normed)).reshape(tokens.shape)
    misc_grad = jnp.concatenate(
        [
            grad_one[:, None],
            grad_two[:, None],
            jnp.zeros((model, experts - 2), F32),
            router_grad,
            jnp.zeros((model, LANES - 2 * experts), F32),
        ],
        axis=1,
    )
    if aligned:
        grad_out = reduce_dense(sliced_outer(mixed, d_attn, None, groups, n, where), 0, where)
        grad_q = reduce_dense(sliced_outer(normed, d_query_low, None, groups, n, where), 1, where)
        grad_rest = reduce_dense(
            sliced_outer(normed, d_kv_low, misc_grad, groups, n, where), 0, where
        )
    else:

        def whole(value):
            low = lax.psum_scatter(value.astype(BF16), "group", scatter_dimension=0, tiled=True)
            return lax.psum(low, "expert").astype(F32)

        grad_out = whole(mm(mixed, d_attn, TN))
        grad_q = whole(mm(normed, d_query_low, TN))
        grad_rest = whole(jnp.concatenate([mm(normed, d_kv_low, TN), misc_grad], axis=1))
    grad_qkv = jnp.concatenate([grad_q, grad_rest[:, : 2 * kv_width]], axis=1)
    misc_sum = grad_rest[:, 2 * kv_width :]
    return (
        block_out,
        input_grad,
        misc_sum[:, 0],
        grad_qkv,
        grad_out,
        misc_sum[:, 1],
        misc_sum[:, experts : 2 * experts],
        *expert_grads,
    )


def flip(e, r):
    for bit in (1, 2, 4):
        if r & bit:
            e = e + bit - 2 * bit * lax.rem(e // bit, 2)
    return e


def partner(z):
    return z + 1 - 2 * lax.rem(z, 2)


def remote(src, dst, send, recv, device):
    return pltpu.make_async_remote_copy(
        src_ref=src,
        dst_ref=dst,
        send_sem=send,
        recv_sem=recv,
        device_id=device,
        device_id_type=pl.DeviceIdType.MESH,
    )


def greet(devices):
    barrier = pltpu.get_barrier_semaphore()
    for device in devices:
        pl.semaphore_signal(barrier, inc=1, device_id=device, device_id_type=pl.DeviceIdType.MESH)
    pl.semaphore_wait(barrier, len(devices))


def plane_devices(e):
    return [{"expert": flip(e, bit)} for bit in (1, 2, 4)]


class Gather:
    def __init__(self, e, own, loc, paths, send, recv):
        self.e, self.own, self.loc, self.paths, self.send, self.recv = e, own, loc, paths, send, recv

    def copy(self, r, bit, c):
        q = r ^ bit
        src = self.own(c) if r == 0 else self.loc(r, r, c)
        return remote(
            src, self.loc(r, q, c), self.send.at[q, c], self.recv.at[q, c],
            {"expert": flip(self.e, bit)},
        )

    def begin(self, c):
        for bit in (2, 4, 1):
            self.copy(0, bit, c).start()

    def arrived(self, q, c):
        here = self.loc(q, q, c)
        remote(
            here, here, self.send.at[q, c], self.recv.at[q, c], {"expert": flip(self.e, 1)}
        ).wait_recv()

    def pass_on(self, q, c):
        if q == 2 and self.paths[c] == 0:
            self.copy(2, 4, c).start()
        if q == 4 and self.paths[c] == 1:
            self.copy(4, 2, c).start()
        if q in (2, 4, 6):
            self.copy(q, 1, c).start()

    def finish(self, c):
        for bit in (2, 4, 1):
            self.copy(0, bit, c).wait_send()
        if self.paths[c] == 0:
            self.copy(2, 4, c).wait_send()
        else:
            self.copy(4, 2, c).wait_send()
        for q in (2, 4, 6):
            self.copy(q, 1, c).wait_send()

    def stage(self, chunks, slots):
        for c in chunks:
            for q in slots:
                self.arrived(q, c)
                self.pass_on(q, c)

    def forward_all(self, chunks, use=None):
        for c in chunks:
            for q in (2, 4):
                self.arrived(q, c)
                self.pass_on(q, c)
        if use:
            for c in chunks:
                self.arrived(1, c)
                use(1, c)
                use(2, c)
                use(4, c)
        for c in chunks:
            self.arrived(6, c)
            self.pass_on(6, c)
            if use:
                use(6, c)
        for c in chunks:
            for q in (3, 5, 7) if use else (1, 3, 5, 7):
                self.arrived(q, c)
                if use:
                    use(q, c)


def add_rows(dst, sources, step=16):
    rows = sources[0].shape[0]

    def one(i, carry):
        at = pl.ds(pl.multiple_of(i * step, step), step)
        total = sources[0][at, :].astype(F32)
        for source in sources[1:]:
            total = total + source[at, :].astype(F32)
        dst[at, :] = total.astype(dst.dtype)
        return carry

    lax.fori_loop(0, rows // step, one, 0)


class Reduce:
    def __init__(self, e, part, paths, core, diag, near, acc, send, recv):
        self.e, self.part, self.paths = e, part, paths
        self.core, self.diag, self.near, self.acc = core, diag, near, acc
        self.send, self.recv = send, recv

    def core_copy(self, h, c):
        return remote(
            self.part(2 * h + 1, c), self.core.at[h, c], self.send.at[h, c], self.recv.at[h, c],
            {"expert": flip(self.e, 1)},
        )

    def diag_copy(self, c):
        return remote(
            self.acc.at[2, c], self.diag.at[c], self.send.at[4, c], self.recv.at[4, c],
            {"expert": flip(self.e, 4 if self.paths[c] == 0 else 2)},
        )

    def near_copy(self, i, c):
        return remote(
            self.acc.at[i, c], self.near.at[i, c], self.send.at[5 + i, c], self.recv.at[5 + i, c],
            {"expert": flip(self.e, 2 if i == 0 else 4)},
        )

    def begin(self, r, c):
        self.core_copy(r // 2, c).start()

    def diagonal(self, chunks):
        for c in chunks:
            self.core_copy(3, c).wait_recv()
            add_rows(self.acc.at[2, c], [self.part(6, c), self.core.at[3, c]])
            self.diag_copy(c).start()

    def sides(self, chunks):
        for c in chunks:
            for i in (0, 1) if self.paths[c] == 1 else (1, 0):
                self.core_copy(1 + i, c).wait_recv()
                terms = [self.part(2 + 2 * i, c), self.core.at[1 + i, c]]
                if self.paths[c] == i:
                    self.diag_copy(c).wait_recv()
                    terms.append(self.diag.at[c])
                add_rows(self.acc.at[i, c], terms)
                self.near_copy(i, c).start()

    def total(self, c):
        self.core_copy(0, c).wait_recv()
        self.near_copy(0, c).wait_recv()
        self.near_copy(1, c).wait_recv()
        return [self.part(0, c), self.core.at[0, c], self.near.at[0, c], self.near.at[1, c]]

    def finish(self, c):
        for h in range(4):
            self.core_copy(h, c).wait_send()
        self.diag_copy(c).wait_send()
        for i in range(2):
            self.near_copy(i, c).wait_send()


def reduce_scratch(count, rows, width):
    return [
        pltpu.VMEM((4, count, rows, width), BF16),
        pltpu.VMEM((count, rows, width), BF16),
        pltpu.VMEM((2, count, rows, width), BF16),
        pltpu.VMEM((3, count, rows, width), BF16),
        pltpu.SemaphoreType.DMA((7, count)),
        pltpu.SemaphoreType.DMA((7, count)),
    ]


def params(identity, vmem=62):
    return pltpu.CompilerParams(
        collective_id=identity, has_side_effects=True, vmem_limit_bytes=vmem * 1024 * 1024
    )


def plane_weights(shares, bank, per):
    n, split = 8, 2
    groups = lax.axis_size("group")
    rows = shares[0].shape[0]
    kinds = len(shares)
    count = groups * kinds

    def kernel(*refs):
        ins, bank_ref, refs = refs[:kinds], refs[kinds], refs[kinds + 1 :]
        outs, far_ref, refs = refs[:kinds], refs[kinds], refs[kinds + 1 :]
        z_send, z_recv, send, recv, local, b_send, b_recv = refs
        e, z = lax.axis_index("expert"), lax.axis_index("group")

        def loc(r, q, c):
            s, kind = c // kinds, c % kinds
            row = (lax.rem(z - s + groups, groups) * n + flip(e, r)) * rows
            return outs[kind].at[pl.ds(pl.multiple_of(row, 16), rows), :]

        def far(c):
            s, kind = c // kinds, c % kinds
            return remote(
                ins[kind], loc(0, 0, kind), z_send.at[c], z_recv.at[c],
                {"group": lax.rem(z + s, groups)},
            )

        def landed(c):
            remote(
                loc(0, 0, c), loc(0, 0, c), z_send.at[c], z_recv.at[c],
                {"group": lax.rem(z + c // kinds, groups)},
            ).wait_recv()

        first = lax.rem(z + 1, split) * per
        follow = remote(
            bank_ref.at[pl.ds(first, per)], far_ref, b_send, b_recv, {"group": lax.rem(z + 1, groups)}
        )
        gather = Gather(
            e, lambda c: ins[c] if c < kinds else loc(0, 0, c), loc,
            [c // kinds % 2 for c in range(count)], send, recv,
        )
        near = list(range(kinds))
        later = list(range(kinds, count))
        greet(
            plane_devices(e) + [{"group": lax.rem(z + s, groups)} for s in range(1, groups)]
        )
        for c in later:
            far(c).start()
        for c in near:
            gather.begin(c)
            pltpu.make_async_copy(ins[c], loc(0, 0, c), local.at[c]).start()
        follow.start()
        gather.stage(near, (2, 4))
        gather.stage(near, (6,))
        for c in later:
            landed(c)
            gather.begin(c)
        gather.stage(later, (2, 4))
        gather.stage(later, (6,))
        gather.stage(near + later, (1, 3, 5, 7))
        for c in later:
            far(c).wait_send()
        for c in near + later:
            gather.finish(c)
        for c in near:
            pltpu.make_async_copy(ins[c], loc(0, 0, c), local.at[c]).wait()
        follow.wait()

    vmem = pl.BlockSpec(memory_space=pltpu.VMEM)
    shapes = [(groups * n * rows, one.shape[1]) for one in shares]
    return pl.pallas_call(
        kernel,
        in_specs=[vmem] * kinds + [ANY_SPEC],
        out_specs=[vmem] * kinds + [ANY_SPEC],
        out_shape=[jax.ShapeDtypeStruct(shape, BF16) for shape in shapes]
        + [jax.ShapeDtypeStruct((per,) + bank.shape[1:], BF16)],
        scratch_shapes=[
            pltpu.SemaphoreType.DMA((count,)),
            pltpu.SemaphoreType.DMA((count,)),
            pltpu.SemaphoreType.DMA((n, count)),
            pltpu.SemaphoreType.DMA((n, count)),
            pltpu.SemaphoreType.DMA((kinds,)),
            pltpu.SemaphoreType.DMA,
            pltpu.SemaphoreType.DMA,
        ],
        compiler_params=params(1),
        cost_estimate=cost(1e9, 1e6),
        name="plane_weights",
    )(*shares, bank)


def attention_pairs(n, at_me, q_ref, keys, out_ref):
    width = KEY_VALUE_HEADS * HEAD_SIZE
    prompt_ok, cont_ok = attention_masks_plain(n, at_me)

    def pair(j, carry):
        q_at = pl.ds(pl.multiple_of(j * 384, 128), 384)
        k_at = pl.ds(pl.multiple_of(j * 128, 128), 128)
        v_at = pl.ds(pl.multiple_of(width + j * 128, 128), 128)
        q_top, q_low = q_ref[:PR_DEV, q_at], q_ref[PR_DEV:, q_at]
        k_two, v_two = keys[:, k_at], keys[:, v_at]
        tops, lows = [], []
        for g in range(2):
            key = k_two[:, g * HEAD_SIZE : (g + 1) * HEAD_SIZE]
            value = v_two[:, g * HEAD_SIZE : (g + 1) * HEAD_SIZE]
            top, low = group_probs(
                head_rows(q_top, g * 192), head_rows(q_low, g * 192), key, prompt_ok, cont_ok, n
            )
            tops.append(row_heads(mm(top.astype(BF16), value[: n * PR_DEV])))
            lows.append(row_heads(mm(low.astype(BF16), value)))
        out_ref[:PR_DEV, q_at] = jnp.concatenate(tops, axis=1).astype(BF16)
        out_ref[PR_DEV:, q_at] = jnp.concatenate(lows, axis=1).astype(BF16)
        return carry

    lax.fori_loop(0, KEY_VALUE_HEADS // 2, pair, 0)


def flip_columns(slot, me, limit):
    bit, total = 1, jnp.zeros_like(slot)
    while bit < limit:
        total = total + bit * lax.rem(slot // bit + me // bit, 2)
        bit *= 2
    return total


def attention_masks_plain(n, me):
    shape = (3 * PR_DEV, n * PR_DEV)
    token = lax.rem(lax.broadcasted_iota(jnp.int32, shape, 0), PR_DEV)
    column = lax.broadcasted_iota(jnp.int32, shape, 1)
    owner = flip_columns(column // PR_DEV, me, n)
    prompt_ok = owner * PR_DEV + lax.rem(column, PR_DEV) <= me * PR_DEV + token
    slots = CONT // PR_DEV
    shape = (3 * PR_DEV, CONT)
    token = lax.rem(lax.broadcasted_iota(jnp.int32, shape, 0), PR_DEV)
    column = lax.broadcasted_iota(jnp.int32, shape, 1)
    local = lax.rem(me, slots)
    owner = flip_columns(column // PR_DEV, local, slots)
    cont_ok = owner * PR_DEV + lax.rem(column, PR_DEV) <= local * PR_DEV + token
    return prompt_ok, cont_ok


def turn_heads(x, cosine, sine):
    half = HEAD_SIZE // 2
    lane = lax.broadcasted_iota(jnp.int32, cosine.shape, 1)
    first = lax.rem(lane, HEAD_SIZE) < half
    blocks = []
    for lo in range(0, x.shape[1], LANES):
        one = x[:, lo : lo + LANES]
        other = jnp.where(first, pltpu.roll(one, LANES - half, 1), pltpu.roll(one, half, 1))
        blocks.append(one * cosine + other * sine)
    return jnp.concatenate(blocks, axis=1)


def plane_attention(normed, weight, cosine, sine, micro):
    rows, model = normed.shape
    tokens = rows // micro
    width = 2 * KEY_VALUE_HEADS * HEAD_SIZE
    query_width = QUERY_HEADS * HEAD_SIZE
    n, tile = 8, 512

    def kernel(x_ref, w_ref, cos_ref, sin_ref, out_ref, q_ref, slots, own, keys, send, recv, local):
        e = lax.axis_index("expert")
        gather = Gather(
            e, lambda c: own.at[c], lambda r, q, c: slots.at[q, c], [c % 2 for c in range(micro)],
            send, recv,
        )

        def project(lo, turned):
            wide = mm(x_ref[...], w_ref[:, lo : lo + tile])
            for c in range(micro):
                part = wide[c * tokens : (c + 1) * tokens]
                if turned:
                    part = turn_heads(part, cos_ref[...], sin_ref[...])
                yield c, part.astype(BF16)

        for lo in range(0, width, tile):
            for c, part in project(query_width + lo, lo < width // 2):
                own[c, :, lo : lo + tile] = part
        greet(plane_devices(e))
        for c in range(micro):
            gather.begin(c)
            pltpu.make_async_copy(own.at[c], slots.at[0, c], local.at[c]).start()
        for lo in range(0, query_width, tile):
            for c, part in project(lo, True):
                q_ref[c, :, lo : lo + tile] = part
        gather.stage(range(micro), (2, 4))
        gather.stage(range(micro), (6,))
        for c in range(micro):
            gather.stage([c], (1, 3, 5, 7))
            pltpu.make_async_copy(own.at[c], slots.at[0, c], local.at[c]).wait()
            load_keys(n, [slots.at[r, c] for r in range(n)], keys)
            attention_pairs(n, e, q_ref.at[c], keys, out_ref.at[c])
        for c in range(micro):
            gather.finish(c)

    vmem = pl.BlockSpec(memory_space=pltpu.VMEM)
    shape = jax.ShapeDtypeStruct((micro, tokens, query_width), BF16)
    return pl.pallas_call(
        kernel,
        in_specs=[vmem] * 4,
        out_specs=[vmem] * 3,
        out_shape=[shape, shape, jax.ShapeDtypeStruct((n, micro, tokens, width), BF16)],
        scratch_shapes=[
            pltpu.VMEM((micro, tokens, width), BF16),
            pltpu.VMEM((n * PR_DEV + CONT, width), BF16),
            pltpu.SemaphoreType.DMA((n, micro)),
            pltpu.SemaphoreType.DMA((n, micro)),
            pltpu.SemaphoreType.DMA((micro,)),
        ],
        compiler_params=params(2),
        cost_estimate=cost(1e9, 1e6),
        name="plane_attention",
    )(normed, weight, cosine, sine)


def plane_attention_backward(query, slots, d_mixed, cosine, sine):
    n, micro, tokens, width = slots.shape
    half = width // 2
    query_width = query.shape[2]
    pr = n * PR_DEV
    total = pr + CONT

    def kernel(q_ref, d_ref, kv_ref, cos_ref, sin_ref, out_ref, keys, grads, parts, *scratch):
        e = lax.axis_index("expert")
        red = Reduce(e, lambda r, c: parts.at[r, c], [c % 2 for c in range(micro)], *scratch)
        greet(plane_devices(e))
        prompt_ok, cont_ok = attention_masks_plain(n, e)

        def one_side(prob, d_rows, key, value, q_rows):
            d_prob = mm(d_rows, value, NT)
            delta = jnp.sum(prob * d_prob, axis=1, keepdims=True)
            d_score = (prob * (d_prob - delta)).astype(BF16)
            return (
                mm(d_score, key) * SCORE_SCALE,
                mm(d_score, q_rows, TN) * SCORE_SCALE,
                mm(prob.astype(BF16), d_rows, TN),
            )

        for c in range(micro):
            load_keys(n, [kv_ref.at[r, c] for r in range(n)], keys)

            def pair(j, carry):
                q_at = pl.ds(pl.multiple_of(j * 384, 128), 384)
                k_at = pl.ds(pl.multiple_of(j * 128, 128), 128)
                v_at = pl.ds(pl.multiple_of(half + j * 128, 128), 128)
                q_top, q_low = q_ref[c, :PR_DEV, q_at], q_ref[c, PR_DEV:, q_at]
                d_top, d_low = d_ref[c, :PR_DEV, q_at], d_ref[c, PR_DEV:, q_at]
                k_two, v_two = keys[:, k_at], keys[:, v_at]
                dq_tops, dq_lows, dks, dvs = [], [], [], []
                for g in range(2):
                    key = k_two[:, g * HEAD_SIZE : (g + 1) * HEAD_SIZE]
                    value = v_two[:, g * HEAD_SIZE : (g + 1) * HEAD_SIZE]
                    rows_top, rows_low = head_rows(q_top, g * 192), head_rows(q_low, g * 192)
                    top, low = group_probs(rows_top, rows_low, key, prompt_ok, cont_ok, n)
                    dq_top, dk_top, dv_top = one_side(
                        top, head_rows(d_top, g * 192), key[:pr], value[:pr], rows_top
                    )
                    dq_low, dk_low, dv_low = one_side(
                        low, head_rows(d_low, g * 192), key, value, rows_low
                    )
                    dq_tops.append(row_heads(dq_top))
                    dq_lows.append(row_heads(dq_low))
                    dks.append(jnp.concatenate([dk_low[:pr] + dk_top, dk_low[pr:]], axis=0))
                    dvs.append(jnp.concatenate([dv_low[:pr] + dv_top, dv_low[pr:]], axis=0))
                for lo, found in ((0, dq_tops), (PR_DEV, dq_lows)):
                    there = slice(lo, lo + PR_DEV)
                    turned = turn_heads(
                        jnp.concatenate(found, axis=1), cos_ref[there, :], sin_ref[there, :]
                    )
                    out_ref[c, there, q_at] = turned.astype(BF16)
                grads[:, k_at] = jnp.concatenate(dks, axis=1).astype(BF16)
                grads[:, v_at] = jnp.concatenate(dvs, axis=1).astype(BF16)
                return carry

            lax.fori_loop(0, KEY_VALUE_HEADS // 2, pair, 0)
            for r in (7, 5, 3, 1, 6, 2, 4, 0):
                parts[r, c, :PR_DEV, :] = grads[r * PR_DEV : (r + 1) * PR_DEV, :]
                if r < CONT // PR_DEV:
                    lo = (n + r) * PR_DEV
                    parts[r, c, PR_DEV:, :] = grads[lo : lo + PR_DEV, :]
                else:
                    parts[r, c, PR_DEV:, :] = jnp.zeros((PR_DEV, width), BF16)
                if r % 2:
                    red.begin(r, c)
        red.diagonal(range(micro))
        red.sides(range(micro))
        step = 16
        for c in range(micro):
            terms = red.total(c)

            def last(i, carry):
                at = pl.ds(pl.multiple_of(i * step, step), step)
                total = terms[0][at, :].astype(F32)
                for term in terms[1:]:
                    total = total + term[at, :].astype(F32)
                turned = turn_heads(total[:, :half], cos_ref[at, :], sin_ref[at, :])
                out_ref[c, at, query_width : query_width + half] = turned.astype(BF16)
                out_ref[c, at, query_width + half :] = total[:, half:].astype(BF16)
                return carry

            lax.fori_loop(0, tokens // step, last, 0)
        for c in range(micro):
            red.finish(c)

    vmem = pl.BlockSpec(memory_space=pltpu.VMEM)
    return pl.pallas_call(
        kernel,
        in_specs=[vmem] * 5,
        out_specs=vmem,
        out_shape=jax.ShapeDtypeStruct((micro, tokens, query_width + width), BF16),
        scratch_shapes=[
            pltpu.VMEM((total, width), BF16),
            pltpu.VMEM((total, width), BF16),
            pltpu.VMEM((n, micro, tokens, width), BF16),
        ]
        + reduce_scratch(micro, tokens, width),
        compiler_params=params(3),
        cost_estimate=cost(1e9, 1e6),
        name="plane_attention_backward",
    )(query, d_mixed, slots, cosine, sine)


def plane_dispatch(payload, ranks, bank, where, per, cap, model, experts):
    micro, tokens, width = payload.shape
    n, split = 8, 2
    groups = lax.axis_size("group")
    count = split * micro

    def kernel(
        at_ref, own_ref, rank_ref, bank_ref, out, weights, far_ref,
        slots, z_send, z_recv, send, recv, b_send, b_recv,
    ):
        e, z = lax.axis_index("expert"), lax.axis_index("group")
        lane = lax.broadcasted_iota(jnp.int32, (cap, LANES), 1)

        def own(c):
            return own_ref.at[c] if c < micro else slots.at[0, c]

        gather = Gather(
            e, own, lambda r, q, c: slots.at[q, c], [c % 2 for c in range(count)], send, recv
        )

        def turned(m):
            return remote(
                own_ref.at[m], slots.at[0, micro + m], z_send.at[m], z_recv.at[m],
                {"group": partner(z)},
            )

        def use(r, c):
            rows = own(c)[...] if r == 0 else slots[r, c]
            b = r * count + c
            for k in range(per):
                got = mm(pick(rank_ref[b, k : k + 1, :], cap), rows)
                out[k, b * cap : (b + 1) * cap, :] = got[:, :model].astype(BF16)
                first = at_ref[2] + k
                mine = (lane == first) | (lane == first + experts)
                total = jnp.sum(jnp.where(mine, got[:, model:], 0.0), axis=1, keepdims=True)
                weights[k, b * cap : (b + 1) * cap, :] = jnp.broadcast_to(total, (cap, LANES))

        last = groups - 1
        first = lax.rem(z + last, split) * per
        follow = remote(
            bank_ref.at[pl.ds(first, per)], far_ref, b_send, b_recv,
            {"group": lax.rem(z + last, groups)},
        )
        greet(plane_devices(e) + [{"group": lax.rem(z + s, groups)} for s in (1, last)])
        for m in range(micro):
            turned(m).start()
        follow.start()
        for m in range(micro):
            gather.begin(m)
        for m in range(micro):
            use(0, m)
        for m in range(micro):
            turned(m).wait_recv()
            gather.begin(micro + m)
            use(0, micro + m)
        gather.forward_all(range(count), use)
        for m in range(micro):
            turned(m).wait_send()
        for c in range(count):
            gather.finish(c)
        follow.wait()

    vmem = pl.BlockSpec(memory_space=pltpu.VMEM)
    total = n * count * cap
    return pl.pallas_call(
        kernel,
        in_specs=[SMEM_SPEC, vmem, vmem, ANY_SPEC],
        out_specs=[vmem, vmem, ANY_SPEC],
        out_shape=[
            jax.ShapeDtypeStruct((per, total, model), BF16),
            jax.ShapeDtypeStruct((per, total, LANES), F32),
            jax.ShapeDtypeStruct((per,) + bank.shape[1:], BF16),
        ],
        scratch_shapes=[
            pltpu.VMEM((n, count, tokens, width), BF16),
            pltpu.SemaphoreType.DMA((micro,)),
            pltpu.SemaphoreType.DMA((micro,)),
            pltpu.SemaphoreType.DMA((n, count)),
            pltpu.SemaphoreType.DMA((n, count)),
            pltpu.SemaphoreType.DMA,
            pltpu.SemaphoreType.DMA,
        ],
        compiler_params=params(4),
        cost_estimate=cost(1e9, 1e6),
        name="plane_dispatch",
    )(where, payload, ranks, bank)


def plane_return(rows, ranks, term, micro, tokens, cap):
    per, _, width = rows.shape
    n, split = 8, 2
    groups = lax.axis_size("group")
    count = split * micro
    chunks = list(range(micro, count)) + list(range(micro))

    def kernel(rank_ref, in_ref, term_ref, out, far_ref, *refs):
        parts, z_out, z_in, z_send, z_recv, t_send, t_recv, scratch = *refs[:7], refs[7:]
        e, z = lax.axis_index("expert"), lax.axis_index("group")
        red = Reduce(e, lambda r, c: parts.at[r, c], [c % 2 for c in range(count)], *scratch)

        def produce(r, c):
            b = r * count + c
            total = None
            for k in range(per):
                one = mm(
                    pick(rank_ref[b, k : k + 1, :], cap), in_ref[k, b * cap : (b + 1) * cap, :], TN
                )
                total = one if total is None else total + one
            parts[r, c] = total.astype(BF16)

        def turned(m):
            return remote(
                z_out.at[m], z_in.at[m], z_send.at[m], z_recv.at[m], {"group": partner(z)}
            )

        follow = remote(term_ref, far_ref, t_send, t_recv, {"group": lax.rem(z + 1, groups)})
        greet(plane_devices(e) + [{"group": lax.rem(z + s, groups)} for s in (1, groups - 1)])
        follow.start()
        for r in (7, 3, 5):
            for c in chunks:
                produce(r, c)
                red.begin(r, c)
        for c in chunks:
            produce(6, c)
        red.diagonal(chunks)
        for r in (2, 4):
            for c in chunks:
                produce(r, c)
        red.sides(chunks)
        for c in chunks:
            produce(1, c)
            red.begin(1, c)
        for c in chunks:
            produce(0, c)
        for c in chunks:
            terms = red.total(c)
            if c >= micro:
                add_rows(z_out.at[c - micro], terms)
                turned(c - micro).start()
            else:
                turned(c).wait_recv()
                add_rows(out.at[c], terms + [z_in.at[c]])
        for m in range(micro):
            turned(m).wait_send()
        for c in chunks:
            red.finish(c)
        follow.wait()

    vmem = pl.BlockSpec(memory_space=pltpu.VMEM)
    return pl.pallas_call(
        kernel,
        in_specs=[vmem, vmem, ANY_SPEC],
        out_specs=[vmem, ANY_SPEC],
        out_shape=[
            jax.ShapeDtypeStruct((micro, tokens, width), F32),
            jax.ShapeDtypeStruct(term.shape, BF16),
        ],
        scratch_shapes=[
            pltpu.VMEM((n, count, tokens, width), BF16),
            pltpu.VMEM((micro, tokens, width), BF16),
            pltpu.VMEM((micro, tokens, width), BF16),
            pltpu.SemaphoreType.DMA((micro,)),
            pltpu.SemaphoreType.DMA((micro,)),
            pltpu.SemaphoreType.DMA,
            pltpu.SemaphoreType.DMA,
        ]
        + reduce_scratch(count, tokens, width),
        compiler_params=params(5),
        cost_estimate=cost(1e9, 1e6),
        name="plane_return",
    )(ranks, rows, term)


def plane_gradients(products, router, gains, term, groups):
    n = 8
    depth = products[0][0].shape[1]
    widths = [b.shape[1] for a, b in products]
    width = sum(widths) + LANES
    experts = router.shape[1]
    rows = depth // (groups * n)
    tile = 512
    flat = [x for pair in products for x in pair]

    def kernel(*refs):
        ins, refs = refs[: len(flat)], refs[len(flat) :]
        router_ref, gains_ref, term_ref, out, far_ref, *refs = refs
        wide, parts, z_out, z_in, z_send, z_recv, send, recv, t_send, t_recv = refs[:10]
        scratch = refs[10:]
        e, z = lax.axis_index("expert"), lax.axis_index("group")
        red = Reduce(e, lambda r, c: parts.at[r, c], [c % 2 for c in range(groups)], *scratch)
        greet(
            plane_devices(e)
            + [{"group": lax.rem(z + s, groups)} for s in range(1, groups)]
        )
        follow = remote(
            term_ref, far_ref, t_send, t_recv, {"group": lax.rem(z + groups - 1, groups)}
        )
        follow.start()

        def cut(lo, size):
            for r in range(n):
                for s in range(groups):
                    row = (lax.rem(z + s, groups) * n + flip(e, r)) * rows
                    at = pl.ds(pl.multiple_of(row, 16), rows)
                    parts[r, s, :, lo : lo + size] = wide[at, :size].astype(BF16)

        lo = 0
        for i, count in enumerate(widths):
            for start in range(0, count, tile):
                size = min(tile, count - start)
                wide[:, :size] = mm(ins[2 * i][...], ins[2 * i + 1][:, start : start + size], TN)
                cut(lo, size)
                lo += size
        wide[:, :LANES] = jnp.zeros((depth, LANES), F32)
        wide[:, experts : 2 * experts] = router_ref[...]
        wide[:, : gains.shape[0]] = gains_ref[...].T
        cut(lo, LANES)

        chunks = list(range(1, groups)) + [0]
        for r in (7, 3, 5, 1):
            for c in chunks:
                red.begin(r, c)
        red.diagonal(chunks)
        red.sides(chunks)

        def far(s):
            return remote(
                z_out.at[s], z_in.at[s], z_send.at[s], z_recv.at[s],
                {"group": lax.rem(z + s, groups)},
            )

        for c in chunks:
            add_rows(z_out.at[c], red.total(c))
            if c:
                far(c).start()
        for c in range(1, groups):
            far(c).wait_recv()
        def place(r):
            return out.at[pl.ds(pl.multiple_of(flip(e, r) * rows, 16), rows), :]

        add_rows(place(0), [z_out.at[0]] + [z_in.at[c] for c in range(1, groups)])
        middle = width // 2 // LANES * LANES
        spans = [(0, middle), (middle, width)]

        def loc(r, q, c):
            row = pl.multiple_of(flip(e, r) * rows, 16)
            return out.at[pl.ds(row, rows), spans[c][0] : spans[c][1]]

        gather = Gather(e, lambda c: loc(0, 0, c), loc, [0, 1], send, recv)
        for c in range(2):
            gather.begin(c)
        gather.forward_all(range(2))
        for c in range(2):
            gather.finish(c)
        follow.wait()
        for c in range(1, groups):
            far(c).wait_send()
        for c in chunks:
            red.finish(c)

    vmem = pl.BlockSpec(memory_space=pltpu.VMEM)
    return pl.pallas_call(
        kernel,
        in_specs=[vmem] * (len(flat) + 2) + [ANY_SPEC],
        out_specs=[vmem, ANY_SPEC],
        out_shape=[
            jax.ShapeDtypeStruct((n * rows, width), BF16),
            jax.ShapeDtypeStruct(term.shape, BF16),
        ],
        scratch_shapes=[
            pltpu.VMEM((depth, tile), F32),
            pltpu.VMEM((n, groups, rows, width), BF16),
            pltpu.VMEM((groups, rows, width), BF16),
            pltpu.VMEM((groups, rows, width), BF16),
            pltpu.SemaphoreType.DMA((groups,)),
            pltpu.SemaphoreType.DMA((groups,)),
            pltpu.SemaphoreType.DMA((n, 2)),
            pltpu.SemaphoreType.DMA((n, 2)),
            pltpu.SemaphoreType.DMA,
            pltpu.SemaphoreType.DMA,
        ]
        + reduce_scratch(groups, rows, width),
        compiler_params=params(6),
        cost_estimate=cost(1e9, 1e6),
        name="plane_gradients",
    )(*flat, router, gains, term)


def gather_flags(slots, where, per, cap, model):
    n, count, tokens, width = slots.shape

    def kernel(at_ref, in_ref, out, ranks, flags):
        row = lax.broadcasted_iota(jnp.int32, (tokens, tokens), 0)
        col = lax.broadcasted_iota(jnp.int32, (tokens, tokens), 1)
        before = jnp.where(row < col, 1.0, 0.0).astype(BF16)
        for b in range(count):
            payload = in_ref[0, b]
            flags[...] = payload[:, model:].astype(F32).T
            picked = jnp.concatenate(
                [flags[pl.ds(at_ref[2] + k, 1), :] for k in range(per)], axis=0
            )
            slot = jnp.where(picked > 0.0, mm(picked.astype(BF16), before), -1.0)
            ranks[b] = slot
            for k in range(per):
                out[k, b * cap : (b + 1) * cap, :] = mm(
                    pick(slot[k : k + 1], cap), payload[:, :model]
                ).astype(BF16)

    return pl.pallas_call(
        kernel,
        grid_spec=pltpu.PrefetchScalarGridSpec(
            num_scalar_prefetch=1,
            grid=(n,),
            in_specs=[
                pl.BlockSpec(
                    (1, count, tokens, width),
                    lambda r, at: (jnp.bitwise_xor(at[1], r), 0, 0, 0),
                )
            ],
            out_specs=[
                pl.BlockSpec((per, count * cap, model), lambda r, at: (0, r, 0)),
                pl.BlockSpec((count, per, tokens), lambda r, at: (r, 0, 0)),
            ],
            scratch_shapes=[pltpu.VMEM((LANES, tokens), F32)],
        ),
        out_shape=[
            jax.ShapeDtypeStruct((per, n * count * cap, model), BF16),
            jax.ShapeDtypeStruct((n * count, per, tokens), F32),
        ],
        cost_estimate=cost(5e9, 3e7),
        name="gather_flags",
    )(where, slots)


def scatter_rows(rows, ranks, where, n, count, tokens, cap):
    per, _, width = rows.shape

    def kernel(at_ref, rank_ref, in_ref, out):
        for b in range(count):
            total = None
            for k in range(per):
                one = mm(
                    pick(rank_ref[b, k : k + 1, :], cap), in_ref[k, b * cap : (b + 1) * cap, :], TN
                )
                total = one if total is None else total + one
            out[0, b] = total.astype(BF16)

    return pl.pallas_call(
        kernel,
        grid_spec=pltpu.PrefetchScalarGridSpec(
            num_scalar_prefetch=1,
            grid=(n,),
            in_specs=[
                pl.BlockSpec((count, per, tokens), lambda r, at: (r, 0, 0)),
                pl.BlockSpec((per, count * cap, width), lambda r, at: (0, r, 0)),
            ],
            out_specs=pl.BlockSpec(
                (1, count, tokens, width), lambda r, at: (jnp.bitwise_xor(at[1], r), 0, 0, 0)
            ),
        ),
        out_shape=jax.ShapeDtypeStruct((n, count, tokens, width), BF16),
        cost_estimate=cost(5e9, 3e7),
        name="scatter_rows",
    )(where, ranks, rows)


def expert_steps(at, rows_in, grads_in, weights, bank, far, experts, tile):
    per, total, model = rows_in.shape
    part, ff = bank.shape[2:]
    groups = model // part
    steps = total // tile

    def kernel(at_ref, x_ref, d_ref, w_ref, *refs):
        sources, o_ref, r_ref, refs = refs[:groups], refs[groups], refs[groups + 1], refs[groups + 2 :]
        outs, (acc_wide, acc_down, wide_all, down_all, sems) = refs[:groups], refs[groups:]
        k, step = pl.program_id(0), pl.program_id(1)

        def loads(index):
            copies = []
            for s in range(groups):
                z = lax.rem(at_ref[0] - s + groups, groups)
                at_z = pl.ds(pl.multiple_of(z * part, 128), part)
                source = sources[s].at[at_ref[3] + index if s == 0 else index]
                wide, down = wide_all.at[index], down_all.at[index]
                for i, dst in enumerate([wide.at[at_z, :ff], wide.at[at_z, ff:], down.at[at_z, :]]):
                    copies.append(
                        pltpu.make_async_copy(source.at[i], dst, sems.at[index, 3 * s + i])
                    )
            return copies

        for index in range(per):

            @pl.when((k == 0) & (step == 0))
            def _():
                for one in loads(index):
                    one.start()

        for index in range(per):

            @pl.when((k == index) & (step == 0))
            def _():
                for one in loads(index):
                    one.wait()

        wide_ref, down_ref = wide_all.at[k], down_all.at[k]
        x, d = x_ref[0], d_ref[0]
        w = w_ref[0, :, 0:1]
        pre = mm(x, wide_ref[...])
        gate_pre, up_pre = pre[:, :ff], pre[:, ff:]
        sig = 1.0 / (1.0 + jnp.exp(-gate_pre))
        silu = gate_pre * sig
        active_wide = silu * up_pre
        active = active_wide.astype(BF16)
        o_ref[0] = (mm(active, down_ref[...], NT) * w).astype(BF16)
        d_raw = mm(d, down_ref[...])
        d_gates = jnp.sum(active.astype(F32) * d_raw, axis=1, keepdims=True)
        d_active = d_raw * w
        d_up = (d_active * silu).astype(BF16)
        d_gate = (d_active * up_pre * sig * (1.0 + gate_pre * (1.0 - sig))).astype(BF16)
        d_both = jnp.concatenate([d_gate, d_up], axis=1)
        r_ref[0, :, :model] = mm(d_both, wide_ref[...], NT).astype(BF16)
        high = d_gates.astype(BF16).astype(F32)
        lane = lax.broadcasted_iota(jnp.int32, (tile, LANES), 1)
        e = at_ref[2] + k
        r_ref[0, :, model:] = (
            jnp.where(lane == e, high, 0.0) + jnp.where(lane == e + experts, d_gates - high, 0.0)
        ).astype(BF16)
        new_wide = mm(x, d_both, TN)
        new_down = mm((active_wide * w).astype(BF16), d, TN)

        @pl.when(step == 0)
        def _():
            acc_wide[...] = new_wide
            acc_down[...] = new_down

        @pl.when(step > 0)
        def _():
            acc_wide[...] += new_wide
            acc_down[...] += new_down

        @pl.when(step == steps - 1)
        def _():
            for s in range(groups):
                z = lax.rem(at_ref[0] + s, groups)
                at_z = pl.ds(pl.multiple_of(z * part, 128), part)
                outs[s][0, 0] = acc_wide[at_z, :ff].astype(BF16)
                outs[s][0, 1] = acc_wide[at_z, ff:].astype(BF16)
                outs[s][0, 2] = acc_down[:, at_z].T.astype(BF16)

    grad = pl.BlockSpec((1, 3, part, ff), lambda k, t: (k, 0, 0, 0), pipeline_mode=pl.Buffered(1))
    rows = lambda width: pl.BlockSpec((1, tile, width), lambda k, t: (k, t, 0))
    out = pl.pallas_call(
        kernel,
        grid=(per, steps),
        in_specs=[SMEM_SPEC, rows(model), rows(model), rows(LANES)] + [ANY_SPEC] * groups,
        out_specs=[rows(model), rows(model + LANES)] + [grad] * groups,
        out_shape=[
            jax.ShapeDtypeStruct((per, total, model), BF16),
            jax.ShapeDtypeStruct((per, total, model + LANES), BF16),
        ]
        + [jax.ShapeDtypeStruct((per, 3, part, ff), BF16)] * groups,
        scratch_shapes=[
            pltpu.VMEM((model, 2 * ff), F32),
            pltpu.VMEM((ff, model), F32),
            pltpu.VMEM((per, model, 2 * ff), BF16),
            pltpu.VMEM((per, model, ff), BF16),
            pltpu.SemaphoreType.DMA((per, 3 * groups)),
        ],
        compiler_params=pltpu.CompilerParams(vmem_limit_bytes=62 * 1024 * 1024),
        cost_estimate=cost(18 * per * total * model * ff, 10 * per * total * model),
        name="expert_steps",
    )(at, rows_in, grads_in, weights, bank, *far)
    return out[0], out[1], list(out[2:])


def merge_grads(which, at, terms):
    per, _, part, ff = terms[0].shape
    split = 2
    tile = LANES

    def kernel(at_ref, *refs):
        ins, out = refs[: len(terms)], refs[len(terms)]
        for k in range(per):
            for parity in range(split):
                value = None
                for one in ins[parity::split]:
                    more = one[k, 0].astype(F32)
                    value = more if value is None else value + more
                index = lax.rem(at_ref[0] + parity, split) * per + k
                out[index] = value.T if which == 2 else value

    if which == 2:
        spec = pl.BlockSpec((split * per, ff, tile), lambda t: (0, 0, t))
        shape = (split * per, ff, part)
    else:
        spec = pl.BlockSpec((split * per, tile, ff), lambda t: (0, t, 0))
        shape = (split * per, part, ff)
    return pl.pallas_call(
        kernel,
        grid=(part // tile,),
        in_specs=[SMEM_SPEC]
        + [pl.BlockSpec((per, 1, tile, ff), lambda t: (0, which, t, 0))] * len(terms),
        out_specs=spec,
        out_shape=jax.ShapeDtypeStruct(shape, F32),
        cost_estimate=cost(1e8, 6e6),
        name="merge_grads",
    )(at, *terms)


def layer_plane(
    tokens,
    cotangent,
    routes,
    norm_one,
    query_key_value_weight,
    out_weight,
    norm_two,
    router_weight,
    gate_weight,
    up_weight,
    down_weight,
):
    n = lax.axis_size("expert")
    groups = lax.axis_size("group")
    me = lax.axis_index("expert")
    z = lax.axis_index("group")
    micro, count, model = tokens.shape
    exp_here, part, ff = gate_weight.shape
    experts = router_weight.shape[1]
    split = 2
    per = exp_here // split
    query_width = QUERY_HEADS * HEAD_SIZE
    kv_width = KEY_VALUE_HEADS * HEAD_SIZE
    cap = max(2, 3 * TOPK * PR_DEV // experts)
    where = jnp.stack([z, me, me * exp_here + (z % split) * per, (z % split) * per]).astype(jnp.int32)
    rows_here = part // n
    rows = micro * count

    misc = jnp.concatenate(
        [
            norm_one[:, None],
            norm_two[:, None],
            jnp.zeros((part, experts - 2), BF16),
            router_weight,
            jnp.zeros((part, LANES - 2 * experts), BF16),
        ],
        axis=1,
    )
    cut = lambda x: lax.dynamic_slice_in_dim(x, me * rows_here, rows_here, axis=0)
    shares = [cut(query_key_value_weight), jnp.concatenate([cut(out_weight), cut(misc)], axis=1)]
    bank = jnp.stack([gate_weight, up_weight, jnp.swapaxes(down_weight, 1, 2)], axis=1)

    expert_ids = jnp.arange(experts, dtype=jnp.int32)
    named = jnp.any(routes[..., None] == expert_ids, axis=2)
    pad = jnp.zeros((micro, count, LANES - experts), BF16)
    d_payload = jnp.concatenate([cotangent, named.astype(BF16), pad], axis=2)
    d_turned = turn(d_payload, 1, split)

    bank_two = lax.dynamic_slice_in_dim(bank, (z % split) * per, per, axis=0)
    qkv_full, rest_full, far_one = plane_weights(shares, bank, per)
    (bank_two, d_payload, d_turned), qkv_full = lax.optimization_barrier(
        ((bank_two, d_payload, d_turned), qkv_full)
    )
    far_two = shift(bank_two, 2)
    both = jnp.concatenate([d_payload, d_turned], axis=0)
    d_slots = lax.all_gather(both, "expert", axis=0)
    out_full, misc_full = rest_full[:, :model], rest_full[:, model:]
    gain_one = misc_full[:, 0].astype(F32)
    gain_two = misc_full[:, 1].astype(F32)
    router_full = misc_full[:, experts : 2 * experts]

    grads_in, ranks = gather_flags(d_slots, where, per, cap, model)

    x = tokens.reshape(rows, model).astype(F32)
    inverse_one = lax.rsqrt(jnp.mean(x * x, axis=-1, keepdims=True) + 1e-05)
    normed = (x * inverse_one * gain_one).astype(BF16)
    cosine, sine = rope_tables(me, PR_DEV * n)
    cosine = jnp.concatenate([cosine] * 4, axis=1)
    sine = jnp.concatenate([-sine, sine] * 2, axis=1)
    mixed, query, kv_slots = plane_attention(normed, qkv_full, cosine, sine, micro)
    mixed = mixed.reshape(rows, query_width)
    hidden = x + mm(mixed, out_full)
    inverse_two = lax.rsqrt(jnp.mean(hidden * hidden, axis=-1, keepdims=True) + 1e-05)
    normed_two = (hidden * inverse_two * gain_two).astype(BF16)
    logits = mm(normed_two, router_full)
    chosen = named.reshape(rows, experts)
    logits = jnp.where(chosen, logits, NEG_FILL)
    top = jnp.max(logits, axis=-1, keepdims=True)
    raised = jnp.where(chosen, jnp.exp(logits - top), 0.0)
    gate_probs = raised / jnp.sum(raised, axis=-1, keepdims=True)

    high = gate_probs.astype(BF16)
    low = (gate_probs - high.astype(F32)).astype(BF16)
    payload = jnp.concatenate(
        [normed_two, high, low, jnp.zeros((rows, LANES - 2 * experts), BF16)], axis=1
    ).reshape(micro, count, model + LANES)
    rows_in, row_weights, far_three = plane_dispatch(
        payload, ranks, bank, where, per, cap, model, experts
    )
    weights_far = [far_one, far_two, far_three]
    tile = 2 * micro * split * cap
    outs, backs, weight_terms = expert_steps(
        where, rows_in, grads_in, row_weights, bank, weights_far, experts, tile
    )
    back, term_one = plane_return(backs, ranks, weight_terms[1], micro, count, cap)
    back = back.reshape(rows, model + LANES)

    outs, back, late = lax.optimization_barrier((outs, back, weight_terms[2]))
    mixture_parts = scatter_rows(outs, ranks, where, n, micro * split, count, cap)
    mixture_sum = lax.psum_scatter(mixture_parts, "expert", scatter_dimension=0, tiled=False)
    term_two = shift(late, 2)

    d_out = cotangent.reshape(rows, model).astype(F32)
    d_gates = back[:, model : model + experts] + back[:, model + experts : model + 2 * experts]
    d_logits = gate_probs * (d_gates - jnp.sum(gate_probs * d_gates, axis=-1, keepdims=True))
    router_grad = lax.dot_general(normed_two.astype(F32), d_logits, TN, precision=HIGHEST)
    d_normed_two = back[:, :model] + lax.dot_general(
        d_logits, router_full.astype(F32), NT, precision=HIGHEST
    )

    def rms_back(inputs, inverse, gain, upstream):
        scaled = gain * upstream
        return inverse * scaled - inputs * inverse * inverse * inverse * jnp.mean(
            scaled * inputs, axis=-1, keepdims=True
        )

    grad_two = jnp.sum(d_normed_two * hidden * inverse_two, axis=0)
    d_hidden = d_out + rms_back(hidden, inverse_two, gain_two, d_normed_two)
    d_attn = d_hidden.astype(BF16)
    d_mixed = mm(d_attn, out_full, NT).astype(BF16).reshape(micro, count, query_width)
    d_project = plane_attention_backward(query, kv_slots, d_mixed, cosine, -sine)
    d_project = d_project.reshape(rows, query_width + 2 * kv_width)
    d_normed = mm(d_project, qkv_full, NT)
    grad_one = jnp.sum(d_normed * x * inverse_one, axis=0)
    input_grad = (d_hidden + rms_back(x, inverse_one, gain_one, d_normed)).reshape(tokens.shape)
    gains = jnp.concatenate([grad_one[None], grad_two[None], jnp.zeros((6, model), F32)], axis=0)
    dense, term_three = plane_gradients(
        [(mixed, d_attn), (normed, d_project)], router_grad, gains, weight_terms[3], groups
    )
    mixture_sum, dense = lax.optimization_barrier((mixture_sum, dense))
    mixture = mixture_sum[:micro].astype(F32) + turn(mixture_sum[micro:], 1, split).astype(F32)
    block_out = (hidden + mixture.reshape(rows, model)).astype(BF16).reshape(tokens.shape)
    terms = [weight_terms[0], term_one, term_two, term_three]
    gate_grad, up_grad, down_grad = [merge_grads(which, where, terms) for which in range(3)]
    misc_sum = dense[:, model + query_width + 2 * kv_width :].astype(F32)
    return (
        block_out,
        input_grad,
        misc_sum[:, 0],
        dense[:, model : model + query_width + 2 * kv_width].astype(F32),
        dense[:, :model].astype(F32),
        misc_sum[:, 1],
        misc_sum[:, experts : 2 * experts],
        gate_grad,
        up_grad,
        down_grad,
    )


def per_device(*arrays):
    n, groups = lax.axis_size("expert"), lax.axis_size("group")
    exp_here, part, ff = arrays[8].shape
    plane = (
        n == 8
        and exp_here % 2 == 0
        and groups == 4
        and part % (16 * n) == 0
        and part % LANES == 0
        and arrays[0].shape[0] == 2
    )
    return (layer_plane if plane else layer_general)(*arrays)


def solution(mesh):
    rows = P(None, ("group", "expert"), None)
    return jax.shard_map(
        per_device,
        mesh=mesh,
        in_specs=(
            rows,
            rows,
            rows,
            P("group"),
            P("group", None),
            P("group", None),
            P("group"),
            P("group", None),
            P("expert", "group", None),
            P("expert", "group", None),
            P("expert", None, "group"),
        ),
        out_specs=(
            rows,
            rows,
            P("group"),
            P("group", None),
            P("group", None),
            P("group"),
            P("group", None),
            P("expert", "group", None),
            P("expert", "group", None),
            P("expert", None, "group"),
        ),
        check_vma=False,
    )
```

```python
import functools

import jax
import jax.numpy as jnp
from jax import lax
from jax.experimental import pallas as pl
from jax.experimental.pallas import tpu as pltpu
from jax.sharding import PartitionSpec as P

QUERY_HEADS = 24
KEY_VALUE_HEADS = 8
HEAD_SIZE = 64
TOPK = 8
CONT = 256
PR_DEV = 64
LANES = 128
SCORE_SCALE = 0.125
NEG_FILL = -1e30
HIGHEST = lax.Precision.HIGHEST
F32 = jnp.float32
BF16 = jnp.bfloat16

NN = (((1,), (0,)), ((), ()))
NT = (((1,), (1,)), ((), ()))
TN = (((0,), (0,)), ((), ()))


def mm(a, b, dims=NN):
    return lax.dot_general(a, b, dims, preferred_element_type=F32)


def swap(x, bit):
    n = lax.axis_size("expert")
    return lax.ppermute(x, "expert", [(i, i ^ bit) for i in range(n)])


def shift(x, step):
    n = lax.axis_size("group")
    return lax.ppermute(x, "group", [(i, (i + step) % n) for i in range(n)])


def turn(x, step, split):
    n = lax.axis_size("group")
    return lax.ppermute(
        x, "group", [((i // split) * split + (i + step) % split, i) for i in range(n)]
    )


def outer_bits(n):
    return [1 << i for i in range(1, n.bit_length() - 1)]


def spread(x, order):
    n = lax.axis_size("expert")
    outer = outer_bits(n)
    if len(outer) == 2:
        a, b = outer
        xa, xb = swap(x, a), swap(x, b)
        slots = {0: x, a: xa, b: xb, a ^ b: swap(xa, b) if order == 0 else swap(xb, a)}
    else:
        slots = {0: x}
        for bit in outer:
            slots.update({r ^ bit: swap(y, bit) for r, y in list(slots.items())})
    if n > 1:
        slots.update({r ^ 1: swap(y, 1) for r, y in list(slots.items())})
    return [slots[r] for r in range(n)]


def plus(a, b):
    return (a.astype(F32) + b.astype(F32)).astype(BF16)


def collect(parts, order):
    n = lax.axis_size("expert")
    outer = outer_bits(n)
    keep = {r: parts[r] for r in range(n)}
    if n > 1:
        keep = {r: plus(keep[r], swap(keep[r ^ 1], 1)) for r in range(0, n, 2)}
    if len(outer) == 2:
        a, b = outer
        if order == 0:
            keep[a] = plus(keep[a], swap(keep[a ^ b], b))
        else:
            keep[b] = plus(keep[b], swap(keep[a ^ b], a))
        return (
            keep[0].astype(F32) + swap(keep[a], a).astype(F32) + swap(keep[b], b).astype(F32)
        )
    for bit in reversed(outer):
        keep = {r: plus(keep[r], swap(keep[r ^ bit], bit)) for r in keep if not r & bit}
    return keep[0].astype(F32)


def full_spec(shape):
    return pl.BlockSpec(shape, lambda *_: (0,) * len(shape))


SMEM_SPEC = pl.BlockSpec(memory_space=pltpu.SMEM)
ANY_SPEC = pl.BlockSpec(memory_space=pl.ANY)


def cost(flops, moved):
    return pl.CostEstimate(flops=int(flops), bytes_accessed=int(moved), transcendentals=0)


def assemble(pieces, place, shape, where):
    count = len(pieces)

    def kernel(at_ref, *refs):
        ins, out, sems = refs[:count], refs[count], refs[count + 1]
        copies = []
        for i in range(count):
            row, column = place(i, at_ref[0], at_ref[1])
            r, c = pieces[i].shape
            copies.append(
                pltpu.make_async_copy(
                    ins[i],
                    out.at[pl.ds(pl.multiple_of(row, 16), r), pl.ds(pl.multiple_of(column, 128), c)],
                    sems.at[i],
                )
            )
        for one in copies:
            one.start()
        for one in copies:
            one.wait()

    return pl.pallas_call(
        kernel,
        grid=(1,),
        in_specs=[SMEM_SPEC] + [ANY_SPEC] * count,
        out_specs=full_spec(shape),
        out_shape=jax.ShapeDtypeStruct(shape, pieces[0].dtype),
        scratch_shapes=[pltpu.SemaphoreType.DMA((count,))],
        cost_estimate=cost(0, 4 * shape[0] * shape[1]),
        name="assemble",
    )(where, *pieces)


def gather_dense(piece, cuts, where):
    groups, n = lax.axis_size("group"), lax.axis_size("expert")
    rows, columns = piece.shape
    own = [piece[:, lo:hi] for lo, hi in cuts]
    far = [[shift(x, s) for x in own] for s in range(1, groups)]
    names, pieces = [], []
    for h, (lo, hi) in enumerate(cuts):
        joined = jnp.concatenate([far[s - 1][h] for s in range(1, groups)], axis=0)
        for r, x in enumerate(spread(own[h], h % 2)):
            names.append((0, r, lo))
            pieces.append(x)
        for r, x in enumerate(spread(joined, h % 2)):
            for s in range(1, groups):
                names.append((s, r, lo))
                pieces.append((x, (s - 1) * rows, rows))
    total = groups * n * rows
    arrays, index = [], []
    for entry in pieces:
        if isinstance(entry, tuple):
            if not arrays or arrays[-1] is not entry[0]:
                arrays.append(entry[0])
            index.append((len(arrays) - 1, entry[1], entry[2]))
        else:
            arrays.append(entry)
            index.append((len(arrays) - 1, 0, rows))
    count, held = len(index), len(arrays)

    def kernel(at_ref, *refs):
        ins, out, sems = refs[:held], refs[held], refs[held + 1]
        copies = []
        for i, (which, start, size) in enumerate(index):
            s, r, lo = names[i]
            z = lax.rem(at_ref[0] - s + groups, groups)
            e = jnp.bitwise_xor(at_ref[1], r)
            row = pl.multiple_of((z * n + e) * rows, 16)
            width = arrays[which].shape[1]
            copies.append(
                pltpu.make_async_copy(
                    ins[which].at[pl.ds(start, size)],
                    out.at[pl.ds(row, rows), pl.ds(lo, width)],
                    sems.at[i],
                )
            )
        for one in copies:
            one.start()
        for one in copies:
            one.wait()

    whole = pl.pallas_call(
        kernel,
        grid=(1,),
        in_specs=[SMEM_SPEC] + [ANY_SPEC] * held,
        out_specs=full_spec((total, columns)),
        out_shape=jax.ShapeDtypeStruct((total, columns), piece.dtype),
        scratch_shapes=[pltpu.SemaphoreType.DMA((count,))],
        cost_estimate=cost(0, 4 * total * columns),
        name="join_rows",
    )(where, *arrays)
    return whole, far


def sliced_outer(a, b, extra, groups, n, where):
    depth = a.shape[1]
    columns = b.shape[1]
    more = 0 if extra is None else extra.shape[1]
    rows = depth // (groups * n)

    def kernel(at_ref, a_ref, b_ref, *refs):
        if more:
            x_ref, refs = refs[0], refs[1:]
        outs, acc = refs[:n], refs[n]
        acc[:, :columns] = mm(a_ref[...], b_ref[...], TN)
        if more:
            acc[:, columns:] = x_ref[...]
        for r in range(n):
            e = jnp.bitwise_xor(at_ref[1], r)
            for s in range(groups):
                z = lax.rem(at_ref[0] + s, groups)
                row = pl.multiple_of((z * n + e) * rows, 16)
                outs[r][s] = acc[pl.ds(row, rows), :].astype(BF16)

    width = columns + more
    return pl.pallas_call(
        kernel,
        grid=(1,),
        in_specs=[SMEM_SPEC, full_spec(a.shape), full_spec(b.shape)]
        + ([full_spec(extra.shape)] if more else []),
        out_specs=[full_spec((groups, rows, width))] * n,
        out_shape=[jax.ShapeDtypeStruct((groups, rows, width), BF16)] * n,
        scratch_shapes=[pltpu.VMEM((depth, width), F32)],
        cost_estimate=cost(2 * a.shape[0] * depth * columns, 2 * depth * width),
        name="sliced_outer",
    )(where, a, b, *([extra] if more else []))


def reduce_dense(parts, order, where):
    groups, n = lax.axis_size("group"), lax.axis_size("expert")
    mine = collect(parts, order)
    total = mine[0]
    low = mine.astype(BF16)
    for s in range(1, groups):
        total = total + shift(low[s], s).astype(F32)
    rows, width = total.shape
    slots = spread(total.astype(BF16), order)

    def kernel(at_ref, *refs):
        out = refs[n]
        for r in range(n):
            e = jnp.bitwise_xor(at_ref[1], r)
            out[pl.ds(pl.multiple_of(e * rows, 16), rows), :] = refs[r][...].astype(F32)

    return pl.pallas_call(
        kernel,
        grid=(1,),
        in_specs=[SMEM_SPEC] + [full_spec((rows, width))] * n,
        out_specs=full_spec((n * rows, width)),
        out_shape=jax.ShapeDtypeStruct((n * rows, width), F32),
        cost_estimate=cost(0, 6 * n * rows * width),
        name="join_sums",
    )(where, *slots)


def attention_masks(n, me):
    shape = (3 * PR_DEV, n * PR_DEV)
    token = lax.rem(lax.broadcasted_iota(jnp.int32, shape, 0), PR_DEV)
    column = lax.broadcasted_iota(jnp.int32, shape, 1)
    key_pos = jnp.bitwise_xor(column // PR_DEV, me) * PR_DEV + lax.rem(column, PR_DEV)
    prompt_ok = key_pos <= me * PR_DEV + token
    slots = CONT // PR_DEV
    shape = (3 * PR_DEV, CONT)
    token = lax.rem(lax.broadcasted_iota(jnp.int32, shape, 0), PR_DEV)
    column = lax.broadcasted_iota(jnp.int32, shape, 1)
    owner = jnp.bitwise_xor(column // PR_DEV, lax.rem(me, slots))
    cont_ok = owner * PR_DEV + lax.rem(column, PR_DEV) <= lax.rem(me, slots) * PR_DEV + token
    return prompt_ok, cont_ok


def head_rows(x, base):
    return jnp.concatenate(
        [x[:, base + i * HEAD_SIZE : base + (i + 1) * HEAD_SIZE] for i in range(3)], axis=0
    )


def row_heads(x):
    return jnp.concatenate([x[i * PR_DEV : (i + 1) * PR_DEV] for i in range(3)], axis=1)


def softmax(scores):
    top = jnp.max(scores, axis=1, keepdims=True)
    weight = jnp.exp(scores - top)
    return weight * (1.0 / jnp.sum(weight, axis=1, keepdims=True))


def load_keys(n, kv_refs, keys):
    for r in range(n):
        keys[r * PR_DEV : (r + 1) * PR_DEV, :] = kv_refs[r][:PR_DEV, :]
    for r in range(CONT // PR_DEV):
        lo = (n + r) * PR_DEV
        keys[lo : lo + PR_DEV, :] = kv_refs[r][PR_DEV:, :]


def group_probs(q_top, q_low, key, prompt_ok, cont_ok, n):
    pr = n * PR_DEV
    top = mm(q_top, key[:pr], NT) * SCORE_SCALE
    top = softmax(jnp.where(prompt_ok, top, NEG_FILL))
    low = mm(q_low, key, NT) * SCORE_SCALE
    low = jnp.concatenate([low[:, :pr], jnp.where(cont_ok, low[:, pr:], NEG_FILL)], axis=1)
    return top, softmax(low)


def attention_forward(query, slots, where):
    n = len(slots)
    width = KEY_VALUE_HEADS * HEAD_SIZE
    tokens = 2 * PR_DEV
    total = n * PR_DEV + CONT

    def kernel(at_ref, q_ref, *refs):
        kv_refs, out_ref, keys = refs[:n], refs[n], refs[n + 1]
        load_keys(n, kv_refs, keys)
        prompt_ok, cont_ok = attention_masks(n, at_ref[1])

        def pair(j, carry):
            q_at = pl.ds(pl.multiple_of(j * 384, 128), 384)
            k_at = pl.ds(pl.multiple_of(j * 128, 128), 128)
            v_at = pl.ds(pl.multiple_of(width + j * 128, 128), 128)
            q_top, q_low = q_ref[:PR_DEV, q_at], q_ref[PR_DEV:, q_at]
            k_two, v_two = keys[:, k_at], keys[:, v_at]
            tops, lows = [], []
            for g in range(2):
                key = k_two[:, g * HEAD_SIZE : (g + 1) * HEAD_SIZE]
                value = v_two[:, g * HEAD_SIZE : (g + 1) * HEAD_SIZE]
                top, low = group_probs(
                    head_rows(q_top, g * 192), head_rows(q_low, g * 192), key, prompt_ok, cont_ok, n
                )
                tops.append(row_heads(mm(top.astype(BF16), value[: n * PR_DEV])))
                lows.append(row_heads(mm(low.astype(BF16), value)))
            out_ref[:PR_DEV, q_at] = jnp.concatenate(tops, axis=1).astype(BF16)
            out_ref[PR_DEV:, q_at] = jnp.concatenate(lows, axis=1).astype(BF16)
            return carry

        lax.fori_loop(0, KEY_VALUE_HEADS // 2, pair, 0)

    return pl.pallas_call(
        kernel,
        grid=(1,),
        in_specs=[SMEM_SPEC, full_spec(query.shape)] + [full_spec((tokens, 2 * width))] * n,
        out_specs=full_spec(query.shape),
        out_shape=jax.ShapeDtypeStruct(query.shape, BF16),
        scratch_shapes=[pltpu.VMEM((total, 2 * width), BF16)],
        cost_estimate=cost(8e9, 4e6),
        name="attention_forward",
    )(where, query, *slots)


def attention_backward(query, slots, d_mixed, where):
    n = len(slots)
    width = KEY_VALUE_HEADS * HEAD_SIZE
    tokens = 2 * PR_DEV
    pr = n * PR_DEV
    total = pr + CONT

    def kernel(at_ref, q_ref, d_ref, *refs):
        kv_refs, refs = refs[:n], refs[n:]
        dq_ref, outs, keys, grads = refs[0], refs[1 : 1 + n], refs[1 + n], refs[2 + n]
        load_keys(n, kv_refs, keys)
        prompt_ok, cont_ok = attention_masks(n, at_ref[1])

        def one_side(prob, d_rows, key, value, q_rows):
            d_prob = mm(d_rows, value, NT)
            delta = jnp.sum(prob * d_prob, axis=1, keepdims=True)
            d_score = (prob * (d_prob - delta)).astype(BF16)
            return (
                mm(d_score, key) * SCORE_SCALE,
                mm(d_score, q_rows, TN) * SCORE_SCALE,
                mm(prob.astype(BF16), d_rows, TN),
            )

        def pair(j, carry):
            q_at = pl.ds(pl.multiple_of(j * 384, 128), 384)
            k_at = pl.ds(pl.multiple_of(j * 128, 128), 128)
            v_at = pl.ds(pl.multiple_of(width + j * 128, 128), 128)
            q_top, q_low = q_ref[:PR_DEV, q_at], q_ref[PR_DEV:, q_at]
            d_top, d_low = d_ref[:PR_DEV, q_at], d_ref[PR_DEV:, q_at]
            k_two, v_two = keys[:, k_at], keys[:, v_at]
            dq_tops, dq_lows, dks, dvs = [], [], [], []
            for g in range(2):
                key = k_two[:, g * HEAD_SIZE : (g + 1) * HEAD_SIZE]
                value = v_two[:, g * HEAD_SIZE : (g + 1) * HEAD_SIZE]
                rows_top, rows_low = head_rows(q_top, g * 192), head_rows(q_low, g * 192)
                top, low = group_probs(rows_top, rows_low, key, prompt_ok, cont_ok, n)
                dq_top, dk_top, dv_top = one_side(
                    top, head_rows(d_top, g * 192), key[:pr], value[:pr], rows_top
                )
                dq_low, dk_low, dv_low = one_side(
                    low, head_rows(d_low, g * 192), key, value, rows_low
                )
                dq_tops.append(row_heads(dq_top))
                dq_lows.append(row_heads(dq_low))
                dks.append(jnp.concatenate([dk_low[:pr] + dk_top, dk_low[pr:]], axis=0))
                dvs.append(jnp.concatenate([dv_low[:pr] + dv_top, dv_low[pr:]], axis=0))
            dq_ref[:PR_DEV, q_at] = jnp.concatenate(dq_tops, axis=1)
            dq_ref[PR_DEV:, q_at] = jnp.concatenate(dq_lows, axis=1)
            grads[:, k_at] = jnp.concatenate(dks, axis=1).astype(BF16)
            grads[:, v_at] = jnp.concatenate(dvs, axis=1).astype(BF16)
            return carry

        lax.fori_loop(0, KEY_VALUE_HEADS // 2, pair, 0)
        for r in range(n):
            outs[r][:PR_DEV, :] = grads[r * PR_DEV : (r + 1) * PR_DEV, :]
            if r < CONT // PR_DEV:
                lo = (n + r) * PR_DEV
                outs[r][PR_DEV:, :] = grads[lo : lo + PR_DEV, :]
            else:
                outs[r][PR_DEV:, :] = jnp.zeros((PR_DEV, 2 * width), BF16)

    out = pl.pallas_call(
        kernel,
        grid=(1,),
        in_specs=[SMEM_SPEC, full_spec(query.shape), full_spec(query.shape)]
        + [full_spec((tokens, 2 * width))] * n,
        out_specs=[full_spec(query.shape)] + [full_spec((tokens, 2 * width))] * n,
        out_shape=[jax.ShapeDtypeStruct(query.shape, F32)]
        + [jax.ShapeDtypeStruct((tokens, 2 * width), BF16)] * n,
        scratch_shapes=[pltpu.VMEM((total, 2 * width), BF16), pltpu.VMEM((total, 2 * width), BF16)],
        cost_estimate=cost(2e10, 8e6),
        name="attention_backward",
    )(where, query, d_mixed, *slots)
    return out[0], out[1:]


def pick(slot_row, cap):
    rows = lax.broadcasted_iota(jnp.int32, (cap, slot_row.shape[1]), 0).astype(F32)
    return jnp.where(slot_row == rows, 1.0, 0.0).astype(BF16)


def dispatch_grads(arrays, at, per, cap, model, buffers, place, blocks_total):
    count = len(arrays)
    split, tokens, width = arrays[0].shape
    blocks = count * split
    first = buffers is None

    def kernel(at_ref, *refs):
        ins = refs[:count]
        out, ranks = refs[-3], refs[-2]
        flags = refs[-1]
        row = lax.broadcasted_iota(jnp.int32, (tokens, tokens), 0)
        col = lax.broadcasted_iota(jnp.int32, (tokens, tokens), 1)
        before = jnp.where(row < col, 1.0, 0.0).astype(BF16)
        for i in range(count):
            for j in range(split):
                b = i * split + j
                payload = ins[i][j]
                flags[...] = payload[:, model:].astype(F32).T
                picked = jnp.concatenate(
                    [flags[pl.ds(at_ref[2] + k, 1), :] for k in range(per)], axis=0
                )
                rank = mm(picked.astype(BF16), before)
                slot = jnp.where(picked > 0.0, rank, -1.0)
                ranks[b] = slot
                for k in range(per):
                    out[k, b * cap : (b + 1) * cap, :] = mm(
                        pick(slot[k : k + 1], cap), payload[:, :model]
                    ).astype(BF16)

    shapes = [
        jax.ShapeDtypeStruct((per, blocks_total * cap, model), BF16),
        jax.ShapeDtypeStruct((blocks_total, per, tokens), F32),
    ]
    return pl.pallas_call(
        kernel,
        grid=(1,),
        in_specs=[SMEM_SPEC]
        + [full_spec(arrays[0].shape)] * count
        + ([] if first else [ANY_SPEC] * 2),
        out_specs=[
            pl.BlockSpec((per, blocks * cap, model), lambda *_: (0, place, 0)),
            pl.BlockSpec((blocks, per, tokens), lambda *_: (place, 0, 0)),
        ],
        out_shape=shapes,
        scratch_shapes=[pltpu.VMEM((LANES, tokens), F32)],
        input_output_aliases={} if first else {1 + count: 0, 2 + count: 1},
        cost_estimate=cost(1e9, 6e6),
        name="dispatch_grads",
    )(at, *arrays, *([] if first else buffers))


def dispatch_rows(arrays, ranks, at, per, cap, model, experts, buffers, place, blocks_total):
    count = len(arrays)
    split, tokens, width = arrays[0].shape
    blocks = count * split
    first = buffers is None

    def kernel(at_ref, rank_ref, *refs):
        ins = refs[:count]
        out, weights = refs[-2], refs[-1]
        lane = lax.broadcasted_iota(jnp.int32, (cap, LANES), 1)
        for i in range(count):
            for j in range(split):
                b = i * split + j
                payload = ins[i][j]
                for k in range(per):
                    got = mm(pick(rank_ref[b, k : k + 1, :], cap), payload)
                    out[k, b * cap : (b + 1) * cap, :] = got[:, :model].astype(BF16)
                    tail = got[:, model:]
                    e = at_ref[2] + k
                    mine = (lane == e) | (lane == e + experts)
                    total = jnp.sum(jnp.where(mine, tail, 0.0), axis=1, keepdims=True)
                    weights[k, b * cap : (b + 1) * cap, :] = jnp.broadcast_to(total, (cap, LANES))

    shapes = [
        jax.ShapeDtypeStruct((per, blocks_total * cap, model), BF16),
        jax.ShapeDtypeStruct((per, blocks_total * cap, LANES), F32),
    ]
    return pl.pallas_call(
        kernel,
        grid=(1,),
        in_specs=[SMEM_SPEC, pl.BlockSpec((blocks, per, tokens), lambda *_: (place, 0, 0))]
        + [full_spec(arrays[0].shape)] * count
        + ([] if first else [ANY_SPEC] * 2),
        out_specs=[
            pl.BlockSpec((per, blocks * cap, model), lambda *_: (0, place, 0)),
            pl.BlockSpec((per, blocks * cap, LANES), lambda *_: (0, place, 0)),
        ],
        out_shape=shapes,
        input_output_aliases={} if first else {2 + count: 0, 3 + count: 1},
        cost_estimate=cost(1e9, 6e6),
        name="dispatch_rows",
    )(at, ranks, *arrays, *([] if first else buffers))


def run_expert(k, at, rows_in, grads_in, weights, gate, up, down, experts, tile, groups, cut):
    per, total, model = rows_in.shape
    ff = gate.shape[1]
    part = model // groups
    steps = total // tile

    def kernel(at_ref, x_ref, d_ref, w_ref, gate_ref, up_ref, down_ref, o_ref, r_ref, *refs):
        outs, (acc_gate, acc_up, acc_down) = refs[:-3], refs[-3:]
        step = pl.program_id(0)
        x, d = x_ref[0], d_ref[0]
        w = w_ref[0, :, 0:1]
        gate_pre = mm(x, gate_ref[...])
        up_pre = mm(x, up_ref[...])
        sig = 1.0 / (1.0 + jnp.exp(-gate_pre))
        silu = gate_pre * sig
        active_wide = silu * up_pre
        active = active_wide.astype(BF16)
        out = mm(active, down_ref[...])
        o_ref[...] = (out * w).astype(BF16)
        d_raw = mm(d, down_ref[...], NT)
        d_gates = jnp.sum(active.astype(F32) * d_raw, axis=1, keepdims=True)
        d_active = d_raw * w
        d_up = (d_active * silu).astype(BF16)
        d_gate = (d_active * up_pre * sig * (1.0 + gate_pre * (1.0 - sig))).astype(BF16)
        d_row = mm(d_gate, gate_ref[...], NT) + mm(d_up, up_ref[...], NT)
        r_ref[:, :model] = d_row.astype(BF16)
        high = d_gates.astype(BF16).astype(F32)
        lane = lax.broadcasted_iota(jnp.int32, (tile, LANES), 1)
        e = at_ref[2] + k
        r_ref[:, model:] = (
            jnp.where(lane == e, high, 0.0) + jnp.where(lane == e + experts, d_gates - high, 0.0)
        ).astype(BF16)
        new_gate = mm(x, d_gate, TN)
        new_up = mm(x, d_up, TN)
        new_down = mm((active_wide * w).astype(BF16), d, TN)

        @pl.when(step == 0)
        def _():
            acc_gate[...] = new_gate
            acc_up[...] = new_up
            acc_down[...] = new_down

        @pl.when(step > 0)
        def _():
            acc_gate[...] += new_gate
            acc_up[...] += new_up
            acc_down[...] += new_down

        @pl.when(step == steps - 1)
        def _():
            if cut:
                for s in range(groups):
                    z = lax.rem(at_ref[0] + s, groups)
                    at_z = pl.ds(pl.multiple_of(z * part, 128), part)
                    outs[s][...] = acc_gate[at_z, :].astype(BF16)
                    outs[groups + s][...] = acc_up[at_z, :].astype(BF16)
                    outs[2 * groups + s][...] = acc_down[:, at_z].astype(BF16)
            else:
                outs[0][...] = acc_gate[...].astype(BF16)
                outs[1][...] = acc_up[...].astype(BF16)
                outs[2][...] = acc_down[...].astype(BF16)

    if cut:
        grads = [(part, ff)] * (2 * groups) + [(ff, part)] * groups
    else:
        grads = [(model, ff)] * 2 + [(ff, model)]
    row_spec = pl.BlockSpec((1, tile, model), lambda t: (k, t, 0))
    held = lambda shape: pl.BlockSpec(shape, lambda t: (0, 0), pipeline_mode=pl.Buffered(1))
    out = pl.pallas_call(
        kernel,
        grid=(steps,),
        in_specs=[
            SMEM_SPEC,
            row_spec,
            row_spec,
            pl.BlockSpec((1, tile, LANES), lambda t: (k, t, 0)),
            held((model, ff)),
            held((model, ff)),
            held((ff, model)),
        ],
        out_specs=[
            pl.BlockSpec((tile, model), lambda t: (t, 0)),
            pl.BlockSpec((tile, model + LANES), lambda t: (t, 0)),
        ]
        + [held(shape) for shape in grads],
        out_shape=[
            jax.ShapeDtypeStruct((total, model), BF16),
            jax.ShapeDtypeStruct((total, model + LANES), BF16),
        ]
        + [jax.ShapeDtypeStruct(shape, BF16) for shape in grads],
        scratch_shapes=[
            pltpu.VMEM((model, ff), F32),
            pltpu.VMEM((model, ff), F32),
            pltpu.VMEM((ff, model), F32),
        ],
        compiler_params=pltpu.CompilerParams(vmem_limit_bytes=62 * 1024 * 1024),
        cost_estimate=cost(18 * total * model * ff, 10 * total * model),
        name="run_expert",
    )(at, rows_in, grads_in, weights, gate, up, down)
    return out[0], out[1], out[2:]


def combine(rows, ranks, count, split, tokens, cap, place):
    per = len(rows)
    width = rows[0].shape[1]
    blocks = count * split

    def kernel(rank_ref, *refs):
        ins, outs = refs[:per], refs[per:]
        for i in range(count):
            for j in range(split):
                b = i * split + j
                total = None
                for k in range(per):
                    one = mm(
                        pick(rank_ref[b, k : k + 1, :], cap), ins[k][b * cap : (b + 1) * cap, :], TN
                    )
                    total = one if total is None else total + one
                outs[i][j] = total.astype(BF16)

    return pl.pallas_call(
        kernel,
        grid=(1,),
        in_specs=[pl.BlockSpec((blocks, per, tokens), lambda *_: (place, 0, 0))]
        + [pl.BlockSpec((blocks * cap, width), lambda *_: (place, 0))] * per,
        out_specs=[full_spec((split, tokens, width))] * count,
        out_shape=[jax.ShapeDtypeStruct((split, tokens, width), BF16)] * count,
        cost_estimate=cost(1e9, 6e6),
        name="combine",
    )(ranks, *rows)


def rope_tables(my_index, prompt_len):
    half = HEAD_SIZE // 2
    local = jnp.arange(2 * PR_DEV, dtype=jnp.int32)
    cont = my_index * PR_DEV + local - PR_DEV
    position = jnp.where(local < PR_DEV, my_index * PR_DEV + local, prompt_len + cont % CONT)
    frequency = 10000.0 ** (-jnp.arange(half, dtype=F32) * (2.0 / HEAD_SIZE))
    angle = position.astype(F32)[:, None] * frequency[None, :]
    return jnp.cos(angle), jnp.sin(angle)


def rotate(x, cosine, sine):
    half = HEAD_SIZE // 2
    column = lax.broadcasted_iota(jnp.int32, x.shape, 1)
    other = jnp.where(column % HEAD_SIZE < half, jnp.roll(x, -half, axis=1), jnp.roll(x, half, axis=1))
    return x * cosine + other * sine


def layer_general(
    tokens,
    cotangent,
    routes,
    norm_one,
    query_key_value_weight,
    out_weight,
    norm_two,
    router_weight,
    gate_weight,
    up_weight,
    down_weight,
):
    n = lax.axis_size("expert")
    groups = lax.axis_size("group")
    me = lax.axis_index("expert")
    z = lax.axis_index("group")
    micro, count, model = tokens.shape
    exp_here, part, ff = gate_weight.shape
    experts = router_weight.shape[1]
    split = 2 if exp_here % 2 == 0 and groups % 2 == 0 else 1
    per = exp_here // split
    query_width = QUERY_HEADS * HEAD_SIZE
    kv_width = KEY_VALUE_HEADS * HEAD_SIZE
    cap = max(2, 3 * TOPK * PR_DEV // experts)
    where = jnp.stack([z, me, me * exp_here + (z % split) * per]).astype(jnp.int32)
    rows_here = part // n if part % n == 0 else 0
    aligned = rows_here > 0 and rows_here % 16 == 0 and part % LANES == 0

    misc = jnp.concatenate(
        [
            norm_one[:, None],
            norm_two[:, None],
            jnp.zeros((part, experts - 2), BF16),
            router_weight,
            jnp.zeros((part, LANES - 2 * experts), BF16),
        ],
        axis=1,
    )
    if aligned:
        first = jnp.concatenate([query_key_value_weight, misc], axis=1)
        cut = lambda x: lax.dynamic_slice_in_dim(x, me * rows_here, rows_here, axis=0)
        width = first.shape[1]
        middle = width // 2 // LANES * LANES
        first_full, far = gather_dense(cut(first), [(0, middle), (middle, width)], where)
        out_full, far_out = gather_dense(
            cut(out_weight), [(0, model // 2), (model // 2, model)], where
        )
        after = (far, far_out)
    else:
        first_full = lax.all_gather(
            jnp.concatenate([query_key_value_weight, misc], axis=1), "group", axis=0, tiled=True
        )
        out_full = lax.all_gather(out_weight, "group", axis=0, tiled=True)
        after = ()
    qkv_columns = query_key_value_weight.shape[1]
    qkv_full = first_full[:, :qkv_columns]
    misc_full = first_full[:, qkv_columns:]
    gain_one = misc_full[:, 0].astype(F32)
    gain_two = misc_full[:, 1].astype(F32)
    router_full = misc_full[:, experts : 2 * experts]

    weights_held = []
    gate_from, up_from, down_from = gate_weight, up_weight, down_weight
    if aligned:
        (gate_from, up_from, down_from), after = lax.optimization_barrier(
            ((gate_weight, up_weight, down_weight), after)
        )
    for k in range(per):
        held = []
        for array, axis in ((gate_from, 0), (up_from, 0), (down_from, 1)):
            if not aligned:
                held.append(lax.all_gather(array[k], "group", axis=axis, tiled=True))
                continue
            pieces = []
            for s in range(groups):
                index = ((z + s) % split) * per + k
                chunk = lax.dynamic_index_in_dim(array, index, 0, keepdims=False)
                pieces.append(shift(chunk, s) if s else chunk)

            def place(i, at_z, at_e, axis=axis):
                start = lax.rem(at_z - i + groups, groups) * part
                return (start, 0) if axis == 0 else (0, start)

            shape = (model, ff) if axis == 0 else (ff, model)
            held.append(assemble(pieces, place, shape, where))
        weights_held.append(held)

    expert_ids = jnp.arange(experts, dtype=jnp.int32)
    named = jnp.any(routes[..., None] == expert_ids, axis=2)
    pad = jnp.zeros((micro, count, LANES - experts), BF16)
    d_payload = jnp.concatenate([cotangent, named.astype(BF16), pad], axis=2)

    def to_experts(payload):
        held = []
        for m in range(micro):
            own = payload[m]
            both = jnp.stack([own] + [turn(own, j, split) for j in range(1, split)])
            held.append(spread(both, m % 2))
        return held

    def to_owners(parts):
        held = []
        for m in range(micro):
            total = collect(parts[m], m % 2)
            mine = total[0]
            for j in range(1, split):
                mine = mine + turn(total[j].astype(BF16), split - j, split).astype(F32)
            held.append(mine)
        return jnp.stack(held)

    slots_per = 2 if n % 2 == 0 else 1
    batches = [list(range(g * slots_per, (g + 1) * slots_per)) for g in range(n // slots_per)]
    blocks_total = n * micro * split

    d_slots = to_experts(d_payload)
    buffers = None
    for g, batch in enumerate(batches):
        buffers = dispatch_grads(
            [d_slots[m][r] for r in batch for m in range(micro)],
            where, per, cap, model, buffers, g, blocks_total,
        )
    grads_in, ranks = buffers

    rows = micro * count
    x = tokens.reshape(rows, model).astype(F32)
    inverse_one = lax.rsqrt(jnp.mean(x * x, axis=-1, keepdims=True) + 1e-05)
    normed = (x * inverse_one * gain_one).astype(BF16)
    cosine, sine = rope_tables(me, PR_DEV * n)
    heads_rope = QUERY_HEADS + KEY_VALUE_HEADS
    cosine = jnp.tile(jnp.concatenate([cosine, cosine], axis=1), (micro, heads_rope))
    sine = jnp.tile(jnp.concatenate([-sine, sine], axis=1), (micro, heads_rope))
    cosine, sine = lax.optimization_barrier((cosine, sine))
    project = mm(normed, qkv_full)
    roped = rotate(project[:, : query_width + kv_width], cosine, sine).astype(BF16)
    query = roped[:, :query_width]
    key_value = jnp.concatenate(
        [roped[:, query_width:], project[:, query_width + kv_width :].astype(BF16)], axis=1
    ).reshape(micro, count, 2 * kv_width)
    query = query.reshape(micro, count, query_width)
    kv_slots = [spread(key_value[m], m % 2) for m in range(micro)]
    mixed = jnp.concatenate(
        [attention_forward(query[m], kv_slots[m], where) for m in range(micro)], axis=0
    )
    hidden = x + mm(mixed, out_full)
    inverse_two = lax.rsqrt(jnp.mean(hidden * hidden, axis=-1, keepdims=True) + 1e-05)
    normed_two = (hidden * inverse_two * gain_two).astype(BF16)
    logits = mm(normed_two, router_full)
    chosen = named.reshape(rows, experts)
    logits = jnp.where(chosen, logits, NEG_FILL)
    top = jnp.max(logits, axis=-1, keepdims=True)
    raised = jnp.where(chosen, jnp.exp(logits - top), 0.0)
    gate_probs = raised / jnp.sum(raised, axis=-1, keepdims=True)

    high = gate_probs.astype(BF16)
    low = (gate_probs - high.astype(F32)).astype(BF16)
    payload = jnp.concatenate(
        [normed_two, high, low, jnp.zeros((rows, LANES - 2 * experts), BF16)], axis=1
    ).reshape(micro, count, model + LANES)
    x_slots = to_experts(payload)
    buffers = None
    for g, batch in enumerate(batches):
        buffers = dispatch_rows(
            [x_slots[m][r] for r in batch for m in range(micro)],
            ranks, where, per, cap, model, experts, buffers, g, blocks_total,
        )
    rows_in, row_weights = buffers
    tile = slots_per * micro * split * cap
    outs, backs, weight_terms = [], [], []
    for k in range(per):
        out_rows, back_rows, terms = run_expert(
            k, where, rows_in, grads_in, row_weights, *weights_held[k], experts, tile, groups, aligned
        )
        outs.append(out_rows)
        backs.append(back_rows)
        weight_terms.append(terms)

    def returned(row_arrays):
        parts = [[None] * n for _ in range(micro)]
        for g in reversed(range(len(batches))):
            got = combine(
                row_arrays, ranks, len(batches[g]) * micro, split, count, cap, g
            )
            for i, (r, m) in enumerate((r, m) for r in batches[g] for m in range(micro)):
                parts[m][r] = got[i]
        return to_owners(parts)

    back = returned(backs).reshape(rows, model + LANES)
    mixture = returned(outs).reshape(rows, model)
    block_out = (hidden + mixture).astype(BF16).reshape(tokens.shape)

    expert_grads = []
    for which in range(3):
        per_class = []
        for k in range(per):
            if not aligned:
                axis = 1 if which == 2 else 0
                per_class.append(
                    [lax.psum_scatter(weight_terms[k][which], "group", scatter_dimension=axis, tiled=True).astype(F32)]
                )
                continue
            sums = [None] * split
            for s in range(groups):
                term = weight_terms[k][which * groups + s]
                term = (shift(term, s) if s else term).astype(F32)
                c = s % split
                sums[c] = term if sums[c] is None else sums[c] + term
            per_class.append(
                [lax.select_n((z - p) % split, *sums) if split > 1 else sums[0] for p in range(split)]
            )
        expert_grads.append(
            jnp.stack([per_class[k][p] for p in range(split) for k in range(per)])
        )

    d_out = cotangent.reshape(rows, model).astype(F32)
    d_gates = back[:, model : model + experts] + back[:, model + experts : model + 2 * experts]
    d_logits = gate_probs * (d_gates - jnp.sum(gate_probs * d_gates, axis=-1, keepdims=True))
    router_grad = lax.dot_general(normed_two.astype(F32), d_logits, TN, precision=HIGHEST)
    d_normed_two = back[:, :model] + lax.dot_general(
        d_logits, router_full.astype(F32), NT, precision=HIGHEST
    )

    def rms_back(inputs, inverse, gain, upstream):
        scaled = gain * upstream
        return inverse * scaled - inputs * inverse * inverse * inverse * jnp.mean(
            scaled * inputs, axis=-1, keepdims=True
        )

    grad_two = jnp.sum(d_normed_two * hidden * inverse_two, axis=0)
    d_hidden = d_out + rms_back(hidden, inverse_two, gain_two, d_normed_two)
    d_attn = d_hidden.astype(BF16)
    d_mixed = mm(d_attn, out_full, NT).astype(BF16).reshape(micro, count, query_width)
    d_query, kv_terms = [], []
    for m in range(micro):
        got, terms = attention_backward(query[m], kv_slots[m], d_mixed[m], where)
        d_query.append(got)
        kv_terms.append(terms)
    d_query = jnp.concatenate(d_query, axis=0)
    q_cos, q_sin = cosine[:, :query_width], sine[:, :query_width]
    d_query_low = rotate(d_query, q_cos, -q_sin).astype(BF16)
    d_kv = jnp.concatenate([collect(kv_terms[m], m % 2) for m in range(micro)], axis=0)
    d_key_low = rotate(d_kv[:, :kv_width], q_cos[:, :kv_width], -q_sin[:, :kv_width]).astype(BF16)
    d_kv_low = jnp.concatenate([d_key_low, d_kv[:, kv_width:].astype(BF16)], axis=1)
    d_normed = mm(d_query_low, qkv_full[:, :query_width], NT) + mm(
        d_kv_low, qkv_full[:, query_width:], NT
    )
    grad_one = jnp.sum(d_normed * x * inverse_one, axis=0)
    input_grad = (d_hidden + rms_back(x, inverse_one, gain_one, d_normed)).reshape(tokens.shape)
    misc_grad = jnp.concatenate(
        [
            grad_one[:, None],
            grad_two[:, None],
            jnp.zeros((model, experts - 2), F32),
            router_grad,
            jnp.zeros((model, LANES - 2 * experts), F32),
        ],
        axis=1,
    )
    if aligned:
        grad_out = reduce_dense(sliced_outer(mixed, d_attn, None, groups, n, where), 0, where)
        grad_q = reduce_dense(sliced_outer(normed, d_query_low, None, groups, n, where), 1, where)
        grad_rest = reduce_dense(
            sliced_outer(normed, d_kv_low, misc_grad, groups, n, where), 0, where
        )
    else:

        def whole(value):
            low = lax.psum_scatter(value.astype(BF16), "group", scatter_dimension=0, tiled=True)
            return lax.psum(low, "expert").astype(F32)

        grad_out = whole(mm(mixed, d_attn, TN))
        grad_q = whole(mm(normed, d_query_low, TN))
        grad_rest = whole(jnp.concatenate([mm(normed, d_kv_low, TN), misc_grad], axis=1))
    grad_qkv = jnp.concatenate([grad_q, grad_rest[:, : 2 * kv_width]], axis=1)
    misc_sum = grad_rest[:, 2 * kv_width :]
    return (
        block_out,
        input_grad,
        misc_sum[:, 0],
        grad_qkv,
        grad_out,
        misc_sum[:, 1],
        misc_sum[:, experts : 2 * experts],
        *expert_grads,
    )


def flip(e, r):
    for bit in (1, 2, 4):
        if r & bit:
            e = e + bit - 2 * bit * lax.rem(e // bit, 2)
    return e


def partner(z):
    return z + 1 - 2 * lax.rem(z, 2)


def remote(src, dst, send, recv, device):
    return pltpu.make_async_remote_copy(
        src_ref=src,
        dst_ref=dst,
        send_sem=send,
        recv_sem=recv,
        device_id=device,
        device_id_type=pl.DeviceIdType.MESH,
    )


def greet(devices):
    barrier = pltpu.get_barrier_semaphore()
    for device in devices:
        pl.semaphore_signal(barrier, inc=1, device_id=device, device_id_type=pl.DeviceIdType.MESH)
    pl.semaphore_wait(barrier, len(devices))


def plane_devices(e):
    return [{"expert": flip(e, bit)} for bit in (1, 2, 4)]


class Gather:
    def __init__(self, e, own, loc, paths, send, recv):
        self.e, self.own, self.loc, self.paths, self.send, self.recv = e, own, loc, paths, send, recv

    def copy(self, r, bit, c):
        q = r ^ bit
        src = self.own(c) if r == 0 else self.loc(r, r, c)
        return remote(
            src, self.loc(r, q, c), self.send.at[q, c], self.recv.at[q, c],
            {"expert": flip(self.e, bit)},
        )

    def begin(self, c):
        for bit in (2, 4, 1):
            self.copy(0, bit, c).start()

    def arrived(self, q, c):
        here = self.loc(q, q, c)
        remote(
            here, here, self.send.at[q, c], self.recv.at[q, c], {"expert": flip(self.e, 1)}
        ).wait_recv()

    def pass_on(self, q, c):
        if q == 2 and self.paths[c] == 0:
            self.copy(2, 4, c).start()
        if q == 4 and self.paths[c] == 1:
            self.copy(4, 2, c).start()
        if q in (2, 4, 6):
            self.copy(q, 1, c).start()

    def finish(self, c):
        for bit in (2, 4, 1):
            self.copy(0, bit, c).wait_send()
        if self.paths[c] == 0:
            self.copy(2, 4, c).wait_send()
        else:
            self.copy(4, 2, c).wait_send()
        for q in (2, 4, 6):
            self.copy(q, 1, c).wait_send()

    def stage(self, chunks, slots):
        for c in chunks:
            for q in slots:
                self.arrived(q, c)
                self.pass_on(q, c)

    def forward_all(self, chunks, use=None):
        for c in chunks:
            for q in (2, 4):
                self.arrived(q, c)
                self.pass_on(q, c)
        if use:
            for c in chunks:
                self.arrived(1, c)
                use(1, c)
                use(2, c)
                use(4, c)
        for c in chunks:
            self.arrived(6, c)
            self.pass_on(6, c)
            if use:
                use(6, c)
        for c in chunks:
            for q in (3, 5, 7) if use else (1, 3, 5, 7):
                self.arrived(q, c)
                if use:
                    use(q, c)


def add_rows(dst, sources, step=16):
    rows = sources[0].shape[0]

    def one(i, carry):
        at = pl.ds(pl.multiple_of(i * step, step), step)
        total = sources[0][at, :].astype(F32)
        for source in sources[1:]:
            total = total + source[at, :].astype(F32)
        dst[at, :] = total.astype(dst.dtype)
        return carry

    lax.fori_loop(0, rows // step, one, 0)


class Reduce:
    def __init__(self, e, part, paths, core, diag, near, acc, send, recv):
        self.e, self.part, self.paths = e, part, paths
        self.core, self.diag, self.near, self.acc = core, diag, near, acc
        self.send, self.recv = send, recv

    def core_copy(self, h, c):
        return remote(
            self.part(2 * h + 1, c), self.core.at[h, c], self.send.at[h, c], self.recv.at[h, c],
            {"expert": flip(self.e, 1)},
        )

    def diag_copy(self, c):
        return remote(
            self.acc.at[2, c], self.diag.at[c], self.send.at[4, c], self.recv.at[4, c],
            {"expert": flip(self.e, 4 if self.paths[c] == 0 else 2)},
        )

    def near_copy(self, i, c):
        return remote(
            self.acc.at[i, c], self.near.at[i, c], self.send.at[5 + i, c], self.recv.at[5 + i, c],
            {"expert": flip(self.e, 2 if i == 0 else 4)},
        )

    def begin(self, r, c):
        self.core_copy(r // 2, c).start()

    def diagonal(self, chunks):
        for c in chunks:
            self.core_copy(3, c).wait_recv()
            add_rows(self.acc.at[2, c], [self.part(6, c), self.core.at[3, c]])
            self.diag_copy(c).start()

    def sides(self, chunks):
        for c in chunks:
            for i in (0, 1) if self.paths[c] == 1 else (1, 0):
                self.core_copy(1 + i, c).wait_recv()
                terms = [self.part(2 + 2 * i, c), self.core.at[1 + i, c]]
                if self.paths[c] == i:
                    self.diag_copy(c).wait_recv()
                    terms.append(self.diag.at[c])
                add_rows(self.acc.at[i, c], terms)
                self.near_copy(i, c).start()

    def total(self, c):
        self.core_copy(0, c).wait_recv()
        self.near_copy(0, c).wait_recv()
        self.near_copy(1, c).wait_recv()
        return [self.part(0, c), self.core.at[0, c], self.near.at[0, c], self.near.at[1, c]]

    def finish(self, c):
        for h in range(4):
            self.core_copy(h, c).wait_send()
        self.diag_copy(c).wait_send()
        for i in range(2):
            self.near_copy(i, c).wait_send()


def reduce_scratch(count, rows, width):
    return [
        pltpu.VMEM((4, count, rows, width), BF16),
        pltpu.VMEM((count, rows, width), BF16),
        pltpu.VMEM((2, count, rows, width), BF16),
        pltpu.VMEM((3, count, rows, width), BF16),
        pltpu.SemaphoreType.DMA((7, count)),
        pltpu.SemaphoreType.DMA((7, count)),
    ]


def params(identity, vmem=62):
    return pltpu.CompilerParams(
        collective_id=identity, has_side_effects=True, vmem_limit_bytes=vmem * 1024 * 1024
    )


def plane_weights(shares, bank, per):
    n, split = 8, 2
    groups = lax.axis_size("group")
    rows = shares[0].shape[0]
    kinds = len(shares)
    count = groups * kinds

    def kernel(*refs):
        ins, bank_ref, refs = refs[:kinds], refs[kinds], refs[kinds + 1 :]
        outs, far_ref, refs = refs[:kinds], refs[kinds], refs[kinds + 1 :]
        z_send, z_recv, send, recv, local, b_send, b_recv = refs
        e, z = lax.axis_index("expert"), lax.axis_index("group")

        def loc(r, q, c):
            s, kind = c // kinds, c % kinds
            row = (lax.rem(z - s + groups, groups) * n + flip(e, r)) * rows
            return outs[kind].at[pl.ds(pl.multiple_of(row, 16), rows), :]

        def far(c):
            s, kind = c // kinds, c % kinds
            return remote(
                ins[kind], loc(0, 0, kind), z_send.at[c], z_recv.at[c],
                {"group": lax.rem(z + s, groups)},
            )

        def landed(c):
            remote(
                loc(0, 0, c), loc(0, 0, c), z_send.at[c], z_recv.at[c],
                {"group": lax.rem(z + c // kinds, groups)},
            ).wait_recv()

        first = lax.rem(z + 1, split) * per
        follow = remote(
            bank_ref.at[pl.ds(first, per)], far_ref, b_send, b_recv, {"group": lax.rem(z + 1, groups)}
        )
        gather = Gather(
            e, lambda c: ins[c] if c < kinds else loc(0, 0, c), loc,
            [c // kinds % 2 for c in range(count)], send, recv,
        )
        near = list(range(kinds))
        later = list(range(kinds, count))
        greet(
            plane_devices(e) + [{"group": lax.rem(z + s, groups)} for s in range(1, groups)]
        )
        for c in later:
            far(c).start()
        for c in near:
            gather.begin(c)
            pltpu.make_async_copy(ins[c], loc(0, 0, c), local.at[c]).start()
        follow.start()
        gather.stage(near, (2, 4))
        gather.stage(near, (6,))
        for c in later:
            landed(c)
            gather.begin(c)
        gather.stage(later, (2, 4))
        gather.stage(later, (6,))
        gather.stage(near + later, (1, 3, 5, 7))
        for c in later:
            far(c).wait_send()
        for c in near + later:
            gather.finish(c)
        for c in near:
            pltpu.make_async_copy(ins[c], loc(0, 0, c), local.at[c]).wait()
        follow.wait()

    vmem = pl.BlockSpec(memory_space=pltpu.VMEM)
    shapes = [(groups * n * rows, one.shape[1]) for one in shares]
    return pl.pallas_call(
        kernel,
        in_specs=[vmem] * kinds + [ANY_SPEC],
        out_specs=[vmem] * kinds + [ANY_SPEC],
        out_shape=[jax.ShapeDtypeStruct(shape, BF16) for shape in shapes]
        + [jax.ShapeDtypeStruct((per,) + bank.shape[1:], BF16)],
        scratch_shapes=[
            pltpu.SemaphoreType.DMA((count,)),
            pltpu.SemaphoreType.DMA((count,)),
            pltpu.SemaphoreType.DMA((n, count)),
            pltpu.SemaphoreType.DMA((n, count)),
            pltpu.SemaphoreType.DMA((kinds,)),
            pltpu.SemaphoreType.DMA,
            pltpu.SemaphoreType.DMA,
        ],
        compiler_params=params(1),
        cost_estimate=cost(1e4, 1e3),
        name="plane_weights",
    )(*shares, bank)


def attention_pairs(n, at_me, q_ref, keys, out_ref):
    width = KEY_VALUE_HEADS * HEAD_SIZE
    prompt_ok, cont_ok = attention_masks_plain(n, at_me)

    def pair(j, carry):
        q_at = pl.ds(pl.multiple_of(j * 384, 128), 384)
        k_at = pl.ds(pl.multiple_of(j * 128, 128), 128)
        v_at = pl.ds(pl.multiple_of(width + j * 128, 128), 128)
        q_top, q_low = q_ref[:PR_DEV, q_at], q_ref[PR_DEV:, q_at]
        k_two, v_two = keys[:, k_at], keys[:, v_at]
        tops, lows = [], []
        for g in range(2):
            key = k_two[:, g * HEAD_SIZE : (g + 1) * HEAD_SIZE]
            value = v_two[:, g * HEAD_SIZE : (g + 1) * HEAD_SIZE]
            top, low = group_probs(
                head_rows(q_top, g * 192), head_rows(q_low, g * 192), key, prompt_ok, cont_ok, n
            )
            tops.append(row_heads(mm(top.astype(BF16), value[: n * PR_DEV])))
            lows.append(row_heads(mm(low.astype(BF16), value)))
        out_ref[:PR_DEV, q_at] = jnp.concatenate(tops, axis=1).astype(BF16)
        out_ref[PR_DEV:, q_at] = jnp.concatenate(lows, axis=1).astype(BF16)
        return carry

    lax.fori_loop(0, KEY_VALUE_HEADS // 2, pair, 0)


def flip_columns(slot, me, limit):
    bit, total = 1, jnp.zeros_like(slot)
    while bit < limit:
        total = total + bit * lax.rem(slot // bit + me // bit, 2)
        bit *= 2
    return total


def attention_masks_plain(n, me):
    shape = (3 * PR_DEV, n * PR_DEV)
    token = lax.rem(lax.broadcasted_iota(jnp.int32, shape, 0), PR_DEV)
    column = lax.broadcasted_iota(jnp.int32, shape, 1)
    owner = flip_columns(column // PR_DEV, me, n)
    prompt_ok = owner * PR_DEV + lax.rem(column, PR_DEV) <= me * PR_DEV + token
    slots = CONT // PR_DEV
    shape = (3 * PR_DEV, CONT)
    token = lax.rem(lax.broadcasted_iota(jnp.int32, shape, 0), PR_DEV)
    column = lax.broadcasted_iota(jnp.int32, shape, 1)
    local = lax.rem(me, slots)
    owner = flip_columns(column // PR_DEV, local, slots)
    cont_ok = owner * PR_DEV + lax.rem(column, PR_DEV) <= local * PR_DEV + token
    return prompt_ok, cont_ok


def turn_heads(x, cosine, sine):
    half = HEAD_SIZE // 2
    lane = lax.broadcasted_iota(jnp.int32, cosine.shape, 1)
    first = lax.rem(lane, HEAD_SIZE) < half
    blocks = []
    for lo in range(0, x.shape[1], LANES):
        one = x[:, lo : lo + LANES]
        other = jnp.where(first, pltpu.roll(one, LANES - half, 1), pltpu.roll(one, half, 1))
        blocks.append(one * cosine + other * sine)
    return jnp.concatenate(blocks, axis=1)


def plane_attention(normed, weight, cosine, sine, micro):
    rows, model = normed.shape
    tokens = rows // micro
    width = 2 * KEY_VALUE_HEADS * HEAD_SIZE
    query_width = QUERY_HEADS * HEAD_SIZE
    n, tile = 8, 512

    def kernel(x_ref, w_ref, cos_ref, sin_ref, out_ref, q_ref, slots, own, keys, send, recv, local):
        e = lax.axis_index("expert")
        gather = Gather(
            e, lambda c: own.at[c], lambda r, q, c: slots.at[q, c], [c % 2 for c in range(micro)],
            send, recv,
        )

        def project(lo, turned):
            wide = mm(x_ref[...], w_ref[:, lo : lo + tile])
            for c in range(micro):
                part = wide[c * tokens : (c + 1) * tokens]
                if turned:
                    part = turn_heads(part, cos_ref[...], sin_ref[...])
                yield c, part.astype(BF16)

        for lo in range(0, width, tile):
            for c, part in project(query_width + lo, lo < width // 2):
                own[c, :, lo : lo + tile] = part
        greet(plane_devices(e))
        for c in range(micro):
            gather.begin(c)
            pltpu.make_async_copy(own.at[c], slots.at[0, c], local.at[c]).start()
        for lo in range(0, query_width, tile):
            for c, part in project(lo, True):
                q_ref[c, :, lo : lo + tile] = part
        gather.stage(range(micro), (2, 4))
        gather.stage(range(micro), (6,))
        for c in range(micro):
            gather.stage([c], (1, 3, 5, 7))
            pltpu.make_async_copy(own.at[c], slots.at[0, c], local.at[c]).wait()
            load_keys(n, [slots.at[r, c] for r in range(n)], keys)
            attention_pairs(n, e, q_ref.at[c], keys, out_ref.at[c])
        for c in range(micro):
            gather.finish(c)

    vmem = pl.BlockSpec(memory_space=pltpu.VMEM)
    shape = jax.ShapeDtypeStruct((micro, tokens, query_width), BF16)
    return pl.pallas_call(
        kernel,
        in_specs=[vmem] * 4,
        out_specs=[vmem] * 3,
        out_shape=[shape, shape, jax.ShapeDtypeStruct((n, micro, tokens, width), BF16)],
        scratch_shapes=[
            pltpu.VMEM((micro, tokens, width), BF16),
            pltpu.VMEM((n * PR_DEV + CONT, width), BF16),
            pltpu.SemaphoreType.DMA((n, micro)),
            pltpu.SemaphoreType.DMA((n, micro)),
            pltpu.SemaphoreType.DMA((micro,)),
        ],
        compiler_params=params(2),
        cost_estimate=cost(1e4, 1e3),
        name="plane_attention",
    )(normed, weight, cosine, sine)


def plane_attention_backward(query, slots, d_mixed, cosine, sine):
    n, micro, tokens, width = slots.shape
    half = width // 2
    query_width = query.shape[2]
    pr = n * PR_DEV
    total = pr + CONT

    def kernel(q_ref, d_ref, kv_ref, cos_ref, sin_ref, out_ref, keys, grads, parts, *scratch):
        e = lax.axis_index("expert")
        red = Reduce(e, lambda r, c: parts.at[r, c], [c % 2 for c in range(micro)], *scratch)
        greet(plane_devices(e))
        prompt_ok, cont_ok = attention_masks_plain(n, e)

        def one_side(prob, d_rows, key, value, q_rows):
            d_prob = mm(d_rows, value, NT)
            delta = jnp.sum(prob * d_prob, axis=1, keepdims=True)
            d_score = (prob * (d_prob - delta)).astype(BF16)
            return (
                mm(d_score, key) * SCORE_SCALE,
                mm(d_score, q_rows, TN) * SCORE_SCALE,
                mm(prob.astype(BF16), d_rows, TN),
            )

        for c in range(micro):
            load_keys(n, [kv_ref.at[r, c] for r in range(n)], keys)

            def pair(j, carry):
                q_at = pl.ds(pl.multiple_of(j * 384, 128), 384)
                k_at = pl.ds(pl.multiple_of(j * 128, 128), 128)
                v_at = pl.ds(pl.multiple_of(half + j * 128, 128), 128)
                q_top, q_low = q_ref[c, :PR_DEV, q_at], q_ref[c, PR_DEV:, q_at]
                d_top, d_low = d_ref[c, :PR_DEV, q_at], d_ref[c, PR_DEV:, q_at]
                k_two, v_two = keys[:, k_at], keys[:, v_at]
                dq_tops, dq_lows, dks, dvs = [], [], [], []
                for g in range(2):
                    key = k_two[:, g * HEAD_SIZE : (g + 1) * HEAD_SIZE]
                    value = v_two[:, g * HEAD_SIZE : (g + 1) * HEAD_SIZE]
                    rows_top, rows_low = head_rows(q_top, g * 192), head_rows(q_low, g * 192)
                    top, low = group_probs(rows_top, rows_low, key, prompt_ok, cont_ok, n)
                    dq_top, dk_top, dv_top = one_side(
                        top, head_rows(d_top, g * 192), key[:pr], value[:pr], rows_top
                    )
                    dq_low, dk_low, dv_low = one_side(
                        low, head_rows(d_low, g * 192), key, value, rows_low
                    )
                    dq_tops.append(row_heads(dq_top))
                    dq_lows.append(row_heads(dq_low))
                    dks.append(jnp.concatenate([dk_low[:pr] + dk_top, dk_low[pr:]], axis=0))
                    dvs.append(jnp.concatenate([dv_low[:pr] + dv_top, dv_low[pr:]], axis=0))
                for lo, found in ((0, dq_tops), (PR_DEV, dq_lows)):
                    there = slice(lo, lo + PR_DEV)
                    turned = turn_heads(
                        jnp.concatenate(found, axis=1), cos_ref[there, :], sin_ref[there, :]
                    )
                    out_ref[c, there, q_at] = turned.astype(BF16)
                grads[:, k_at] = jnp.concatenate(dks, axis=1).astype(BF16)
                grads[:, v_at] = jnp.concatenate(dvs, axis=1).astype(BF16)
                return carry

            lax.fori_loop(0, KEY_VALUE_HEADS // 2, pair, 0)
            for r in (7, 5, 3, 1, 6, 2, 4, 0):
                parts[r, c, :PR_DEV, :] = grads[r * PR_DEV : (r + 1) * PR_DEV, :]
                if r < CONT // PR_DEV:
                    lo = (n + r) * PR_DEV
                    parts[r, c, PR_DEV:, :] = grads[lo : lo + PR_DEV, :]
                else:
                    parts[r, c, PR_DEV:, :] = jnp.zeros((PR_DEV, width), BF16)
                if r % 2:
                    red.begin(r, c)
        red.diagonal(range(micro))
        red.sides(range(micro))
        step = 16
        for c in range(micro):
            terms = red.total(c)

            def last(i, carry):
                at = pl.ds(pl.multiple_of(i * step, step), step)
                total = terms[0][at, :].astype(F32)
                for term in terms[1:]:
                    total = total + term[at, :].astype(F32)
                turned = turn_heads(total[:, :half], cos_ref[at, :], sin_ref[at, :])
                out_ref[c, at, query_width : query_width + half] = turned.astype(BF16)
                out_ref[c, at, query_width + half :] = total[:, half:].astype(BF16)
                return carry

            lax.fori_loop(0, tokens // step, last, 0)
        for c in range(micro):
            red.finish(c)

    vmem = pl.BlockSpec(memory_space=pltpu.VMEM)
    return pl.pallas_call(
        kernel,
        in_specs=[vmem] * 5,
        out_specs=vmem,
        out_shape=jax.ShapeDtypeStruct((micro, tokens, query_width + width), BF16),
        scratch_shapes=[
            pltpu.VMEM((total, width), BF16),
            pltpu.VMEM((total, width), BF16),
            pltpu.VMEM((n, micro, tokens, width), BF16),
        ]
        + reduce_scratch(micro, tokens, width),
        compiler_params=params(3),
        cost_estimate=cost(1e4, 1e3),
        name="plane_attention_backward",
    )(query, d_mixed, slots, cosine, sine)


def plane_dispatch(payload, ranks, bank, where, per, cap, model, experts):
    micro, tokens, width = payload.shape
    n, split = 8, 2
    groups = lax.axis_size("group")
    count = split * micro

    def kernel(
        at_ref, own_ref, rank_ref, bank_ref, out, weights, far_ref,
        slots, z_send, z_recv, send, recv, b_send, b_recv,
    ):
        e, z = lax.axis_index("expert"), lax.axis_index("group")
        lane = lax.broadcasted_iota(jnp.int32, (cap, LANES), 1)

        def own(c):
            return own_ref.at[c] if c < micro else slots.at[0, c]

        gather = Gather(
            e, own, lambda r, q, c: slots.at[q, c], [c % 2 for c in range(count)], send, recv
        )

        def turned(m):
            return remote(
                own_ref.at[m], slots.at[0, micro + m], z_send.at[m], z_recv.at[m],
                {"group": partner(z)},
            )

        def use(r, c):
            rows = own(c)[...] if r == 0 else slots[r, c]
            b = r * count + c
            for k in range(per):
                got = mm(pick(rank_ref[b, k : k + 1, :], cap), rows)
                out[k, b * cap : (b + 1) * cap, :] = got[:, :model].astype(BF16)
                first = at_ref[2] + k
                mine = (lane == first) | (lane == first + experts)
                total = jnp.sum(jnp.where(mine, got[:, model:], 0.0), axis=1, keepdims=True)
                weights[k, b * cap : (b + 1) * cap, :] = jnp.broadcast_to(total, (cap, LANES))

        last = groups - 1
        first = lax.rem(z + last, split) * per
        follow = remote(
            bank_ref.at[pl.ds(first, per)], far_ref, b_send, b_recv,
            {"group": lax.rem(z + last, groups)},
        )
        greet(plane_devices(e) + [{"group": lax.rem(z + s, groups)} for s in (1, last)])
        for m in range(micro):
            turned(m).start()
        follow.start()
        for m in range(micro):
            gather.begin(m)
        for m in range(micro):
            use(0, m)
        for m in range(micro):
            turned(m).wait_recv()
            gather.begin(micro + m)
            use(0, micro + m)
        gather.forward_all(range(count), use)
        for m in range(micro):
            turned(m).wait_send()
        for c in range(count):
            gather.finish(c)
        follow.wait()

    vmem = pl.BlockSpec(memory_space=pltpu.VMEM)
    total = n * count * cap
    return pl.pallas_call(
        kernel,
        in_specs=[SMEM_SPEC, vmem, vmem, ANY_SPEC],
        out_specs=[vmem, vmem, ANY_SPEC],
        out_shape=[
            jax.ShapeDtypeStruct((per, total, model), BF16),
            jax.ShapeDtypeStruct((per, total, LANES), F32),
            jax.ShapeDtypeStruct((per,) + bank.shape[1:], BF16),
        ],
        scratch_shapes=[
            pltpu.VMEM((n, count, tokens, width), BF16),
            pltpu.SemaphoreType.DMA((micro,)),
            pltpu.SemaphoreType.DMA((micro,)),
            pltpu.SemaphoreType.DMA((n, count)),
            pltpu.SemaphoreType.DMA((n, count)),
            pltpu.SemaphoreType.DMA,
            pltpu.SemaphoreType.DMA,
        ],
        compiler_params=params(4),
        cost_estimate=cost(1e4, 1e3),
        name="plane_dispatch",
    )(where, payload, ranks, bank)


def plane_return(rows, ranks, term, micro, tokens, cap):
    per, _, width = rows.shape
    n, split = 8, 2
    groups = lax.axis_size("group")
    count = split * micro
    chunks = list(range(micro, count)) + list(range(micro))

    def kernel(rank_ref, in_ref, term_ref, out, far_ref, *refs):
        parts, z_out, z_in, z_send, z_recv, t_send, t_recv, scratch = *refs[:7], refs[7:]
        e, z = lax.axis_index("expert"), lax.axis_index("group")
        red = Reduce(e, lambda r, c: parts.at[r, c], [c % 2 for c in range(count)], *scratch)

        def produce(r, c):
            b = r * count + c
            total = None
            for k in range(per):
                one = mm(
                    pick(rank_ref[b, k : k + 1, :], cap), in_ref[k, b * cap : (b + 1) * cap, :], TN
                )
                total = one if total is None else total + one
            parts[r, c] = total.astype(BF16)

        def turned(m):
            return remote(
                z_out.at[m], z_in.at[m], z_send.at[m], z_recv.at[m], {"group": partner(z)}
            )

        follow = remote(term_ref, far_ref, t_send, t_recv, {"group": lax.rem(z + 1, groups)})
        greet(plane_devices(e) + [{"group": lax.rem(z + s, groups)} for s in (1, groups - 1)])
        follow.start()
        for r in (7, 3, 5):
            for c in chunks:
                produce(r, c)
                red.begin(r, c)
        for c in chunks:
            produce(6, c)
        red.diagonal(chunks)
        for r in (2, 4):
            for c in chunks:
                produce(r, c)
        red.sides(chunks)
        for c in chunks:
            produce(1, c)
            red.begin(1, c)
        for c in chunks:
            produce(0, c)
        for c in chunks:
            terms = red.total(c)
            if c >= micro:
                add_rows(z_out.at[c - micro], terms)
                turned(c - micro).start()
            else:
                turned(c).wait_recv()
                add_rows(out.at[c], terms + [z_in.at[c]])
        for m in range(micro):
            turned(m).wait_send()
        for c in chunks:
            red.finish(c)
        follow.wait()

    vmem = pl.BlockSpec(memory_space=pltpu.VMEM)
    return pl.pallas_call(
        kernel,
        in_specs=[vmem, vmem, ANY_SPEC],
        out_specs=[vmem, ANY_SPEC],
        out_shape=[
            jax.ShapeDtypeStruct((micro, tokens, width), F32),
            jax.ShapeDtypeStruct(term.shape, BF16),
        ],
        scratch_shapes=[
            pltpu.VMEM((n, count, tokens, width), BF16),
            pltpu.VMEM((micro, tokens, width), BF16),
            pltpu.VMEM((micro, tokens, width), BF16),
            pltpu.SemaphoreType.DMA((micro,)),
            pltpu.SemaphoreType.DMA((micro,)),
            pltpu.SemaphoreType.DMA,
            pltpu.SemaphoreType.DMA,
        ]
        + reduce_scratch(count, tokens, width),
        compiler_params=params(5),
        cost_estimate=cost(1e4, 1e3),
        name="plane_return",
    )(ranks, rows, term)


def plane_gradients(products, router, gains, term, groups):
    n = 8
    depth = products[0][0].shape[1]
    widths = [b.shape[1] for a, b in products]
    width = sum(widths) + LANES
    experts = router.shape[1]
    rows = depth // (groups * n)
    tile = 512
    flat = [x for pair in products for x in pair]

    def kernel(*refs):
        ins, refs = refs[: len(flat)], refs[len(flat) :]
        router_ref, gains_ref, term_ref, out, far_ref, *refs = refs
        wide, parts, z_out, z_in, z_send, z_recv, send, recv, t_send, t_recv = refs[:10]
        scratch = refs[10:]
        e, z = lax.axis_index("expert"), lax.axis_index("group")
        red = Reduce(e, lambda r, c: parts.at[r, c], [c % 2 for c in range(groups)], *scratch)
        greet(
            plane_devices(e)
            + [{"group": lax.rem(z + s, groups)} for s in range(1, groups)]
        )
        follow = remote(
            term_ref, far_ref, t_send, t_recv, {"group": lax.rem(z + groups - 1, groups)}
        )
        follow.start()

        def cut(lo, size):
            for r in range(n):
                for s in range(groups):
                    row = (lax.rem(z + s, groups) * n + flip(e, r)) * rows
                    at = pl.ds(pl.multiple_of(row, 16), rows)
                    parts[r, s, :, lo : lo + size] = wide[at, :size].astype(BF16)

        lo = 0
        for i, count in enumerate(widths):
            for start in range(0, count, tile):
                size = min(tile, count - start)
                wide[:, :size] = mm(ins[2 * i][...], ins[2 * i + 1][:, start : start + size], TN)
                cut(lo, size)
                lo += size
        wide[:, :LANES] = jnp.zeros((depth, LANES), F32)
        wide[:, experts : 2 * experts] = router_ref[...]
        wide[:, : gains.shape[0]] = gains_ref[...].T
        cut(lo, LANES)

        chunks = list(range(1, groups)) + [0]
        for r in (7, 3, 5, 1):
            for c in chunks:
                red.begin(r, c)
        red.diagonal(chunks)
        red.sides(chunks)

        def far(s):
            return remote(
                z_out.at[s], z_in.at[s], z_send.at[s], z_recv.at[s],
                {"group": lax.rem(z + s, groups)},
            )

        for c in chunks:
            add_rows(z_out.at[c], red.total(c))
            if c:
                far(c).start()
        for c in range(1, groups):
            far(c).wait_recv()
        def place(r):
            return out.at[pl.ds(pl.multiple_of(flip(e, r) * rows, 16), rows), :]

        add_rows(place(0), [z_out.at[0]] + [z_in.at[c] for c in range(1, groups)])
        middle = width // 2 // LANES * LANES
        spans = [(0, middle), (middle, width)]

        def loc(r, q, c):
            row = pl.multiple_of(flip(e, r) * rows, 16)
            return out.at[pl.ds(row, rows), spans[c][0] : spans[c][1]]

        gather = Gather(e, lambda c: loc(0, 0, c), loc, [0, 1], send, recv)
        for c in range(2):
            gather.begin(c)
        gather.forward_all(range(2))
        for c in range(2):
            gather.finish(c)
        follow.wait()
        for c in range(1, groups):
            far(c).wait_send()
        for c in chunks:
            red.finish(c)

    vmem = pl.BlockSpec(memory_space=pltpu.VMEM)
    return pl.pallas_call(
        kernel,
        in_specs=[vmem] * (len(flat) + 2) + [ANY_SPEC],
        out_specs=[vmem, ANY_SPEC],
        out_shape=[
            jax.ShapeDtypeStruct((n * rows, width), BF16),
            jax.ShapeDtypeStruct(term.shape, BF16),
        ],
        scratch_shapes=[
            pltpu.VMEM((depth, tile), F32),
            pltpu.VMEM((n, groups, rows, width), BF16),
            pltpu.VMEM((groups, rows, width), BF16),
            pltpu.VMEM((groups, rows, width), BF16),
            pltpu.SemaphoreType.DMA((groups,)),
            pltpu.SemaphoreType.DMA((groups,)),
            pltpu.SemaphoreType.DMA((n, 2)),
            pltpu.SemaphoreType.DMA((n, 2)),
            pltpu.SemaphoreType.DMA,
            pltpu.SemaphoreType.DMA,
        ]
        + reduce_scratch(groups, rows, width),
        compiler_params=params(6),
        cost_estimate=cost(1e4, 1e3),
        name="plane_gradients",
    )(*flat, router, gains, term)


def gather_flags(slots, where, per, cap, model):
    n, count, tokens, width = slots.shape

    def kernel(at_ref, in_ref, out, ranks, flags):
        row = lax.broadcasted_iota(jnp.int32, (tokens, tokens), 0)
        col = lax.broadcasted_iota(jnp.int32, (tokens, tokens), 1)
        before = jnp.where(row < col, 1.0, 0.0).astype(BF16)
        for b in range(count):
            payload = in_ref[0, b]
            flags[...] = payload[:, model:].astype(F32).T
            picked = jnp.concatenate(
                [flags[pl.ds(at_ref[2] + k, 1), :] for k in range(per)], axis=0
            )
            slot = jnp.where(picked > 0.0, mm(picked.astype(BF16), before), -1.0)
            ranks[b] = slot
            for k in range(per):
                out[k, b * cap : (b + 1) * cap, :] = mm(
                    pick(slot[k : k + 1], cap), payload[:, :model]
                ).astype(BF16)

    return pl.pallas_call(
        kernel,
        grid_spec=pltpu.PrefetchScalarGridSpec(
            num_scalar_prefetch=1,
            grid=(n,),
            in_specs=[
                pl.BlockSpec(
                    (1, count, tokens, width),
                    lambda r, at: (jnp.bitwise_xor(at[1], r), 0, 0, 0),
                )
            ],
            out_specs=[
                pl.BlockSpec((per, count * cap, model), lambda r, at: (0, r, 0)),
                pl.BlockSpec((count, per, tokens), lambda r, at: (r, 0, 0)),
            ],
            scratch_shapes=[pltpu.VMEM((LANES, tokens), F32)],
        ),
        out_shape=[
            jax.ShapeDtypeStruct((per, n * count * cap, model), BF16),
            jax.ShapeDtypeStruct((n * count, per, tokens), F32),
        ],
        cost_estimate=cost(5e9, 3e7),
        name="gather_flags",
    )(where, slots)


def scatter_rows(rows, ranks, where, n, count, tokens, cap):
    per, _, width = rows.shape

    def kernel(at_ref, rank_ref, in_ref, out):
        for b in range(count):
            total = None
            for k in range(per):
                one = mm(
                    pick(rank_ref[b, k : k + 1, :], cap), in_ref[k, b * cap : (b + 1) * cap, :], TN
                )
                total = one if total is None else total + one
            out[0, b] = total.astype(BF16)

    return pl.pallas_call(
        kernel,
        grid_spec=pltpu.PrefetchScalarGridSpec(
            num_scalar_prefetch=1,
            grid=(n,),
            in_specs=[
                pl.BlockSpec((count, per, tokens), lambda r, at: (r, 0, 0)),
                pl.BlockSpec((per, count * cap, width), lambda r, at: (0, r, 0)),
            ],
            out_specs=pl.BlockSpec(
                (1, count, tokens, width), lambda r, at: (jnp.bitwise_xor(at[1], r), 0, 0, 0)
            ),
        ),
        out_shape=jax.ShapeDtypeStruct((n, count, tokens, width), BF16),
        cost_estimate=cost(1e4, 1e3),
        name="scatter_rows",
    )(where, ranks, rows)


def expert_steps(at, rows_in, grads_in, weights, bank, far, experts, tile):
    per, total, model = rows_in.shape
    part, ff = bank.shape[2:]
    groups = model // part
    steps = total // tile

    def kernel(at_ref, x_ref, d_ref, w_ref, *refs):
        sources, o_ref, r_ref, refs = refs[:groups], refs[groups], refs[groups + 1], refs[groups + 2 :]
        outs, (acc_wide, acc_down, wide_all, down_all, sems) = refs[:groups], refs[groups:]
        k, step = pl.program_id(0), pl.program_id(1)

        def loads(index):
            copies = []
            for s in range(groups):
                z = lax.rem(at_ref[0] - s + groups, groups)
                at_z = pl.ds(pl.multiple_of(z * part, 128), part)
                source = sources[s].at[at_ref[3] + index if s == 0 else index]
                wide, down = wide_all.at[index], down_all.at[index]
                for i, dst in enumerate([wide.at[at_z, :ff], wide.at[at_z, ff:], down.at[at_z, :]]):
                    copies.append(
                        pltpu.make_async_copy(source.at[i], dst, sems.at[index, 3 * s + i])
                    )
            return copies

        for index in range(per):

            @pl.when((k == 0) & (step == 0))
            def _():
                for one in loads(index):
                    one.start()

        for index in range(per):

            @pl.when((k == index) & (step == 0))
            def _():
                for one in loads(index):
                    one.wait()

        wide_ref, down_ref = wide_all.at[k], down_all.at[k]
        x, d = x_ref[0], d_ref[0]
        w = w_ref[0, :, 0:1]
        pre = mm(x, wide_ref[...])
        gate_pre, up_pre = pre[:, :ff], pre[:, ff:]
        sig = 1.0 / (1.0 + jnp.exp(-gate_pre))
        silu = gate_pre * sig
        active_wide = silu * up_pre
        active = active_wide.astype(BF16)
        o_ref[0] = (mm(active, down_ref[...], NT) * w).astype(BF16)
        d_raw = mm(d, down_ref[...])
        d_gates = jnp.sum(active.astype(F32) * d_raw, axis=1, keepdims=True)
        d_active = d_raw * w
        d_up = (d_active * silu).astype(BF16)
        d_gate = (d_active * up_pre * sig * (1.0 + gate_pre * (1.0 - sig))).astype(BF16)
        d_both = jnp.concatenate([d_gate, d_up], axis=1)
        r_ref[0, :, :model] = mm(d_both, wide_ref[...], NT).astype(BF16)
        high = d_gates.astype(BF16).astype(F32)
        lane = lax.broadcasted_iota(jnp.int32, (tile, LANES), 1)
        e = at_ref[2] + k
        r_ref[0, :, model:] = (
            jnp.where(lane == e, high, 0.0) + jnp.where(lane == e + experts, d_gates - high, 0.0)
        ).astype(BF16)
        new_wide = mm(x, d_both, TN)
        new_down = mm((active_wide * w).astype(BF16), d, TN)

        @pl.when(step == 0)
        def _():
            acc_wide[...] = new_wide
            acc_down[...] = new_down

        @pl.when(step > 0)
        def _():
            acc_wide[...] += new_wide
            acc_down[...] += new_down

        @pl.when(step == steps - 1)
        def _():
            for s in range(groups):
                z = lax.rem(at_ref[0] + s, groups)
                at_z = pl.ds(pl.multiple_of(z * part, 128), part)
                outs[s][0, 0] = acc_wide[at_z, :ff].astype(BF16)
                outs[s][0, 1] = acc_wide[at_z, ff:].astype(BF16)
                outs[s][0, 2] = acc_down[:, at_z].T.astype(BF16)

    grad = pl.BlockSpec((1, 3, part, ff), lambda k, t: (k, 0, 0, 0), pipeline_mode=pl.Buffered(1))
    rows = lambda width: pl.BlockSpec((1, tile, width), lambda k, t: (k, t, 0))
    out = pl.pallas_call(
        kernel,
        grid=(per, steps),
        in_specs=[SMEM_SPEC, rows(model), rows(model), rows(LANES)] + [ANY_SPEC] * groups,
        out_specs=[rows(model), rows(model + LANES)] + [grad] * groups,
        out_shape=[
            jax.ShapeDtypeStruct((per, total, model), BF16),
            jax.ShapeDtypeStruct((per, total, model + LANES), BF16),
        ]
        + [jax.ShapeDtypeStruct((per, 3, part, ff), BF16)] * groups,
        scratch_shapes=[
            pltpu.VMEM((model, 2 * ff), F32),
            pltpu.VMEM((ff, model), F32),
            pltpu.VMEM((per, model, 2 * ff), BF16),
            pltpu.VMEM((per, model, ff), BF16),
            pltpu.SemaphoreType.DMA((per, 3 * groups)),
        ],
        compiler_params=pltpu.CompilerParams(vmem_limit_bytes=62 * 1024 * 1024),
        cost_estimate=cost(18 * per * total * model * ff, 10 * per * total * model),
        name="expert_steps",
    )(at, rows_in, grads_in, weights, bank, *far)
    return out[0], out[1], list(out[2:])


def merge_grads(which, at, terms):
    per, _, part, ff = terms[0].shape
    split = 2
    tile = LANES

    def kernel(at_ref, *refs):
        ins, out = refs[: len(terms)], refs[len(terms)]
        for k in range(per):
            for parity in range(split):
                value = None
                for one in ins[parity::split]:
                    more = one[k, 0].astype(F32)
                    value = more if value is None else value + more
                index = lax.rem(at_ref[0] + parity, split) * per + k
                out[index] = value.T if which == 2 else value

    if which == 2:
        spec = pl.BlockSpec((split * per, ff, tile), lambda t: (0, 0, t))
        shape = (split * per, ff, part)
    else:
        spec = pl.BlockSpec((split * per, tile, ff), lambda t: (0, t, 0))
        shape = (split * per, part, ff)
    return pl.pallas_call(
        kernel,
        grid=(part // tile,),
        in_specs=[SMEM_SPEC]
        + [pl.BlockSpec((per, 1, tile, ff), lambda t: (0, which, t, 0))] * len(terms),
        out_specs=spec,
        out_shape=jax.ShapeDtypeStruct(shape, F32),
        cost_estimate=cost(1e5, 1e4),
        name="merge_grads",
    )(at, *terms)


def layer_plane(
    tokens,
    cotangent,
    routes,
    norm_one,
    query_key_value_weight,
    out_weight,
    norm_two,
    router_weight,
    gate_weight,
    up_weight,
    down_weight,
):
    n = lax.axis_size("expert")
    groups = lax.axis_size("group")
    me = lax.axis_index("expert")
    z = lax.axis_index("group")
    micro, count, model = tokens.shape
    exp_here, part, ff = gate_weight.shape
    experts = router_weight.shape[1]
    split = 2
    per = exp_here // split
    query_width = QUERY_HEADS * HEAD_SIZE
    kv_width = KEY_VALUE_HEADS * HEAD_SIZE
    cap = max(2, 3 * TOPK * PR_DEV // experts)
    where = jnp.stack([z, me, me * exp_here + (z % split) * per, (z % split) * per]).astype(jnp.int32)
    rows_here = part // n
    rows = micro * count

    misc = jnp.concatenate(
        [
            norm_one[:, None],
            norm_two[:, None],
            jnp.zeros((part, experts - 2), BF16),
            router_weight,
            jnp.zeros((part, LANES - 2 * experts), BF16),
        ],
        axis=1,
    )
    cut = lambda x: lax.dynamic_slice_in_dim(x, me * rows_here, rows_here, axis=0)
    shares = [cut(query_key_value_weight), jnp.concatenate([cut(out_weight), cut(misc)], axis=1)]
    bank = jnp.stack([gate_weight, up_weight, jnp.swapaxes(down_weight, 1, 2)], axis=1)

    expert_ids = jnp.arange(experts, dtype=jnp.int32)
    named = jnp.any(routes[..., None] == expert_ids, axis=2)
    pad = jnp.zeros((micro, count, LANES - experts), BF16)
    d_payload = jnp.concatenate([cotangent, named.astype(BF16), pad], axis=2)
    d_turned = turn(d_payload, 1, split)

    bank_two = lax.dynamic_slice_in_dim(bank, (z % split) * per, per, axis=0)
    x = tokens.reshape(rows, model).astype(F32)
    inverse_one = lax.rsqrt(jnp.mean(x * x, axis=-1, keepdims=True) + 1e-05)
    cosine, sine = rope_tables(me, PR_DEV * n)
    cosine = jnp.concatenate([cosine] * 4, axis=1)
    sine = jnp.concatenate([-sine, sine] * 2, axis=1)
    both = jnp.concatenate([d_payload, d_turned], axis=0)
    both, bank_two, inverse_one, cosine, sine, shares = lax.optimization_barrier(
        (both, bank_two, inverse_one, cosine, sine, shares)
    )
    d_slots = lax.all_gather(both, "expert", axis=0)
    qkv_full, rest_full, far_one = plane_weights(shares, bank, per)
    bank_two, qkv_full = lax.optimization_barrier((bank_two, qkv_full))
    far_two = shift(bank_two, 2)
    out_full, misc_full = rest_full[:, :model], rest_full[:, model:]
    gain_one = misc_full[:, 0].astype(F32)
    gain_two = misc_full[:, 1].astype(F32)
    router_full = misc_full[:, experts : 2 * experts]

    grads_in, ranks = gather_flags(d_slots, where, per, cap, model)

    normed = (x * inverse_one * gain_one).astype(BF16)
    mixed, query, kv_slots = plane_attention(normed, qkv_full, cosine, sine, micro)
    mixed = mixed.reshape(rows, query_width)
    hidden = x + mm(mixed, out_full)
    inverse_two = lax.rsqrt(jnp.mean(hidden * hidden, axis=-1, keepdims=True) + 1e-05)
    normed_two = (hidden * inverse_two * gain_two).astype(BF16)
    logits = mm(normed_two, router_full)
    chosen = named.reshape(rows, experts)
    logits = jnp.where(chosen, logits, NEG_FILL)
    top = jnp.max(logits, axis=-1, keepdims=True)
    raised = jnp.where(chosen, jnp.exp(logits - top), 0.0)
    gate_probs = raised / jnp.sum(raised, axis=-1, keepdims=True)

    high = gate_probs.astype(BF16)
    low = (gate_probs - high.astype(F32)).astype(BF16)
    payload = jnp.concatenate(
        [normed_two, high, low, jnp.zeros((rows, LANES - 2 * experts), BF16)], axis=1
    ).reshape(micro, count, model + LANES)
    rows_in, row_weights, far_three = plane_dispatch(
        payload, ranks, bank, where, per, cap, model, experts
    )
    weights_far = [far_one, far_two, far_three]
    tile = 2 * micro * split * cap
    outs, backs, weight_terms = expert_steps(
        where, rows_in, grads_in, row_weights, bank, weights_far, experts, tile
    )
    back, term_one = plane_return(backs, ranks, weight_terms[1], micro, count, cap)
    back = back.reshape(rows, model + LANES)

    late, back = lax.optimization_barrier((weight_terms[2], back))
    term_two = shift(late, 2)

    d_out = cotangent.reshape(rows, model).astype(F32)
    d_gates = back[:, model : model + experts] + back[:, model + experts : model + 2 * experts]
    d_logits = gate_probs * (d_gates - jnp.sum(gate_probs * d_gates, axis=-1, keepdims=True))
    router_grad = lax.dot_general(normed_two.astype(F32), d_logits, TN, precision=HIGHEST)
    d_normed_two = back[:, :model] + lax.dot_general(
        d_logits, router_full.astype(F32), NT, precision=HIGHEST
    )

    def rms_back(inputs, inverse, gain, upstream):
        scaled = gain * upstream
        return inverse * scaled - inputs * inverse * inverse * inverse * jnp.mean(
            scaled * inputs, axis=-1, keepdims=True
        )

    grad_two = jnp.sum(d_normed_two * hidden * inverse_two, axis=0)
    d_hidden = d_out + rms_back(hidden, inverse_two, gain_two, d_normed_two)
    d_attn = d_hidden.astype(BF16)
    outs, d_attn = lax.optimization_barrier((outs, d_attn))
    mixture_parts = scatter_rows(outs, ranks, where, n, micro * split, count, cap)
    mixture_sum = lax.psum_scatter(mixture_parts, "expert", scatter_dimension=0, tiled=False)
    d_mixed = mm(d_attn, out_full, NT).astype(BF16).reshape(micro, count, query_width)
    d_project = plane_attention_backward(query, kv_slots, d_mixed, cosine, -sine)
    d_project = d_project.reshape(rows, query_width + 2 * kv_width)
    d_normed = mm(d_project, qkv_full, NT)
    grad_one = jnp.sum(d_normed * x * inverse_one, axis=0)
    input_grad = (d_hidden + rms_back(x, inverse_one, gain_one, d_normed)).reshape(tokens.shape)
    gains = jnp.concatenate([grad_one[None], grad_two[None], jnp.zeros((6, model), F32)], axis=0)
    dense, term_three = plane_gradients(
        [(mixed, d_attn), (normed, d_project)], router_grad, gains, weight_terms[3], groups
    )
    mixture_sum, dense = lax.optimization_barrier((mixture_sum, dense))
    mixture_far, dense = lax.optimization_barrier((turn(mixture_sum[micro:], 1, split), dense))
    mixture = mixture_sum[:micro].astype(F32) + mixture_far.astype(F32)
    block_out = (hidden + mixture.reshape(rows, model)).astype(BF16).reshape(tokens.shape)
    terms = [weight_terms[0], term_one, term_two, term_three]
    gate_grad, up_grad, down_grad = [merge_grads(which, where, terms) for which in range(3)]
    misc_sum = dense[:, model + query_width + 2 * kv_width :].astype(F32)
    return (
        block_out,
        input_grad,
        misc_sum[:, 0],
        dense[:, model : model + query_width + 2 * kv_width].astype(F32),
        dense[:, :model].astype(F32),
        misc_sum[:, 1],
        misc_sum[:, experts : 2 * experts],
        gate_grad,
        up_grad,
        down_grad,
    )


def per_device(*arrays):
    n, groups = lax.axis_size("expert"), lax.axis_size("group")
    exp_here, part, ff = arrays[8].shape
    plane = (
        n == 8
        and exp_here % 2 == 0
        and groups == 4
        and part % (16 * n) == 0
        and part % LANES == 0
        and arrays[0].shape[0] == 2
    )
    return (layer_plane if plane else layer_general)(*arrays)


def solution(mesh):
    rows = P(None, ("group", "expert"), None)
    return jax.shard_map(
        per_device,
        mesh=mesh,
        in_specs=(
            rows,
            rows,
            rows,
            P("group"),
            P("group", None),
            P("group", None),
            P("group"),
            P("group", None),
            P("expert", "group", None),
            P("expert", "group", None),
            P("expert", None, "group"),
        ),
        out_specs=(
            rows,
            rows,
            P("group"),
            P("group", None),
            P("group", None),
            P("group"),
            P("group", None),
            P("expert", "group", None),
            P("expert", "group", None),
            P("expert", None, "group"),
        ),
        check_vma=False,
    )
```

```python
import functools

import jax
import jax.numpy as jnp
from jax import lax
from jax.experimental import pallas as pl
from jax.experimental.pallas import tpu as pltpu
from jax.sharding import PartitionSpec as P

QUERY_HEADS = 24
KEY_VALUE_HEADS = 8
HEAD_SIZE = 64
TOPK = 8
CONT = 256
PR_DEV = 64
LANES = 128
SCORE_SCALE = 0.125
NEG_FILL = -1e30
HIGHEST = lax.Precision.HIGHEST
F32 = jnp.float32
BF16 = jnp.bfloat16

NN = (((1,), (0,)), ((), ()))
NT = (((1,), (1,)), ((), ()))
TN = (((0,), (0,)), ((), ()))


def mm(a, b, dims=NN):
    return lax.dot_general(a, b, dims, preferred_element_type=F32)


def swap(x, bit):
    n = lax.axis_size("expert")
    return lax.ppermute(x, "expert", [(i, i ^ bit) for i in range(n)])


def shift(x, step):
    n = lax.axis_size("group")
    return lax.ppermute(x, "group", [(i, (i + step) % n) for i in range(n)])


def turn(x, step, split):
    n = lax.axis_size("group")
    return lax.ppermute(
        x, "group", [((i // split) * split + (i + step) % split, i) for i in range(n)]
    )


def outer_bits(n):
    return [1 << i for i in range(1, n.bit_length() - 1)]


def spread(x, order):
    n = lax.axis_size("expert")
    outer = outer_bits(n)
    if len(outer) == 2:
        a, b = outer
        xa, xb = swap(x, a), swap(x, b)
        slots = {0: x, a: xa, b: xb, a ^ b: swap(xa, b) if order == 0 else swap(xb, a)}
    else:
        slots = {0: x}
        for bit in outer:
            slots.update({r ^ bit: swap(y, bit) for r, y in list(slots.items())})
    if n > 1:
        slots.update({r ^ 1: swap(y, 1) for r, y in list(slots.items())})
    return [slots[r] for r in range(n)]


def plus(a, b):
    return (a.astype(F32) + b.astype(F32)).astype(BF16)


def collect(parts, order):
    n = lax.axis_size("expert")
    outer = outer_bits(n)
    keep = {r: parts[r] for r in range(n)}
    if n > 1:
        keep = {r: plus(keep[r], swap(keep[r ^ 1], 1)) for r in range(0, n, 2)}
    if len(outer) == 2:
        a, b = outer
        if order == 0:
            keep[a] = plus(keep[a], swap(keep[a ^ b], b))
        else:
            keep[b] = plus(keep[b], swap(keep[a ^ b], a))
        return (
            keep[0].astype(F32) + swap(keep[a], a).astype(F32) + swap(keep[b], b).astype(F32)
        )
    for bit in reversed(outer):
        keep = {r: plus(keep[r], swap(keep[r ^ bit], bit)) for r in keep if not r & bit}
    return keep[0].astype(F32)


def full_spec(shape):
    return pl.BlockSpec(shape, lambda *_: (0,) * len(shape))


SMEM_SPEC = pl.BlockSpec(memory_space=pltpu.SMEM)
ANY_SPEC = pl.BlockSpec(memory_space=pl.ANY)


def cost(flops, moved):
    return pl.CostEstimate(flops=int(flops), bytes_accessed=int(moved), transcendentals=0)


def assemble(pieces, place, shape, where):
    count = len(pieces)

    def kernel(at_ref, *refs):
        ins, out, sems = refs[:count], refs[count], refs[count + 1]
        copies = []
        for i in range(count):
            row, column = place(i, at_ref[0], at_ref[1])
            r, c = pieces[i].shape
            copies.append(
                pltpu.make_async_copy(
                    ins[i],
                    out.at[pl.ds(pl.multiple_of(row, 16), r), pl.ds(pl.multiple_of(column, 128), c)],
                    sems.at[i],
                )
            )
        for one in copies:
            one.start()
        for one in copies:
            one.wait()

    return pl.pallas_call(
        kernel,
        grid=(1,),
        in_specs=[SMEM_SPEC] + [ANY_SPEC] * count,
        out_specs=full_spec(shape),
        out_shape=jax.ShapeDtypeStruct(shape, pieces[0].dtype),
        scratch_shapes=[pltpu.SemaphoreType.DMA((count,))],
        cost_estimate=cost(0, 4 * shape[0] * shape[1]),
        name="assemble",
    )(where, *pieces)


def gather_dense(piece, cuts, where):
    groups, n = lax.axis_size("group"), lax.axis_size("expert")
    rows, columns = piece.shape
    own = [piece[:, lo:hi] for lo, hi in cuts]
    far = [[shift(x, s) for x in own] for s in range(1, groups)]
    names, pieces = [], []
    for h, (lo, hi) in enumerate(cuts):
        joined = jnp.concatenate([far[s - 1][h] for s in range(1, groups)], axis=0)
        for r, x in enumerate(spread(own[h], h % 2)):
            names.append((0, r, lo))
            pieces.append(x)
        for r, x in enumerate(spread(joined, h % 2)):
            for s in range(1, groups):
                names.append((s, r, lo))
                pieces.append((x, (s - 1) * rows, rows))
    total = groups * n * rows
    arrays, index = [], []
    for entry in pieces:
        if isinstance(entry, tuple):
            if not arrays or arrays[-1] is not entry[0]:
                arrays.append(entry[0])
            index.append((len(arrays) - 1, entry[1], entry[2]))
        else:
            arrays.append(entry)
            index.append((len(arrays) - 1, 0, rows))
    count, held = len(index), len(arrays)

    def kernel(at_ref, *refs):
        ins, out, sems = refs[:held], refs[held], refs[held + 1]
        copies = []
        for i, (which, start, size) in enumerate(index):
            s, r, lo = names[i]
            z = lax.rem(at_ref[0] - s + groups, groups)
            e = jnp.bitwise_xor(at_ref[1], r)
            row = pl.multiple_of((z * n + e) * rows, 16)
            width = arrays[which].shape[1]
            copies.append(
                pltpu.make_async_copy(
                    ins[which].at[pl.ds(start, size)],
                    out.at[pl.ds(row, rows), pl.ds(lo, width)],
                    sems.at[i],
                )
            )
        for one in copies:
            one.start()
        for one in copies:
            one.wait()

    whole = pl.pallas_call(
        kernel,
        grid=(1,),
        in_specs=[SMEM_SPEC] + [ANY_SPEC] * held,
        out_specs=full_spec((total, columns)),
        out_shape=jax.ShapeDtypeStruct((total, columns), piece.dtype),
        scratch_shapes=[pltpu.SemaphoreType.DMA((count,))],
        cost_estimate=cost(0, 4 * total * columns),
        name="join_rows",
    )(where, *arrays)
    return whole, far


def sliced_outer(a, b, extra, groups, n, where):
    depth = a.shape[1]
    columns = b.shape[1]
    more = 0 if extra is None else extra.shape[1]
    rows = depth // (groups * n)

    def kernel(at_ref, a_ref, b_ref, *refs):
        if more:
            x_ref, refs = refs[0], refs[1:]
        outs, acc = refs[:n], refs[n]
        acc[:, :columns] = mm(a_ref[...], b_ref[...], TN)
        if more:
            acc[:, columns:] = x_ref[...]
        for r in range(n):
            e = jnp.bitwise_xor(at_ref[1], r)
            for s in range(groups):
                z = lax.rem(at_ref[0] + s, groups)
                row = pl.multiple_of((z * n + e) * rows, 16)
                outs[r][s] = acc[pl.ds(row, rows), :].astype(BF16)

    width = columns + more
    return pl.pallas_call(
        kernel,
        grid=(1,),
        in_specs=[SMEM_SPEC, full_spec(a.shape), full_spec(b.shape)]
        + ([full_spec(extra.shape)] if more else []),
        out_specs=[full_spec((groups, rows, width))] * n,
        out_shape=[jax.ShapeDtypeStruct((groups, rows, width), BF16)] * n,
        scratch_shapes=[pltpu.VMEM((depth, width), F32)],
        cost_estimate=cost(2 * a.shape[0] * depth * columns, 2 * depth * width),
        name="sliced_outer",
    )(where, a, b, *([extra] if more else []))


def reduce_dense(parts, order, where):
    groups, n = lax.axis_size("group"), lax.axis_size("expert")
    mine = collect(parts, order)
    total = mine[0]
    low = mine.astype(BF16)
    for s in range(1, groups):
        total = total + shift(low[s], s).astype(F32)
    rows, width = total.shape
    slots = spread(total.astype(BF16), order)

    def kernel(at_ref, *refs):
        out = refs[n]
        for r in range(n):
            e = jnp.bitwise_xor(at_ref[1], r)
            out[pl.ds(pl.multiple_of(e * rows, 16), rows), :] = refs[r][...].astype(F32)

    return pl.pallas_call(
        kernel,
        grid=(1,),
        in_specs=[SMEM_SPEC] + [full_spec((rows, width))] * n,
        out_specs=full_spec((n * rows, width)),
        out_shape=jax.ShapeDtypeStruct((n * rows, width), F32),
        cost_estimate=cost(0, 6 * n * rows * width),
        name="join_sums",
    )(where, *slots)


def attention_masks(n, me):
    shape = (3 * PR_DEV, n * PR_DEV)
    token = lax.rem(lax.broadcasted_iota(jnp.int32, shape, 0), PR_DEV)
    column = lax.broadcasted_iota(jnp.int32, shape, 1)
    key_pos = jnp.bitwise_xor(column // PR_DEV, me) * PR_DEV + lax.rem(column, PR_DEV)
    prompt_ok = key_pos <= me * PR_DEV + token
    slots = CONT // PR_DEV
    shape = (3 * PR_DEV, CONT)
    token = lax.rem(lax.broadcasted_iota(jnp.int32, shape, 0), PR_DEV)
    column = lax.broadcasted_iota(jnp.int32, shape, 1)
    owner = jnp.bitwise_xor(column // PR_DEV, lax.rem(me, slots))
    cont_ok = owner * PR_DEV + lax.rem(column, PR_DEV) <= lax.rem(me, slots) * PR_DEV + token
    return prompt_ok, cont_ok


def head_rows(x, base):
    return jnp.concatenate(
        [x[:, base + i * HEAD_SIZE : base + (i + 1) * HEAD_SIZE] for i in range(3)], axis=0
    )


def row_heads(x):
    return jnp.concatenate([x[i * PR_DEV : (i + 1) * PR_DEV] for i in range(3)], axis=1)


def softmax(scores):
    top = jnp.max(scores, axis=1, keepdims=True)
    weight = jnp.exp(scores - top)
    return weight * (1.0 / jnp.sum(weight, axis=1, keepdims=True))


def load_keys(n, kv_refs, keys):
    for r in range(n):
        keys[r * PR_DEV : (r + 1) * PR_DEV, :] = kv_refs[r][:PR_DEV, :]
    for r in range(CONT // PR_DEV):
        lo = (n + r) * PR_DEV
        keys[lo : lo + PR_DEV, :] = kv_refs[r][PR_DEV:, :]


def group_probs(q_top, q_low, key, prompt_ok, cont_ok, n):
    pr = n * PR_DEV
    top = mm(q_top, key[:pr], NT) * SCORE_SCALE
    top = softmax(jnp.where(prompt_ok, top, NEG_FILL))
    low = mm(q_low, key, NT) * SCORE_SCALE
    low = jnp.concatenate([low[:, :pr], jnp.where(cont_ok, low[:, pr:], NEG_FILL)], axis=1)
    return top, softmax(low)


def attention_forward(query, slots, where):
    n = len(slots)
    width = KEY_VALUE_HEADS * HEAD_SIZE
    tokens = 2 * PR_DEV
    total = n * PR_DEV + CONT

    def kernel(at_ref, q_ref, *refs):
        kv_refs, out_ref, keys = refs[:n], refs[n], refs[n + 1]
        load_keys(n, kv_refs, keys)
        prompt_ok, cont_ok = attention_masks(n, at_ref[1])

        def pair(j, carry):
            q_at = pl.ds(pl.multiple_of(j * 384, 128), 384)
            k_at = pl.ds(pl.multiple_of(j * 128, 128), 128)
            v_at = pl.ds(pl.multiple_of(width + j * 128, 128), 128)
            q_top, q_low = q_ref[:PR_DEV, q_at], q_ref[PR_DEV:, q_at]
            k_two, v_two = keys[:, k_at], keys[:, v_at]
            tops, lows = [], []
            for g in range(2):
                key = k_two[:, g * HEAD_SIZE : (g + 1) * HEAD_SIZE]
                value = v_two[:, g * HEAD_SIZE : (g + 1) * HEAD_SIZE]
                top, low = group_probs(
                    head_rows(q_top, g * 192), head_rows(q_low, g * 192), key, prompt_ok, cont_ok, n
                )
                tops.append(row_heads(mm(top.astype(BF16), value[: n * PR_DEV])))
                lows.append(row_heads(mm(low.astype(BF16), value)))
            out_ref[:PR_DEV, q_at] = jnp.concatenate(tops, axis=1).astype(BF16)
            out_ref[PR_DEV:, q_at] = jnp.concatenate(lows, axis=1).astype(BF16)
            return carry

        lax.fori_loop(0, KEY_VALUE_HEADS // 2, pair, 0)

    return pl.pallas_call(
        kernel,
        grid=(1,),
        in_specs=[SMEM_SPEC, full_spec(query.shape)] + [full_spec((tokens, 2 * width))] * n,
        out_specs=full_spec(query.shape),
        out_shape=jax.ShapeDtypeStruct(query.shape, BF16),
        scratch_shapes=[pltpu.VMEM((total, 2 * width), BF16)],
        cost_estimate=cost(8e9, 4e6),
        name="attention_forward",
    )(where, query, *slots)


def attention_backward(query, slots, d_mixed, where):
    n = len(slots)
    width = KEY_VALUE_HEADS * HEAD_SIZE
    tokens = 2 * PR_DEV
    pr = n * PR_DEV
    total = pr + CONT

    def kernel(at_ref, q_ref, d_ref, *refs):
        kv_refs, refs = refs[:n], refs[n:]
        dq_ref, outs, keys, grads = refs[0], refs[1 : 1 + n], refs[1 + n], refs[2 + n]
        load_keys(n, kv_refs, keys)
        prompt_ok, cont_ok = attention_masks(n, at_ref[1])

        def one_side(prob, d_rows, key, value, q_rows):
            d_prob = mm(d_rows, value, NT)
            delta = jnp.sum(prob * d_prob, axis=1, keepdims=True)
            d_score = (prob * (d_prob - delta)).astype(BF16)
            return (
                mm(d_score, key) * SCORE_SCALE,
                mm(d_score, q_rows, TN) * SCORE_SCALE,
                mm(prob.astype(BF16), d_rows, TN),
            )

        def pair(j, carry):
            q_at = pl.ds(pl.multiple_of(j * 384, 128), 384)
            k_at = pl.ds(pl.multiple_of(j * 128, 128), 128)
            v_at = pl.ds(pl.multiple_of(width + j * 128, 128), 128)
            q_top, q_low = q_ref[:PR_DEV, q_at], q_ref[PR_DEV:, q_at]
            d_top, d_low = d_ref[:PR_DEV, q_at], d_ref[PR_DEV:, q_at]
            k_two, v_two = keys[:, k_at], keys[:, v_at]
            dq_tops, dq_lows, dks, dvs = [], [], [], []
            for g in range(2):
                key = k_two[:, g * HEAD_SIZE : (g + 1) * HEAD_SIZE]
                value = v_two[:, g * HEAD_SIZE : (g + 1) * HEAD_SIZE]
                rows_top, rows_low = head_rows(q_top, g * 192), head_rows(q_low, g * 192)
                top, low = group_probs(rows_top, rows_low, key, prompt_ok, cont_ok, n)
                dq_top, dk_top, dv_top = one_side(
                    top, head_rows(d_top, g * 192), key[:pr], value[:pr], rows_top
                )
                dq_low, dk_low, dv_low = one_side(
                    low, head_rows(d_low, g * 192), key, value, rows_low
                )
                dq_tops.append(row_heads(dq_top))
                dq_lows.append(row_heads(dq_low))
                dks.append(jnp.concatenate([dk_low[:pr] + dk_top, dk_low[pr:]], axis=0))
                dvs.append(jnp.concatenate([dv_low[:pr] + dv_top, dv_low[pr:]], axis=0))
            dq_ref[:PR_DEV, q_at] = jnp.concatenate(dq_tops, axis=1)
            dq_ref[PR_DEV:, q_at] = jnp.concatenate(dq_lows, axis=1)
            grads[:, k_at] = jnp.concatenate(dks, axis=1).astype(BF16)
            grads[:, v_at] = jnp.concatenate(dvs, axis=1).astype(BF16)
            return carry

        lax.fori_loop(0, KEY_VALUE_HEADS // 2, pair, 0)
        for r in range(n):
            outs[r][:PR_DEV, :] = grads[r * PR_DEV : (r + 1) * PR_DEV, :]
            if r < CONT // PR_DEV:
                lo = (n + r) * PR_DEV
                outs[r][PR_DEV:, :] = grads[lo : lo + PR_DEV, :]
            else:
                outs[r][PR_DEV:, :] = jnp.zeros((PR_DEV, 2 * width), BF16)

    out = pl.pallas_call(
        kernel,
        grid=(1,),
        in_specs=[SMEM_SPEC, full_spec(query.shape), full_spec(query.shape)]
        + [full_spec((tokens, 2 * width))] * n,
        out_specs=[full_spec(query.shape)] + [full_spec((tokens, 2 * width))] * n,
        out_shape=[jax.ShapeDtypeStruct(query.shape, F32)]
        + [jax.ShapeDtypeStruct((tokens, 2 * width), BF16)] * n,
        scratch_shapes=[pltpu.VMEM((total, 2 * width), BF16), pltpu.VMEM((total, 2 * width), BF16)],
        cost_estimate=cost(2e10, 8e6),
        name="attention_backward",
    )(where, query, d_mixed, *slots)
    return out[0], out[1:]


def pick(slot_row, cap):
    rows = lax.broadcasted_iota(jnp.int32, (cap, slot_row.shape[1]), 0).astype(F32)
    return jnp.where(slot_row == rows, 1.0, 0.0).astype(BF16)


def dispatch_grads(arrays, at, per, cap, model, buffers, place, blocks_total):
    count = len(arrays)
    split, tokens, width = arrays[0].shape
    blocks = count * split
    first = buffers is None

    def kernel(at_ref, *refs):
        ins = refs[:count]
        out, ranks = refs[-3], refs[-2]
        flags = refs[-1]
        row = lax.broadcasted_iota(jnp.int32, (tokens, tokens), 0)
        col = lax.broadcasted_iota(jnp.int32, (tokens, tokens), 1)
        before = jnp.where(row < col, 1.0, 0.0).astype(BF16)
        for i in range(count):
            for j in range(split):
                b = i * split + j
                payload = ins[i][j]
                flags[...] = payload[:, model:].astype(F32).T
                picked = jnp.concatenate(
                    [flags[pl.ds(at_ref[2] + k, 1), :] for k in range(per)], axis=0
                )
                rank = mm(picked.astype(BF16), before)
                slot = jnp.where(picked > 0.0, rank, -1.0)
                ranks[b] = slot
                for k in range(per):
                    out[k, b * cap : (b + 1) * cap, :] = mm(
                        pick(slot[k : k + 1], cap), payload[:, :model]
                    ).astype(BF16)

    shapes = [
        jax.ShapeDtypeStruct((per, blocks_total * cap, model), BF16),
        jax.ShapeDtypeStruct((blocks_total, per, tokens), F32),
    ]
    return pl.pallas_call(
        kernel,
        grid=(1,),
        in_specs=[SMEM_SPEC]
        + [full_spec(arrays[0].shape)] * count
        + ([] if first else [ANY_SPEC] * 2),
        out_specs=[
            pl.BlockSpec((per, blocks * cap, model), lambda *_: (0, place, 0)),
            pl.BlockSpec((blocks, per, tokens), lambda *_: (place, 0, 0)),
        ],
        out_shape=shapes,
        scratch_shapes=[pltpu.VMEM((LANES, tokens), F32)],
        input_output_aliases={} if first else {1 + count: 0, 2 + count: 1},
        cost_estimate=cost(1e9, 6e6),
        name="dispatch_grads",
    )(at, *arrays, *([] if first else buffers))


def dispatch_rows(arrays, ranks, at, per, cap, model, experts, buffers, place, blocks_total):
    count = len(arrays)
    split, tokens, width = arrays[0].shape
    blocks = count * split
    first = buffers is None

    def kernel(at_ref, rank_ref, *refs):
        ins = refs[:count]
        out, weights = refs[-2], refs[-1]
        lane = lax.broadcasted_iota(jnp.int32, (cap, LANES), 1)
        for i in range(count):
            for j in range(split):
                b = i * split + j
                payload = ins[i][j]
                for k in range(per):
                    got = mm(pick(rank_ref[b, k : k + 1, :], cap), payload)
                    out[k, b * cap : (b + 1) * cap, :] = got[:, :model].astype(BF16)
                    tail = got[:, model:]
                    e = at_ref[2] + k
                    mine = (lane == e) | (lane == e + experts)
                    total = jnp.sum(jnp.where(mine, tail, 0.0), axis=1, keepdims=True)
                    weights[k, b * cap : (b + 1) * cap, :] = jnp.broadcast_to(total, (cap, LANES))

    shapes = [
        jax.ShapeDtypeStruct((per, blocks_total * cap, model), BF16),
        jax.ShapeDtypeStruct((per, blocks_total * cap, LANES), F32),
    ]
    return pl.pallas_call(
        kernel,
        grid=(1,),
        in_specs=[SMEM_SPEC, pl.BlockSpec((blocks, per, tokens), lambda *_: (place, 0, 0))]
        + [full_spec(arrays[0].shape)] * count
        + ([] if first else [ANY_SPEC] * 2),
        out_specs=[
            pl.BlockSpec((per, blocks * cap, model), lambda *_: (0, place, 0)),
            pl.BlockSpec((per, blocks * cap, LANES), lambda *_: (0, place, 0)),
        ],
        out_shape=shapes,
        input_output_aliases={} if first else {2 + count: 0, 3 + count: 1},
        cost_estimate=cost(1e9, 6e6),
        name="dispatch_rows",
    )(at, ranks, *arrays, *([] if first else buffers))


def run_expert(k, at, rows_in, grads_in, weights, gate, up, down, experts, tile, groups, cut):
    per, total, model = rows_in.shape
    ff = gate.shape[1]
    part = model // groups
    steps = total // tile

    def kernel(at_ref, x_ref, d_ref, w_ref, gate_ref, up_ref, down_ref, o_ref, r_ref, *refs):
        outs, (acc_gate, acc_up, acc_down) = refs[:-3], refs[-3:]
        step = pl.program_id(0)
        x, d = x_ref[0], d_ref[0]
        w = w_ref[0, :, 0:1]
        gate_pre = mm(x, gate_ref[...])
        up_pre = mm(x, up_ref[...])
        sig = 1.0 / (1.0 + jnp.exp(-gate_pre))
        silu = gate_pre * sig
        active_wide = silu * up_pre
        active = active_wide.astype(BF16)
        out = mm(active, down_ref[...])
        o_ref[...] = (out * w).astype(BF16)
        d_raw = mm(d, down_ref[...], NT)
        d_gates = jnp.sum(active.astype(F32) * d_raw, axis=1, keepdims=True)
        d_active = d_raw * w
        d_up = (d_active * silu).astype(BF16)
        d_gate = (d_active * up_pre * sig * (1.0 + gate_pre * (1.0 - sig))).astype(BF16)
        d_row = mm(d_gate, gate_ref[...], NT) + mm(d_up, up_ref[...], NT)
        r_ref[:, :model] = d_row.astype(BF16)
        high = d_gates.astype(BF16).astype(F32)
        lane = lax.broadcasted_iota(jnp.int32, (tile, LANES), 1)
        e = at_ref[2] + k
        r_ref[:, model:] = (
            jnp.where(lane == e, high, 0.0) + jnp.where(lane == e + experts, d_gates - high, 0.0)
        ).astype(BF16)
        new_gate = mm(x, d_gate, TN)
        new_up = mm(x, d_up, TN)
        new_down = mm((active_wide * w).astype(BF16), d, TN)

        @pl.when(step == 0)
        def _():
            acc_gate[...] = new_gate
            acc_up[...] = new_up
            acc_down[...] = new_down

        @pl.when(step > 0)
        def _():
            acc_gate[...] += new_gate
            acc_up[...] += new_up
            acc_down[...] += new_down

        @pl.when(step == steps - 1)
        def _():
            if cut:
                for s in range(groups):
                    z = lax.rem(at_ref[0] + s, groups)
                    at_z = pl.ds(pl.multiple_of(z * part, 128), part)
                    outs[s][...] = acc_gate[at_z, :].astype(BF16)
                    outs[groups + s][...] = acc_up[at_z, :].astype(BF16)
                    outs[2 * groups + s][...] = acc_down[:, at_z].astype(BF16)
            else:
                outs[0][...] = acc_gate[...].astype(BF16)
                outs[1][...] = acc_up[...].astype(BF16)
                outs[2][...] = acc_down[...].astype(BF16)

    if cut:
        grads = [(part, ff)] * (2 * groups) + [(ff, part)] * groups
    else:
        grads = [(model, ff)] * 2 + [(ff, model)]
    row_spec = pl.BlockSpec((1, tile, model), lambda t: (k, t, 0))
    held = lambda shape: pl.BlockSpec(shape, lambda t: (0, 0), pipeline_mode=pl.Buffered(1))
    out = pl.pallas_call(
        kernel,
        grid=(steps,),
        in_specs=[
            SMEM_SPEC,
            row_spec,
            row_spec,
            pl.BlockSpec((1, tile, LANES), lambda t: (k, t, 0)),
            held((model, ff)),
            held((model, ff)),
            held((ff, model)),
        ],
        out_specs=[
            pl.BlockSpec((tile, model), lambda t: (t, 0)),
            pl.BlockSpec((tile, model + LANES), lambda t: (t, 0)),
        ]
        + [held(shape) for shape in grads],
        out_shape=[
            jax.ShapeDtypeStruct((total, model), BF16),
            jax.ShapeDtypeStruct((total, model + LANES), BF16),
        ]
        + [jax.ShapeDtypeStruct(shape, BF16) for shape in grads],
        scratch_shapes=[
            pltpu.VMEM((model, ff), F32),
            pltpu.VMEM((model, ff), F32),
            pltpu.VMEM((ff, model), F32),
        ],
        compiler_params=pltpu.CompilerParams(vmem_limit_bytes=62 * 1024 * 1024),
        cost_estimate=cost(18 * total * model * ff, 10 * total * model),
        name="run_expert",
    )(at, rows_in, grads_in, weights, gate, up, down)
    return out[0], out[1], out[2:]


def combine(rows, ranks, count, split, tokens, cap, place):
    per = len(rows)
    width = rows[0].shape[1]
    blocks = count * split

    def kernel(rank_ref, *refs):
        ins, outs = refs[:per], refs[per:]
        for i in range(count):
            for j in range(split):
                b = i * split + j
                total = None
                for k in range(per):
                    one = mm(
                        pick(rank_ref[b, k : k + 1, :], cap), ins[k][b * cap : (b + 1) * cap, :], TN
                    )
                    total = one if total is None else total + one
                outs[i][j] = total.astype(BF16)

    return pl.pallas_call(
        kernel,
        grid=(1,),
        in_specs=[pl.BlockSpec((blocks, per, tokens), lambda *_: (place, 0, 0))]
        + [pl.BlockSpec((blocks * cap, width), lambda *_: (place, 0))] * per,
        out_specs=[full_spec((split, tokens, width))] * count,
        out_shape=[jax.ShapeDtypeStruct((split, tokens, width), BF16)] * count,
        cost_estimate=cost(1e9, 6e6),
        name="combine",
    )(ranks, *rows)


def rope_tables(my_index, prompt_len):
    half = HEAD_SIZE // 2
    local = jnp.arange(2 * PR_DEV, dtype=jnp.int32)
    cont = my_index * PR_DEV + local - PR_DEV
    position = jnp.where(local < PR_DEV, my_index * PR_DEV + local, prompt_len + cont % CONT)
    frequency = 10000.0 ** (-jnp.arange(half, dtype=F32) * (2.0 / HEAD_SIZE))
    angle = position.astype(F32)[:, None] * frequency[None, :]
    return jnp.cos(angle), jnp.sin(angle)


def rotate(x, cosine, sine):
    half = HEAD_SIZE // 2
    column = lax.broadcasted_iota(jnp.int32, x.shape, 1)
    other = jnp.where(column % HEAD_SIZE < half, jnp.roll(x, -half, axis=1), jnp.roll(x, half, axis=1))
    return x * cosine + other * sine


def layer_general(
    tokens,
    cotangent,
    routes,
    norm_one,
    query_key_value_weight,
    out_weight,
    norm_two,
    router_weight,
    gate_weight,
    up_weight,
    down_weight,
):
    n = lax.axis_size("expert")
    groups = lax.axis_size("group")
    me = lax.axis_index("expert")
    z = lax.axis_index("group")
    micro, count, model = tokens.shape
    exp_here, part, ff = gate_weight.shape
    experts = router_weight.shape[1]
    split = 2 if exp_here % 2 == 0 and groups % 2 == 0 else 1
    per = exp_here // split
    query_width = QUERY_HEADS * HEAD_SIZE
    kv_width = KEY_VALUE_HEADS * HEAD_SIZE
    cap = max(2, 3 * TOPK * PR_DEV // experts)
    where = jnp.stack([z, me, me * exp_here + (z % split) * per]).astype(jnp.int32)
    rows_here = part // n if part % n == 0 else 0
    aligned = rows_here > 0 and rows_here % 16 == 0 and part % LANES == 0

    misc = jnp.concatenate(
        [
            norm_one[:, None],
            norm_two[:, None],
            jnp.zeros((part, experts - 2), BF16),
            router_weight,
            jnp.zeros((part, LANES - 2 * experts), BF16),
        ],
        axis=1,
    )
    if aligned:
        first = jnp.concatenate([query_key_value_weight, misc], axis=1)
        cut = lambda x: lax.dynamic_slice_in_dim(x, me * rows_here, rows_here, axis=0)
        width = first.shape[1]
        middle = width // 2 // LANES * LANES
        first_full, far = gather_dense(cut(first), [(0, middle), (middle, width)], where)
        out_full, far_out = gather_dense(
            cut(out_weight), [(0, model // 2), (model // 2, model)], where
        )
        after = (far, far_out)
    else:
        first_full = lax.all_gather(
            jnp.concatenate([query_key_value_weight, misc], axis=1), "group", axis=0, tiled=True
        )
        out_full = lax.all_gather(out_weight, "group", axis=0, tiled=True)
        after = ()
    qkv_columns = query_key_value_weight.shape[1]
    qkv_full = first_full[:, :qkv_columns]
    misc_full = first_full[:, qkv_columns:]
    gain_one = misc_full[:, 0].astype(F32)
    gain_two = misc_full[:, 1].astype(F32)
    router_full = misc_full[:, experts : 2 * experts]

    weights_held = []
    gate_from, up_from, down_from = gate_weight, up_weight, down_weight
    if aligned:
        (gate_from, up_from, down_from), after = lax.optimization_barrier(
            ((gate_weight, up_weight, down_weight), after)
        )
    for k in range(per):
        held = []
        for array, axis in ((gate_from, 0), (up_from, 0), (down_from, 1)):
            if not aligned:
                held.append(lax.all_gather(array[k], "group", axis=axis, tiled=True))
                continue
            pieces = []
            for s in range(groups):
                index = ((z + s) % split) * per + k
                chunk = lax.dynamic_index_in_dim(array, index, 0, keepdims=False)
                pieces.append(shift(chunk, s) if s else chunk)

            def place(i, at_z, at_e, axis=axis):
                start = lax.rem(at_z - i + groups, groups) * part
                return (start, 0) if axis == 0 else (0, start)

            shape = (model, ff) if axis == 0 else (ff, model)
            held.append(assemble(pieces, place, shape, where))
        weights_held.append(held)

    expert_ids = jnp.arange(experts, dtype=jnp.int32)
    named = jnp.any(routes[..., None] == expert_ids, axis=2)
    pad = jnp.zeros((micro, count, LANES - experts), BF16)
    d_payload = jnp.concatenate([cotangent, named.astype(BF16), pad], axis=2)

    def to_experts(payload):
        held = []
        for m in range(micro):
            own = payload[m]
            both = jnp.stack([own] + [turn(own, j, split) for j in range(1, split)])
            held.append(spread(both, m % 2))
        return held

    def to_owners(parts):
        held = []
        for m in range(micro):
            total = collect(parts[m], m % 2)
            mine = total[0]
            for j in range(1, split):
                mine = mine + turn(total[j].astype(BF16), split - j, split).astype(F32)
            held.append(mine)
        return jnp.stack(held)

    slots_per = 2 if n % 2 == 0 else 1
    batches = [list(range(g * slots_per, (g + 1) * slots_per)) for g in range(n // slots_per)]
    blocks_total = n * micro * split

    d_slots = to_experts(d_payload)
    buffers = None
    for g, batch in enumerate(batches):
        buffers = dispatch_grads(
            [d_slots[m][r] for r in batch for m in range(micro)],
            where, per, cap, model, buffers, g, blocks_total,
        )
    grads_in, ranks = buffers

    rows = micro * count
    x = tokens.reshape(rows, model).astype(F32)
    inverse_one = lax.rsqrt(jnp.mean(x * x, axis=-1, keepdims=True) + 1e-05)
    normed = (x * inverse_one * gain_one).astype(BF16)
    cosine, sine = rope_tables(me, PR_DEV * n)
    heads_rope = QUERY_HEADS + KEY_VALUE_HEADS
    cosine = jnp.tile(jnp.concatenate([cosine, cosine], axis=1), (micro, heads_rope))
    sine = jnp.tile(jnp.concatenate([-sine, sine], axis=1), (micro, heads_rope))
    cosine, sine = lax.optimization_barrier((cosine, sine))
    project = mm(normed, qkv_full)
    roped = rotate(project[:, : query_width + kv_width], cosine, sine).astype(BF16)
    query = roped[:, :query_width]
    key_value = jnp.concatenate(
        [roped[:, query_width:], project[:, query_width + kv_width :].astype(BF16)], axis=1
    ).reshape(micro, count, 2 * kv_width)
    query = query.reshape(micro, count, query_width)
    kv_slots = [spread(key_value[m], m % 2) for m in range(micro)]
    mixed = jnp.concatenate(
        [attention_forward(query[m], kv_slots[m], where) for m in range(micro)], axis=0
    )
    hidden = x + mm(mixed, out_full)
    inverse_two = lax.rsqrt(jnp.mean(hidden * hidden, axis=-1, keepdims=True) + 1e-05)
    normed_two = (hidden * inverse_two * gain_two).astype(BF16)
    logits = mm(normed_two, router_full)
    chosen = named.reshape(rows, experts)
    logits = jnp.where(chosen, logits, NEG_FILL)
    top = jnp.max(logits, axis=-1, keepdims=True)
    raised = jnp.where(chosen, jnp.exp(logits - top), 0.0)
    gate_probs = raised / jnp.sum(raised, axis=-1, keepdims=True)

    high = gate_probs.astype(BF16)
    low = (gate_probs - high.astype(F32)).astype(BF16)
    payload = jnp.concatenate(
        [normed_two, high, low, jnp.zeros((rows, LANES - 2 * experts), BF16)], axis=1
    ).reshape(micro, count, model + LANES)
    x_slots = to_experts(payload)
    buffers = None
    for g, batch in enumerate(batches):
        buffers = dispatch_rows(
            [x_slots[m][r] for r in batch for m in range(micro)],
            ranks, where, per, cap, model, experts, buffers, g, blocks_total,
        )
    rows_in, row_weights = buffers
    tile = slots_per * micro * split * cap
    outs, backs, weight_terms = [], [], []
    for k in range(per):
        out_rows, back_rows, terms = run_expert(
            k, where, rows_in, grads_in, row_weights, *weights_held[k], experts, tile, groups, aligned
        )
        outs.append(out_rows)
        backs.append(back_rows)
        weight_terms.append(terms)

    def returned(row_arrays):
        parts = [[None] * n for _ in range(micro)]
        for g in reversed(range(len(batches))):
            got = combine(
                row_arrays, ranks, len(batches[g]) * micro, split, count, cap, g
            )
            for i, (r, m) in enumerate((r, m) for r in batches[g] for m in range(micro)):
                parts[m][r] = got[i]
        return to_owners(parts)

    back = returned(backs).reshape(rows, model + LANES)
    mixture = returned(outs).reshape(rows, model)
    block_out = (hidden + mixture).astype(BF16).reshape(tokens.shape)

    expert_grads = []
    for which in range(3):
        per_class = []
        for k in range(per):
            if not aligned:
                axis = 1 if which == 2 else 0
                per_class.append(
                    [lax.psum_scatter(weight_terms[k][which], "group", scatter_dimension=axis, tiled=True).astype(F32)]
                )
                continue
            sums = [None] * split
            for s in range(groups):
                term = weight_terms[k][which * groups + s]
                term = (shift(term, s) if s else term).astype(F32)
                c = s % split
                sums[c] = term if sums[c] is None else sums[c] + term
            per_class.append(
                [lax.select_n((z - p) % split, *sums) if split > 1 else sums[0] for p in range(split)]
            )
        expert_grads.append(
            jnp.stack([per_class[k][p] for p in range(split) for k in range(per)])
        )

    d_out = cotangent.reshape(rows, model).astype(F32)
    d_gates = back[:, model : model + experts] + back[:, model + experts : model + 2 * experts]
    d_logits = gate_probs * (d_gates - jnp.sum(gate_probs * d_gates, axis=-1, keepdims=True))
    router_grad = lax.dot_general(normed_two.astype(F32), d_logits, TN, precision=HIGHEST)
    d_normed_two = back[:, :model] + lax.dot_general(
        d_logits, router_full.astype(F32), NT, precision=HIGHEST
    )

    def rms_back(inputs, inverse, gain, upstream):
        scaled = gain * upstream
        return inverse * scaled - inputs * inverse * inverse * inverse * jnp.mean(
            scaled * inputs, axis=-1, keepdims=True
        )

    grad_two = jnp.sum(d_normed_two * hidden * inverse_two, axis=0)
    d_hidden = d_out + rms_back(hidden, inverse_two, gain_two, d_normed_two)
    d_attn = d_hidden.astype(BF16)
    d_mixed = mm(d_attn, out_full, NT).astype(BF16).reshape(micro, count, query_width)
    d_query, kv_terms = [], []
    for m in range(micro):
        got, terms = attention_backward(query[m], kv_slots[m], d_mixed[m], where)
        d_query.append(got)
        kv_terms.append(terms)
    d_query = jnp.concatenate(d_query, axis=0)
    q_cos, q_sin = cosine[:, :query_width], sine[:, :query_width]
    d_query_low = rotate(d_query, q_cos, -q_sin).astype(BF16)
    d_kv = jnp.concatenate([collect(kv_terms[m], m % 2) for m in range(micro)], axis=0)
    d_key_low = rotate(d_kv[:, :kv_width], q_cos[:, :kv_width], -q_sin[:, :kv_width]).astype(BF16)
    d_kv_low = jnp.concatenate([d_key_low, d_kv[:, kv_width:].astype(BF16)], axis=1)
    d_normed = mm(d_query_low, qkv_full[:, :query_width], NT) + mm(
        d_kv_low, qkv_full[:, query_width:], NT
    )
    grad_one = jnp.sum(d_normed * x * inverse_one, axis=0)
    input_grad = (d_hidden + rms_back(x, inverse_one, gain_one, d_normed)).reshape(tokens.shape)
    misc_grad = jnp.concatenate(
        [
            grad_one[:, None],
            grad_two[:, None],
            jnp.zeros((model, experts - 2), F32),
            router_grad,
            jnp.zeros((model, LANES - 2 * experts), F32),
        ],
        axis=1,
    )
    if aligned:
        grad_out = reduce_dense(sliced_outer(mixed, d_attn, None, groups, n, where), 0, where)
        grad_q = reduce_dense(sliced_outer(normed, d_query_low, None, groups, n, where), 1, where)
        grad_rest = reduce_dense(
            sliced_outer(normed, d_kv_low, misc_grad, groups, n, where), 0, where
        )
    else:

        def whole(value):
            low = lax.psum_scatter(value.astype(BF16), "group", scatter_dimension=0, tiled=True)
            return lax.psum(low, "expert").astype(F32)

        grad_out = whole(mm(mixed, d_attn, TN))
        grad_q = whole(mm(normed, d_query_low, TN))
        grad_rest = whole(jnp.concatenate([mm(normed, d_kv_low, TN), misc_grad], axis=1))
    grad_qkv = jnp.concatenate([grad_q, grad_rest[:, : 2 * kv_width]], axis=1)
    misc_sum = grad_rest[:, 2 * kv_width :]
    return (
        block_out,
        input_grad,
        misc_sum[:, 0],
        grad_qkv,
        grad_out,
        misc_sum[:, 1],
        misc_sum[:, experts : 2 * experts],
        *expert_grads,
    )


def flip(e, r):
    for bit in (1, 2, 4):
        if r & bit:
            e = e + bit - 2 * bit * lax.rem(e // bit, 2)
    return e


def partner(z):
    return z + 1 - 2 * lax.rem(z, 2)


def remote(src, dst, send, recv, device):
    return pltpu.make_async_remote_copy(
        src_ref=src,
        dst_ref=dst,
        send_sem=send,
        recv_sem=recv,
        device_id=device,
        device_id_type=pl.DeviceIdType.MESH,
    )


def greet(devices):
    barrier = pltpu.get_barrier_semaphore()
    for device in devices:
        pl.semaphore_signal(barrier, inc=1, device_id=device, device_id_type=pl.DeviceIdType.MESH)
    pl.semaphore_wait(barrier, len(devices))


def plane_devices(e):
    return [{"expert": flip(e, bit)} for bit in (1, 2, 4)]


class Gather:
    def __init__(self, e, own, loc, paths, send, recv):
        self.e, self.own, self.loc, self.paths, self.send, self.recv = e, own, loc, paths, send, recv

    def copy(self, r, bit, c):
        q = r ^ bit
        src = self.own(c) if r == 0 else self.loc(r, r, c)
        return remote(
            src, self.loc(r, q, c), self.send.at[q, c], self.recv.at[q, c],
            {"expert": flip(self.e, bit)},
        )

    def begin(self, c):
        for bit in (2, 4, 1):
            self.copy(0, bit, c).start()

    def arrived(self, q, c):
        here = self.loc(q, q, c)
        remote(
            here, here, self.send.at[q, c], self.recv.at[q, c], {"expert": flip(self.e, 1)}
        ).wait_recv()

    def pass_on(self, q, c):
        if q == 2 and self.paths[c] == 0:
            self.copy(2, 4, c).start()
        if q == 4 and self.paths[c] == 1:
            self.copy(4, 2, c).start()
        if q in (2, 4, 6):
            self.copy(q, 1, c).start()

    def finish(self, c):
        for bit in (2, 4, 1):
            self.copy(0, bit, c).wait_send()
        if self.paths[c] == 0:
            self.copy(2, 4, c).wait_send()
        else:
            self.copy(4, 2, c).wait_send()
        for q in (2, 4, 6):
            self.copy(q, 1, c).wait_send()

    def stage(self, chunks, slots):
        for c in chunks:
            for q in slots:
                self.arrived(q, c)
                self.pass_on(q, c)

    def forward_all(self, chunks, use=None):
        for c in chunks:
            for q in (2, 4):
                self.arrived(q, c)
                self.pass_on(q, c)
        if use:
            for c in chunks:
                self.arrived(1, c)
                use(1, c)
                use(2, c)
                use(4, c)
        for c in chunks:
            self.arrived(6, c)
            self.pass_on(6, c)
            if use:
                use(6, c)
        for c in chunks:
            for q in (3, 5, 7) if use else (1, 3, 5, 7):
                self.arrived(q, c)
                if use:
                    use(q, c)


def add_rows(dst, sources, step=16):
    rows = sources[0].shape[0]

    def one(i, carry):
        at = pl.ds(pl.multiple_of(i * step, step), step)
        total = sources[0][at, :].astype(F32)
        for source in sources[1:]:
            total = total + source[at, :].astype(F32)
        dst[at, :] = total.astype(dst.dtype)
        return carry

    lax.fori_loop(0, rows // step, one, 0)


class Reduce:
    def __init__(self, e, part, paths, core, diag, near, acc, send, recv):
        self.e, self.part, self.paths = e, part, paths
        self.core, self.diag, self.near, self.acc = core, diag, near, acc
        self.send, self.recv = send, recv

    def core_copy(self, h, c):
        return remote(
            self.part(2 * h + 1, c), self.core.at[h, c], self.send.at[h, c], self.recv.at[h, c],
            {"expert": flip(self.e, 1)},
        )

    def diag_copy(self, c):
        return remote(
            self.acc.at[2, c], self.diag.at[c], self.send.at[4, c], self.recv.at[4, c],
            {"expert": flip(self.e, 4 if self.paths[c] == 0 else 2)},
        )

    def near_copy(self, i, c):
        return remote(
            self.acc.at[i, c], self.near.at[i, c], self.send.at[5 + i, c], self.recv.at[5 + i, c],
            {"expert": flip(self.e, 2 if i == 0 else 4)},
        )

    def begin(self, r, c):
        self.core_copy(r // 2, c).start()

    def diagonal(self, chunks):
        for c in chunks:
            self.core_copy(3, c).wait_recv()
            add_rows(self.acc.at[2, c], [self.part(6, c), self.core.at[3, c]])
            self.diag_copy(c).start()

    def sides(self, chunks):
        for c in chunks:
            for i in (0, 1) if self.paths[c] == 1 else (1, 0):
                self.core_copy(1 + i, c).wait_recv()
                terms = [self.part(2 + 2 * i, c), self.core.at[1 + i, c]]
                if self.paths[c] == i:
                    self.diag_copy(c).wait_recv()
                    terms.append(self.diag.at[c])
                add_rows(self.acc.at[i, c], terms)
                self.near_copy(i, c).start()

    def total(self, c):
        self.core_copy(0, c).wait_recv()
        self.near_copy(0, c).wait_recv()
        self.near_copy(1, c).wait_recv()
        return [self.part(0, c), self.core.at[0, c], self.near.at[0, c], self.near.at[1, c]]

    def finish(self, c):
        for h in range(4):
            self.core_copy(h, c).wait_send()
        self.diag_copy(c).wait_send()
        for i in range(2):
            self.near_copy(i, c).wait_send()


def reduce_scratch(count, rows, width):
    return [
        pltpu.VMEM((4, count, rows, width), BF16),
        pltpu.VMEM((count, rows, width), BF16),
        pltpu.VMEM((2, count, rows, width), BF16),
        pltpu.VMEM((3, count, rows, width), BF16),
        pltpu.SemaphoreType.DMA((7, count)),
        pltpu.SemaphoreType.DMA((7, count)),
    ]


def params(identity, vmem=62):
    return pltpu.CompilerParams(
        collective_id=identity, has_side_effects=True, vmem_limit_bytes=vmem * 1024 * 1024
    )


def plane_weights(shares, bank, per):
    n, split = 8, 2
    groups = lax.axis_size("group")
    rows = shares[0].shape[0]
    kinds = len(shares)
    count = groups * kinds

    def kernel(*refs):
        ins, bank_ref, refs = refs[:kinds], refs[kinds], refs[kinds + 1 :]
        outs, far_ref, refs = refs[:kinds], refs[kinds], refs[kinds + 1 :]
        z_send, z_recv, send, recv, local, b_send, b_recv = refs
        e, z = lax.axis_index("expert"), lax.axis_index("group")

        def loc(r, q, c):
            s, kind = c // kinds, c % kinds
            row = (lax.rem(z - s + groups, groups) * n + flip(e, r)) * rows
            return outs[kind].at[pl.ds(pl.multiple_of(row, 16), rows), :]

        def far(c):
            s, kind = c // kinds, c % kinds
            return remote(
                ins[kind], loc(0, 0, kind), z_send.at[c], z_recv.at[c],
                {"group": lax.rem(z + s, groups)},
            )

        def landed(c):
            remote(
                loc(0, 0, c), loc(0, 0, c), z_send.at[c], z_recv.at[c],
                {"group": lax.rem(z + c // kinds, groups)},
            ).wait_recv()

        first = lax.rem(z + 1, split) * per
        follow = remote(
            bank_ref.at[pl.ds(first, per)], far_ref, b_send, b_recv, {"group": lax.rem(z + 1, groups)}
        )
        gather = Gather(
            e, lambda c: ins[c] if c < kinds else loc(0, 0, c), loc,
            [c // kinds % 2 for c in range(count)], send, recv,
        )
        near = list(range(kinds))
        later = list(range(kinds, count))
        greet(
            plane_devices(e) + [{"group": lax.rem(z + s, groups)} for s in range(1, groups)]
        )
        for c in later:
            far(c).start()
        for c in near:
            gather.begin(c)
            pltpu.make_async_copy(ins[c], loc(0, 0, c), local.at[c]).start()
        follow.start()
        gather.stage(near, (2, 4))
        gather.stage(near, (6,))
        for c in later:
            landed(c)
            gather.begin(c)
        gather.stage(later, (2, 4))
        gather.stage(later, (6,))
        gather.stage(near + later, (1, 3, 5, 7))
        for c in later:
            far(c).wait_send()
        for c in near + later:
            gather.finish(c)
        for c in near:
            pltpu.make_async_copy(ins[c], loc(0, 0, c), local.at[c]).wait()
        follow.wait()

    vmem = pl.BlockSpec(memory_space=pltpu.VMEM)
    shapes = [(groups * n * rows, one.shape[1]) for one in shares]
    return pl.pallas_call(
        kernel,
        in_specs=[vmem] * kinds + [ANY_SPEC],
        out_specs=[vmem] * kinds + [ANY_SPEC],
        out_shape=[jax.ShapeDtypeStruct(shape, BF16) for shape in shapes]
        + [jax.ShapeDtypeStruct((per,) + bank.shape[1:], BF16)],
        scratch_shapes=[
            pltpu.SemaphoreType.DMA((count,)),
            pltpu.SemaphoreType.DMA((count,)),
            pltpu.SemaphoreType.DMA((n, count)),
            pltpu.SemaphoreType.DMA((n, count)),
            pltpu.SemaphoreType.DMA((kinds,)),
            pltpu.SemaphoreType.DMA,
            pltpu.SemaphoreType.DMA,
        ],
        compiler_params=params(1),
        cost_estimate=cost(1e9, 1e6),
        name="plane_weights",
    )(*shares, bank)


def attention_pairs(n, at_me, q_ref, keys, out_ref):
    width = KEY_VALUE_HEADS * HEAD_SIZE
    prompt_ok, cont_ok = attention_masks_plain(n, at_me)

    def pair(j, carry):
        q_at = pl.ds(pl.multiple_of(j * 384, 128), 384)
        k_at = pl.ds(pl.multiple_of(j * 128, 128), 128)
        v_at = pl.ds(pl.multiple_of(width + j * 128, 128), 128)
        q_top, q_low = q_ref[:PR_DEV, q_at], q_ref[PR_DEV:, q_at]
        k_two, v_two = keys[:, k_at], keys[:, v_at]
        tops, lows = [], []
        for g in range(2):
            key = k_two[:, g * HEAD_SIZE : (g + 1) * HEAD_SIZE]
            value = v_two[:, g * HEAD_SIZE : (g + 1) * HEAD_SIZE]
            top, low = group_probs(
                head_rows(q_top, g * 192), head_rows(q_low, g * 192), key, prompt_ok, cont_ok, n
            )
            tops.append(row_heads(mm(top.astype(BF16), value[: n * PR_DEV])))
            lows.append(row_heads(mm(low.astype(BF16), value)))
        out_ref[:PR_DEV, q_at] = jnp.concatenate(tops, axis=1).astype(BF16)
        out_ref[PR_DEV:, q_at] = jnp.concatenate(lows, axis=1).astype(BF16)
        return carry

    lax.fori_loop(0, KEY_VALUE_HEADS // 2, pair, 0)


def flip_columns(slot, me, limit):
    bit, total = 1, jnp.zeros_like(slot)
    while bit < limit:
        total = total + bit * lax.rem(slot // bit + me // bit, 2)
        bit *= 2
    return total


def attention_masks_plain(n, me):
    shape = (3 * PR_DEV, n * PR_DEV)
    token = lax.rem(lax.broadcasted_iota(jnp.int32, shape, 0), PR_DEV)
    column = lax.broadcasted_iota(jnp.int32, shape, 1)
    owner = flip_columns(column // PR_DEV, me, n)
    prompt_ok = owner * PR_DEV + lax.rem(column, PR_DEV) <= me * PR_DEV + token
    slots = CONT // PR_DEV
    shape = (3 * PR_DEV, CONT)
    token = lax.rem(lax.broadcasted_iota(jnp.int32, shape, 0), PR_DEV)
    column = lax.broadcasted_iota(jnp.int32, shape, 1)
    local = lax.rem(me, slots)
    owner = flip_columns(column // PR_DEV, local, slots)
    cont_ok = owner * PR_DEV + lax.rem(column, PR_DEV) <= local * PR_DEV + token
    return prompt_ok, cont_ok


def turn_heads(x, cosine, sine):
    half = HEAD_SIZE // 2
    lane = lax.broadcasted_iota(jnp.int32, cosine.shape, 1)
    first = lax.rem(lane, HEAD_SIZE) < half
    blocks = []
    for lo in range(0, x.shape[1], LANES):
        one = x[:, lo : lo + LANES]
        other = jnp.where(first, pltpu.roll(one, LANES - half, 1), pltpu.roll(one, half, 1))
        blocks.append(one * cosine + other * sine)
    return jnp.concatenate(blocks, axis=1)


def plane_attention(normed, weight, cosine, sine, micro):
    rows, model = normed.shape
    tokens = rows // micro
    width = 2 * KEY_VALUE_HEADS * HEAD_SIZE
    query_width = QUERY_HEADS * HEAD_SIZE
    n, tile = 8, 512

    def kernel(x_ref, w_ref, cos_ref, sin_ref, out_ref, q_ref, slots, own, keys, send, recv, local):
        e = lax.axis_index("expert")
        gather = Gather(
            e, lambda c: own.at[c], lambda r, q, c: slots.at[q, c], [c % 2 for c in range(micro)],
            send, recv,
        )

        def project(lo, turned):
            wide = mm(x_ref[...], w_ref[:, lo : lo + tile])
            for c in range(micro):
                part = wide[c * tokens : (c + 1) * tokens]
                if turned:
                    part = turn_heads(part, cos_ref[...], sin_ref[...])
                yield c, part.astype(BF16)

        for lo in range(0, width, tile):
            for c, part in project(query_width + lo, lo < width // 2):
                own[c, :, lo : lo + tile] = part
        greet(plane_devices(e))
        for c in range(micro):
            gather.begin(c)
            pltpu.make_async_copy(own.at[c], slots.at[0, c], local.at[c]).start()
        for lo in range(0, query_width, tile):
            for c, part in project(lo, True):
                q_ref[c, :, lo : lo + tile] = part
        gather.stage(range(micro), (2, 4))
        gather.stage(range(micro), (6,))
        for c in range(micro):
            gather.stage([c], (1, 3, 5, 7))
            pltpu.make_async_copy(own.at[c], slots.at[0, c], local.at[c]).wait()
            load_keys(n, [slots.at[r, c] for r in range(n)], keys)
            attention_pairs(n, e, q_ref.at[c], keys, out_ref.at[c])
        for c in range(micro):
            gather.finish(c)

    vmem = pl.BlockSpec(memory_space=pltpu.VMEM)
    shape = jax.ShapeDtypeStruct((micro, tokens, query_width), BF16)
    return pl.pallas_call(
        kernel,
        in_specs=[vmem] * 4,
        out_specs=[vmem] * 3,
        out_shape=[shape, shape, jax.ShapeDtypeStruct((n, micro, tokens, width), BF16)],
        scratch_shapes=[
            pltpu.VMEM((micro, tokens, width), BF16),
            pltpu.VMEM((n * PR_DEV + CONT, width), BF16),
            pltpu.SemaphoreType.DMA((n, micro)),
            pltpu.SemaphoreType.DMA((n, micro)),
            pltpu.SemaphoreType.DMA((micro,)),
        ],
        compiler_params=params(2),
        cost_estimate=cost(1e9, 1e6),
        name="plane_attention",
    )(normed, weight, cosine, sine)


def plane_attention_backward(query, slots, d_mixed, cosine, sine):
    n, micro, tokens, width = slots.shape
    half = width // 2
    query_width = query.shape[2]
    pr = n * PR_DEV
    total = pr + CONT

    def kernel(q_ref, d_ref, kv_ref, cos_ref, sin_ref, out_ref, keys, grads, parts, *scratch):
        e = lax.axis_index("expert")
        red = Reduce(e, lambda r, c: parts.at[r, c], [c % 2 for c in range(micro)], *scratch)
        greet(plane_devices(e))
        prompt_ok, cont_ok = attention_masks_plain(n, e)

        def one_side(prob, d_rows, key, value, q_rows):
            d_prob = mm(d_rows, value, NT)
            delta = jnp.sum(prob * d_prob, axis=1, keepdims=True)
            d_score = (prob * (d_prob - delta)).astype(BF16)
            return (
                mm(d_score, key) * SCORE_SCALE,
                mm(d_score, q_rows, TN) * SCORE_SCALE,
                mm(prob.astype(BF16), d_rows, TN),
            )

        for c in range(micro):
            load_keys(n, [kv_ref.at[r, c] for r in range(n)], keys)

            def pair(j, carry):
                q_at = pl.ds(pl.multiple_of(j * 384, 128), 384)
                k_at = pl.ds(pl.multiple_of(j * 128, 128), 128)
                v_at = pl.ds(pl.multiple_of(half + j * 128, 128), 128)
                q_top, q_low = q_ref[c, :PR_DEV, q_at], q_ref[c, PR_DEV:, q_at]
                d_top, d_low = d_ref[c, :PR_DEV, q_at], d_ref[c, PR_DEV:, q_at]
                k_two, v_two = keys[:, k_at], keys[:, v_at]
                dq_tops, dq_lows, dks, dvs = [], [], [], []
                for g in range(2):
                    key = k_two[:, g * HEAD_SIZE : (g + 1) * HEAD_SIZE]
                    value = v_two[:, g * HEAD_SIZE : (g + 1) * HEAD_SIZE]
                    rows_top, rows_low = head_rows(q_top, g * 192), head_rows(q_low, g * 192)
                    top, low = group_probs(rows_top, rows_low, key, prompt_ok, cont_ok, n)
                    dq_top, dk_top, dv_top = one_side(
                        top, head_rows(d_top, g * 192), key[:pr], value[:pr], rows_top
                    )
                    dq_low, dk_low, dv_low = one_side(
                        low, head_rows(d_low, g * 192), key, value, rows_low
                    )
                    dq_tops.append(row_heads(dq_top))
                    dq_lows.append(row_heads(dq_low))
                    dks.append(jnp.concatenate([dk_low[:pr] + dk_top, dk_low[pr:]], axis=0))
                    dvs.append(jnp.concatenate([dv_low[:pr] + dv_top, dv_low[pr:]], axis=0))
                for lo, found in ((0, dq_tops), (PR_DEV, dq_lows)):
                    there = slice(lo, lo + PR_DEV)
                    turned = turn_heads(
                        jnp.concatenate(found, axis=1), cos_ref[there, :], sin_ref[there, :]
                    )
                    out_ref[c, there, q_at] = turned.astype(BF16)
                grads[:, k_at] = jnp.concatenate(dks, axis=1).astype(BF16)
                grads[:, v_at] = jnp.concatenate(dvs, axis=1).astype(BF16)
                return carry

            lax.fori_loop(0, KEY_VALUE_HEADS // 2, pair, 0)
            for r in (7, 5, 3, 1, 6, 2, 4, 0):
                parts[r, c, :PR_DEV, :] = grads[r * PR_DEV : (r + 1) * PR_DEV, :]
                if r < CONT // PR_DEV:
                    lo = (n + r) * PR_DEV
                    parts[r, c, PR_DEV:, :] = grads[lo : lo + PR_DEV, :]
                else:
                    parts[r, c, PR_DEV:, :] = jnp.zeros((PR_DEV, width), BF16)
                if r % 2:
                    red.begin(r, c)
        red.diagonal(range(micro))
        red.sides(range(micro))
        step = 16
        for c in range(micro):
            terms = red.total(c)

            def last(i, carry):
                at = pl.ds(pl.multiple_of(i * step, step), step)
                total = terms[0][at, :].astype(F32)
                for term in terms[1:]:
                    total = total + term[at, :].astype(F32)
                turned = turn_heads(total[:, :half], cos_ref[at, :], sin_ref[at, :])
                out_ref[c, at, query_width : query_width + half] = turned.astype(BF16)
                out_ref[c, at, query_width + half :] = total[:, half:].astype(BF16)
                return carry

            lax.fori_loop(0, tokens // step, last, 0)
        for c in range(micro):
            red.finish(c)

    vmem = pl.BlockSpec(memory_space=pltpu.VMEM)
    return pl.pallas_call(
        kernel,
        in_specs=[vmem] * 5,
        out_specs=vmem,
        out_shape=jax.ShapeDtypeStruct((micro, tokens, query_width + width), BF16),
        scratch_shapes=[
            pltpu.VMEM((total, width), BF16),
            pltpu.VMEM((total, width), BF16),
            pltpu.VMEM((n, micro, tokens, width), BF16),
        ]
        + reduce_scratch(micro, tokens, width),
        compiler_params=params(3),
        cost_estimate=cost(1e9, 1e6),
        name="plane_attention_backward",
    )(query, d_mixed, slots, cosine, sine)


def plane_dispatch(payload, ranks, bank, where, per, cap, model, experts):
    micro, tokens, width = payload.shape
    n, split = 8, 2
    groups = lax.axis_size("group")
    count = split * micro

    def kernel(
        at_ref, own_ref, rank_ref, bank_ref, out, weights, far_ref,
        slots, z_send, z_recv, send, recv, b_send, b_recv,
    ):
        e, z = lax.axis_index("expert"), lax.axis_index("group")
        lane = lax.broadcasted_iota(jnp.int32, (cap, LANES), 1)

        def own(c):
            return own_ref.at[c] if c < micro else slots.at[0, c]

        gather = Gather(
            e, own, lambda r, q, c: slots.at[q, c], [c % 2 for c in range(count)], send, recv
        )

        def turned(m):
            return remote(
                own_ref.at[m], slots.at[0, micro + m], z_send.at[m], z_recv.at[m],
                {"group": partner(z)},
            )

        def use(r, c):
            rows = own(c)[...] if r == 0 else slots[r, c]
            b = r * count + c
            for k in range(per):
                got = mm(pick(rank_ref[b, k : k + 1, :], cap), rows)
                out[k, b * cap : (b + 1) * cap, :] = got[:, :model].astype(BF16)
                first = at_ref[2] + k
                mine = (lane == first) | (lane == first + experts)
                total = jnp.sum(jnp.where(mine, got[:, model:], 0.0), axis=1, keepdims=True)
                weights[k, b * cap : (b + 1) * cap, :] = jnp.broadcast_to(total, (cap, LANES))

        last = groups - 1
        first = lax.rem(z + last, split) * per
        follow = remote(
            bank_ref.at[pl.ds(first, 1)], far_ref, b_send, b_recv,
            {"group": lax.rem(z + last, groups)},
        )
        greet(plane_devices(e) + [{"group": lax.rem(z + s, groups)} for s in (1, last)])
        for m in range(micro):
            turned(m).start()
        follow.start()
        for m in range(micro):
            gather.begin(m)
        for m in range(micro):
            use(0, m)
        for m in range(micro):
            turned(m).wait_recv()
            gather.begin(micro + m)
            use(0, micro + m)
        gather.forward_all(range(count), use)
        for m in range(micro):
            turned(m).wait_send()
        for c in range(count):
            gather.finish(c)
        follow.wait()

    vmem = pl.BlockSpec(memory_space=pltpu.VMEM)
    total = n * count * cap
    return pl.pallas_call(
        kernel,
        in_specs=[SMEM_SPEC, vmem, vmem, ANY_SPEC],
        out_specs=[vmem, vmem, ANY_SPEC],
        out_shape=[
            jax.ShapeDtypeStruct((per, total, model), BF16),
            jax.ShapeDtypeStruct((per, total, LANES), F32),
            jax.ShapeDtypeStruct((1,) + bank.shape[1:], BF16),
        ],
        scratch_shapes=[
            pltpu.VMEM((n, count, tokens, width), BF16),
            pltpu.SemaphoreType.DMA((micro,)),
            pltpu.SemaphoreType.DMA((micro,)),
            pltpu.SemaphoreType.DMA((n, count)),
            pltpu.SemaphoreType.DMA((n, count)),
            pltpu.SemaphoreType.DMA,
            pltpu.SemaphoreType.DMA,
        ],
        compiler_params=params(4),
        cost_estimate=cost(1e9, 1e6),
        name="plane_dispatch",
    )(where, payload, ranks, bank)


def plane_return(rows, ranks, next_term, last_terms, micro, tokens, cap):
    per, _, width = rows.shape
    n, split = 8, 2
    groups = lax.axis_size("group")
    count = split * micro
    chunks = list(range(micro, count)) + list(range(micro))

    def kernel(rank_ref, in_ref, next_ref, last_ref, out, next_far, last_far, *refs):
        parts, z_out, z_in, z_send, z_recv, t_send, t_recv, scratch = *refs[:7], refs[7:]
        e, z = lax.axis_index("expert"), lax.axis_index("group")
        red = Reduce(e, lambda r, c: parts.at[r, c], [c % 2 for c in range(count)], *scratch)

        def produce(r, c):
            b = r * count + c
            total = None
            for k in range(per):
                one = mm(
                    pick(rank_ref[b, k : k + 1, :], cap), in_ref[k, b * cap : (b + 1) * cap, :], TN
                )
                total = one if total is None else total + one
            parts[r, c] = total.astype(BF16)

        def turned(m):
            return remote(
                z_out.at[m], z_in.at[m], z_send.at[m], z_recv.at[m], {"group": partner(z)}
            )

        follow = [
            remote(
                next_ref, next_far, t_send.at[0], t_recv.at[0], {"group": lax.rem(z + 1, groups)}
            ),
            remote(
                last_ref.at[0], last_far, t_send.at[1], t_recv.at[1],
                {"group": lax.rem(z + groups - 1, groups)},
            ),
        ]
        greet(plane_devices(e) + [{"group": lax.rem(z + s, groups)} for s in (1, groups - 1)])
        for one in follow:
            one.start()
        for r in (7, 3, 5):
            for c in chunks:
                produce(r, c)
                red.begin(r, c)
        for c in chunks:
            produce(6, c)
        red.diagonal(chunks)
        for r in (2, 4):
            for c in chunks:
                produce(r, c)
        red.sides(chunks)
        for c in chunks:
            produce(1, c)
            red.begin(1, c)
        for c in chunks:
            produce(0, c)
        for c in chunks:
            terms = red.total(c)
            if c >= micro:
                add_rows(z_out.at[c - micro], terms)
                turned(c - micro).start()
            else:
                turned(c).wait_recv()
                add_rows(out.at[c], terms + [z_in.at[c]])
        for m in range(micro):
            turned(m).wait_send()
        for c in chunks:
            red.finish(c)
        for one in follow:
            one.wait()

    vmem = pl.BlockSpec(memory_space=pltpu.VMEM)
    return pl.pallas_call(
        kernel,
        in_specs=[vmem, vmem, ANY_SPEC, ANY_SPEC],
        out_specs=[vmem, ANY_SPEC, ANY_SPEC],
        out_shape=[
            jax.ShapeDtypeStruct((micro, tokens, width), F32),
            jax.ShapeDtypeStruct(next_term.shape, BF16),
            jax.ShapeDtypeStruct(next_term.shape, BF16),
        ],
        scratch_shapes=[
            pltpu.VMEM((n, count, tokens, width), BF16),
            pltpu.VMEM((micro, tokens, width), BF16),
            pltpu.VMEM((micro, tokens, width), BF16),
            pltpu.SemaphoreType.DMA((micro,)),
            pltpu.SemaphoreType.DMA((micro,)),
            pltpu.SemaphoreType.DMA((2,)),
            pltpu.SemaphoreType.DMA((2,)),
        ]
        + reduce_scratch(count, tokens, width),
        compiler_params=params(5),
        cost_estimate=cost(1e9, 1e6),
        name="plane_return",
    )(ranks, rows, next_term, last_terms)


def plane_gradients(products, router, gains, terms, groups):
    n = 8
    depth = products[0][0].shape[1]
    widths = [b.shape[1] for a, b in products]
    width = sum(widths) + LANES
    experts = router.shape[1]
    rows = depth // (groups * n)
    tile = 512
    flat = [x for pair in products for x in pair]

    def kernel(*refs):
        ins, refs = refs[: len(flat)], refs[len(flat) :]
        router_ref, gains_ref, term_ref, out, far_ref, *refs = refs
        wide, parts, z_out, z_in, z_send, z_recv, send, recv, t_send, t_recv = refs[:10]
        scratch = refs[10:]
        e, z = lax.axis_index("expert"), lax.axis_index("group")
        red = Reduce(e, lambda r, c: parts.at[r, c], [c % 2 for c in range(groups)], *scratch)
        greet(
            plane_devices(e)
            + [{"group": lax.rem(z + s, groups)} for s in range(1, groups)]
        )
        follow = remote(
            term_ref.at[1], far_ref, t_send, t_recv, {"group": lax.rem(z + groups - 1, groups)}
        )
        follow.start()

        def cut(lo, size):
            for r in range(n):
                for s in range(groups):
                    row = (lax.rem(z + s, groups) * n + flip(e, r)) * rows
                    at = pl.ds(pl.multiple_of(row, 16), rows)
                    parts[r, s, :, lo : lo + size] = wide[at, :size].astype(BF16)

        lo = 0
        for i, count in enumerate(widths):
            for start in range(0, count, tile):
                size = min(tile, count - start)
                wide[:, :size] = mm(ins[2 * i][...], ins[2 * i + 1][:, start : start + size], TN)
                cut(lo, size)
                lo += size
        wide[:, :LANES] = jnp.zeros((depth, LANES), F32)
        wide[:, experts : 2 * experts] = router_ref[...]
        wide[:, : gains.shape[0]] = gains_ref[...].T
        cut(lo, LANES)

        chunks = list(range(1, groups)) + [0]
        for r in (7, 3, 5, 1):
            for c in chunks:
                red.begin(r, c)
        red.diagonal(chunks)
        red.sides(chunks)

        def far(s):
            return remote(
                z_out.at[s], z_in.at[s], z_send.at[s], z_recv.at[s],
                {"group": lax.rem(z + s, groups)},
            )

        for c in chunks:
            add_rows(z_out.at[c], red.total(c))
            if c:
                far(c).start()
        for c in range(1, groups):
            far(c).wait_recv()
        def place(r):
            return out.at[pl.ds(pl.multiple_of(flip(e, r) * rows, 16), rows), :]

        add_rows(place(0), [z_out.at[0]] + [z_in.at[c] for c in range(1, groups)])
        middle = width // 2 // LANES * LANES
        spans = [(0, middle), (middle, width)]

        def loc(r, q, c):
            row = pl.multiple_of(flip(e, r) * rows, 16)
            return out.at[pl.ds(row, rows), spans[c][0] : spans[c][1]]

        gather = Gather(e, lambda c: loc(0, 0, c), loc, [0, 1], send, recv)
        for c in range(2):
            gather.begin(c)
        gather.forward_all(range(2))
        for c in range(2):
            gather.finish(c)
        follow.wait()
        for c in range(1, groups):
            far(c).wait_send()
        for c in chunks:
            red.finish(c)

    vmem = pl.BlockSpec(memory_space=pltpu.VMEM)
    return pl.pallas_call(
        kernel,
        in_specs=[vmem] * (len(flat) + 2) + [ANY_SPEC],
        out_specs=[vmem, ANY_SPEC],
        out_shape=[
            jax.ShapeDtypeStruct((n * rows, width), BF16),
            jax.ShapeDtypeStruct(terms.shape[1:], BF16),
        ],
        scratch_shapes=[
            pltpu.VMEM((depth, tile), F32),
            pltpu.VMEM((n, groups, rows, width), BF16),
            pltpu.VMEM((groups, rows, width), BF16),
            pltpu.VMEM((groups, rows, width), BF16),
            pltpu.SemaphoreType.DMA((groups,)),
            pltpu.SemaphoreType.DMA((groups,)),
            pltpu.SemaphoreType.DMA((n, 2)),
            pltpu.SemaphoreType.DMA((n, 2)),
            pltpu.SemaphoreType.DMA,
            pltpu.SemaphoreType.DMA,
        ]
        + reduce_scratch(groups, rows, width),
        compiler_params=params(6),
        cost_estimate=cost(1e9, 1e6),
        name="plane_gradients",
    )(*flat, router, gains, terms)


def gather_flags(slots, where, per, cap, model):
    n, count, tokens, width = slots.shape

    def kernel(at_ref, in_ref, out, ranks, flags):
        row = lax.broadcasted_iota(jnp.int32, (tokens, tokens), 0)
        col = lax.broadcasted_iota(jnp.int32, (tokens, tokens), 1)
        before = jnp.where(row < col, 1.0, 0.0).astype(BF16)
        for b in range(count):
            payload = in_ref[0, b]
            flags[...] = payload[:, model:].astype(F32).T
            picked = jnp.concatenate(
                [flags[pl.ds(at_ref[2] + k, 1), :] for k in range(per)], axis=0
            )
            slot = jnp.where(picked > 0.0, mm(picked.astype(BF16), before), -1.0)
            ranks[b] = slot
            for k in range(per):
                out[k, b * cap : (b + 1) * cap, :] = mm(
                    pick(slot[k : k + 1], cap), payload[:, :model]
                ).astype(BF16)

    return pl.pallas_call(
        kernel,
        grid_spec=pltpu.PrefetchScalarGridSpec(
            num_scalar_prefetch=1,
            grid=(n,),
            in_specs=[
                pl.BlockSpec(
                    (1, count, tokens, width),
                    lambda r, at: (jnp.bitwise_xor(at[1], r), 0, 0, 0),
                )
            ],
            out_specs=[
                pl.BlockSpec((per, count * cap, model), lambda r, at: (0, r, 0)),
                pl.BlockSpec((count, per, tokens), lambda r, at: (r, 0, 0)),
            ],
            scratch_shapes=[pltpu.VMEM((LANES, tokens), F32)],
        ),
        out_shape=[
            jax.ShapeDtypeStruct((per, n * count * cap, model), BF16),
            jax.ShapeDtypeStruct((n * count, per, tokens), F32),
        ],
        cost_estimate=cost(5e9, 3e7),
        name="gather_flags",
    )(where, slots)


def scatter_rows(rows, ranks, where, n, count, tokens, cap):
    per, _, width = rows.shape

    def kernel(at_ref, rank_ref, in_ref, out):
        for b in range(count):
            total = None
            for k in range(per):
                one = mm(
                    pick(rank_ref[b, k : k + 1, :], cap), in_ref[k, b * cap : (b + 1) * cap, :], TN
                )
                total = one if total is None else total + one
            out[0, b] = total.astype(BF16)

    return pl.pallas_call(
        kernel,
        grid_spec=pltpu.PrefetchScalarGridSpec(
            num_scalar_prefetch=1,
            grid=(n,),
            in_specs=[
                pl.BlockSpec((count, per, tokens), lambda r, at: (r, 0, 0)),
                pl.BlockSpec((per, count * cap, width), lambda r, at: (0, r, 0)),
            ],
            out_specs=pl.BlockSpec(
                (1, count, tokens, width), lambda r, at: (jnp.bitwise_xor(at[1], r), 0, 0, 0)
            ),
        ),
        out_shape=jax.ShapeDtypeStruct((n, count, tokens, width), BF16),
        cost_estimate=cost(5e9, 3e7),
        name="scatter_rows",
    )(where, ranks, rows)


def expert_steps(rows_in, grads_in, weights, bank, far, experts, tile):
    per, total, model = rows_in.shape
    part, ff = bank.shape[2:]
    groups = model // part
    steps = total // tile
    split = 2
    here = bank.shape[0]
    last = groups - 1

    def kernel(x_ref, d_ref, w_ref, *refs):
        sources, o_ref, r_ref, refs = refs[:groups], refs[groups], refs[groups + 1], refs[groups + 2 :]
        outs, got_ref, refs = refs[:groups], refs[groups], refs[groups + 1 :]
        acc_wide, acc_down, wide_all, down_all, early, sems, w_send, w_recv, g_send, g_recv = refs
        k, step = pl.program_id(0), pl.program_id(1)
        me, mine_z = lax.axis_index("expert"), lax.axis_index("group")
        own_first = lax.rem(mine_z, split) * per

        def rows_of(index, z):
            at_z = pl.ds(pl.multiple_of(z * part, 128), part)
            wide, down = wide_all.at[index], down_all.at[index]
            return [wide.at[at_z, :ff], wide.at[at_z, ff:], down.at[at_z, :]]

        def loads(index):
            copies = []
            for s in range(groups - index):
                source = sources[s].at[own_first + index if s == 0 else index]
                there = rows_of(index, lax.rem(mine_z - s + groups, groups))
                for i, dst in enumerate(there):
                    copies.append(
                        pltpu.make_async_copy(source.at[i], dst, sems.at[index, 3 * s + i])
                    )
            return copies

        def late_weights(z):
            source = sources[0].at[lax.rem(mine_z + last, split) * per + 1]
            return [
                remote(
                    source.at[i], dst, w_send.at[i], w_recv.at[i],
                    {"group": lax.rem(mine_z + last, groups)},
                )
                for i, dst in enumerate(rows_of(1, z))
            ]

        early_term = remote(
            early, got_ref, g_send, g_recv, {"group": lax.rem(mine_z + 1, groups)}
        )

        @pl.when((k == 0) & (step == 0))
        def _():
            for index in range(per):
                for one in loads(index):
                    one.start()
            greet([{"group": lax.rem(mine_z + s, groups)} for s in (1, last)])
            for one in late_weights(mine_z):
                one.start()
            for one in loads(0):
                one.wait()

        @pl.when((k == 1) & (step == 0))
        def _():
            early_term.start()
            for one in loads(1):
                one.wait()
            for one in late_weights(lax.rem(mine_z + 1, groups)):
                one.wait_recv()
            for one in late_weights(mine_z):
                one.wait_send()

        wide_ref, down_ref = wide_all.at[k], down_all.at[k]
        x, d = x_ref[0], d_ref[0]
        w = w_ref[0, :, 0:1]
        pre = mm(x, wide_ref[...])
        gate_pre, up_pre = pre[:, :ff], pre[:, ff:]
        sig = 1.0 / (1.0 + jnp.exp(-gate_pre))
        silu = gate_pre * sig
        active_wide = silu * up_pre
        active = active_wide.astype(BF16)
        o_ref[0] = (mm(active, down_ref[...], NT) * w).astype(BF16)
        d_raw = mm(d, down_ref[...])
        d_gates = jnp.sum(active.astype(F32) * d_raw, axis=1, keepdims=True)
        d_active = d_raw * w
        d_up = (d_active * silu).astype(BF16)
        d_gate = (d_active * up_pre * sig * (1.0 + gate_pre * (1.0 - sig))).astype(BF16)
        d_both = jnp.concatenate([d_gate, d_up], axis=1)
        r_ref[0, :, :model] = mm(d_both, wide_ref[...], NT).astype(BF16)
        high = d_gates.astype(BF16).astype(F32)
        lane = lax.broadcasted_iota(jnp.int32, (tile, LANES), 1)
        e = me * here + own_first + k
        r_ref[0, :, model:] = (
            jnp.where(lane == e, high, 0.0) + jnp.where(lane == e + experts, d_gates - high, 0.0)
        ).astype(BF16)
        new_wide = mm(x, d_both, TN)
        new_down = mm((active_wide * w).astype(BF16), d, TN)

        @pl.when(step == 0)
        def _():
            acc_wide[...] = new_wide
            acc_down[...] = new_down

        @pl.when(step > 0)
        def _():
            acc_wide[...] += new_wide
            acc_down[...] += new_down

        @pl.when(step == steps - 1)
        def _():
            for s in range(groups):
                z = lax.rem(mine_z + s, groups)
                at_z = pl.ds(pl.multiple_of(z * part, 128), part)

                def put(dst):
                    dst[0] = acc_wide[at_z, :ff].astype(BF16)
                    dst[1] = acc_wide[at_z, ff:].astype(BF16)
                    dst[2] = acc_down[:, at_z].T.astype(BF16)

                if s == 1:
                    pl.when(k == 0)(lambda: put(early))
                    pl.when(k == 1)(lambda: put(outs[s]))
                else:
                    put(outs[s].at[0])

        @pl.when((k == per - 1) & (step == steps - 1))
        def _():
            early_term.wait()

    grad = pl.BlockSpec((1, 3, part, ff), lambda k, t: (k, 0, 0, 0), pipeline_mode=pl.Buffered(1))
    single = pl.BlockSpec((3, part, ff), lambda k, t: (0, 0, 0), pipeline_mode=pl.Buffered(1))
    rows = lambda width: pl.BlockSpec((1, tile, width), lambda k, t: (k, t, 0))
    out = pl.pallas_call(
        kernel,
        grid=(per, steps),
        in_specs=[rows(model), rows(model), rows(LANES)] + [ANY_SPEC] * groups,
        out_specs=[rows(model), rows(model + LANES)]
        + [single if s == 1 else grad for s in range(groups)]
        + [ANY_SPEC],
        out_shape=[
            jax.ShapeDtypeStruct((per, total, model), BF16),
            jax.ShapeDtypeStruct((per, total, model + LANES), BF16),
        ]
        + [
            jax.ShapeDtypeStruct((3, part, ff) if s == 1 else (per, 3, part, ff), BF16)
            for s in range(groups)
        ]
        + [jax.ShapeDtypeStruct((3, part, ff), BF16)],
        scratch_shapes=[
            pltpu.VMEM((model, 2 * ff), F32),
            pltpu.VMEM((ff, model), F32),
            pltpu.VMEM((per, model, 2 * ff), BF16),
            pltpu.VMEM((per, model, ff), BF16),
            pltpu.VMEM((3, part, ff), BF16),
            pltpu.SemaphoreType.DMA((per, 3 * groups)),
            pltpu.SemaphoreType.DMA((3,)),
            pltpu.SemaphoreType.DMA((3,)),
            pltpu.SemaphoreType.DMA,
            pltpu.SemaphoreType.DMA,
        ],
        compiler_params=params(7),
        cost_estimate=cost(18 * per * total * model * ff, 10 * per * total * model),
        name="expert_steps",
    )(rows_in, grads_in, weights, bank, *far)
    return out[0], out[1], list(out[2 : 2 + groups]), out[2 + groups]


def merge_grads(which, at, terms):
    per, _, part, ff = terms[0].shape
    flat, places = [], []
    for one in terms:
        places.append(len(flat))
        flat += one if isinstance(one, list) else [one]
    split = 2
    tile = LANES

    def kernel(at_ref, *refs):
        ins, out = refs[: len(flat)], refs[len(flat)]
        for k in range(per):
            for parity in range(split):
                value = None
                for s in range(parity, len(terms), split):
                    whole = not isinstance(terms[s], list)
                    more = ins[places[s]][k, 0] if whole else ins[places[s] + k][0]
                    more = more.astype(F32)
                    value = more if value is None else value + more
                index = lax.rem(at_ref[0] + parity, split) * per + k
                out[index] = value.T if which == 2 else value

    if which == 2:
        spec = pl.BlockSpec((split * per, ff, tile), lambda t: (0, 0, t))
        shape = (split * per, ff, part)
    else:
        spec = pl.BlockSpec((split * per, tile, ff), lambda t: (0, t, 0))
        shape = (split * per, part, ff)
    return pl.pallas_call(
        kernel,
        grid=(part // tile,),
        in_specs=[SMEM_SPEC]
        + [
            pl.BlockSpec((per, 1, tile, ff), lambda t: (0, which, t, 0))
            if one.ndim == 4
            else pl.BlockSpec((1, tile, ff), lambda t: (which, t, 0))
            for one in flat
        ],
        out_specs=spec,
        out_shape=jax.ShapeDtypeStruct(shape, F32),
        cost_estimate=cost(1e8, 6e6),
        name="merge_grads",
    )(at, *flat)


def layer_plane(
    tokens,
    cotangent,
    routes,
    norm_one,
    query_key_value_weight,
    out_weight,
    norm_two,
    router_weight,
    gate_weight,
    up_weight,
    down_weight,
):
    n = lax.axis_size("expert")
    groups = lax.axis_size("group")
    me = lax.axis_index("expert")
    z = lax.axis_index("group")
    micro, count, model = tokens.shape
    exp_here, part, ff = gate_weight.shape
    experts = router_weight.shape[1]
    split = 2
    per = exp_here // split
    query_width = QUERY_HEADS * HEAD_SIZE
    kv_width = KEY_VALUE_HEADS * HEAD_SIZE
    cap = max(2, 3 * TOPK * PR_DEV // experts)
    where = jnp.stack([z, me, me * exp_here + (z % split) * per, (z % split) * per]).astype(jnp.int32)
    rows_here = part // n
    rows = micro * count

    misc = jnp.concatenate(
        [
            norm_one[:, None],
            norm_two[:, None],
            jnp.zeros((part, experts - 2), BF16),
            router_weight,
            jnp.zeros((part, LANES - 2 * experts), BF16),
        ],
        axis=1,
    )
    cut = lambda x: lax.dynamic_slice_in_dim(x, me * rows_here, rows_here, axis=0)
    shares = [cut(query_key_value_weight), jnp.concatenate([cut(out_weight), cut(misc)], axis=1)]
    bank = jnp.stack([gate_weight, up_weight, jnp.swapaxes(down_weight, 1, 2)], axis=1)

    expert_ids = jnp.arange(experts, dtype=jnp.int32)
    named = jnp.any(routes[..., None] == expert_ids, axis=2)
    pad = jnp.zeros((micro, count, LANES - experts), BF16)
    d_payload = jnp.concatenate([cotangent, named.astype(BF16), pad], axis=2)
    d_turned = turn(d_payload, 1, split)

    bank_two = lax.dynamic_slice_in_dim(bank, (z % split) * per, per, axis=0)
    qkv_full, rest_full, far_one = plane_weights(shares, bank, per)
    (bank_two, d_payload, d_turned), qkv_full = lax.optimization_barrier(
        ((bank_two, d_payload, d_turned), qkv_full)
    )
    far_two = shift(bank_two, 2)
    both = jnp.concatenate([d_payload, d_turned], axis=0)
    d_slots = lax.all_gather(both, "expert", axis=0)
    out_full, misc_full = rest_full[:, :model], rest_full[:, model:]
    gain_one = misc_full[:, 0].astype(F32)
    gain_two = misc_full[:, 1].astype(F32)
    router_full = misc_full[:, experts : 2 * experts]

    grads_in, ranks = gather_flags(d_slots, where, per, cap, model)

    x = tokens.reshape(rows, model).astype(F32)
    inverse_one = lax.rsqrt(jnp.mean(x * x, axis=-1, keepdims=True) + 1e-05)
    normed = (x * inverse_one * gain_one).astype(BF16)
    cosine, sine = rope_tables(me, PR_DEV * n)
    cosine = jnp.concatenate([cosine] * 4, axis=1)
    sine = jnp.concatenate([-sine, sine] * 2, axis=1)
    mixed, query, kv_slots = plane_attention(normed, qkv_full, cosine, sine, micro)
    mixed = mixed.reshape(rows, query_width)
    hidden = x + mm(mixed, out_full)
    inverse_two = lax.rsqrt(jnp.mean(hidden * hidden, axis=-1, keepdims=True) + 1e-05)
    normed_two = (hidden * inverse_two * gain_two).astype(BF16)
    logits = mm(normed_two, router_full)
    chosen = named.reshape(rows, experts)
    logits = jnp.where(chosen, logits, NEG_FILL)
    top = jnp.max(logits, axis=-1, keepdims=True)
    raised = jnp.where(chosen, jnp.exp(logits - top), 0.0)
    gate_probs = raised / jnp.sum(raised, axis=-1, keepdims=True)

    high = gate_probs.astype(BF16)
    low = (gate_probs - high.astype(F32)).astype(BF16)
    payload = jnp.concatenate(
        [normed_two, high, low, jnp.zeros((rows, LANES - 2 * experts), BF16)], axis=1
    ).reshape(micro, count, model + LANES)
    rows_in, row_weights, far_three = plane_dispatch(
        payload, ranks, bank, where, per, cap, model, experts
    )
    weights_far = [far_one, far_two, far_three]
    tile = 2 * micro * split * cap
    outs, backs, weight_terms, one_early = expert_steps(
        rows_in, grads_in, row_weights, bank, weights_far, experts, tile
    )
    back, one_late, three_early = plane_return(
        backs, ranks, weight_terms[1], weight_terms[3], micro, count, cap
    )
    back = back.reshape(rows, model + LANES)

    outs, back, late = lax.optimization_barrier((outs, back, weight_terms[2]))
    mixture_parts = scatter_rows(outs, ranks, where, n, micro * split, count, cap)
    mixture_sum = lax.psum_scatter(mixture_parts, "expert", scatter_dimension=0, tiled=False)
    term_two = shift(late, 2)

    d_out = cotangent.reshape(rows, model).astype(F32)
    d_gates = back[:, model : model + experts] + back[:, model + experts : model + 2 * experts]
    d_logits = gate_probs * (d_gates - jnp.sum(gate_probs * d_gates, axis=-1, keepdims=True))
    router_grad = lax.dot_general(normed_two.astype(F32), d_logits, TN, precision=HIGHEST)
    d_normed_two = back[:, :model] + lax.dot_general(
        d_logits, router_full.astype(F32), NT, precision=HIGHEST
    )

    def rms_back(inputs, inverse, gain, upstream):
        scaled = gain * upstream
        return inverse * scaled - inputs * inverse * inverse * inverse * jnp.mean(
            scaled * inputs, axis=-1, keepdims=True
        )

    grad_two = jnp.sum(d_normed_two * hidden * inverse_two, axis=0)
    d_hidden = d_out + rms_back(hidden, inverse_two, gain_two, d_normed_two)
    d_attn = d_hidden.astype(BF16)
    d_mixed = mm(d_attn, out_full, NT).astype(BF16).reshape(micro, count, query_width)
    d_project = plane_attention_backward(query, kv_slots, d_mixed, cosine, -sine)
    d_project = d_project.reshape(rows, query_width + 2 * kv_width)
    d_normed = mm(d_project, qkv_full, NT)
    grad_one = jnp.sum(d_normed * x * inverse_one, axis=0)
    input_grad = (d_hidden + rms_back(x, inverse_one, gain_one, d_normed)).reshape(tokens.shape)
    gains = jnp.concatenate([grad_one[None], grad_two[None], jnp.zeros((6, model), F32)], axis=0)
    dense, three_late = plane_gradients(
        [(mixed, d_attn), (normed, d_project)], router_grad, gains, weight_terms[3], groups
    )
    mixture_sum, dense = lax.optimization_barrier((mixture_sum, dense))
    mixture = mixture_sum[:micro].astype(F32) + turn(mixture_sum[micro:], 1, split).astype(F32)
    block_out = (hidden + mixture.reshape(rows, model)).astype(BF16).reshape(tokens.shape)
    terms = [weight_terms[0], [one_early, one_late], term_two, [three_early, three_late]]
    gate_grad, up_grad, down_grad = [merge_grads(which, where, terms) for which in range(3)]
    misc_sum = dense[:, model + query_width + 2 * kv_width :].astype(F32)
    return (
        block_out,
        input_grad,
        misc_sum[:, 0],
        dense[:, model : model + query_width + 2 * kv_width].astype(F32),
        dense[:, :model].astype(F32),
        misc_sum[:, 1],
        misc_sum[:, experts : 2 * experts],
        gate_grad,
        up_grad,
        down_grad,
    )


def per_device(*arrays):
    n, groups = lax.axis_size("expert"), lax.axis_size("group")
    exp_here, part, ff = arrays[8].shape
    plane = (
        n == 8
        and exp_here % 2 == 0
        and groups == 4
        and exp_here == 4
        and part % (16 * n) == 0
        and part % LANES == 0
        and arrays[0].shape[0] == 2
    )
    return (layer_plane if plane else layer_general)(*arrays)


def solution(mesh):
    rows = P(None, ("group", "expert"), None)
    return jax.shard_map(
        per_device,
        mesh=mesh,
        in_specs=(
            rows,
            rows,
            rows,
            P("group"),
            P("group", None),
            P("group", None),
            P("group"),
            P("group", None),
            P("expert", "group", None),
            P("expert", "group", None),
            P("expert", None, "group"),
        ),
        out_specs=(
            rows,
            rows,
            P("group"),
            P("group", None),
            P("group", None),
            P("group"),
            P("group", None),
            P("expert", "group", None),
            P("expert", "group", None),
            P("expert", None, "group"),
        ),
        check_vma=False,
    )
```

```python
import functools

import jax
import jax.numpy as jnp
from jax import lax
from jax.experimental import pallas as pl
from jax.experimental.pallas import tpu as pltpu
from jax.sharding import PartitionSpec as P

QUERY_HEADS = 24
KEY_VALUE_HEADS = 8
HEAD_SIZE = 64
TOPK = 8
CONT = 256
PR_DEV = 64
LANES = 128
SCORE_SCALE = 0.125
NEG_FILL = -1e30
HIGHEST = lax.Precision.HIGHEST
F32 = jnp.float32
BF16 = jnp.bfloat16

NN = (((1,), (0,)), ((), ()))
NT = (((1,), (1,)), ((), ()))
TN = (((0,), (0,)), ((), ()))


def mm(a, b, dims=NN):
    return lax.dot_general(a, b, dims, preferred_element_type=F32)


def swap(x, bit):
    n = lax.axis_size("expert")
    return lax.ppermute(x, "expert", [(i, i ^ bit) for i in range(n)])


def shift(x, step):
    n = lax.axis_size("group")
    return lax.ppermute(x, "group", [(i, (i + step) % n) for i in range(n)])


def turn(x, step, split):
    n = lax.axis_size("group")
    return lax.ppermute(
        x, "group", [((i // split) * split + (i + step) % split, i) for i in range(n)]
    )


def outer_bits(n):
    return [1 << i for i in range(1, n.bit_length() - 1)]


def spread(x, order):
    n = lax.axis_size("expert")
    outer = outer_bits(n)
    if len(outer) == 2:
        a, b = outer
        xa, xb = swap(x, a), swap(x, b)
        slots = {0: x, a: xa, b: xb, a ^ b: swap(xa, b) if order == 0 else swap(xb, a)}
    else:
        slots = {0: x}
        for bit in outer:
            slots.update({r ^ bit: swap(y, bit) for r, y in list(slots.items())})
    if n > 1:
        slots.update({r ^ 1: swap(y, 1) for r, y in list(slots.items())})
    return [slots[r] for r in range(n)]


def plus(a, b):
    return (a.astype(F32) + b.astype(F32)).astype(BF16)


def collect(parts, order):
    n = lax.axis_size("expert")
    outer = outer_bits(n)
    keep = {r: parts[r] for r in range(n)}
    if n > 1:
        keep = {r: plus(keep[r], swap(keep[r ^ 1], 1)) for r in range(0, n, 2)}
    if len(outer) == 2:
        a, b = outer
        if order == 0:
            keep[a] = plus(keep[a], swap(keep[a ^ b], b))
        else:
            keep[b] = plus(keep[b], swap(keep[a ^ b], a))
        return (
            keep[0].astype(F32) + swap(keep[a], a).astype(F32) + swap(keep[b], b).astype(F32)
        )
    for bit in reversed(outer):
        keep = {r: plus(keep[r], swap(keep[r ^ bit], bit)) for r in keep if not r & bit}
    return keep[0].astype(F32)


def full_spec(shape):
    return pl.BlockSpec(shape, lambda *_: (0,) * len(shape))


SMEM_SPEC = pl.BlockSpec(memory_space=pltpu.SMEM)
ANY_SPEC = pl.BlockSpec(memory_space=pl.ANY)


def cost(flops, moved):
    return pl.CostEstimate(flops=int(flops), bytes_accessed=int(moved), transcendentals=0)


def assemble(pieces, place, shape, where):
    count = len(pieces)

    def kernel(at_ref, *refs):
        ins, out, sems = refs[:count], refs[count], refs[count + 1]
        copies = []
        for i in range(count):
            row, column = place(i, at_ref[0], at_ref[1])
            r, c = pieces[i].shape
            copies.append(
                pltpu.make_async_copy(
                    ins[i],
                    out.at[pl.ds(pl.multiple_of(row, 16), r), pl.ds(pl.multiple_of(column, 128), c)],
                    sems.at[i],
                )
            )
        for one in copies:
            one.start()
        for one in copies:
            one.wait()

    return pl.pallas_call(
        kernel,
        grid=(1,),
        in_specs=[SMEM_SPEC] + [ANY_SPEC] * count,
        out_specs=full_spec(shape),
        out_shape=jax.ShapeDtypeStruct(shape, pieces[0].dtype),
        scratch_shapes=[pltpu.SemaphoreType.DMA((count,))],
        cost_estimate=cost(0, 4 * shape[0] * shape[1]),
        name="assemble",
    )(where, *pieces)


def gather_dense(piece, cuts, where):
    groups, n = lax.axis_size("group"), lax.axis_size("expert")
    rows, columns = piece.shape
    own = [piece[:, lo:hi] for lo, hi in cuts]
    far = [[shift(x, s) for x in own] for s in range(1, groups)]
    names, pieces = [], []
    for h, (lo, hi) in enumerate(cuts):
        joined = jnp.concatenate([far[s - 1][h] for s in range(1, groups)], axis=0)
        for r, x in enumerate(spread(own[h], h % 2)):
            names.append((0, r, lo))
            pieces.append(x)
        for r, x in enumerate(spread(joined, h % 2)):
            for s in range(1, groups):
                names.append((s, r, lo))
                pieces.append((x, (s - 1) * rows, rows))
    total = groups * n * rows
    arrays, index = [], []
    for entry in pieces:
        if isinstance(entry, tuple):
            if not arrays or arrays[-1] is not entry[0]:
                arrays.append(entry[0])
            index.append((len(arrays) - 1, entry[1], entry[2]))
        else:
            arrays.append(entry)
            index.append((len(arrays) - 1, 0, rows))
    count, held = len(index), len(arrays)

    def kernel(at_ref, *refs):
        ins, out, sems = refs[:held], refs[held], refs[held + 1]
        copies = []
        for i, (which, start, size) in enumerate(index):
            s, r, lo = names[i]
            z = lax.rem(at_ref[0] - s + groups, groups)
            e = jnp.bitwise_xor(at_ref[1], r)
            row = pl.multiple_of((z * n + e) * rows, 16)
            width = arrays[which].shape[1]
            copies.append(
                pltpu.make_async_copy(
                    ins[which].at[pl.ds(start, size)],
                    out.at[pl.ds(row, rows), pl.ds(lo, width)],
                    sems.at[i],
                )
            )
        for one in copies:
            one.start()
        for one in copies:
            one.wait()

    whole = pl.pallas_call(
        kernel,
        grid=(1,),
        in_specs=[SMEM_SPEC] + [ANY_SPEC] * held,
        out_specs=full_spec((total, columns)),
        out_shape=jax.ShapeDtypeStruct((total, columns), piece.dtype),
        scratch_shapes=[pltpu.SemaphoreType.DMA((count,))],
        cost_estimate=cost(0, 4 * total * columns),
        name="join_rows",
    )(where, *arrays)
    return whole, far


def sliced_outer(a, b, extra, groups, n, where):
    depth = a.shape[1]
    columns = b.shape[1]
    more = 0 if extra is None else extra.shape[1]
    rows = depth // (groups * n)

    def kernel(at_ref, a_ref, b_ref, *refs):
        if more:
            x_ref, refs = refs[0], refs[1:]
        outs, acc = refs[:n], refs[n]
        acc[:, :columns] = mm(a_ref[...], b_ref[...], TN)
        if more:
            acc[:, columns:] = x_ref[...]
        for r in range(n):
            e = jnp.bitwise_xor(at_ref[1], r)
            for s in range(groups):
                z = lax.rem(at_ref[0] + s, groups)
                row = pl.multiple_of((z * n + e) * rows, 16)
                outs[r][s] = acc[pl.ds(row, rows), :].astype(BF16)

    width = columns + more
    return pl.pallas_call(
        kernel,
        grid=(1,),
        in_specs=[SMEM_SPEC, full_spec(a.shape), full_spec(b.shape)]
        + ([full_spec(extra.shape)] if more else []),
        out_specs=[full_spec((groups, rows, width))] * n,
        out_shape=[jax.ShapeDtypeStruct((groups, rows, width), BF16)] * n,
        scratch_shapes=[pltpu.VMEM((depth, width), F32)],
        cost_estimate=cost(2 * a.shape[0] * depth * columns, 2 * depth * width),
        name="sliced_outer",
    )(where, a, b, *([extra] if more else []))


def reduce_dense(parts, order, where):
    groups, n = lax.axis_size("group"), lax.axis_size("expert")
    mine = collect(parts, order)
    total = mine[0]
    low = mine.astype(BF16)
    for s in range(1, groups):
        total = total + shift(low[s], s).astype(F32)
    rows, width = total.shape
    slots = spread(total.astype(BF16), order)

    def kernel(at_ref, *refs):
        out = refs[n]
        for r in range(n):
            e = jnp.bitwise_xor(at_ref[1], r)
            out[pl.ds(pl.multiple_of(e * rows, 16), rows), :] = refs[r][...].astype(F32)

    return pl.pallas_call(
        kernel,
        grid=(1,),
        in_specs=[SMEM_SPEC] + [full_spec((rows, width))] * n,
        out_specs=full_spec((n * rows, width)),
        out_shape=jax.ShapeDtypeStruct((n * rows, width), F32),
        cost_estimate=cost(0, 6 * n * rows * width),
        name="join_sums",
    )(where, *slots)


def attention_masks(n, me):
    shape = (3 * PR_DEV, n * PR_DEV)
    token = lax.rem(lax.broadcasted_iota(jnp.int32, shape, 0), PR_DEV)
    column = lax.broadcasted_iota(jnp.int32, shape, 1)
    key_pos = jnp.bitwise_xor(column // PR_DEV, me) * PR_DEV + lax.rem(column, PR_DEV)
    prompt_ok = key_pos <= me * PR_DEV + token
    slots = CONT // PR_DEV
    shape = (3 * PR_DEV, CONT)
    token = lax.rem(lax.broadcasted_iota(jnp.int32, shape, 0), PR_DEV)
    column = lax.broadcasted_iota(jnp.int32, shape, 1)
    owner = jnp.bitwise_xor(column // PR_DEV, lax.rem(me, slots))
    cont_ok = owner * PR_DEV + lax.rem(column, PR_DEV) <= lax.rem(me, slots) * PR_DEV + token
    return prompt_ok, cont_ok


def head_rows(x, base):
    return jnp.concatenate(
        [x[:, base + i * HEAD_SIZE : base + (i + 1) * HEAD_SIZE] for i in range(3)], axis=0
    )


def row_heads(x):
    return jnp.concatenate([x[i * PR_DEV : (i + 1) * PR_DEV] for i in range(3)], axis=1)


def softmax(scores):
    top = jnp.max(scores, axis=1, keepdims=True)
    weight = jnp.exp(scores - top)
    return weight * (1.0 / jnp.sum(weight, axis=1, keepdims=True))


def load_keys(n, kv_refs, keys):
    for r in range(n):
        keys[r * PR_DEV : (r + 1) * PR_DEV, :] = kv_refs[r][:PR_DEV, :]
    for r in range(CONT // PR_DEV):
        lo = (n + r) * PR_DEV
        keys[lo : lo + PR_DEV, :] = kv_refs[r][PR_DEV:, :]


def group_probs(q_top, q_low, key, prompt_ok, cont_ok, n):
    pr = n * PR_DEV
    top = mm(q_top, key[:pr], NT) * SCORE_SCALE
    top = softmax(jnp.where(prompt_ok, top, NEG_FILL))
    low = mm(q_low, key, NT) * SCORE_SCALE
    low = jnp.concatenate([low[:, :pr], jnp.where(cont_ok, low[:, pr:], NEG_FILL)], axis=1)
    return top, softmax(low)


def attention_forward(query, slots, where):
    n = len(slots)
    width = KEY_VALUE_HEADS * HEAD_SIZE
    tokens = 2 * PR_DEV
    total = n * PR_DEV + CONT

    def kernel(at_ref, q_ref, *refs):
        kv_refs, out_ref, keys = refs[:n], refs[n], refs[n + 1]
        load_keys(n, kv_refs, keys)
        prompt_ok, cont_ok = attention_masks(n, at_ref[1])

        def pair(j, carry):
            q_at = pl.ds(pl.multiple_of(j * 384, 128), 384)
            k_at = pl.ds(pl.multiple_of(j * 128, 128), 128)
            v_at = pl.ds(pl.multiple_of(width + j * 128, 128), 128)
            q_top, q_low = q_ref[:PR_DEV, q_at], q_ref[PR_DEV:, q_at]
            k_two, v_two = keys[:, k_at], keys[:, v_at]
            tops, lows = [], []
            for g in range(2):
                key = k_two[:, g * HEAD_SIZE : (g + 1) * HEAD_SIZE]
                value = v_two[:, g * HEAD_SIZE : (g + 1) * HEAD_SIZE]
                top, low = group_probs(
                    head_rows(q_top, g * 192), head_rows(q_low, g * 192), key, prompt_ok, cont_ok, n
                )
                tops.append(row_heads(mm(top.astype(BF16), value[: n * PR_DEV])))
                lows.append(row_heads(mm(low.astype(BF16), value)))
            out_ref[:PR_DEV, q_at] = jnp.concatenate(tops, axis=1).astype(BF16)
            out_ref[PR_DEV:, q_at] = jnp.concatenate(lows, axis=1).astype(BF16)
            return carry

        lax.fori_loop(0, KEY_VALUE_HEADS // 2, pair, 0)

    return pl.pallas_call(
        kernel,
        grid=(1,),
        in_specs=[SMEM_SPEC, full_spec(query.shape)] + [full_spec((tokens, 2 * width))] * n,
        out_specs=full_spec(query.shape),
        out_shape=jax.ShapeDtypeStruct(query.shape, BF16),
        scratch_shapes=[pltpu.VMEM((total, 2 * width), BF16)],
        cost_estimate=cost(8e9, 4e6),
        name="attention_forward",
    )(where, query, *slots)


def attention_backward(query, slots, d_mixed, where):
    n = len(slots)
    width = KEY_VALUE_HEADS * HEAD_SIZE
    tokens = 2 * PR_DEV
    pr = n * PR_DEV
    total = pr + CONT

    def kernel(at_ref, q_ref, d_ref, *refs):
        kv_refs, refs = refs[:n], refs[n:]
        dq_ref, outs, keys, grads = refs[0], refs[1 : 1 + n], refs[1 + n], refs[2 + n]
        load_keys(n, kv_refs, keys)
        prompt_ok, cont_ok = attention_masks(n, at_ref[1])

        def one_side(prob, d_rows, key, value, q_rows):
            d_prob = mm(d_rows, value, NT)
            delta = jnp.sum(prob * d_prob, axis=1, keepdims=True)
            d_score = (prob * (d_prob - delta)).astype(BF16)
            return (
                mm(d_score, key) * SCORE_SCALE,
                mm(d_score, q_rows, TN) * SCORE_SCALE,
                mm(prob.astype(BF16), d_rows, TN),
            )

        def pair(j, carry):
            q_at = pl.ds(pl.multiple_of(j * 384, 128), 384)
            k_at = pl.ds(pl.multiple_of(j * 128, 128), 128)
            v_at = pl.ds(pl.multiple_of(width + j * 128, 128), 128)
            q_top, q_low = q_ref[:PR_DEV, q_at], q_ref[PR_DEV:, q_at]
            d_top, d_low = d_ref[:PR_DEV, q_at], d_ref[PR_DEV:, q_at]
            k_two, v_two = keys[:, k_at], keys[:, v_at]
            dq_tops, dq_lows, dks, dvs = [], [], [], []
            for g in range(2):
                key = k_two[:, g * HEAD_SIZE : (g + 1) * HEAD_SIZE]
                value = v_two[:, g * HEAD_SIZE : (g + 1) * HEAD_SIZE]
                rows_top, rows_low = head_rows(q_top, g * 192), head_rows(q_low, g * 192)
                top, low = group_probs(rows_top, rows_low, key, prompt_ok, cont_ok, n)
                dq_top, dk_top, dv_top = one_side(
                    top, head_rows(d_top, g * 192), key[:pr], value[:pr], rows_top
                )
                dq_low, dk_low, dv_low = one_side(
                    low, head_rows(d_low, g * 192), key, value, rows_low
                )
                dq_tops.append(row_heads(dq_top))
                dq_lows.append(row_heads(dq_low))
                dks.append(jnp.concatenate([dk_low[:pr] + dk_top, dk_low[pr:]], axis=0))
                dvs.append(jnp.concatenate([dv_low[:pr] + dv_top, dv_low[pr:]], axis=0))
            dq_ref[:PR_DEV, q_at] = jnp.concatenate(dq_tops, axis=1)
            dq_ref[PR_DEV:, q_at] = jnp.concatenate(dq_lows, axis=1)
            grads[:, k_at] = jnp.concatenate(dks, axis=1).astype(BF16)
            grads[:, v_at] = jnp.concatenate(dvs, axis=1).astype(BF16)
            return carry

        lax.fori_loop(0, KEY_VALUE_HEADS // 2, pair, 0)
        for r in range(n):
            outs[r][:PR_DEV, :] = grads[r * PR_DEV : (r + 1) * PR_DEV, :]
            if r < CONT // PR_DEV:
                lo = (n + r) * PR_DEV
                outs[r][PR_DEV:, :] = grads[lo : lo + PR_DEV, :]
            else:
                outs[r][PR_DEV:, :] = jnp.zeros((PR_DEV, 2 * width), BF16)

    out = pl.pallas_call(
        kernel,
        grid=(1,),
        in_specs=[SMEM_SPEC, full_spec(query.shape), full_spec(query.shape)]
        + [full_spec((tokens, 2 * width))] * n,
        out_specs=[full_spec(query.shape)] + [full_spec((tokens, 2 * width))] * n,
        out_shape=[jax.ShapeDtypeStruct(query.shape, F32)]
        + [jax.ShapeDtypeStruct((tokens, 2 * width), BF16)] * n,
        scratch_shapes=[pltpu.VMEM((total, 2 * width), BF16), pltpu.VMEM((total, 2 * width), BF16)],
        cost_estimate=cost(2e10, 8e6),
        name="attention_backward",
    )(where, query, d_mixed, *slots)
    return out[0], out[1:]


def pick(slot_row, cap):
    rows = lax.broadcasted_iota(jnp.int32, (cap, slot_row.shape[1]), 0).astype(F32)
    return jnp.where(slot_row == rows, 1.0, 0.0).astype(BF16)


def dispatch_grads(arrays, at, per, cap, model, buffers, place, blocks_total):
    count = len(arrays)
    split, tokens, width = arrays[0].shape
    blocks = count * split
    first = buffers is None

    def kernel(at_ref, *refs):
        ins = refs[:count]
        out, ranks = refs[-3], refs[-2]
        flags = refs[-1]
        row = lax.broadcasted_iota(jnp.int32, (tokens, tokens), 0)
        col = lax.broadcasted_iota(jnp.int32, (tokens, tokens), 1)
        before = jnp.where(row < col, 1.0, 0.0).astype(BF16)
        for i in range(count):
            for j in range(split):
                b = i * split + j
                payload = ins[i][j]
                flags[...] = payload[:, model:].astype(F32).T
                picked = jnp.concatenate(
                    [flags[pl.ds(at_ref[2] + k, 1), :] for k in range(per)], axis=0
                )
                rank = mm(picked.astype(BF16), before)
                slot = jnp.where(picked > 0.0, rank, -1.0)
                ranks[b] = slot
                for k in range(per):
                    out[k, b * cap : (b + 1) * cap, :] = mm(
                        pick(slot[k : k + 1], cap), payload[:, :model]
                    ).astype(BF16)

    shapes = [
        jax.ShapeDtypeStruct((per, blocks_total * cap, model), BF16),
        jax.ShapeDtypeStruct((blocks_total, per, tokens), F32),
    ]
    return pl.pallas_call(
        kernel,
        grid=(1,),
        in_specs=[SMEM_SPEC]
        + [full_spec(arrays[0].shape)] * count
        + ([] if first else [ANY_SPEC] * 2),
        out_specs=[
            pl.BlockSpec((per, blocks * cap, model), lambda *_: (0, place, 0)),
            pl.BlockSpec((blocks, per, tokens), lambda *_: (place, 0, 0)),
        ],
        out_shape=shapes,
        scratch_shapes=[pltpu.VMEM((LANES, tokens), F32)],
        input_output_aliases={} if first else {1 + count: 0, 2 + count: 1},
        cost_estimate=cost(1e9, 6e6),
        name="dispatch_grads",
    )(at, *arrays, *([] if first else buffers))


def dispatch_rows(arrays, ranks, at, per, cap, model, experts, buffers, place, blocks_total):
    count = len(arrays)
    split, tokens, width = arrays[0].shape
    blocks = count * split
    first = buffers is None

    def kernel(at_ref, rank_ref, *refs):
        ins = refs[:count]
        out, weights = refs[-2], refs[-1]
        lane = lax.broadcasted_iota(jnp.int32, (cap, LANES), 1)
        for i in range(count):
            for j in range(split):
                b = i * split + j
                payload = ins[i][j]
                for k in range(per):
                    got = mm(pick(rank_ref[b, k : k + 1, :], cap), payload)
                    out[k, b * cap : (b + 1) * cap, :] = got[:, :model].astype(BF16)
                    tail = got[:, model:]
                    e = at_ref[2] + k
                    mine = (lane == e) | (lane == e + experts)
                    total = jnp.sum(jnp.where(mine, tail, 0.0), axis=1, keepdims=True)
                    weights[k, b * cap : (b + 1) * cap, :] = jnp.broadcast_to(total, (cap, LANES))

    shapes = [
        jax.ShapeDtypeStruct((per, blocks_total * cap, model), BF16),
        jax.ShapeDtypeStruct((per, blocks_total * cap, LANES), F32),
    ]
    return pl.pallas_call(
        kernel,
        grid=(1,),
        in_specs=[SMEM_SPEC, pl.BlockSpec((blocks, per, tokens), lambda *_: (place, 0, 0))]
        + [full_spec(arrays[0].shape)] * count
        + ([] if first else [ANY_SPEC] * 2),
        out_specs=[
            pl.BlockSpec((per, blocks * cap, model), lambda *_: (0, place, 0)),
            pl.BlockSpec((per, blocks * cap, LANES), lambda *_: (0, place, 0)),
        ],
        out_shape=shapes,
        input_output_aliases={} if first else {2 + count: 0, 3 + count: 1},
        cost_estimate=cost(1e9, 6e6),
        name="dispatch_rows",
    )(at, ranks, *arrays, *([] if first else buffers))


def run_expert(k, at, rows_in, grads_in, weights, gate, up, down, experts, tile, groups, cut):
    per, total, model = rows_in.shape
    ff = gate.shape[1]
    part = model // groups
    steps = total // tile

    def kernel(at_ref, x_ref, d_ref, w_ref, gate_ref, up_ref, down_ref, o_ref, r_ref, *refs):
        outs, (acc_gate, acc_up, acc_down) = refs[:-3], refs[-3:]
        step = pl.program_id(0)
        x, d = x_ref[0], d_ref[0]
        w = w_ref[0, :, 0:1]
        gate_pre = mm(x, gate_ref[...])
        up_pre = mm(x, up_ref[...])
        sig = 1.0 / (1.0 + jnp.exp(-gate_pre))
        silu = gate_pre * sig
        active_wide = silu * up_pre
        active = active_wide.astype(BF16)
        out = mm(active, down_ref[...])
        o_ref[...] = (out * w).astype(BF16)
        d_raw = mm(d, down_ref[...], NT)
        d_gates = jnp.sum(active.astype(F32) * d_raw, axis=1, keepdims=True)
        d_active = d_raw * w
        d_up = (d_active * silu).astype(BF16)
        d_gate = (d_active * up_pre * sig * (1.0 + gate_pre * (1.0 - sig))).astype(BF16)
        d_row = mm(d_gate, gate_ref[...], NT) + mm(d_up, up_ref[...], NT)
        r_ref[:, :model] = d_row.astype(BF16)
        high = d_gates.astype(BF16).astype(F32)
        lane = lax.broadcasted_iota(jnp.int32, (tile, LANES), 1)
        e = at_ref[2] + k
        r_ref[:, model:] = (
            jnp.where(lane == e, high, 0.0) + jnp.where(lane == e + experts, d_gates - high, 0.0)
        ).astype(BF16)
        new_gate = mm(x, d_gate, TN)
        new_up = mm(x, d_up, TN)
        new_down = mm((active_wide * w).astype(BF16), d, TN)

        @pl.when(step == 0)
        def _():
            acc_gate[...] = new_gate
            acc_up[...] = new_up
            acc_down[...] = new_down

        @pl.when(step > 0)
        def _():
            acc_gate[...] += new_gate
            acc_up[...] += new_up
            acc_down[...] += new_down

        @pl.when(step == steps - 1)
        def _():
            if cut:
                for s in range(groups):
                    z = lax.rem(at_ref[0] + s, groups)
                    at_z = pl.ds(pl.multiple_of(z * part, 128), part)
                    outs[s][...] = acc_gate[at_z, :].astype(BF16)
                    outs[groups + s][...] = acc_up[at_z, :].astype(BF16)
                    outs[2 * groups + s][...] = acc_down[:, at_z].astype(BF16)
            else:
                outs[0][...] = acc_gate[...].astype(BF16)
                outs[1][...] = acc_up[...].astype(BF16)
                outs[2][...] = acc_down[...].astype(BF16)

    if cut:
        grads = [(part, ff)] * (2 * groups) + [(ff, part)] * groups
    else:
        grads = [(model, ff)] * 2 + [(ff, model)]
    row_spec = pl.BlockSpec((1, tile, model), lambda t: (k, t, 0))
    held = lambda shape: pl.BlockSpec(shape, lambda t: (0, 0), pipeline_mode=pl.Buffered(1))
    out = pl.pallas_call(
        kernel,
        grid=(steps,),
        in_specs=[
            SMEM_SPEC,
            row_spec,
            row_spec,
            pl.BlockSpec((1, tile, LANES), lambda t: (k, t, 0)),
            held((model, ff)),
            held((model, ff)),
            held((ff, model)),
        ],
        out_specs=[
            pl.BlockSpec((tile, model), lambda t: (t, 0)),
            pl.BlockSpec((tile, model + LANES), lambda t: (t, 0)),
        ]
        + [held(shape) for shape in grads],
        out_shape=[
            jax.ShapeDtypeStruct((total, model), BF16),
            jax.ShapeDtypeStruct((total, model + LANES), BF16),
        ]
        + [jax.ShapeDtypeStruct(shape, BF16) for shape in grads],
        scratch_shapes=[
            pltpu.VMEM((model, ff), F32),
            pltpu.VMEM((model, ff), F32),
            pltpu.VMEM((ff, model), F32),
        ],
        compiler_params=pltpu.CompilerParams(vmem_limit_bytes=62 * 1024 * 1024),
        cost_estimate=cost(18 * total * model * ff, 10 * total * model),
        name="run_expert",
    )(at, rows_in, grads_in, weights, gate, up, down)
    return out[0], out[1], out[2:]


def combine(rows, ranks, count, split, tokens, cap, place):
    per = len(rows)
    width = rows[0].shape[1]
    blocks = count * split

    def kernel(rank_ref, *refs):
        ins, outs = refs[:per], refs[per:]
        for i in range(count):
            for j in range(split):
                b = i * split + j
                total = None
                for k in range(per):
                    one = mm(
                        pick(rank_ref[b, k : k + 1, :], cap), ins[k][b * cap : (b + 1) * cap, :], TN
                    )
                    total = one if total is None else total + one
                outs[i][j] = total.astype(BF16)

    return pl.pallas_call(
        kernel,
        grid=(1,),
        in_specs=[pl.BlockSpec((blocks, per, tokens), lambda *_: (place, 0, 0))]
        + [pl.BlockSpec((blocks * cap, width), lambda *_: (place, 0))] * per,
        out_specs=[full_spec((split, tokens, width))] * count,
        out_shape=[jax.ShapeDtypeStruct((split, tokens, width), BF16)] * count,
        cost_estimate=cost(1e9, 6e6),
        name="combine",
    )(ranks, *rows)


def rope_tables(my_index, prompt_len):
    half = HEAD_SIZE // 2
    local = jnp.arange(2 * PR_DEV, dtype=jnp.int32)
    cont = my_index * PR_DEV + local - PR_DEV
    position = jnp.where(local < PR_DEV, my_index * PR_DEV + local, prompt_len + cont % CONT)
    frequency = 10000.0 ** (-jnp.arange(half, dtype=F32) * (2.0 / HEAD_SIZE))
    angle = position.astype(F32)[:, None] * frequency[None, :]
    return jnp.cos(angle), jnp.sin(angle)


def rotate(x, cosine, sine):
    half = HEAD_SIZE // 2
    column = lax.broadcasted_iota(jnp.int32, x.shape, 1)
    other = jnp.where(column % HEAD_SIZE < half, jnp.roll(x, -half, axis=1), jnp.roll(x, half, axis=1))
    return x * cosine + other * sine


def layer_general(
    tokens,
    cotangent,
    routes,
    norm_one,
    query_key_value_weight,
    out_weight,
    norm_two,
    router_weight,
    gate_weight,
    up_weight,
    down_weight,
):
    n = lax.axis_size("expert")
    groups = lax.axis_size("group")
    me = lax.axis_index("expert")
    z = lax.axis_index("group")
    micro, count, model = tokens.shape
    exp_here, part, ff = gate_weight.shape
    experts = router_weight.shape[1]
    split = 2 if exp_here % 2 == 0 and groups % 2 == 0 else 1
    per = exp_here // split
    query_width = QUERY_HEADS * HEAD_SIZE
    kv_width = KEY_VALUE_HEADS * HEAD_SIZE
    cap = max(2, 3 * TOPK * PR_DEV // experts)
    where = jnp.stack([z, me, me * exp_here + (z % split) * per]).astype(jnp.int32)
    rows_here = part // n if part % n == 0 else 0
    aligned = rows_here > 0 and rows_here % 16 == 0 and part % LANES == 0

    misc = jnp.concatenate(
        [
            norm_one[:, None],
            norm_two[:, None],
            jnp.zeros((part, experts - 2), BF16),
            router_weight,
            jnp.zeros((part, LANES - 2 * experts), BF16),
        ],
        axis=1,
    )
    if aligned:
        first = jnp.concatenate([query_key_value_weight, misc], axis=1)
        cut = lambda x: lax.dynamic_slice_in_dim(x, me * rows_here, rows_here, axis=0)
        width = first.shape[1]
        middle = width // 2 // LANES * LANES
        first_full, far = gather_dense(cut(first), [(0, middle), (middle, width)], where)
        out_full, far_out = gather_dense(
            cut(out_weight), [(0, model // 2), (model // 2, model)], where
        )
        after = (far, far_out)
    else:
        first_full = lax.all_gather(
            jnp.concatenate([query_key_value_weight, misc], axis=1), "group", axis=0, tiled=True
        )
        out_full = lax.all_gather(out_weight, "group", axis=0, tiled=True)
        after = ()
    qkv_columns = query_key_value_weight.shape[1]
    qkv_full = first_full[:, :qkv_columns]
    misc_full = first_full[:, qkv_columns:]
    gain_one = misc_full[:, 0].astype(F32)
    gain_two = misc_full[:, 1].astype(F32)
    router_full = misc_full[:, experts : 2 * experts]

    weights_held = []
    gate_from, up_from, down_from = gate_weight, up_weight, down_weight
    if aligned:
        (gate_from, up_from, down_from), after = lax.optimization_barrier(
            ((gate_weight, up_weight, down_weight), after)
        )
    for k in range(per):
        held = []
        for array, axis in ((gate_from, 0), (up_from, 0), (down_from, 1)):
            if not aligned:
                held.append(lax.all_gather(array[k], "group", axis=axis, tiled=True))
                continue
            pieces = []
            for s in range(groups):
                index = ((z + s) % split) * per + k
                chunk = lax.dynamic_index_in_dim(array, index, 0, keepdims=False)
                pieces.append(shift(chunk, s) if s else chunk)

            def place(i, at_z, at_e, axis=axis):
                start = lax.rem(at_z - i + groups, groups) * part
                return (start, 0) if axis == 0 else (0, start)

            shape = (model, ff) if axis == 0 else (ff, model)
            held.append(assemble(pieces, place, shape, where))
        weights_held.append(held)

    expert_ids = jnp.arange(experts, dtype=jnp.int32)
    named = jnp.any(routes[..., None] == expert_ids, axis=2)
    pad = jnp.zeros((micro, count, LANES - experts), BF16)
    d_payload = jnp.concatenate([cotangent, named.astype(BF16), pad], axis=2)

    def to_experts(payload):
        held = []
        for m in range(micro):
            own = payload[m]
            both = jnp.stack([own] + [turn(own, j, split) for j in range(1, split)])
            held.append(spread(both, m % 2))
        return held

    def to_owners(parts):
        held = []
        for m in range(micro):
            total = collect(parts[m], m % 2)
            mine = total[0]
            for j in range(1, split):
                mine = mine + turn(total[j].astype(BF16), split - j, split).astype(F32)
            held.append(mine)
        return jnp.stack(held)

    slots_per = 2 if n % 2 == 0 else 1
    batches = [list(range(g * slots_per, (g + 1) * slots_per)) for g in range(n // slots_per)]
    blocks_total = n * micro * split

    d_slots = to_experts(d_payload)
    buffers = None
    for g, batch in enumerate(batches):
        buffers = dispatch_grads(
            [d_slots[m][r] for r in batch for m in range(micro)],
            where, per, cap, model, buffers, g, blocks_total,
        )
    grads_in, ranks = buffers

    rows = micro * count
    x = tokens.reshape(rows, model).astype(F32)
    inverse_one = lax.rsqrt(jnp.mean(x * x, axis=-1, keepdims=True) + 1e-05)
    normed = (x * inverse_one * gain_one).astype(BF16)
    cosine, sine = rope_tables(me, PR_DEV * n)
    heads_rope = QUERY_HEADS + KEY_VALUE_HEADS
    cosine = jnp.tile(jnp.concatenate([cosine, cosine], axis=1), (micro, heads_rope))
    sine = jnp.tile(jnp.concatenate([-sine, sine], axis=1), (micro, heads_rope))
    cosine, sine = lax.optimization_barrier((cosine, sine))
    project = mm(normed, qkv_full)
    roped = rotate(project[:, : query_width + kv_width], cosine, sine).astype(BF16)
    query = roped[:, :query_width]
    key_value = jnp.concatenate(
        [roped[:, query_width:], project[:, query_width + kv_width :].astype(BF16)], axis=1
    ).reshape(micro, count, 2 * kv_width)
    query = query.reshape(micro, count, query_width)
    kv_slots = [spread(key_value[m], m % 2) for m in range(micro)]
    mixed = jnp.concatenate(
        [attention_forward(query[m], kv_slots[m], where) for m in range(micro)], axis=0
    )
    hidden = x + mm(mixed, out_full)
    inverse_two = lax.rsqrt(jnp.mean(hidden * hidden, axis=-1, keepdims=True) + 1e-05)
    normed_two = (hidden * inverse_two * gain_two).astype(BF16)
    logits = mm(normed_two, router_full)
    chosen = named.reshape(rows, experts)
    logits = jnp.where(chosen, logits, NEG_FILL)
    top = jnp.max(logits, axis=-1, keepdims=True)
    raised = jnp.where(chosen, jnp.exp(logits - top), 0.0)
    gate_probs = raised / jnp.sum(raised, axis=-1, keepdims=True)

    high = gate_probs.astype(BF16)
    low = (gate_probs - high.astype(F32)).astype(BF16)
    payload = jnp.concatenate(
        [normed_two, high, low, jnp.zeros((rows, LANES - 2 * experts), BF16)], axis=1
    ).reshape(micro, count, model + LANES)
    x_slots = to_experts(payload)
    buffers = None
    for g, batch in enumerate(batches):
        buffers = dispatch_rows(
            [x_slots[m][r] for r in batch for m in range(micro)],
            ranks, where, per, cap, model, experts, buffers, g, blocks_total,
        )
    rows_in, row_weights = buffers
    tile = slots_per * micro * split * cap
    outs, backs, weight_terms = [], [], []
    for k in range(per):
        out_rows, back_rows, terms = run_expert(
            k, where, rows_in, grads_in, row_weights, *weights_held[k], experts, tile, groups, aligned
        )
        outs.append(out_rows)
        backs.append(back_rows)
        weight_terms.append(terms)

    def returned(row_arrays):
        parts = [[None] * n for _ in range(micro)]
        for g in reversed(range(len(batches))):
            got = combine(
                row_arrays, ranks, len(batches[g]) * micro, split, count, cap, g
            )
            for i, (r, m) in enumerate((r, m) for r in batches[g] for m in range(micro)):
                parts[m][r] = got[i]
        return to_owners(parts)

    back = returned(backs).reshape(rows, model + LANES)
    mixture = returned(outs).reshape(rows, model)
    block_out = (hidden + mixture).astype(BF16).reshape(tokens.shape)

    expert_grads = []
    for which in range(3):
        per_class = []
        for k in range(per):
            if not aligned:
                axis = 1 if which == 2 else 0
                per_class.append(
                    [lax.psum_scatter(weight_terms[k][which], "group", scatter_dimension=axis, tiled=True).astype(F32)]
                )
                continue
            sums = [None] * split
            for s in range(groups):
                term = weight_terms[k][which * groups + s]
                term = (shift(term, s) if s else term).astype(F32)
                c = s % split
                sums[c] = term if sums[c] is None else sums[c] + term
            per_class.append(
                [lax.select_n((z - p) % split, *sums) if split > 1 else sums[0] for p in range(split)]
            )
        expert_grads.append(
            jnp.stack([per_class[k][p] for p in range(split) for k in range(per)])
        )

    d_out = cotangent.reshape(rows, model).astype(F32)
    d_gates = back[:, model : model + experts] + back[:, model + experts : model + 2 * experts]
    d_logits = gate_probs * (d_gates - jnp.sum(gate_probs * d_gates, axis=-1, keepdims=True))
    router_grad = lax.dot_general(normed_two.astype(F32), d_logits, TN, precision=HIGHEST)
    d_normed_two = back[:, :model] + lax.dot_general(
        d_logits, router_full.astype(F32), NT, precision=HIGHEST
    )

    def rms_back(inputs, inverse, gain, upstream):
        scaled = gain * upstream
        return inverse * scaled - inputs * inverse * inverse * inverse * jnp.mean(
            scaled * inputs, axis=-1, keepdims=True
        )

    grad_two = jnp.sum(d_normed_two * hidden * inverse_two, axis=0)
    d_hidden = d_out + rms_back(hidden, inverse_two, gain_two, d_normed_two)
    d_attn = d_hidden.astype(BF16)
    d_mixed = mm(d_attn, out_full, NT).astype(BF16).reshape(micro, count, query_width)
    d_query, kv_terms = [], []
    for m in range(micro):
        got, terms = attention_backward(query[m], kv_slots[m], d_mixed[m], where)
        d_query.append(got)
        kv_terms.append(terms)
    d_query = jnp.concatenate(d_query, axis=0)
    q_cos, q_sin = cosine[:, :query_width], sine[:, :query_width]
    d_query_low = rotate(d_query, q_cos, -q_sin).astype(BF16)
    d_kv = jnp.concatenate([collect(kv_terms[m], m % 2) for m in range(micro)], axis=0)
    d_key_low = rotate(d_kv[:, :kv_width], q_cos[:, :kv_width], -q_sin[:, :kv_width]).astype(BF16)
    d_kv_low = jnp.concatenate([d_key_low, d_kv[:, kv_width:].astype(BF16)], axis=1)
    d_normed = mm(d_query_low, qkv_full[:, :query_width], NT) + mm(
        d_kv_low, qkv_full[:, query_width:], NT
    )
    grad_one = jnp.sum(d_normed * x * inverse_one, axis=0)
    input_grad = (d_hidden + rms_back(x, inverse_one, gain_one, d_normed)).reshape(tokens.shape)
    misc_grad = jnp.concatenate(
        [
            grad_one[:, None],
            grad_two[:, None],
            jnp.zeros((model, experts - 2), F32),
            router_grad,
            jnp.zeros((model, LANES - 2 * experts), F32),
        ],
        axis=1,
    )
    if aligned:
        grad_out = reduce_dense(sliced_outer(mixed, d_attn, None, groups, n, where), 0, where)
        grad_q = reduce_dense(sliced_outer(normed, d_query_low, None, groups, n, where), 1, where)
        grad_rest = reduce_dense(
            sliced_outer(normed, d_kv_low, misc_grad, groups, n, where), 0, where
        )
    else:

        def whole(value):
            low = lax.psum_scatter(value.astype(BF16), "group", scatter_dimension=0, tiled=True)
            return lax.psum(low, "expert").astype(F32)

        grad_out = whole(mm(mixed, d_attn, TN))
        grad_q = whole(mm(normed, d_query_low, TN))
        grad_rest = whole(jnp.concatenate([mm(normed, d_kv_low, TN), misc_grad], axis=1))
    grad_qkv = jnp.concatenate([grad_q, grad_rest[:, : 2 * kv_width]], axis=1)
    misc_sum = grad_rest[:, 2 * kv_width :]
    return (
        block_out,
        input_grad,
        misc_sum[:, 0],
        grad_qkv,
        grad_out,
        misc_sum[:, 1],
        misc_sum[:, experts : 2 * experts],
        *expert_grads,
    )


def flip(e, r):
    for bit in (1, 2, 4):
        if r & bit:
            e = e + bit - 2 * bit * lax.rem(e // bit, 2)
    return e


def partner(z):
    return z + 1 - 2 * lax.rem(z, 2)


def remote(src, dst, send, recv, device):
    return pltpu.make_async_remote_copy(
        src_ref=src,
        dst_ref=dst,
        send_sem=send,
        recv_sem=recv,
        device_id=device,
        device_id_type=pl.DeviceIdType.MESH,
    )


def greet(devices):
    barrier = pltpu.get_barrier_semaphore()
    for device in devices:
        pl.semaphore_signal(barrier, inc=1, device_id=device, device_id_type=pl.DeviceIdType.MESH)
    pl.semaphore_wait(barrier, len(devices))


def plane_devices(e):
    return [{"expert": flip(e, bit)} for bit in (1, 2, 4)]


class Gather:
    def __init__(self, e, own, loc, paths, send, recv):
        self.e, self.own, self.loc, self.paths, self.send, self.recv = e, own, loc, paths, send, recv

    def copy(self, r, bit, c):
        q = r ^ bit
        src = self.own(c) if r == 0 else self.loc(r, r, c)
        return remote(
            src, self.loc(r, q, c), self.send.at[q, c], self.recv.at[q, c],
            {"expert": flip(self.e, bit)},
        )

    def begin(self, c):
        for bit in (2, 4, 1):
            self.copy(0, bit, c).start()

    def arrived(self, q, c):
        here = self.loc(q, q, c)
        remote(
            here, here, self.send.at[q, c], self.recv.at[q, c], {"expert": flip(self.e, 1)}
        ).wait_recv()

    def pass_on(self, q, c):
        if q == 2 and self.paths[c] == 0:
            self.copy(2, 4, c).start()
        if q == 4 and self.paths[c] == 1:
            self.copy(4, 2, c).start()
        if q in (2, 4, 6):
            self.copy(q, 1, c).start()

    def finish(self, c):
        for bit in (2, 4, 1):
            self.copy(0, bit, c).wait_send()
        if self.paths[c] == 0:
            self.copy(2, 4, c).wait_send()
        else:
            self.copy(4, 2, c).wait_send()
        for q in (2, 4, 6):
            self.copy(q, 1, c).wait_send()

    def stage(self, chunks, slots):
        for c in chunks:
            for q in slots:
                self.arrived(q, c)
                self.pass_on(q, c)

    def forward_all(self, chunks, use=None):
        for c in chunks:
            for q in (2, 4):
                self.arrived(q, c)
                self.pass_on(q, c)
        if use:
            for c in chunks:
                self.arrived(1, c)
                use(1, c)
                use(2, c)
                use(4, c)
        for c in chunks:
            self.arrived(6, c)
            self.pass_on(6, c)
            if use:
                use(6, c)
        for c in chunks:
            for q in (3, 5, 7) if use else (1, 3, 5, 7):
                self.arrived(q, c)
                if use:
                    use(q, c)


def add_rows(dst, sources, step=16):
    rows = sources[0].shape[0]

    def one(i, carry):
        at = pl.ds(pl.multiple_of(i * step, step), step)
        total = sources[0][at, :].astype(F32)
        for source in sources[1:]:
            total = total + source[at, :].astype(F32)
        dst[at, :] = total.astype(dst.dtype)
        return carry

    lax.fori_loop(0, rows // step, one, 0)


class Reduce:
    def __init__(self, e, part, paths, core, diag, near, acc, send, recv):
        self.e, self.part, self.paths = e, part, paths
        self.core, self.diag, self.near, self.acc = core, diag, near, acc
        self.send, self.recv = send, recv

    def core_copy(self, h, c):
        return remote(
            self.part(2 * h + 1, c), self.core.at[h, c], self.send.at[h, c], self.recv.at[h, c],
            {"expert": flip(self.e, 1)},
        )

    def diag_copy(self, c):
        return remote(
            self.acc.at[2, c], self.diag.at[c], self.send.at[4, c], self.recv.at[4, c],
            {"expert": flip(self.e, 4 if self.paths[c] == 0 else 2)},
        )

    def near_copy(self, i, c):
        return remote(
            self.acc.at[i, c], self.near.at[i, c], self.send.at[5 + i, c], self.recv.at[5 + i, c],
            {"expert": flip(self.e, 2 if i == 0 else 4)},
        )

    def begin(self, r, c):
        self.core_copy(r // 2, c).start()

    def diagonal(self, chunks):
        for c in chunks:
            self.core_copy(3, c).wait_recv()
            add_rows(self.acc.at[2, c], [self.part(6, c), self.core.at[3, c]])
            self.diag_copy(c).start()

    def sides(self, chunks):
        for c in chunks:
            for i in (0, 1) if self.paths[c] == 1 else (1, 0):
                self.core_copy(1 + i, c).wait_recv()
                terms = [self.part(2 + 2 * i, c), self.core.at[1 + i, c]]
                if self.paths[c] == i:
                    self.diag_copy(c).wait_recv()
                    terms.append(self.diag.at[c])
                add_rows(self.acc.at[i, c], terms)
                self.near_copy(i, c).start()

    def total(self, c):
        self.core_copy(0, c).wait_recv()
        self.near_copy(0, c).wait_recv()
        self.near_copy(1, c).wait_recv()
        return [self.part(0, c), self.core.at[0, c], self.near.at[0, c], self.near.at[1, c]]

    def finish(self, c):
        for h in range(4):
            self.core_copy(h, c).wait_send()
        self.diag_copy(c).wait_send()
        for i in range(2):
            self.near_copy(i, c).wait_send()


def reduce_scratch(count, rows, width):
    return [
        pltpu.VMEM((4, count, rows, width), BF16),
        pltpu.VMEM((count, rows, width), BF16),
        pltpu.VMEM((2, count, rows, width), BF16),
        pltpu.VMEM((3, count, rows, width), BF16),
        pltpu.SemaphoreType.DMA((7, count)),
        pltpu.SemaphoreType.DMA((7, count)),
    ]


def params(identity, vmem=62):
    return pltpu.CompilerParams(
        collective_id=identity, has_side_effects=True, vmem_limit_bytes=vmem * 1024 * 1024
    )


def plane_weights(shares, bank, per):
    n, split = 8, 2
    groups = lax.axis_size("group")
    rows = shares[0].shape[0]
    kinds = len(shares)
    count = groups * kinds

    def kernel(*refs):
        ins, bank_ref, refs = refs[:kinds], refs[kinds], refs[kinds + 1 :]
        outs, far_ref, refs = refs[:kinds], refs[kinds], refs[kinds + 1 :]
        z_send, z_recv, send, recv, local, b_send, b_recv = refs
        e, z = lax.axis_index("expert"), lax.axis_index("group")

        def loc(r, q, c):
            s, kind = c // kinds, c % kinds
            row = (lax.rem(z - s + groups, groups) * n + flip(e, r)) * rows
            return outs[kind].at[pl.ds(pl.multiple_of(row, 16), rows), :]

        def far(c):
            s, kind = c // kinds, c % kinds
            return remote(
                ins[kind], loc(0, 0, kind), z_send.at[c], z_recv.at[c],
                {"group": lax.rem(z + s, groups)},
            )

        def landed(c):
            remote(
                loc(0, 0, c), loc(0, 0, c), z_send.at[c], z_recv.at[c],
                {"group": lax.rem(z + c // kinds, groups)},
            ).wait_recv()

        first = lax.rem(z + 1, split) * per
        follow = remote(
            bank_ref.at[pl.ds(first, per)], far_ref, b_send, b_recv, {"group": lax.rem(z + 1, groups)}
        )
        gather = Gather(
            e, lambda c: ins[c] if c < kinds else loc(0, 0, c), loc,
            [c // kinds % 2 for c in range(count)], send, recv,
        )
        near = list(range(kinds))
        later = list(range(kinds, count))
        greet(
            plane_devices(e) + [{"group": lax.rem(z + s, groups)} for s in range(1, groups)]
        )
        for c in later:
            far(c).start()
        for c in near:
            gather.begin(c)
            pltpu.make_async_copy(ins[c], loc(0, 0, c), local.at[c]).start()
        follow.start()
        gather.stage(near, (2, 4))
        gather.stage(near, (6,))
        for c in later:
            landed(c)
            gather.begin(c)
        gather.stage(later, (2, 4))
        gather.stage(later, (6,))
        gather.stage(near + later, (1, 3, 5, 7))
        for c in later:
            far(c).wait_send()
        for c in near + later:
            gather.finish(c)
        for c in near:
            pltpu.make_async_copy(ins[c], loc(0, 0, c), local.at[c]).wait()
        follow.wait()

    vmem = pl.BlockSpec(memory_space=pltpu.VMEM)
    shapes = [(groups * n * rows, one.shape[1]) for one in shares]
    return pl.pallas_call(
        kernel,
        in_specs=[vmem] * kinds + [ANY_SPEC],
        out_specs=[vmem] * kinds + [ANY_SPEC],
        out_shape=[jax.ShapeDtypeStruct(shape, BF16) for shape in shapes]
        + [jax.ShapeDtypeStruct((per,) + bank.shape[1:], BF16)],
        scratch_shapes=[
            pltpu.SemaphoreType.DMA((count,)),
            pltpu.SemaphoreType.DMA((count,)),
            pltpu.SemaphoreType.DMA((n, count)),
            pltpu.SemaphoreType.DMA((n, count)),
            pltpu.SemaphoreType.DMA((kinds,)),
            pltpu.SemaphoreType.DMA,
            pltpu.SemaphoreType.DMA,
        ],
        compiler_params=params(1),
        cost_estimate=cost(1e9, 1e6),
        name="plane_weights",
    )(*shares, bank)


def attention_pairs(n, at_me, q_ref, keys, out_ref):
    width = KEY_VALUE_HEADS * HEAD_SIZE
    prompt_ok, cont_ok = attention_masks_plain(n, at_me)

    def pair(j, carry):
        q_at = pl.ds(pl.multiple_of(j * 384, 128), 384)
        k_at = pl.ds(pl.multiple_of(j * 128, 128), 128)
        v_at = pl.ds(pl.multiple_of(width + j * 128, 128), 128)
        q_top, q_low = q_ref[:PR_DEV, q_at], q_ref[PR_DEV:, q_at]
        k_two, v_two = keys[:, k_at], keys[:, v_at]
        tops, lows = [], []
        for g in range(2):
            key = k_two[:, g * HEAD_SIZE : (g + 1) * HEAD_SIZE]
            value = v_two[:, g * HEAD_SIZE : (g + 1) * HEAD_SIZE]
            top, low = group_probs(
                head_rows(q_top, g * 192), head_rows(q_low, g * 192), key, prompt_ok, cont_ok, n
            )
            tops.append(row_heads(mm(top.astype(BF16), value[: n * PR_DEV])))
            lows.append(row_heads(mm(low.astype(BF16), value)))
        out_ref[:PR_DEV, q_at] = jnp.concatenate(tops, axis=1).astype(BF16)
        out_ref[PR_DEV:, q_at] = jnp.concatenate(lows, axis=1).astype(BF16)
        return carry

    lax.fori_loop(0, KEY_VALUE_HEADS // 2, pair, 0)


def flip_columns(slot, me, limit):
    bit, total = 1, jnp.zeros_like(slot)
    while bit < limit:
        total = total + bit * lax.rem(slot // bit + me // bit, 2)
        bit *= 2
    return total


def attention_masks_plain(n, me):
    shape = (3 * PR_DEV, n * PR_DEV)
    token = lax.rem(lax.broadcasted_iota(jnp.int32, shape, 0), PR_DEV)
    column = lax.broadcasted_iota(jnp.int32, shape, 1)
    owner = flip_columns(column // PR_DEV, me, n)
    prompt_ok = owner * PR_DEV + lax.rem(column, PR_DEV) <= me * PR_DEV + token
    slots = CONT // PR_DEV
    shape = (3 * PR_DEV, CONT)
    token = lax.rem(lax.broadcasted_iota(jnp.int32, shape, 0), PR_DEV)
    column = lax.broadcasted_iota(jnp.int32, shape, 1)
    local = lax.rem(me, slots)
    owner = flip_columns(column // PR_DEV, local, slots)
    cont_ok = owner * PR_DEV + lax.rem(column, PR_DEV) <= local * PR_DEV + token
    return prompt_ok, cont_ok


def turn_heads(x, cosine, sine):
    half = HEAD_SIZE // 2
    lane = lax.broadcasted_iota(jnp.int32, cosine.shape, 1)
    first = lax.rem(lane, HEAD_SIZE) < half
    blocks = []
    for lo in range(0, x.shape[1], LANES):
        one = x[:, lo : lo + LANES]
        other = jnp.where(first, pltpu.roll(one, LANES - half, 1), pltpu.roll(one, half, 1))
        blocks.append(one * cosine + other * sine)
    return jnp.concatenate(blocks, axis=1)


def plane_attention(normed, weight, cosine, sine, micro):
    rows, model = normed.shape
    tokens = rows // micro
    width = 2 * KEY_VALUE_HEADS * HEAD_SIZE
    query_width = QUERY_HEADS * HEAD_SIZE
    n, tile = 8, 512

    def kernel(x_ref, w_ref, cos_ref, sin_ref, out_ref, q_ref, slots, own, keys, send, recv, local):
        e = lax.axis_index("expert")
        gather = Gather(
            e, lambda c: own.at[c], lambda r, q, c: slots.at[q, c], [c % 2 for c in range(micro)],
            send, recv,
        )

        def project(lo, turned):
            wide = mm(x_ref[...], w_ref[:, lo : lo + tile])
            for c in range(micro):
                part = wide[c * tokens : (c + 1) * tokens]
                if turned:
                    part = turn_heads(part, cos_ref[...], sin_ref[...])
                yield c, part.astype(BF16)

        for lo in range(0, width, tile):
            for c, part in project(query_width + lo, lo < width // 2):
                own[c, :, lo : lo + tile] = part
        greet(plane_devices(e))
        for c in range(micro):
            gather.begin(c)
            pltpu.make_async_copy(own.at[c], slots.at[0, c], local.at[c]).start()
        for lo in range(0, query_width, tile):
            for c, part in project(lo, True):
                q_ref[c, :, lo : lo + tile] = part
        gather.stage(range(micro), (2, 4))
        gather.stage(range(micro), (6,))
        for c in range(micro):
            gather.stage([c], (1, 3, 5, 7))
            pltpu.make_async_copy(own.at[c], slots.at[0, c], local.at[c]).wait()
            load_keys(n, [slots.at[r, c] for r in range(n)], keys)
            attention_pairs(n, e, q_ref.at[c], keys, out_ref.at[c])
        for c in range(micro):
            gather.finish(c)

    vmem = pl.BlockSpec(memory_space=pltpu.VMEM)
    shape = jax.ShapeDtypeStruct((micro, tokens, query_width), BF16)
    return pl.pallas_call(
        kernel,
        in_specs=[vmem] * 4,
        out_specs=[vmem] * 3,
        out_shape=[shape, shape, jax.ShapeDtypeStruct((n, micro, tokens, width), BF16)],
        scratch_shapes=[
            pltpu.VMEM((micro, tokens, width), BF16),
            pltpu.VMEM((n * PR_DEV + CONT, width), BF16),
            pltpu.SemaphoreType.DMA((n, micro)),
            pltpu.SemaphoreType.DMA((n, micro)),
            pltpu.SemaphoreType.DMA((micro,)),
        ],
        compiler_params=params(2),
        cost_estimate=cost(1e9, 1e6),
        name="plane_attention",
    )(normed, weight, cosine, sine)


def plane_attention_backward(query, slots, d_mixed, cosine, sine):
    n, micro, tokens, width = slots.shape
    half = width // 2
    query_width = query.shape[2]
    pr = n * PR_DEV
    total = pr + CONT

    def kernel(q_ref, d_ref, kv_ref, cos_ref, sin_ref, out_ref, keys, grads, parts, *scratch):
        e = lax.axis_index("expert")
        red = Reduce(e, lambda r, c: parts.at[r, c], [c % 2 for c in range(micro)], *scratch)
        greet(plane_devices(e))
        prompt_ok, cont_ok = attention_masks_plain(n, e)

        def one_side(prob, d_rows, key, value, q_rows):
            d_prob = mm(d_rows, value, NT)
            delta = jnp.sum(prob * d_prob, axis=1, keepdims=True)
            d_score = (prob * (d_prob - delta)).astype(BF16)
            return (
                mm(d_score, key) * SCORE_SCALE,
                mm(d_score, q_rows, TN) * SCORE_SCALE,
                mm(prob.astype(BF16), d_rows, TN),
            )

        for c in range(micro):
            load_keys(n, [kv_ref.at[r, c] for r in range(n)], keys)

            def pair(j, carry):
                q_at = pl.ds(pl.multiple_of(j * 384, 128), 384)
                k_at = pl.ds(pl.multiple_of(j * 128, 128), 128)
                v_at = pl.ds(pl.multiple_of(half + j * 128, 128), 128)
                q_top, q_low = q_ref[c, :PR_DEV, q_at], q_ref[c, PR_DEV:, q_at]
                d_top, d_low = d_ref[c, :PR_DEV, q_at], d_ref[c, PR_DEV:, q_at]
                k_two, v_two = keys[:, k_at], keys[:, v_at]
                dq_tops, dq_lows, dks, dvs = [], [], [], []
                for g in range(2):
                    key = k_two[:, g * HEAD_SIZE : (g + 1) * HEAD_SIZE]
                    value = v_two[:, g * HEAD_SIZE : (g + 1) * HEAD_SIZE]
                    rows_top, rows_low = head_rows(q_top, g * 192), head_rows(q_low, g * 192)
                    top, low = group_probs(rows_top, rows_low, key, prompt_ok, cont_ok, n)
                    dq_top, dk_top, dv_top = one_side(
                        top, head_rows(d_top, g * 192), key[:pr], value[:pr], rows_top
                    )
                    dq_low, dk_low, dv_low = one_side(
                        low, head_rows(d_low, g * 192), key, value, rows_low
                    )
                    dq_tops.append(row_heads(dq_top))
                    dq_lows.append(row_heads(dq_low))
                    dks.append(jnp.concatenate([dk_low[:pr] + dk_top, dk_low[pr:]], axis=0))
                    dvs.append(jnp.concatenate([dv_low[:pr] + dv_top, dv_low[pr:]], axis=0))
                for lo, found in ((0, dq_tops), (PR_DEV, dq_lows)):
                    there = slice(lo, lo + PR_DEV)
                    turned = turn_heads(
                        jnp.concatenate(found, axis=1), cos_ref[there, :], sin_ref[there, :]
                    )
                    out_ref[c, there, q_at] = turned.astype(BF16)
                grads[:, k_at] = jnp.concatenate(dks, axis=1).astype(BF16)
                grads[:, v_at] = jnp.concatenate(dvs, axis=1).astype(BF16)
                return carry

            lax.fori_loop(0, KEY_VALUE_HEADS // 2, pair, 0)
            for r in (7, 5, 3, 1, 6, 2, 4, 0):
                parts[r, c, :PR_DEV, :] = grads[r * PR_DEV : (r + 1) * PR_DEV, :]
                if r < CONT // PR_DEV:
                    lo = (n + r) * PR_DEV
                    parts[r, c, PR_DEV:, :] = grads[lo : lo + PR_DEV, :]
                else:
                    parts[r, c, PR_DEV:, :] = jnp.zeros((PR_DEV, width), BF16)
                if r % 2:
                    red.begin(r, c)
        red.diagonal(range(micro))
        red.sides(range(micro))
        step = 16
        for c in range(micro):
            terms = red.total(c)

            def last(i, carry):
                at = pl.ds(pl.multiple_of(i * step, step), step)
                total = terms[0][at, :].astype(F32)
                for term in terms[1:]:
                    total = total + term[at, :].astype(F32)
                turned = turn_heads(total[:, :half], cos_ref[at, :], sin_ref[at, :])
                out_ref[c, at, query_width : query_width + half] = turned.astype(BF16)
                out_ref[c, at, query_width + half :] = total[:, half:].astype(BF16)
                return carry

            lax.fori_loop(0, tokens // step, last, 0)
        for c in range(micro):
            red.finish(c)

    vmem = pl.BlockSpec(memory_space=pltpu.VMEM)
    return pl.pallas_call(
        kernel,
        in_specs=[vmem] * 5,
        out_specs=vmem,
        out_shape=jax.ShapeDtypeStruct((micro, tokens, query_width + width), BF16),
        scratch_shapes=[
            pltpu.VMEM((total, width), BF16),
            pltpu.VMEM((total, width), BF16),
            pltpu.VMEM((n, micro, tokens, width), BF16),
        ]
        + reduce_scratch(micro, tokens, width),
        compiler_params=params(3),
        cost_estimate=cost(1e9, 1e6),
        name="plane_attention_backward",
    )(query, d_mixed, slots, cosine, sine)


def plane_dispatch(payload, ranks, bank, where, per, cap, model, experts):
    micro, tokens, width = payload.shape
    n, split = 8, 2
    groups = lax.axis_size("group")
    count = split * micro

    def kernel(
        at_ref, own_ref, rank_ref, bank_ref, out, weights, far_ref,
        slots, z_send, z_recv, send, recv, b_send, b_recv,
    ):
        e, z = lax.axis_index("expert"), lax.axis_index("group")
        lane = lax.broadcasted_iota(jnp.int32, (cap, LANES), 1)

        def own(c):
            return own_ref.at[c] if c < micro else slots.at[0, c]

        gather = Gather(
            e, own, lambda r, q, c: slots.at[q, c], [c % 2 for c in range(count)], send, recv
        )

        def turned(m):
            return remote(
                own_ref.at[m], slots.at[0, micro + m], z_send.at[m], z_recv.at[m],
                {"group": partner(z)},
            )

        def use(r, c):
            rows = own(c)[...] if r == 0 else slots[r, c]
            b = r * count + c
            for k in range(per):
                got = mm(pick(rank_ref[b, k : k + 1, :], cap), rows)
                out[k, b * cap : (b + 1) * cap, :] = got[:, :model].astype(BF16)
                first = at_ref[2] + k
                mine = (lane == first) | (lane == first + experts)
                total = jnp.sum(jnp.where(mine, got[:, model:], 0.0), axis=1, keepdims=True)
                weights[k, b * cap : (b + 1) * cap, :] = jnp.broadcast_to(total, (cap, LANES))

        last = groups - 1
        first = lax.rem(z + last, split) * per
        follow = remote(
            bank_ref.at[pl.ds(first, 1)], far_ref, b_send, b_recv,
            {"group": lax.rem(z + last, groups)},
        )
        greet(plane_devices(e) + [{"group": lax.rem(z + s, groups)} for s in (1, last)])
        for m in range(micro):
            turned(m).start()
        follow.start()
        for m in range(micro):
            gather.begin(m)
        for m in range(micro):
            use(0, m)
        for m in range(micro):
            turned(m).wait_recv()
            gather.begin(micro + m)
            use(0, micro + m)
        gather.forward_all(range(count), use)
        for m in range(micro):
            turned(m).wait_send()
        for c in range(count):
            gather.finish(c)
        follow.wait()

    vmem = pl.BlockSpec(memory_space=pltpu.VMEM)
    total = n * count * cap
    return pl.pallas_call(
        kernel,
        in_specs=[SMEM_SPEC, vmem, vmem, ANY_SPEC],
        out_specs=[vmem, vmem, ANY_SPEC],
        out_shape=[
            jax.ShapeDtypeStruct((per, total, model), BF16),
            jax.ShapeDtypeStruct((per, total, LANES), F32),
            jax.ShapeDtypeStruct((1,) + bank.shape[1:], BF16),
        ],
        scratch_shapes=[
            pltpu.VMEM((n, count, tokens, width), BF16),
            pltpu.SemaphoreType.DMA((micro,)),
            pltpu.SemaphoreType.DMA((micro,)),
            pltpu.SemaphoreType.DMA((n, count)),
            pltpu.SemaphoreType.DMA((n, count)),
            pltpu.SemaphoreType.DMA,
            pltpu.SemaphoreType.DMA,
        ],
        compiler_params=params(4),
        cost_estimate=cost(1e9, 1e6),
        name="plane_dispatch",
    )(where, payload, ranks, bank)


def plane_return(rows, ranks, next_term, last_terms, micro, tokens, cap):
    per, _, width = rows.shape
    n, split = 8, 2
    groups = lax.axis_size("group")
    count = split * micro
    chunks = list(range(micro, count)) + list(range(micro))

    def kernel(rank_ref, in_ref, next_ref, last_ref, out, next_far, last_far, *refs):
        parts, z_out, z_in, z_send, z_recv, t_send, t_recv, scratch = *refs[:7], refs[7:]
        e, z = lax.axis_index("expert"), lax.axis_index("group")
        red = Reduce(e, lambda r, c: parts.at[r, c], [c % 2 for c in range(count)], *scratch)

        def produce(r, c):
            b = r * count + c
            total = None
            for k in range(per):
                one = mm(
                    pick(rank_ref[b, k : k + 1, :], cap), in_ref[k, b * cap : (b + 1) * cap, :], TN
                )
                total = one if total is None else total + one
            parts[r, c] = total.astype(BF16)

        def turned(m):
            return remote(
                z_out.at[m], z_in.at[m], z_send.at[m], z_recv.at[m], {"group": partner(z)}
            )

        follow = [
            remote(
                next_ref, next_far, t_send.at[0], t_recv.at[0], {"group": lax.rem(z + 1, groups)}
            ),
            remote(
                last_ref.at[0], last_far, t_send.at[1], t_recv.at[1],
                {"group": lax.rem(z + groups - 1, groups)},
            ),
        ]
        greet(plane_devices(e) + [{"group": lax.rem(z + s, groups)} for s in (1, groups - 1)])
        for one in follow:
            one.start()
        for r in (7, 3, 5):
            for c in chunks:
                produce(r, c)
                red.begin(r, c)
        for c in chunks:
            produce(6, c)
        red.diagonal(chunks)
        for r in (2, 4):
            for c in chunks:
                produce(r, c)
        red.sides(chunks)
        for c in chunks:
            produce(1, c)
            red.begin(1, c)
        for c in chunks:
            produce(0, c)
        for c in chunks:
            terms = red.total(c)
            if c >= micro:
                add_rows(z_out.at[c - micro], terms)
                turned(c - micro).start()
            else:
                turned(c).wait_recv()
                add_rows(out.at[c], terms + [z_in.at[c]])
        for m in range(micro):
            turned(m).wait_send()
        for c in chunks:
            red.finish(c)
        for one in follow:
            one.wait()

    vmem = pl.BlockSpec(memory_space=pltpu.VMEM)
    return pl.pallas_call(
        kernel,
        in_specs=[vmem, vmem, ANY_SPEC, ANY_SPEC],
        out_specs=[vmem, ANY_SPEC, ANY_SPEC],
        out_shape=[
            jax.ShapeDtypeStruct((micro, tokens, width), F32),
            jax.ShapeDtypeStruct(next_term.shape, BF16),
            jax.ShapeDtypeStruct(next_term.shape, BF16),
        ],
        scratch_shapes=[
            pltpu.VMEM((n, count, tokens, width), BF16),
            pltpu.VMEM((micro, tokens, width), BF16),
            pltpu.VMEM((micro, tokens, width), BF16),
            pltpu.SemaphoreType.DMA((micro,)),
            pltpu.SemaphoreType.DMA((micro,)),
            pltpu.SemaphoreType.DMA((2,)),
            pltpu.SemaphoreType.DMA((2,)),
        ]
        + reduce_scratch(count, tokens, width),
        compiler_params=params(5),
        cost_estimate=cost(1e9, 1e6),
        name="plane_return",
    )(ranks, rows, next_term, last_terms)


def plane_gradients(products, router, gains, terms, swapped, groups):
    n = 8
    depth = products[0][0].shape[1]
    widths = [b.shape[1] for a, b in products]
    width = sum(widths) + LANES
    experts = router.shape[1]
    rows = depth // (groups * n)
    tile = 512
    flat = [x for pair in products for x in pair]

    def kernel(*refs):
        ins, refs = refs[: len(flat)], refs[len(flat) :]
        router_ref, gains_ref, term_ref, swap_ref, out, far_ref, swap_far, *refs = refs
        wide, parts, z_out, z_in, z_send, z_recv, send, recv, t_send, t_recv, s_send, s_recv = refs[:12]
        scratch = refs[12:]
        e, z = lax.axis_index("expert"), lax.axis_index("group")
        red = Reduce(e, lambda r, c: parts.at[r, c], [c % 2 for c in range(groups)], *scratch)
        greet(
            plane_devices(e)
            + [{"group": lax.rem(z + s, groups)} for s in range(1, groups)]
        )
        follow = remote(
            term_ref.at[1], far_ref, t_send, t_recv, {"group": lax.rem(z + groups - 1, groups)}
        )
        exchange = remote(swap_ref, swap_far, s_send, s_recv, {"group": partner(z)})
        exchange.start()
        follow.start()

        def cut(lo, size):
            for r in range(n):
                for s in range(groups):
                    row = (lax.rem(z + s, groups) * n + flip(e, r)) * rows
                    at = pl.ds(pl.multiple_of(row, 16), rows)
                    parts[r, s, :, lo : lo + size] = wide[at, :size].astype(BF16)

        lo = 0
        for i, count in enumerate(widths):
            for start in range(0, count, tile):
                size = min(tile, count - start)
                wide[:, :size] = mm(ins[2 * i][...], ins[2 * i + 1][:, start : start + size], TN)
                cut(lo, size)
                lo += size
        wide[:, :LANES] = jnp.zeros((depth, LANES), F32)
        wide[:, experts : 2 * experts] = router_ref[...]
        wide[:, : gains.shape[0]] = gains_ref[...].T
        cut(lo, LANES)

        chunks = list(range(1, groups)) + [0]
        for r in (7, 3, 5, 1):
            for c in chunks:
                red.begin(r, c)
        red.diagonal(chunks)
        red.sides(chunks)

        def far(s):
            return remote(
                z_out.at[s], z_in.at[s], z_send.at[s], z_recv.at[s],
                {"group": lax.rem(z + s, groups)},
            )

        for c in chunks:
            add_rows(z_out.at[c], red.total(c))
            if c:
                far(c).start()
        for c in range(1, groups):
            far(c).wait_recv()
        def place(r):
            return out.at[pl.ds(pl.multiple_of(flip(e, r) * rows, 16), rows), :]

        add_rows(place(0), [z_out.at[0]] + [z_in.at[c] for c in range(1, groups)])
        middle = width // 2 // LANES * LANES
        spans = [(0, middle), (middle, width)]

        def loc(r, q, c):
            row = pl.multiple_of(flip(e, r) * rows, 16)
            return out.at[pl.ds(row, rows), spans[c][0] : spans[c][1]]

        gather = Gather(e, lambda c: loc(0, 0, c), loc, [0, 1], send, recv)
        for c in range(2):
            gather.begin(c)
        gather.forward_all(range(2))
        for c in range(2):
            gather.finish(c)
        follow.wait()
        exchange.wait()
        for c in range(1, groups):
            far(c).wait_send()
        for c in chunks:
            red.finish(c)

    vmem = pl.BlockSpec(memory_space=pltpu.VMEM)
    return pl.pallas_call(
        kernel,
        in_specs=[vmem] * (len(flat) + 2) + [ANY_SPEC] * 2,
        out_specs=[vmem, ANY_SPEC, ANY_SPEC],
        out_shape=[
            jax.ShapeDtypeStruct((n * rows, width), BF16),
            jax.ShapeDtypeStruct(terms.shape[1:], BF16),
            jax.ShapeDtypeStruct(swapped.shape, BF16),
        ],
        scratch_shapes=[
            pltpu.VMEM((depth, tile), F32),
            pltpu.VMEM((n, groups, rows, width), BF16),
            pltpu.VMEM((groups, rows, width), BF16),
            pltpu.VMEM((groups, rows, width), BF16),
            pltpu.SemaphoreType.DMA((groups,)),
            pltpu.SemaphoreType.DMA((groups,)),
            pltpu.SemaphoreType.DMA((n, 2)),
            pltpu.SemaphoreType.DMA((n, 2)),
            pltpu.SemaphoreType.DMA,
            pltpu.SemaphoreType.DMA,
            pltpu.SemaphoreType.DMA,
            pltpu.SemaphoreType.DMA,
        ]
        + reduce_scratch(groups, rows, width),
        compiler_params=params(6),
        cost_estimate=cost(1e9, 1e6),
        name="plane_gradients",
    )(*flat, router, gains, terms, swapped)


def gather_flags(halves, where, per, cap, model):
    n, each, tokens, width = halves[0].shape
    count = each * len(halves)

    def kernel(at_ref, *refs):
        ins, (out, ranks, flags) = refs[: len(halves)], refs[len(halves) :]
        row = lax.broadcasted_iota(jnp.int32, (tokens, tokens), 0)
        col = lax.broadcasted_iota(jnp.int32, (tokens, tokens), 1)
        before = jnp.where(row < col, 1.0, 0.0).astype(BF16)
        for b in range(count):
            payload = ins[b // each][0, b % each]
            flags[...] = payload[:, model:].astype(F32).T
            picked = jnp.concatenate(
                [flags[pl.ds(at_ref[2] + k, 1), :] for k in range(per)], axis=0
            )
            slot = jnp.where(picked > 0.0, mm(picked.astype(BF16), before), -1.0)
            ranks[b] = slot
            for k in range(per):
                out[k, b * cap : (b + 1) * cap, :] = mm(
                    pick(slot[k : k + 1], cap), payload[:, :model]
                ).astype(BF16)

    return pl.pallas_call(
        kernel,
        grid_spec=pltpu.PrefetchScalarGridSpec(
            num_scalar_prefetch=1,
            grid=(n,),
            in_specs=[
                pl.BlockSpec(
                    (1, each, tokens, width),
                    lambda r, at: (jnp.bitwise_xor(at[1], r), 0, 0, 0),
                )
            ]
            * len(halves),
            out_specs=[
                pl.BlockSpec((per, count * cap, model), lambda r, at: (0, r, 0)),
                pl.BlockSpec((count, per, tokens), lambda r, at: (r, 0, 0)),
            ],
            scratch_shapes=[pltpu.VMEM((LANES, tokens), F32)],
        ),
        out_shape=[
            jax.ShapeDtypeStruct((per, n * count * cap, model), BF16),
            jax.ShapeDtypeStruct((n * count, per, tokens), F32),
        ],
        cost_estimate=cost(5e9, 3e7),
        name="gather_flags",
    )(where, *halves)


def scatter_rows(rows, ranks, where, n, count, tokens, cap):
    per, _, width = rows.shape

    half = count // 2

    def kernel(at_ref, rank_ref, in_ref, *outs):
        for b in range(count):
            total = None
            for k in range(per):
                one = mm(
                    pick(rank_ref[b, k : k + 1, :], cap), in_ref[k, b * cap : (b + 1) * cap, :], TN
                )
                total = one if total is None else total + one
            outs[b // half][0, b % half] = total.astype(BF16)

    return pl.pallas_call(
        kernel,
        grid_spec=pltpu.PrefetchScalarGridSpec(
            num_scalar_prefetch=1,
            grid=(n,),
            in_specs=[
                pl.BlockSpec((count, per, tokens), lambda r, at: (r, 0, 0)),
                pl.BlockSpec((per, count * cap, width), lambda r, at: (0, r, 0)),
            ],
            out_specs=[
                pl.BlockSpec(
                    (1, half, tokens, width), lambda r, at: (jnp.bitwise_xor(at[1], r), 0, 0, 0)
                )
            ]
            * 2,
        ),
        out_shape=[jax.ShapeDtypeStruct((n, half, tokens, width), BF16)] * 2,
        cost_estimate=cost(5e9, 3e7),
        name="scatter_rows",
    )(where, ranks, rows)


def expert_steps(rows_in, grads_in, weights, bank, far, experts, tile):
    per, total, model = rows_in.shape
    part, ff = bank.shape[2:]
    groups = model // part
    steps = total // tile
    split = 2
    here = bank.shape[0]
    last = groups - 1

    def kernel(x_ref, d_ref, w_ref, *refs):
        sources, o_ref, r_ref, refs = refs[:groups], refs[groups], refs[groups + 1], refs[groups + 2 :]
        outs, got_ref, refs = refs[:groups], refs[groups], refs[groups + 1 :]
        acc_wide, acc_down, wide_all, down_all, early, sems, w_send, w_recv, g_send, g_recv = refs
        k, step = pl.program_id(0), pl.program_id(1)
        me, mine_z = lax.axis_index("expert"), lax.axis_index("group")
        own_first = lax.rem(mine_z, split) * per

        def rows_of(index, z):
            at_z = pl.ds(pl.multiple_of(z * part, 128), part)
            wide, down = wide_all.at[index], down_all.at[index]
            return [wide.at[at_z, :ff], wide.at[at_z, ff:], down.at[at_z, :]]

        def loads(index):
            copies = []
            for s in range(groups - index):
                source = sources[s].at[own_first + index if s == 0 else index]
                there = rows_of(index, lax.rem(mine_z - s + groups, groups))
                for i, dst in enumerate(there):
                    copies.append(
                        pltpu.make_async_copy(source.at[i], dst, sems.at[index, 3 * s + i])
                    )
            return copies

        def late_weights(z):
            source = sources[0].at[lax.rem(mine_z + last, split) * per + 1]
            return [
                remote(
                    source.at[i], dst, w_send.at[i], w_recv.at[i],
                    {"group": lax.rem(mine_z + last, groups)},
                )
                for i, dst in enumerate(rows_of(1, z))
            ]

        early_term = remote(
            early, got_ref, g_send, g_recv, {"group": lax.rem(mine_z + 1, groups)}
        )

        @pl.when((k == 0) & (step == 0))
        def _():
            for index in range(per):
                for one in loads(index):
                    one.start()
            greet([{"group": lax.rem(mine_z + s, groups)} for s in (1, last)])
            for one in late_weights(mine_z):
                one.start()
            for one in loads(0):
                one.wait()

        @pl.when((k == 1) & (step == 0))
        def _():
            early_term.start()
            for one in loads(1):
                one.wait()
            for one in late_weights(lax.rem(mine_z + 1, groups)):
                one.wait_recv()
            for one in late_weights(mine_z):
                one.wait_send()

        wide_ref, down_ref = wide_all.at[k], down_all.at[k]
        x, d = x_ref[0], d_ref[0]
        w = w_ref[0, :, 0:1]
        pre = mm(x, wide_ref[...])
        gate_pre, up_pre = pre[:, :ff], pre[:, ff:]
        sig = 1.0 / (1.0 + jnp.exp(-gate_pre))
        silu = gate_pre * sig
        active_wide = silu * up_pre
        active = active_wide.astype(BF16)
        o_ref[0] = (mm(active, down_ref[...], NT) * w).astype(BF16)
        d_raw = mm(d, down_ref[...])
        d_gates = jnp.sum(active.astype(F32) * d_raw, axis=1, keepdims=True)
        d_active = d_raw * w
        d_up = (d_active * silu).astype(BF16)
        d_gate = (d_active * up_pre * sig * (1.0 + gate_pre * (1.0 - sig))).astype(BF16)
        d_both = jnp.concatenate([d_gate, d_up], axis=1)
        r_ref[0, :, :model] = mm(d_both, wide_ref[...], NT).astype(BF16)
        high = d_gates.astype(BF16).astype(F32)
        lane = lax.broadcasted_iota(jnp.int32, (tile, LANES), 1)
        e = me * here + own_first + k
        r_ref[0, :, model:] = (
            jnp.where(lane == e, high, 0.0) + jnp.where(lane == e + experts, d_gates - high, 0.0)
        ).astype(BF16)
        new_wide = mm(x, d_both, TN)
        new_down = mm((active_wide * w).astype(BF16), d, TN)

        @pl.when(step == 0)
        def _():
            acc_wide[...] = new_wide
            acc_down[...] = new_down

        @pl.when(step > 0)
        def _():
            acc_wide[...] += new_wide
            acc_down[...] += new_down

        @pl.when(step == steps - 1)
        def _():
            for s in range(groups):
                z = lax.rem(mine_z + s, groups)
                at_z = pl.ds(pl.multiple_of(z * part, 128), part)

                def put(dst):
                    dst[0] = acc_wide[at_z, :ff].astype(BF16)
                    dst[1] = acc_wide[at_z, ff:].astype(BF16)
                    dst[2] = acc_down[:, at_z].T.astype(BF16)

                if s == 1:
                    pl.when(k == 0)(lambda: put(early))
                    pl.when(k == 1)(lambda: put(outs[s]))
                else:
                    put(outs[s].at[0])

        @pl.when((k == per - 1) & (step == steps - 1))
        def _():
            early_term.wait()

    grad = pl.BlockSpec((1, 3, part, ff), lambda k, t: (k, 0, 0, 0), pipeline_mode=pl.Buffered(1))
    single = pl.BlockSpec((3, part, ff), lambda k, t: (0, 0, 0), pipeline_mode=pl.Buffered(1))
    rows = lambda width: pl.BlockSpec((1, tile, width), lambda k, t: (k, t, 0))
    out = pl.pallas_call(
        kernel,
        grid=(per, steps),
        in_specs=[rows(model), rows(model), rows(LANES)] + [ANY_SPEC] * groups,
        out_specs=[rows(model), rows(model + LANES)]
        + [single if s == 1 else grad for s in range(groups)]
        + [ANY_SPEC],
        out_shape=[
            jax.ShapeDtypeStruct((per, total, model), BF16),
            jax.ShapeDtypeStruct((per, total, model + LANES), BF16),
        ]
        + [
            jax.ShapeDtypeStruct((3, part, ff) if s == 1 else (per, 3, part, ff), BF16)
            for s in range(groups)
        ]
        + [jax.ShapeDtypeStruct((3, part, ff), BF16)],
        scratch_shapes=[
            pltpu.VMEM((model, 2 * ff), F32),
            pltpu.VMEM((ff, model), F32),
            pltpu.VMEM((per, model, 2 * ff), BF16),
            pltpu.VMEM((per, model, ff), BF16),
            pltpu.VMEM((3, part, ff), BF16),
            pltpu.SemaphoreType.DMA((per, 3 * groups)),
            pltpu.SemaphoreType.DMA((3,)),
            pltpu.SemaphoreType.DMA((3,)),
            pltpu.SemaphoreType.DMA,
            pltpu.SemaphoreType.DMA,
        ],
        compiler_params=params(7),
        cost_estimate=cost(18 * per * total * model * ff, 10 * per * total * model),
        name="expert_steps",
    )(rows_in, grads_in, weights, bank, *far)
    return out[0], out[1], list(out[2 : 2 + groups]), out[2 + groups]


def merge_grads(which, at, terms):
    per, _, part, ff = terms[0].shape
    flat, places = [], []
    for one in terms:
        places.append(len(flat))
        flat += one if isinstance(one, list) else [one]
    split = 2
    tile = LANES

    def kernel(at_ref, *refs):
        ins, out = refs[: len(flat)], refs[len(flat)]
        for k in range(per):
            for parity in range(split):
                value = None
                for s in range(parity, len(terms), split):
                    whole = not isinstance(terms[s], list)
                    more = ins[places[s]][k, 0] if whole else ins[places[s] + k][0]
                    more = more.astype(F32)
                    value = more if value is None else value + more
                index = lax.rem(at_ref[0] + parity, split) * per + k
                out[index] = value.T if which == 2 else value

    if which == 2:
        spec = pl.BlockSpec((split * per, ff, tile), lambda t: (0, 0, t))
        shape = (split * per, ff, part)
    else:
        spec = pl.BlockSpec((split * per, tile, ff), lambda t: (0, t, 0))
        shape = (split * per, part, ff)
    return pl.pallas_call(
        kernel,
        grid=(part // tile,),
        in_specs=[SMEM_SPEC]
        + [
            pl.BlockSpec((per, 1, tile, ff), lambda t: (0, which, t, 0))
            if one.ndim == 4
            else pl.BlockSpec((1, tile, ff), lambda t: (which, t, 0))
            for one in flat
        ],
        out_specs=spec,
        out_shape=jax.ShapeDtypeStruct(shape, F32),
        cost_estimate=cost(1e8, 6e6),
        name="merge_grads",
    )(at, *flat)


def layer_plane(
    tokens,
    cotangent,
    routes,
    norm_one,
    query_key_value_weight,
    out_weight,
    norm_two,
    router_weight,
    gate_weight,
    up_weight,
    down_weight,
):
    n = lax.axis_size("expert")
    groups = lax.axis_size("group")
    me = lax.axis_index("expert")
    z = lax.axis_index("group")
    micro, count, model = tokens.shape
    exp_here, part, ff = gate_weight.shape
    experts = router_weight.shape[1]
    split = 2
    per = exp_here // split
    query_width = QUERY_HEADS * HEAD_SIZE
    kv_width = KEY_VALUE_HEADS * HEAD_SIZE
    cap = max(2, 3 * TOPK * PR_DEV // experts)
    where = jnp.stack([z, me, me * exp_here + (z % split) * per, (z % split) * per]).astype(jnp.int32)
    rows_here = part // n
    rows = micro * count

    misc = jnp.concatenate(
        [
            norm_one[:, None],
            norm_two[:, None],
            jnp.zeros((part, experts - 2), BF16),
            router_weight,
            jnp.zeros((part, LANES - 2 * experts), BF16),
        ],
        axis=1,
    )
    cut = lambda x: lax.dynamic_slice_in_dim(x, me * rows_here, rows_here, axis=0)
    shares = [cut(query_key_value_weight), jnp.concatenate([cut(out_weight), cut(misc)], axis=1)]
    bank = jnp.stack([gate_weight, up_weight, jnp.swapaxes(down_weight, 1, 2)], axis=1)

    expert_ids = jnp.arange(experts, dtype=jnp.int32)
    named = jnp.any(routes[..., None] == expert_ids, axis=2)
    pad = jnp.zeros((micro, count, LANES - experts), BF16)
    d_payload = jnp.concatenate([cotangent, named.astype(BF16), pad], axis=2)
    d_turned = turn(d_payload, 1, split)
    d_near = lax.all_gather(d_payload, "expert", axis=0)

    bank_two = lax.dynamic_slice_in_dim(bank, (z % split) * per, per, axis=0)
    qkv_full, rest_full, far_one = plane_weights(shares, bank, per)
    (bank_two, d_turned), qkv_full = lax.optimization_barrier(((bank_two, d_turned), qkv_full))
    far_two = shift(bank_two, 2)
    d_slots = [d_near, lax.all_gather(d_turned, "expert", axis=0)]
    out_full, misc_full = rest_full[:, :model], rest_full[:, model:]
    gain_one = misc_full[:, 0].astype(F32)
    gain_two = misc_full[:, 1].astype(F32)
    router_full = misc_full[:, experts : 2 * experts]

    grads_in, ranks = gather_flags(d_slots, where, per, cap, model)

    x = tokens.reshape(rows, model).astype(F32)
    inverse_one = lax.rsqrt(jnp.mean(x * x, axis=-1, keepdims=True) + 1e-05)
    normed = (x * inverse_one * gain_one).astype(BF16)
    cosine, sine = rope_tables(me, PR_DEV * n)
    cosine = jnp.concatenate([cosine] * 4, axis=1)
    sine = jnp.concatenate([-sine, sine] * 2, axis=1)
    mixed, query, kv_slots = plane_attention(normed, qkv_full, cosine, sine, micro)
    mixed = mixed.reshape(rows, query_width)
    hidden = x + mm(mixed, out_full)
    inverse_two = lax.rsqrt(jnp.mean(hidden * hidden, axis=-1, keepdims=True) + 1e-05)
    normed_two = (hidden * inverse_two * gain_two).astype(BF16)
    logits = mm(normed_two, router_full)
    chosen = named.reshape(rows, experts)
    logits = jnp.where(chosen, logits, NEG_FILL)
    top = jnp.max(logits, axis=-1, keepdims=True)
    raised = jnp.where(chosen, jnp.exp(logits - top), 0.0)
    gate_probs = raised / jnp.sum(raised, axis=-1, keepdims=True)

    high = gate_probs.astype(BF16)
    low = (gate_probs - high.astype(F32)).astype(BF16)
    payload = jnp.concatenate(
        [normed_two, high, low, jnp.zeros((rows, LANES - 2 * experts), BF16)], axis=1
    ).reshape(micro, count, model + LANES)
    rows_in, row_weights, far_three = plane_dispatch(
        payload, ranks, bank, where, per, cap, model, experts
    )
    weights_far = [far_one, far_two, far_three]
    tile = 512 if rows_in.shape[1] % 512 == 0 else 2 * micro * split * cap
    outs, backs, weight_terms, one_early = expert_steps(
        rows_in, grads_in, row_weights, bank, weights_far, experts, tile
    )
    back, one_late, three_early = plane_return(
        backs, ranks, weight_terms[1], weight_terms[3], micro, count, cap
    )
    back = back.reshape(rows, model + LANES)

    outs, back, late = lax.optimization_barrier((outs, back, weight_terms[2]))
    parts_near, parts_far = scatter_rows(outs, ranks, where, n, micro * split, count, cap)
    mixture_far = lax.psum_scatter(parts_far, "expert", scatter_dimension=0, tiled=False)
    mixture_near = lax.psum_scatter(parts_near, "expert", scatter_dimension=0, tiled=False)
    term_two = shift(late, 2)

    d_out = cotangent.reshape(rows, model).astype(F32)
    d_gates = back[:, model : model + experts] + back[:, model + experts : model + 2 * experts]
    d_logits = gate_probs * (d_gates - jnp.sum(gate_probs * d_gates, axis=-1, keepdims=True))
    router_grad = lax.dot_general(normed_two.astype(F32), d_logits, TN, precision=HIGHEST)
    d_normed_two = back[:, :model] + lax.dot_general(
        d_logits, router_full.astype(F32), NT, precision=HIGHEST
    )

    def rms_back(inputs, inverse, gain, upstream):
        scaled = gain * upstream
        return inverse * scaled - inputs * inverse * inverse * inverse * jnp.mean(
            scaled * inputs, axis=-1, keepdims=True
        )

    grad_two = jnp.sum(d_normed_two * hidden * inverse_two, axis=0)
    d_hidden = d_out + rms_back(hidden, inverse_two, gain_two, d_normed_two)
    d_attn = d_hidden.astype(BF16)
    d_mixed = mm(d_attn, out_full, NT).astype(BF16).reshape(micro, count, query_width)
    d_project = plane_attention_backward(query, kv_slots, d_mixed, cosine, -sine)
    d_project = d_project.reshape(rows, query_width + 2 * kv_width)
    d_normed = mm(d_project, qkv_full, NT)
    grad_one = jnp.sum(d_normed * x * inverse_one, axis=0)
    input_grad = (d_hidden + rms_back(x, inverse_one, gain_one, d_normed)).reshape(tokens.shape)
    gains = jnp.concatenate([grad_one[None], grad_two[None], jnp.zeros((6, model), F32)], axis=0)
    term_two, gains = lax.optimization_barrier((term_two, gains))
    dense, three_late, mixture_far = plane_gradients(
        [(mixed, d_attn), (normed, d_project)], router_grad, gains, weight_terms[3], mixture_far, groups
    )
    mixture = mixture_near.astype(F32) + mixture_far.astype(F32)
    block_out = (hidden + mixture.reshape(rows, model)).astype(BF16).reshape(tokens.shape)
    terms = [weight_terms[0], [one_early, one_late], term_two, [three_early, three_late]]
    gate_grad, up_grad, down_grad = [merge_grads(which, where, terms) for which in range(3)]
    misc_sum = dense[:, model + query_width + 2 * kv_width :].astype(F32)
    return (
        block_out,
        input_grad,
        misc_sum[:, 0],
        dense[:, model : model + query_width + 2 * kv_width].astype(F32),
        dense[:, :model].astype(F32),
        misc_sum[:, 1],
        misc_sum[:, experts : 2 * experts],
        gate_grad,
        up_grad,
        down_grad,
    )


def per_device(*arrays):
    n, groups = lax.axis_size("expert"), lax.axis_size("group")
    exp_here, part, ff = arrays[8].shape
    plane = (
        n == 8
        and exp_here % 2 == 0
        and groups == 4
        and exp_here == 4
        and part % (16 * n) == 0
        and part % LANES == 0
        and arrays[0].shape[0] == 2
    )
    return (layer_plane if plane else layer_general)(*arrays)


def solution(mesh):
    rows = P(None, ("group", "expert"), None)
    return jax.shard_map(
        per_device,
        mesh=mesh,
        in_specs=(
            rows,
            rows,
            rows,
            P("group"),
            P("group", None),
            P("group", None),
            P("group"),
            P("group", None),
            P("expert", "group", None),
            P("expert", "group", None),
            P("expert", None, "group"),
        ),
        out_specs=(
            rows,
            rows,
            P("group"),
            P("group", None),
            P("group", None),
            P("group"),
            P("group", None),
            P("expert", "group", None),
            P("expert", "group", None),
            P("expert", None, "group"),
        ),
        check_vma=False,
    )
```
